32 devices in a mesh: wide: 8 (over y, x, core), narrow: 4 (over z).
Axes of the slice: x: 2, y: 2, z: 4, core: 2. Of those that a mesh axis runs over, the one named last changes fastest.
Arguments:
- hidden_in: bfloat16 [4096, 1536], P('wide'), may hold values from -6 to 6
- cotangent: bfloat16 [4096, 1536], P('wide'), may hold values from -6 to 6
- lengths: int32 [8], replicated, may hold values from 1 to 2048, 4096 in all
- valid: int32 [4096], P('wide'), may hold values 0 or 1
- gain_one: bfloat16 [1536], replicated, may hold values from 0.5 to 1.5
- w_query: bfloat16 [1536, 1536], P(None, 'narrow'), may hold values from -0.15625 to 0.15625
- b_query: bfloat16 [1536], P('narrow'), may hold values from -3 to 3
- key_projection: bfloat16 [1536, 256], replicated, may hold values from -0.15625 to 0.15625
- key_bias_vector: bfloat16 [256], replicated, may hold values from -3 to 3
- value_projection: bfloat16 [1536, 256], replicated, may hold values from -0.15625 to 0.15625
- value_bias_vector: bfloat16 [256], replicated, may hold values from -3 to 3
- w_out: bfloat16 [1536, 1536], P('narrow'), may hold values from -0.625 to 0.625
- gain_two: bfloat16 [1536], replicated, may hold values from 0.5 to 1.5
- w_gate: bfloat16 [1536, 8960], P(None, 'narrow'), may hold values from -0.15625 to 0.15625
- w_up: bfloat16 [1536, 8960], P(None, 'narrow'), may hold values from -0.15625 to 0.15625
- w_down: bfloat16 [8960, 1536], P('narrow'), may hold values from -0.0625 to 0.0625
Outputs:
- output: bfloat16 [4096, 1536], P('wide')
- grad_hidden_in: bfloat16 [4096, 1536], P('wide')
- grad_gain_one: float32 [1536], P('wide')
- grad_w_query: float32 [1536, 1536], P('wide', 'narrow')
- grad_b_query: float32 [12, 128], P('narrow', 'wide')
- grad_w_key: float32 [1536, 256], P('wide')
- grad_b_key: float32 [256], P('wide')
- grad_w_value: float32 [1536, 256], P('wide')
- grad_b_value: float32 [256], P('wide')
- grad_w_out: float32 [1536, 1536], P('narrow', 'wide')
- grad_gain_two: float32 [1536], P('wide')
- grad_w_gate: float32 [1536, 8960], P('wide', 'narrow')
- grad_w_up: float32 [1536, 8960], P('wide', 'narrow')
- grad_w_down: float32 [8960, 1536], P('narrow', 'wide')
The draws below stay inside these ranges and needn't reach their ends.
Inputs may be any that keep to these rules, and one draw needn't show every extreme that they name: lengths in order of the sequences in the pack; they sum to 4096 and the longest is exactly 2048. `valid`: 1 marks a real token, 0 padding.
All inputs are finite; a program needn't handle non-finite values. No bound on the sum of `valid` on one device may be relied on, other than what follows from the above.
Results may differ from the reference program's by a relative error of at most 0.028.
Values may be sent and summed in bfloat16 or wider, within the bound.
No kernel may reach another device: no remote copies, remote signals or barrier semaphores. Data moves between devices by JAX's collectives and lax.ppermute only.
A program may use at most 256 MiB of HBM per device.

```python
import math
import jax
import jax.numpy as jnp
import numpy as np
from jax import lax

MODEL_WIDTH = 1536
QUERY_HEADS = 12
KEY_VALUE_HEADS = 2
HEAD_SIZE = 128
FF = 8960
PACKED_TOKENS = 4096
NSEQ = 8
SEQ_MOST = 2048
KEYBLK = 1024


def with_ends(values, own_key, smallest, top_value):
    longest = values.shape.index(max(values.shape))
    spots = []
    for shift in (0, 1):
        where = [jax.random.randint(jax.random.fold_in(own_key, axis), (), 0, length) for axis, length in enumerate(values.shape)]
        where[longest] = (where[longest] + shift) % values.shape[longest]
        spots.append(tuple(where))
    return values.at[spots[0]].set(smallest).at[spots[1]].set(top_value)


def block_levels(stream_key, extent, shards, low, top_value):
    level = 1.0
    for position, blocks in shards:
        steps = jax.random.uniform(jax.random.fold_in(jax.random.fold_in(stream_key, 6), position), (blocks,), jnp.float32, low / len(shards), top_value / len(shards))
        level = level * jnp.repeat(jnp.exp(steps), extent[position] // blocks).reshape((-1,) + (1,) * (len(extent) - 1 - position))
    return level


def split_up(number_of, total, reach, lean):
    portions = [(1 << 20) // math.isqrt(rank ** lean) + 1 for rank in range(2, number_of + 1)]
    spare, holding = total - reach - (number_of - 1), [1] * (number_of - 1)
    while spare > 0:
        movable = [i for i in range(number_of - 1) if holding[i] < reach]
        mass, left = sum([portions[i] for i in movable]), spare
        for i in movable:
            extra = min(reach - holding[i], max(1, left * portions[i] // mass), spare)
            holding[i] = holding[i] + extra
            spare = spare - extra
    return np.array([reach] + holding)


def ragged(own_key, count, total, most, lean):
    if count == 2:
        one = jax.random.randint(own_key, (), max(1, total - most), min(most, total - 1) + 1)
        return jnp.stack([one, total - one])
    sizes = jnp.asarray(split_up(count, total, most, lean), jnp.int32)
    pairs = (count - 1) // 2
    giver, taker = sizes[1:1 + 2 * pairs:2], sizes[2:2 + 2 * pairs:2]
    margin = jnp.minimum(giver - 1, most - taker)
    shifted = jax.random.randint(jax.random.fold_in(own_key, 1), (pairs,), 0, 1 << 20) % (margin + 1)
    sizes = sizes.at[1:1 + 2 * pairs:2].set(giver - shifted).at[2:2 + 2 * pairs:2].set(taker + shifted)
    return sizes[jax.random.permutation(jax.random.fold_in(own_key, 2), count)]


def bell_draw(key, shape, spread, limit, cuts=(), held_as=jnp.bfloat16):
    array = jax.random.normal(key, shape, jnp.float32) * spread
    if len(cuts) > 0:
        array = block_levels(key, shape, cuts, -0.22, 0.18) * array
    return jnp.clip(array, min=-limit, max=limit).astype(held_as)


def setup_inputs(seed: int = 0) -> dict:
    splits = jax.random.split(jax.random.key(seed), 17)
    hidden_in = bell_draw(splits[0], (PACKED_TOKENS, MODEL_WIDTH), 1.0, 6.0, ((0, 8),))
    cotangent = bell_draw(splits[1], (PACKED_TOKENS, MODEL_WIDTH), 1.0, 6.0, ((0, 8),))
    lengths = ragged(splits[2], NSEQ, PACKED_TOKENS, SEQ_MOST, 2).astype(jnp.int32)
    valid = with_ends((jax.random.randint(splits[3], (PACKED_TOKENS,), 0, 8) < 7).astype(jnp.int32), jax.random.fold_in(splits[3], 1), 0, 1)
    gain_one = jnp.clip(1.0 + 0.1 * jax.random.normal(splits[4], (MODEL_WIDTH,), jnp.float32), 0.5, 1.5).astype(jnp.bfloat16)
    w_query = bell_draw(splits[5], (MODEL_WIDTH, QUERY_HEADS * HEAD_SIZE), MODEL_WIDTH ** -0.5, 0.15625, ((1, 4),))
    b_query = bell_draw(splits[6], (QUERY_HEADS * HEAD_SIZE,), 0.5, 3.0, ((0, 4),))
    key_projection = bell_draw(splits[7], (MODEL_WIDTH, KEY_VALUE_HEADS * HEAD_SIZE), MODEL_WIDTH ** -0.5, 0.15625)
    key_bias_vector = bell_draw(splits[8], (KEY_VALUE_HEADS * HEAD_SIZE,), 0.5, 3.0)
    value_projection = bell_draw(splits[9], (MODEL_WIDTH, KEY_VALUE_HEADS * HEAD_SIZE), MODEL_WIDTH ** -0.5, 0.15625)
    value_bias_vector = bell_draw(splits[10], (KEY_VALUE_HEADS * HEAD_SIZE,), 0.5, 3.0)
    w_out = bell_draw(splits[11], (QUERY_HEADS * HEAD_SIZE, MODEL_WIDTH), (QUERY_HEADS * HEAD_SIZE // 16) ** -0.5, 0.625, ((0, 4),))
    gain_two = jnp.clip(1.0 + 0.1 * jax.random.normal(splits[12], (MODEL_WIDTH,), jnp.float32), 0.5, 1.5).astype(jnp.bfloat16)
    w_gate = bell_draw(splits[13], (MODEL_WIDTH, FF), MODEL_WIDTH ** -0.5, 0.15625, ((1, 4),))
    w_up = bell_draw(splits[14], (MODEL_WIDTH, FF), MODEL_WIDTH ** -0.5, 0.15625, ((1, 4),))
    w_down = bell_draw(splits[15], (FF, MODEL_WIDTH), FF ** -0.5, 0.0625, ((0, 4),))
    return dict(hidden_in=hidden_in, cotangent=cotangent, lengths=lengths, valid=valid, gain_one=gain_one, w_query=w_query, b_query=b_query, key_projection=key_projection, key_bias_vector=key_bias_vector, value_projection=value_projection, value_bias_vector=value_bias_vector, w_out=w_out, gain_two=gain_two, w_gate=w_gate, w_up=w_up, w_down=w_down)


eps = 1e-06
big_negative = -1e+30

@jax.custom_vjp
def low(v):
    return lax.optimization_barrier(v.astype(jnp.bfloat16)).astype(jnp.float32)

@jax.custom_vjp
def low_back(v):
    return v

def low_keep(v):
    return (low(v), None)

def low_pass(kept, grad):
    return (grad,)

def back_keep(v):
    return (v, None)

def back_low(kept, grad):
    return (low(grad),)
low.defvjp(low_keep, low_pass)
low_back.defvjp(back_keep, back_low)

def product(left, right):
    return jnp.dot(left, right, precision=lax.Precision.HIGHEST, preferred_element_type=jnp.float32)

def place_tokens(index, lengths):
    ends = jnp.cumsum(lengths)
    before = (ends[None, :] <= index[:, None]).astype(jnp.int32)
    return (lax.optimization_barrier(jnp.sum(before, axis=1)).astype(jnp.int32), (index - lax.optimization_barrier(jnp.sum(before * lengths[None, :], axis=1))).astype(jnp.int32))

def rotary_tables(positions, width):
    freqs = 10000.0 ** (-(jnp.arange(width // 2, dtype=jnp.float32) * 2.0) / width)
    angles = positions.astype(jnp.float32)[:, None] * freqs[None, :]
    cosine_table = jnp.cos(angles)
    sine_table = jnp.sin(angles)
    return (jnp.concatenate([cosine_table, cosine_table], axis=1)[:, None, :], jnp.concatenate([sine_table, sine_table], axis=1)[:, None, :])

def apply_rotary(value_tensor, cosine_table, sine_table):
    half = value_tensor.shape[-1] // 2
    turned = jnp.concatenate([-value_tensor[..., half:], value_tensor[..., :half]], axis=-1)
    return value_tensor * cosine_table + turned * sine_table

def visible(query_index, query_seg, key_index, key_seg, key_flags):
    same = query_seg[:, None] == key_seg[None, :]
    causal = key_index[None, :] <= query_index[:, None]
    usable = (key_flags[None, :] > 0) | (key_index[None, :] == query_index[:, None])
    return same & causal & usable

def rms_normed(value_tensor, gain):
    return value_tensor * lax.rsqrt(lax.optimization_barrier(jnp.mean(value_tensor * value_tensor, axis=1, keepdims=True)) + eps) * gain

def head_block(item, key_major, value_major, token_seg, key_flags):
    query, head_number, start = item
    key_value_head = head_number // (QUERY_HEADS // KEY_VALUE_HEADS)
    key_rows = lax.dynamic_index_in_dim(key_major, key_value_head, 0, keepdims=False)
    value_rows = lax.dynamic_index_in_dim(value_major, key_value_head, 0, keepdims=False)
    rows_here = query.shape[0]
    key_index = jnp.arange(key_rows.shape[0], dtype=jnp.int32)
    query_index = start + jnp.arange(rows_here, dtype=jnp.int32)
    query_seg = lax.dynamic_slice_in_dim(token_seg, start, rows_here)
    allowed = visible(query_index, query_seg, key_index, token_seg, key_flags)
    scores = low_back(product(query, key_rows.T) * (1.0 / math.sqrt(HEAD_SIZE)))
    masked = jnp.where(allowed, scores, big_negative)
    peak = lax.optimization_barrier(jnp.max(masked, axis=1, keepdims=True))
    weights = jnp.where(allowed, jnp.exp(masked - peak), 0.0)
    attention = low(weights / lax.optimization_barrier(jnp.sum(weights, axis=1, keepdims=True)))
    return product(attention, value_rows)

def layer(x, gain_one, w_query, b_query, key_projection, key_bias_vector, value_projection, value_bias_vector, w_out, gain_two, w_gate, w_up, w_down, token_seg, cosine_table, sine_table, key_flags):
    acts_one = low(rms_normed(x, gain_one))
    q_lin = low_back(product(acts_one, w_query) + b_query)
    key_linear = low_back(product(acts_one, key_projection) + key_bias_vector)
    value_linear = low_back(product(acts_one, value_projection) + value_bias_vector)
    queries = low(apply_rotary(q_lin.reshape(PACKED_TOKENS, QUERY_HEADS, HEAD_SIZE), cosine_table, sine_table))
    key_tensor = low(apply_rotary(key_linear.reshape(PACKED_TOKENS, KEY_VALUE_HEADS, HEAD_SIZE), cosine_table, sine_table))
    value_tensor = low(value_linear.reshape(PACKED_TOKENS, KEY_VALUE_HEADS, HEAD_SIZE))
    blocks = PACKED_TOKENS // KEYBLK
    items = (jnp.transpose(queries, (1, 0, 2)).reshape(QUERY_HEADS * blocks, KEYBLK, HEAD_SIZE), jnp.repeat(jnp.arange(QUERY_HEADS, dtype=jnp.int32), blocks), jnp.tile(jnp.arange(blocks, dtype=jnp.int32) * KEYBLK, QUERY_HEADS))
    key_major = jnp.transpose(key_tensor, (1, 0, 2))
    value_major = jnp.transpose(value_tensor, (1, 0, 2))
    attend = jax.checkpoint(lambda item: head_block(item, key_major, value_major, token_seg, key_flags))
    attended = lax.map(attend, items)
    context = jnp.transpose(attended.reshape(QUERY_HEADS, PACKED_TOKENS, HEAD_SIZE), (1, 0, 2)).reshape(PACKED_TOKENS, QUERY_HEADS * HEAD_SIZE)
    context = low(low_back(context))
    attn_out = low_back(product(context, w_out))
    middle = x + attn_out
    acts_two = low(rms_normed(middle, gain_two))
    gate = low_back(product(acts_two, w_gate))
    up = low_back(product(acts_two, w_up))
    hidden = low(jax.nn.silu(gate) * up)
    ffn_out = low_back(product(hidden, w_down))
    return middle + ffn_out

def reference(hidden_in, cotangent, lengths, valid, gain_one, w_query, b_query, key_projection, key_bias_vector, value_projection, value_bias_vector, w_out, gain_two, w_gate, w_up, w_down):
    index = jnp.arange(PACKED_TOKENS, dtype=jnp.int32)
    token_seg, positions = place_tokens(index, lengths)
    cosine_table, sine_table = rotary_tables(positions, HEAD_SIZE)
    params = [member.astype(jnp.float32) for member in (hidden_in, gain_one, w_query, b_query, key_projection, key_bias_vector, value_projection, value_bias_vector, w_out, gain_two, w_gate, w_up, w_down)]

    def forward(*inputs):
        return layer(*inputs, token_seg, cosine_table, sine_table, valid)
    result, pullback = jax.vjp(forward, *params)
    grads = pullback(cotangent.astype(jnp.float32))
    return (result.astype(jnp.bfloat16), grads[0].astype(jnp.bfloat16), grads[1], grads[2], grads[3].reshape(QUERY_HEADS, HEAD_SIZE), grads[4], grads[5], grads[6], grads[7], grads[8], grads[9], grads[10], grads[11], grads[12])
```

```python
import functools
import math

import jax
import jax.numpy as jnp
from jax import lax
from jax.experimental import pallas as pl
from jax.experimental.pallas import tpu as pltpu
from jax.sharding import PartitionSpec as P

QUERY_HEADS = 12
KEY_VALUE_HEADS = 2
HEAD_SIZE = 128
FLAG_ROWS = 16

eps = 1e-06
big_negative = -1e30
score_scale = 1.0 / math.sqrt(HEAD_SIZE)
log2_scale = score_scale * math.log2(math.e)

bf16 = jnp.bfloat16
f32 = jnp.float32
ANY = pl.BlockSpec(memory_space=pl.ANY)
VMEM = pl.BlockSpec(memory_space=pltpu.VMEM)
SMEM = pl.BlockSpec(memory_space=pltpu.SMEM)


def dot(a, b, dims=((1,), (0,))):
    return lax.dot_general(a, b, (dims, ((), ())), preferred_element_type=f32)


NT = ((1,), (1,))
TN = ((0,), (0,))


def swap_wide(array, bit):
    n = lax.axis_size("wide")
    return lax.ppermute(array, "wide", [(i, i ^ bit) for i in range(n)])


def shift_narrow(array, by):
    n = lax.axis_size("narrow")
    return lax.ppermute(array, "narrow", [(i, (i + by) % n) for i in range(n)])


def ring_gather(block):
    half = block.shape[0] // 2
    below = shift_narrow(block, 1)
    above = shift_narrow(block, -1)
    far_a = shift_narrow(below[:half], 1)
    far_b = shift_narrow(above[half:], -1)
    return [block, above, jnp.concatenate([far_a, far_b], axis=0), below]


def ring_scatter(parts):
    half = parts[0].shape[0] // 2
    add = lambda a, b: (a.astype(f32) + b.astype(f32)).astype(bf16)
    up = shift_narrow(parts[2][:half], 1)
    down = shift_narrow(parts[2][half:], -1)
    to_above = jnp.concatenate([add(parts[1][:half], up), parts[1][half:]], axis=0)
    to_below = jnp.concatenate([parts[3][:half], add(parts[3][half:], down)], axis=0)
    from_below = shift_narrow(to_above, 1)
    from_above = shift_narrow(to_below, -1)
    return parts[0].astype(f32) + from_below.astype(f32) + from_above.astype(f32)


def xor_gather(block, bits):
    slots, held = [0], [block[None]]
    pieces = [((0,), block[None])]
    for bit in bits:
        payload = held[0] if len(held) == 1 else jnp.concatenate(held, axis=0)
        received = swap_wide(payload, bit)
        new = [s ^ bit for s in slots]
        pieces.append((tuple(new), received))
        slots, held = slots + new, [payload, received]
    return pieces


def add_rounded(a, b):
    return (a.astype(f32) + b.astype(f32)).astype(bf16)


def xor_scatter(array, bits, order):
    bits = list(bits)
    for bit in order:
        axis = bits.index(bit)
        keep = lax.index_in_dim(array, 0, axis, keepdims=False)
        send = lax.index_in_dim(array, 1, axis, keepdims=False)
        array = add_rounded(keep, swap_wide(send, bit))
        bits.remove(bit)
    return array


def tie(values, *gates):
    return lax.optimization_barrier((values, gates))[0]


class Halving:
    def __init__(self, pair, orders):
        self.sends, keeps = pair
        self.terms = [[k] for k in keeps]
        self.views = [[k] for k in keeps]
        self.orders = [list(o) for o in orders]

    def exchange(self):
        return [swap_wide(s, order.pop(0)) for s, order in zip(self.sends, self.orders)]

    def settle(self, received):
        for part in range(2):
            self.terms[part].append(received[part])
            self.views[part].append(received[part])
        if not self.orders[0]:
            return None
        n = self.views[0][0].shape[1]
        total = lambda terms: sum(t.astype(f32) for t in terms).astype(bf16)
        self.sends = [
            total([t[:, 1::2] for t in self.views[0]]),
            total([t[:, n // 2 :] for t in self.views[1]]),
        ]
        self.views = [
            [t[:, ::2] for t in self.views[0]],
            [t[:, : n // 2] for t in self.views[1]],
        ]
        return self.sends

    def rest(self):
        while self.orders[0]:
            self.settle(self.exchange())


def as_row(vector):
    return vector[...].astype(f32).reshape(1, -1)


def rope(value, cosine, signed_sine):
    return value * cosine + pltpu.roll(value, HEAD_SIZE // 2, 1) * signed_sine


def front_kernel(head, x, gain, wk, wv, bk, bv, cosine, sine, flags, acts_out, k_out, v_out):
    rows = x.shape[0]
    of_head = lambda b: jnp.where(
        head[0] == 0, as_row(b)[:, :HEAD_SIZE], as_row(b)[:, HEAD_SIZE:]
    )
    xf = x[...].astype(f32)
    scale = lax.rsqrt(jnp.mean(xf * xf, axis=1, keepdims=True) + eps)
    acts = (xf * scale * as_row(gain)).astype(bf16)
    acts_out[...] = acts
    key = dot(acts, wk[...]) + of_head(bk)
    k_out[:rows, :] = rope(key, cosine[...], sine[...]).astype(bf16)
    k_out[rows:, :] = flags[...]
    v_out[...] = (dot(acts, wv[...]) + of_head(bv)).astype(bf16)


def front(head, x, gain, wk, wv, bk, bv, cosine, sine, flags):
    rows, width = x.shape
    whole = lambda *shape: pl.BlockSpec(shape, lambda i, h: (0,) * len(shape))
    column = lambda r: pl.BlockSpec((r, HEAD_SIZE), lambda i, h: (0, h[0]))
    return pl.pallas_call(
        front_kernel,
        name="front",
        grid_spec=pltpu.PrefetchScalarGridSpec(
            num_scalar_prefetch=1,
            grid=(1,),
            in_specs=[
                whole(rows, width),
                whole(width),
                column(width),
                column(width),
                whole(*bk.shape),
                whole(*bv.shape),
                whole(rows, HEAD_SIZE),
                whole(rows, HEAD_SIZE),
                whole(FLAG_ROWS, HEAD_SIZE),
            ],
            out_specs=[
                whole(rows, width),
                whole(rows + FLAG_ROWS, HEAD_SIZE),
                whole(rows, HEAD_SIZE),
            ],
        ),
        out_shape=[
            jax.ShapeDtypeStruct((rows, width), bf16),
            jax.ShapeDtypeStruct((rows + FLAG_ROWS, HEAD_SIZE), bf16),
            jax.ShapeDtypeStruct((rows, HEAD_SIZE), bf16),
        ],
    )(head, x, gain, wk, wv, bk, bv, cosine, sine, flags)


def query_kernel(acts, cot, w, b, cosine, sine, out, turned):
    lin = dot(acts[...], w[...]) + as_row(b)
    for h in range(out.shape[1] // HEAD_SIZE):
        cols = slice(h * HEAD_SIZE, (h + 1) * HEAD_SIZE)
        out[:, cols] = rope(lin[:, cols], cosine[...], sine[...]).astype(bf16)
    turned[0] = jnp.transpose(cot[...])
    turned[1] = jnp.transpose(acts[...])


def project_queries(acts, cot, w, b, cosine, sine):
    rows, width = acts.shape
    return pl.pallas_call(
        query_kernel,
        name="queries",
        in_specs=[VMEM] * 6,
        out_specs=[VMEM, VMEM],
        out_shape=[
            jax.ShapeDtypeStruct((rows, w.shape[1]), bf16),
            jax.ShapeDtypeStruct((2, width, rows), bf16),
        ],
    )(acts, cot, w, b, cosine, sine)


def load_pieces(k_refs, v_refs, k_slots, v_slots, kbuf, vbuf, sem):
    copies = []
    for which, refs, slots, buf in ((0, k_refs, k_slots, kbuf), (1, v_refs, v_slots, vbuf)):
        for ref, names in zip(refs, slots):
            for at, slot in enumerate(names):
                copies.append(
                    pltpu.make_async_copy(ref.at[at], buf.at[slot], sem.at[which, slot])
                )
    for copy in copies:
        copy.start()
    return copies


def key_codes(kbuf, slot, half, base, chunk):
    rows = kbuf.shape[1] - FLAG_ROWS
    per = chunk // HEAD_SIZE
    flags = jnp.transpose(kbuf[slot, rows:, :].astype(f32))
    columns = []
    for c in range(per):
        first = flags[:, c : c + 1]
        second = flags[:, per + c : per + c + 1]
        columns.append(jnp.where(half == 1, second, first))
    column = jnp.concatenate(columns, axis=0)
    index = base + lax.broadcasted_iota(jnp.int32, (chunk, 1), 0)
    return jnp.where(column > 0, index, -1)


def visible(codes, start, diagonal):
    seen = codes >= start
    if diagonal:
        shape = (codes.shape[0], start.shape[1])
        row = lax.broadcasted_iota(jnp.int32, shape, 0)
        col = lax.broadcasted_iota(jnp.int32, shape, 1)
        seen = (seen & (row < col)) | (row == col)
    return seen


def first_chunk(info, rows, chunk):
    base = info[0] * rows
    end = first = jnp.int32(0)
    for s in range(1, info.shape[0]):
        end = end + info[s]
        first = jnp.where(end <= base, end, first)
    return first // chunk


def forward_kernel(k_slots, v_slots, info, q, start, *refs):
    nk, nv = len(k_slots), len(v_slots)
    k_refs, v_refs = refs[:nk], refs[nk : nk + nv]
    out, lse, kbuf, vbuf, sem, acc_s, m_s, l_s = refs[nk + nv :]
    rows = q.shape[0]
    heads = q.shape[1] // HEAD_SIZE
    chunk = rows // 2
    own = info[0]
    copies = load_pieces(k_refs, v_refs, k_slots, v_slots, kbuf, vbuf, sem)
    for copy in copies:
        copy.wait()

    def tile(h, k, v, codes, lo, n, diagonal):
        qh = q[lo : lo + n, h * HEAD_SIZE : (h + 1) * HEAD_SIZE]
        s = dot(k, qh, NT) * log2_scale
        s = jnp.where(visible(codes, start[:, lo : lo + n], diagonal), s, big_negative)
        peak = jnp.max(s, axis=0, keepdims=True)
        cols = slice(lo, lo + n)
        if diagonal:
            p = jnp.exp2(s - peak)
            m_s[h : h + 1, cols] = peak
            l_s[h : h + 1, cols] = jnp.sum(p, axis=0, keepdims=True)
            acc_s[h, :, cols] = dot(v, p.astype(bf16), TN)
        else:
            old = m_s[h : h + 1, cols]
            new = jnp.maximum(old, peak)
            alpha = jnp.exp2(old - new)
            p = jnp.exp2(s - new)
            m_s[h : h + 1, cols] = new
            l_s[h : h + 1, cols] = alpha * l_s[h : h + 1, cols] + jnp.sum(p, axis=0, keepdims=True)
            acc_s[h, :, cols] = alpha * acc_s[h, :, cols] + dot(v, p.astype(bf16), TN)

    base = own * rows
    for half in (1, 0):
        k = kbuf[0, half * chunk : (half + 1) * chunk, :]
        v = vbuf[0, half * chunk : (half + 1) * chunk, :]
        codes = key_codes(kbuf, 0, half, base + half * chunk, chunk)
        for h in range(heads):
            tile(h, k, v, codes, half * chunk, chunk, True)
            if half == 0:
                tile(h, k, v, codes, chunk, chunk, False)

    def step(c, carry):
        block, half = c // 2, c % 2
        slot = lax.bitwise_xor(block, own)
        at = pl.multiple_of(half * chunk, chunk)
        k = kbuf[slot, pl.ds(at, chunk), :]
        v = vbuf[slot, pl.ds(at, chunk), :]
        codes = key_codes(kbuf, slot, half, c * chunk, chunk)
        for h in range(heads):
            tile(h, k, v, codes, 0, rows, False)
        return carry

    lax.fori_loop(first_chunk(info, rows, chunk), own * 2, step, 0)
    lse[...] = jnp.zeros_like(lse)
    for h in range(heads):
        total = l_s[h : h + 1, :]
        lse[h : h + 1, :] = m_s[h : h + 1, :] + jnp.log2(total)
        o = acc_s[h] * (1.0 / total)
        out[:, h * HEAD_SIZE : (h + 1) * HEAD_SIZE] = jnp.transpose(o).astype(bf16)


def attend(info, q, start, k_pieces, v_pieces):
    rows, width = q.shape
    heads = width // HEAD_SIZE
    slots = sum(len(s) for s, _ in k_pieces)
    return pl.pallas_call(
        functools.partial(
            forward_kernel, [s for s, _ in k_pieces], [s for s, _ in v_pieces]
        ),
        name="attend",
        in_specs=[SMEM, VMEM, VMEM] + [ANY] * (len(k_pieces) + len(v_pieces)),
        out_specs=[VMEM, VMEM],
        out_shape=[
            jax.ShapeDtypeStruct((rows, width), bf16),
            jax.ShapeDtypeStruct((8, rows), f32),
        ],
        scratch_shapes=[
            pltpu.VMEM((slots, rows + FLAG_ROWS, HEAD_SIZE), bf16),
            pltpu.VMEM((slots, rows, HEAD_SIZE), bf16),
            pltpu.SemaphoreType.DMA((2, slots)),
            pltpu.VMEM((heads, HEAD_SIZE, rows), f32),
            pltpu.VMEM((8, rows), f32),
            pltpu.VMEM((8, rows), f32),
        ],
    )(info, q, start, *[a for _, a in k_pieces], *[a for _, a in v_pieces])


def backward_kernel(k_slots, v_slots, info, q, do, ctx, start, lse, cosine, sine, *refs):
    nk, nv = len(k_slots), len(v_slots)
    k_refs, v_refs = refs[:nk], refs[nk : nk + nv]
    dq_out, send, keep, kbuf, vbuf, sem, dq_s, delta_s = refs[nk + nv :]
    rows = q.shape[0]
    heads = q.shape[1] // HEAD_SIZE
    chunk = rows // 2
    own = info[0]
    copies = load_pieces(k_refs, v_refs, k_slots, v_slots, kbuf, vbuf, sem)
    send[...] = jnp.zeros_like(send)
    keep[...] = jnp.zeros_like(keep)
    for h in range(heads):
        cols = slice(h * HEAD_SIZE, (h + 1) * HEAD_SIZE)
        both = do[:, cols].astype(f32) * ctx[:, cols].astype(f32)
        delta_s[h : h + 1, :] = jnp.sum(jnp.transpose(both), axis=0, keepdims=True)
        dq_s[h] = jnp.zeros((HEAD_SIZE, rows), f32)
    for copy in copies:
        copy.wait()

    def tile(h, k, v, codes, lo, n, diagonal):
        cols = slice(lo, lo + n)
        qh = q[cols, h * HEAD_SIZE : (h + 1) * HEAD_SIZE]
        doh = do[cols, h * HEAD_SIZE : (h + 1) * HEAD_SIZE]
        s = dot(k, qh, NT) * log2_scale - lse[h : h + 1, cols]
        s = jnp.where(visible(codes, start[:, cols], diagonal), s, big_negative)
        p = jnp.exp2(s)
        dv = dot(p.astype(bf16), doh)
        ds = (p * (dot(v, doh, NT) - delta_s[h : h + 1, cols])).astype(bf16)
        dk = dot(ds, qh)
        dq_s[h, :, cols] = dq_s[h, :, cols] + dot(k, ds, TN)
        return dk, dv

    def both(h, k, v, codes, spans):
        dk = dv = None
        for lo, n, diagonal in spans:
            a, b = tile(h, k, v, codes, lo, n, diagonal)
            dk, dv = (a, b) if dk is None else (dk + a, dv + b)
        return dk, dv

    def all_heads(k, v, codes, spans):
        dk = dv = None
        for h in range(heads):
            a, b = both(h, k, v, codes, spans)
            dk, dv = (a, b) if dk is None else (dk + a, dv + b)
        return (dk * score_scale).astype(bf16), dv.astype(bf16)

    base = own * rows
    for half in (1, 0):
        span = slice(half * chunk, (half + 1) * chunk)
        codes = key_codes(kbuf, 0, half, base + half * chunk, chunk)
        spans = [(chunk, chunk, True)] if half else [(0, chunk, True), (chunk, chunk, False)]
        dk, dv = all_heads(kbuf[0, span, :], vbuf[0, span, :], codes, spans)
        keep[0, 0, span, :] = dk
        keep[1, 0, span, :] = dv

    def step(c, carry):
        block, half = c // 2, c % 2
        slot = lax.bitwise_xor(block, own)
        at = pl.multiple_of(half * chunk, chunk)
        k = kbuf[slot, pl.ds(at, chunk), :]
        v = vbuf[slot, pl.ds(at, chunk), :]
        codes = key_codes(kbuf, slot, half, c * chunk, chunk)
        dk, dv = all_heads(k, v, codes, [(0, rows, False)])

        @pl.when(slot % 2 == 0)
        def _():
            keep[0, slot // 2, pl.ds(at, chunk), :] = dk
            keep[1, slot // 2, pl.ds(at, chunk), :] = dv

        @pl.when(slot % 2 == 1)
        def _():
            send[0, slot // 2, pl.ds(at, chunk), :] = dk
            send[1, slot // 2, pl.ds(at, chunk), :] = dv

        return carry

    lax.fori_loop(first_chunk(info, rows, chunk), own * 2, step, 0)
    for h in range(heads):
        g = jnp.transpose(dq_s[h]) * score_scale
        back = g * cosine[...] - pltpu.roll(g, HEAD_SIZE // 2, 1) * sine[...]
        dq_out[:, h * HEAD_SIZE : (h + 1) * HEAD_SIZE] = back.astype(bf16)


def attend_back(info, q, do, ctx, start, lse, cosine, sine, k_pieces, v_pieces):
    rows, width = q.shape
    heads = width // HEAD_SIZE
    slots = sum(len(s) for s, _ in k_pieces)
    half = jax.ShapeDtypeStruct((2, slots // 2, rows, HEAD_SIZE), bf16)
    return pl.pallas_call(
        functools.partial(
            backward_kernel, [s for s, _ in k_pieces], [s for s, _ in v_pieces]
        ),
        name="attend_back",
        in_specs=[SMEM] + [VMEM] * 7 + [ANY] * (len(k_pieces) + len(v_pieces)),
        out_specs=[VMEM] * 3,
        out_shape=[jax.ShapeDtypeStruct((rows, width), bf16), half, half],
        scratch_shapes=[
            pltpu.VMEM((slots, rows + FLAG_ROWS, HEAD_SIZE), bf16),
            pltpu.VMEM((slots, rows, HEAD_SIZE), bf16),
            pltpu.SemaphoreType.DMA((2, slots)),
            pltpu.VMEM((heads, HEAD_SIZE, rows), f32),
            pltpu.VMEM((8, rows), f32),
        ],
    )(
        info, q, do, ctx, start, lse, cosine, sine,
        *[a for _, a in k_pieces], *[a for _, a in v_pieces],
    )


def whole(shape):
    return pl.BlockSpec(shape, lambda *_: (0,) * len(shape))


def struct(shape, dtype):
    return jax.ShapeDtypeStruct(shape, dtype)


def project_out_kernel(
    core, x, own, above, fa, fb, below, w_own, mine, other, gain, middle, acts, turned, scale
):
    n = w_own.shape[0]
    width = x.shape[1]
    far = jnp.where(pl.program_id(0) == 0, fa[...].astype(f32), fb[...].astype(f32)).astype(bf16)
    part = lambda m: (
        dot(above[...], m[:n, :]) + dot(below[...], m[n : 2 * n, :]) + dot(far, m[2 * n :, :])
    )
    a, b = part(mine), part(other)
    first = core[0] == 0
    out = dot(own[...], w_own[...]) + jnp.concatenate(
        [jnp.where(first, a, b), jnp.where(first, b, a)], axis=1
    )
    mid = x[...].astype(f32) + out
    r = lax.rsqrt(jnp.mean(mid * mid, axis=1, keepdims=True) + eps)
    middle[...] = mid
    scale[...] = r
    normed = mid * r * as_row(gain)
    acts[...] = normed.astype(bf16)
    turned[:width, :] = jnp.transpose(normed).astype(bf16)
    turned[width:, :] = jnp.transpose(own[...].astype(f32)).astype(bf16)


def project_out(core, x, pieces, w_own, mine, other, gain):
    rows, width = x.shape
    n = w_own.shape[0]
    half = rows // 2
    own, above, (fa, fb), below = pieces
    block = lambda c: pl.BlockSpec((half, c), lambda i, s: (i, 0))
    return pl.pallas_call(
        project_out_kernel,
        name="project_out",
        grid_spec=pltpu.PrefetchScalarGridSpec(
            num_scalar_prefetch=1,
            grid=(2,),
            in_specs=[
                block(width), block(n), block(n), whole((half, n)), whole((half, n)), block(n),
                whole(w_own.shape), whole(mine.shape), whole(other.shape), whole(gain.shape),
            ],
            out_specs=[
                block(width), block(width),
                pl.BlockSpec((width + n, half), lambda i, s: (0, i)),
                block(1),
            ],
        ),
        out_shape=[
            struct((rows, width), f32), struct((rows, width), bf16),
            struct((width + n, rows), bf16), struct((rows, 1), f32),
        ],
    )(core, x, own, above, fa, fb, below, w_own, mine, other, gain)


def feed_kernel(n, acts, cot, wg, wu, wd, hidden, grads):
    tile = wg.shape[0]
    gate = dot(acts[...], wg[...], NT)
    up = dot(acts[...], wu[...], NT)
    g = dot(cot[...], wd[...], NT)
    sig = 1.0 / (1.0 + jnp.exp(-gate))
    silu = gate * sig
    column = pl.program_id(0) * tile + lax.broadcasted_iota(jnp.int32, (1, tile), 1)
    keep = lambda v: jnp.where(column < n, v, 0.0).astype(bf16)
    hidden[...] = keep(silu * up)
    grads[0] = keep(g * up * (sig * (1.0 + gate * (1.0 - sig))))
    grads[1] = keep(g * silu)


def feed(acts, cot, wg, wu, wd, tile=384):
    rows, width = acts.shape
    n = wg.shape[0]
    steps = pl.cdiv(n, tile)
    w_spec = pl.BlockSpec((tile, width), lambda j: (j, 0))
    return pl.pallas_call(
        functools.partial(feed_kernel, n),
        name="feed",
        grid=(steps,),
        in_specs=[whole((rows, width)), whole((rows, width)), w_spec, w_spec, w_spec],
        out_specs=[
            pl.BlockSpec((rows, tile), lambda j: (0, j)),
            pl.BlockSpec((2, rows, tile), lambda j: (0, 0, j)),
        ],
        out_shape=[struct((rows, steps * tile), bf16), struct((2, rows, steps * tile), bf16)],
    )(acts, cot, wg, wu, wd)


def partial_kernel(mine, a, *refs):
    n = a.shape[0]
    ws, outs, acc = refs[:n], refs[n:-1], refs[-1]
    inner = ws[0].shape[0]
    total = None
    for k in range(n):
        g = dot(a[k, :, :inner], ws[k][...])
        total = g if total is None else total + g
    acc[...] = total
    block = acc.shape[0] // 4
    own, above, far_a, far_b, below = outs

    def take(k, first, size):
        at = ((mine[0] + k) % 4) * block + first
        return acc[pl.ds(pl.multiple_of(at, size), size), :].astype(bf16)

    own[...] = take(0, 0, block)
    above[...] = take(1, 0, block)
    far_a[...] = take(2, 0, block // 2)
    far_b[...] = take(2, block // 2, block // 2)
    below[...] = take(3, 0, block)


def partial_rows(name, mine, a, ws, tile=512):
    n, rows, _ = a.shape
    inner, width = ws[0].shape
    sizes = [rows // 4, rows // 4, rows // 8, rows // 8, rows // 4]
    return pl.pallas_call(
        partial_kernel,
        name=name,
        grid_spec=pltpu.PrefetchScalarGridSpec(
            num_scalar_prefetch=1,
            grid=(width // tile,),
            in_specs=[whole(a.shape)]
            + [pl.BlockSpec((inner, tile), lambda j, s: (0, j))] * n,
            out_specs=[pl.BlockSpec((r, tile), lambda j, s: (0, j)) for r in sizes],
            scratch_shapes=[pltpu.VMEM((rows, tile), f32)],
        ),
        out_shape=[struct((r, width), bf16) for r in sizes],
    )(mine, a, *ws)


def pass_on_kernel(above, below, up, down, to_above, to_below):
    half = up.shape[0]
    to_above[:half, :] = (above[:half, :].astype(f32) + up[...].astype(f32)).astype(bf16)
    to_above[half:, :] = above[half:, :]
    to_below[:half, :] = below[:half, :]
    to_below[half:, :] = (below[half:, :].astype(f32) + down[...].astype(f32)).astype(bf16)


def pass_on(above, below, up, down):
    return pl.pallas_call(
        pass_on_kernel,
        name="pass_on",
        in_specs=[VMEM] * 4,
        out_specs=[VMEM] * 2,
        out_shape=[struct(above.shape, bf16)] * 2,
    )(above, below, up, down)


def weigh_kernel(slots, half, mine, a_own, a_other, b_own, b_other, *refs):
    send_a, keep_a, send_b, keep_b, lhs = refs
    rows = a_own.shape[1]
    block = 2 * half

    @pl.when(pl.program_id(0) == 0)
    def _():
        for s in range(slots):
            at = pl.multiple_of(lax.bitwise_xor(mine[0], 2 * s) * block, 16)
            lhs[s * block : (s + 1) * block, :rows] = a_own[pl.ds(at, block), :]
            lhs[s * block : (s + 1) * block, rows:] = a_other[pl.ds(at, block), :]

    g = dot(lhs[:, :rows], b_own[0]) + dot(lhs[:, rows:], b_other[0])
    place_slots(g, slots, half, 0, send_a, keep_a, send_b, keep_b)


def place_slots(g, slots, half, group, send_a, keep_a, send_b, keep_b):
    cols = slice(0, g.shape[1])
    for s in range(slots):
        first = g[2 * s * half : (2 * s + 1) * half].astype(bf16)
        second = g[(2 * s + 1) * half : (2 * s + 2) * half].astype(bf16)
        (send_a if s % 2 else keep_a)[group, s // 2, :, cols] = first
        (send_b if s >= slots // 2 else keep_b)[group, s % (slots // 2), :, cols] = second


def weigh(mine, slots, width, a_own, a_other, b_own, b_other, group=0, tile=768):
    rows = a_own.shape[-1]
    n = b_own.shape[2]
    if a_own.ndim == 3:
        a_spec = pl.BlockSpec((None, width, rows), lambda j, s: (0, 0, 0))
    else:
        a_spec = pl.BlockSpec((width, rows), lambda j, s: (0, 0))
    half = width // slots // 4
    b_spec = pl.BlockSpec((1, rows, tile), lambda j, s: (group, 0, j))
    out = pl.BlockSpec((1, slots // 2, half, tile), lambda j, s: (0, 0, 0, j))
    outs = pl.pallas_call(
        functools.partial(weigh_kernel, slots, half),
        name="weigh",
        grid_spec=pltpu.PrefetchScalarGridSpec(
            num_scalar_prefetch=1,
            grid=(pl.cdiv(n, tile),),
            in_specs=[a_spec, a_spec, b_spec, b_spec],
            out_specs=[out] * 4,
            scratch_shapes=[pltpu.VMEM((width // 2, 2 * rows), bf16)],
        ),
        out_shape=[struct((1, slots // 2, half, n), bf16)] * 4,
    )(mine, a_own, a_other, b_own, b_other)
    return [outs[0], outs[2]], [outs[1], outs[3]]


def weigh_late_kernel(
    slots, half, mine, t_own, t_other, c_own, c_other, a_own, a_other, b_own, b_other, *refs
):
    send_a, keep_a, send_b, keep_b = refs
    block = 2 * half

    def gather(ref):
        pieces = []
        for s in range(slots):
            at = pl.multiple_of(lax.bitwise_xor(mine[0], 2 * s) * block, 16)
            pieces.append(ref[pl.ds(at, block), :])
        return jnp.concatenate(pieces, axis=0)

    n = c_own.shape[0]
    g = dot(gather(t_own), c_own[...], NT) + dot(gather(t_other), c_other[...], NT)
    late = dot(gather(a_own), b_own[...]) + dot(gather(a_other), b_other[...])
    g = jnp.concatenate([g, late], axis=1)
    place_slots(g, slots, half, 0, send_a, keep_a, send_b, keep_b)


def weigh_late(mine, slots, t_own, t_other, c_own, c_other, a_own, a_other, b_own, b_other):
    width, rows = t_own.shape
    n = c_own.shape[0] - width
    half = width // slots // 4
    total = n + b_own.shape[1]
    t_spec = whole((width, rows))
    c_spec = pl.BlockSpec((n, rows), lambda i, s: (width // n, 0))
    a_spec = pl.BlockSpec((None, width, rows), lambda i, s: (1, 0, 0))
    b_spec = whole(b_own.shape)
    shape = (1, slots // 2, half, total)
    outs = pl.pallas_call(
        functools.partial(weigh_late_kernel, slots, half),
        name="weigh_late",
        grid_spec=pltpu.PrefetchScalarGridSpec(
            num_scalar_prefetch=1,
            grid=(1,),
            in_specs=[t_spec, t_spec, c_spec, c_spec, a_spec, a_spec, b_spec, b_spec],
            out_specs=[whole(shape)] * 4,
        ),
        out_shape=[struct(shape, bf16)] * 4,
    )(mine, t_own, t_other, c_own, c_other, a_own, a_other, b_own, b_other)
    return [outs[0], outs[2]], [outs[1], outs[3]]


def finish_kernel(n, *refs):
    terms, outs = refs[: 2 * n], refs[2 * n :]
    half = terms[0].shape[2]
    for g, out in enumerate(outs):
        for part in range(2):
            total = None
            for t in terms[part * n : (part + 1) * n]:
                value = t[g, 0, :, : out.shape[1]].astype(f32)
                total = value if total is None else total + value
            out[part * half : (part + 1) * half, :] = total


def finish(terms, columns):
    flat = terms[0] + terms[1]
    groups, _, half, n = flat[0].shape
    return pl.pallas_call(
        functools.partial(finish_kernel, len(terms[0])),
        name="finish",
        grid=(1,),
        in_specs=[whole((groups, 1, half, n))] * len(flat),
        out_specs=[whole((2 * half, columns))] * groups,
        out_shape=[struct((2 * half, columns), f32)] * groups,
    )(*flat)


def middle_back_kernel(
    mine, own, above, fa, fb, below, middle, scale, cot, gain, w_out,
    grad_middle, turned, grad_context, gain_grad, g_s,
):
    k = pl.program_id(0)
    half = fa.shape[0]
    for at, ref in ((0, own), (1, above), (3, below)):
        @pl.when(k == at)
        def _():
            g_s[...] = ref[...].astype(f32)

    @pl.when(k == 2)
    def _():
        g_s[:half, :] = fa[...].astype(f32)
        g_s[half:, :] = fb[...].astype(f32)

    g = g_s[...]
    r = scale[...]
    n2 = middle[...] * r
    u2 = g * as_row(gain)
    gm = cot[...].astype(f32) + r * (u2 - n2 * jnp.mean(u2 * n2, axis=1, keepdims=True))
    part = jnp.sum(g * n2, axis=0, keepdims=True)

    @pl.when(k == 0)
    def _():
        gain_grad[...] = part

    @pl.when(k > 0)
    def _():
        gain_grad[...] = gain_grad[...] + part

    grad_middle[...] = gm
    turned[...] = jnp.transpose(gm).astype(bf16)
    grad_context[...] = dot(gm.astype(bf16), w_out[...], NT).astype(bf16)


def middle_back(mine, pieces, middle, scale, cot, gain, w_out):
    rows, width = middle.shape
    block = rows // 4
    own, above, (fa, fb), below = pieces
    at = lambda c: pl.BlockSpec((block, c), lambda k, s: ((s[0] + k) % 4, 0))
    n = w_out.shape[0]
    return pl.pallas_call(
        middle_back_kernel,
        name="middle_back",
        grid_spec=pltpu.PrefetchScalarGridSpec(
            num_scalar_prefetch=1,
            grid=(4,),
            in_specs=[
                whole((block, width)), whole((block, width)),
                whole((block // 2, width)), whole((block // 2, width)), whole((block, width)),
                at(width), at(1), at(width), whole(gain.shape), whole(w_out.shape),
            ],
            out_specs=[
                at(width),
                pl.BlockSpec((width, block), lambda k, s: (0, (s[0] + k) % 4)),
                at(n),
                whole((1, width)),
            ],
            scratch_shapes=[pltpu.VMEM((block, width), f32)],
        ),
        out_shape=[
            struct((rows, width), f32), struct((width, rows), bf16),
            struct((rows, n), bf16), struct((1, width), f32),
        ],
    )(mine, own, above, fa, fb, below, middle, scale, cot, gain, w_out)


def in_rows_kernel(mine, own, above, fa, fb, below, out):
    block = own.shape[0]
    at = lambda k: pl.ds(pl.multiple_of((mine[0] + k) % 4 * block, block), block)
    out[at(0), :] = own[...]
    out[at(1), :] = above[...]
    out[at(2), :] = jnp.concatenate([fa[...], fb[...]], axis=0)
    out[at(3), :] = below[...]


def in_rows(mine, pieces):
    own, above, (fa, fb), below = pieces
    rows, width = own.shape
    return pl.pallas_call(
        in_rows_kernel,
        name="in_rows",
        in_specs=[SMEM] + [VMEM] * 5,
        out_specs=VMEM,
        out_shape=struct((4 * rows, width), bf16),
    )(mine, own, above, fa, fb, below)


def late_kernel(head, q, pair, cross, cosine, sine, late, bias):
    rows, n = q.shape
    kv = KEY_VALUE_HEADS * HEAD_SIZE

    def lin(ref):
        g = ref[:, :HEAD_SIZE].astype(f32)
        key = g * cosine[...] - pltpu.roll(g, HEAD_SIZE // 2, 1) * sine[...]
        return key, ref[:, HEAD_SIZE:].astype(f32)

    (own_k, own_v), (other_k, other_v) = lin(pair), lin(cross)
    first = head[0] == 0
    late[:, :n] = q[...]
    columns = [
        jnp.where(first, own_k, other_k), jnp.where(first, other_k, own_k),
        jnp.where(first, own_v, other_v), jnp.where(first, other_v, own_v),
    ]
    for c, value in enumerate(columns):
        late[:, n + c * HEAD_SIZE : n + (c + 1) * HEAD_SIZE] = value.astype(bf16)
    bias[...] = jnp.sum(late[...].astype(f32), axis=0, keepdims=True)


def late_grads(head, q, pair, cross, cosine, sine):
    rows, n = q.shape
    total = n + 2 * KEY_VALUE_HEADS * HEAD_SIZE
    return pl.pallas_call(
        late_kernel,
        name="late_grads",
        in_specs=[SMEM] + [VMEM] * 5,
        out_specs=[VMEM] * 2,
        out_shape=[struct((rows, total), bf16), struct((1, total), f32)],
    )(head, q, pair, cross, cosine, sine)


def project_back_kernel(
    core, x, late, above, fa, fb, below, w_own, mine, other, wk, wv, gain, grad_middle,
    gain_two_grad, bias, out, vectors,
):
    i = pl.program_id(0)
    n = w_own.shape[1]
    kv = wk.shape[1]
    far = jnp.where(i == 0, fa[...].astype(f32), fb[...].astype(f32)).astype(bf16)
    part = lambda m: (
        dot(above[...], m[:n, :]) + dot(below[...], m[n : 2 * n, :]) + dot(far, m[2 * n :, :])
    )
    a, b = part(mine), part(other)
    first = core[0] == 0
    g = jnp.concatenate([jnp.where(first, a, b), jnp.where(first, b, a)], axis=1)
    g = g + dot(late[:, :n], w_own[...], NT)
    g = g + dot(late[:, n : n + kv], wk[...], NT) + dot(late[:, n + kv :], wv[...], NT)
    xf = x[...].astype(f32)
    r = lax.rsqrt(jnp.mean(xf * xf, axis=1, keepdims=True) + eps)
    n1 = xf * r
    u1 = g * as_row(gain)
    out[...] = (
        grad_middle[...] + r * (u1 - n1 * jnp.mean(u1 * n1, axis=1, keepdims=True))
    ).astype(bf16)
    total = jnp.sum(g * n1, axis=0, keepdims=True)
    width = x.shape[1]

    @pl.when(i == 0)
    def _():
        vectors[:, :width] = total
        vectors[:, width : 2 * width] = gain_two_grad[...]
        vectors[:, 2 * width :] = bias[...]

    @pl.when(i > 0)
    def _():
        vectors[:, :width] = vectors[:, :width] + total


def project_back(
    core, x, late, pieces, w_own, mine, other, wk, wv, gain, grad_middle, gain_two_grad, bias
):
    rows, width = x.shape
    n = w_own.shape[1]
    half = rows // 2
    above, (fa, fb), below = pieces
    block = lambda c: pl.BlockSpec((half, c), lambda i, s: (i, 0))
    return pl.pallas_call(
        project_back_kernel,
        name="project_back",
        grid_spec=pltpu.PrefetchScalarGridSpec(
            num_scalar_prefetch=1,
            grid=(2,),
            in_specs=[
                block(width), block(late.shape[1]), block(n), whole((half, n)), whole((half, n)),
                block(n), whole(w_own.shape), whole(mine.shape), whole(other.shape),
                whole(wk.shape), whole(wv.shape), whole(gain.shape), block(width),
                whole(gain_two_grad.shape), whole(bias.shape),
            ],
            out_specs=[block(width), whole((1, 2 * width + bias.shape[1]))],
        ),
        out_shape=[struct((rows, width), bf16), struct((1, 2 * width + bias.shape[1]), f32)],
    )(
        core, x, late, above, fa, fb, below, w_own, mine, other, wk, wv, gain, grad_middle,
        gain_two_grad, bias,
    )


def place_tokens(index, lengths):
    ends = jnp.cumsum(lengths)
    before = (ends[None, :] <= index[:, None]).astype(jnp.int32)
    return index - jnp.sum(before * lengths[None, :], axis=1)


def on_device(
    hidden_in,
    cotangent,
    lengths,
    valid,
    gain_one,
    w_query,
    b_query,
    key_projection,
    key_bias_vector,
    value_projection,
    value_bias_vector,
    w_out,
    gain_two,
    w_gate,
    w_up,
    w_down,
):
    rows, width = hidden_in.shape
    n_wide = lax.axis_size("wide")
    wide_index = lax.axis_index("wide")
    narrow_index = lax.axis_index("narrow")
    heads = w_query.shape[1] // HEAD_SIZE
    n_query = heads * HEAD_SIZE
    kv_width = KEY_VALUE_HEADS * HEAD_SIZE
    head = narrow_index * heads // (QUERY_HEADS // KEY_VALUE_HEADS)
    bits = [1 << b for b in reversed(range(n_wide.bit_length() - 1))]
    chip_bits = bits[:-1]
    up_first, down_first = bits, chip_bits[::-1] + [1]
    slots = n_wide // 2
    core = wide_index % 2
    base = wide_index * rows
    as_scalar = lambda v: v.astype(jnp.int32).reshape(1)
    mine_wide, mine_narrow, core_s, head_s = map(
        as_scalar, (wide_index, narrow_index, core, head)
    )
    swap_core = lambda v: swap_wide(v, 1)

    token_index = base + jnp.arange(rows, dtype=jnp.int32)
    positions = place_tokens(token_index, lengths)
    start = (token_index - positions)[None, :]
    info = jnp.concatenate([mine_wide, lengths])
    freqs = 10000.0 ** (-(jnp.arange(HEAD_SIZE // 2, dtype=f32) * 2.0) / HEAD_SIZE)
    angles = positions.astype(f32)[:, None] * freqs[None, :]
    cos_half, sin_half = jnp.cos(angles), jnp.sin(angles)
    cosine = jnp.concatenate([cos_half, cos_half], axis=1)
    sine = jnp.concatenate([-sin_half, sin_half], axis=1)

    flags = jnp.pad(
        valid.astype(bf16).reshape(rows // HEAD_SIZE, HEAD_SIZE),
        ((0, FLAG_ROWS - rows // HEAD_SIZE), (0, 0)),
    )
    acts_one, key_own, value_own = front(
        head_s,
        hidden_in,
        gain_one,
        key_projection,
        value_projection,
        key_bias_vector,
        value_bias_vector,
        cosine,
        sine,
        flags,
    )

    col = width // 2
    n_half = n_query // 2
    half_out = lax.dynamic_slice_in_dim(w_out, core * col, col, 1)
    half_query = lax.dynamic_slice_in_dim(w_query, core * col, col, 0).T
    half_out = tie(half_out, key_own)
    out_below, out_above = shift_narrow(half_out, 1), shift_narrow(half_out, -1)

    k_slots, keys = [(0,)], [key_own[None]]
    v_slots, values = [(0,)], [value_own[None]]
    join = lambda pieces: pieces[0] if len(pieces) == 1 else jnp.concatenate(pieces, axis=0)
    queries = turned_one = None
    for step, (k_bit, v_bit) in enumerate(zip(up_first, down_first)):
        k_send, v_send = join(keys), join(values)
        if step + 1 == len(up_first):
            k_send, v_send, queries, half_query, out_below, out_above = tie(
                (k_send, v_send, queries, half_query, out_below, out_above)
            )
            out_far_a = shift_narrow(out_below[:n_half], 1)
            out_far_b = shift_narrow(out_above[n_half:], -1)
        for names, pieces, send, bit in (
            (k_slots, keys, k_send, k_bit), (v_slots, values, v_send, v_bit)
        ):
            pieces.append(swap_wide(send, bit))
            names.append(tuple(s ^ bit for group in names for s in group))
        if step == 0:
            acts_late = tie(acts_one, keys[1], values[1])
            queries, turned_one = project_queries(
                acts_late, cotangent, w_query, b_query, cosine, sine
            )
    k_pieces, v_pieces = list(zip(k_slots, keys)), list(zip(v_slots, values))
    out_far_a, out_far_b = tie((out_far_a, out_far_b), keys[-1], values[-1])
    context, lse = attend(info, queries, start, k_pieces, v_pieces)
    out_mine = jnp.concatenate([out_above, out_below, out_far_a, out_far_b], axis=0)
    out_other = swap_core(out_mine)

    half = rows // 2
    ctx_below, ctx_above = shift_narrow(context, 1), shift_narrow(context, -1)
    ctx_far = (shift_narrow(ctx_below[:half], 1), shift_narrow(ctx_above[half:], -1))
    turned_one_other = swap_core(turned_one)
    ctx_far, half_query = tie((ctx_far, half_query), turned_one_other, out_other)
    w_gate_t, w_up_t = w_gate.T, w_up.T
    middle, acts_two, turned_two, scale_two = project_out(
        core_s, hidden_in, (context, ctx_above, ctx_far, ctx_below),
        w_out, out_mine, out_other, gain_two,
    )

    query_below, query_above = shift_narrow(half_query, 1), shift_narrow(half_query, -1)
    hidden, grads = feed(acts_two, cotangent, w_gate_t, w_up_t, w_down)
    turned_two_other = swap_core(turned_two)
    (hidden, grads), query_below, query_above = tie(
        ((hidden, grads), query_below, query_above), turned_two_other
    )
    hidden_other = swap_core(hidden)
    query_far_a = shift_narrow(query_below[:n_half], 1)
    query_far_b = shift_narrow(query_above[n_half:], -1)
    own, above, far_a, far_b, below = partial_rows(
        "partial_back", mine_narrow, grads, [w_gate_t, w_up_t]
    )
    (own, above, far_a, far_b, below), hidden = tie(
        ((own, above, far_a, far_b, below), hidden), hidden_other, query_far_a, query_far_b
    )
    up, down = shift_narrow(far_a, 1), shift_narrow(far_b, -1)
    down_pair = weigh(
        mine_wide, slots, width, turned_one, turned_one_other, hidden[None], hidden_other[None]
    )
    grads_other = swap_core(grads)
    up, down, down_pair = tie((up, down, down_pair))
    low_chip = chip_bits[::-1]
    orders = (low_chip, chip_bits)
    down_steps = Halving(down_pair, orders)
    down_moved = down_steps.exchange()
    to_above, to_below = pass_on(above, below, up, down)
    from_below, from_above = shift_narrow(to_above, 1), shift_narrow(to_below, -1)
    grads_here = tie(grads, to_above, to_below, grads_other)
    gate_pair = weigh(
        mine_wide, slots, width, turned_two, turned_two_other, grads_here, grads_other, 0
    )
    from_below, from_above, gate_pair = tie((from_below, from_above, gate_pair))
    gate_steps = Halving(gate_pair, orders)
    gate_moved = gate_steps.exchange()
    own = (own.astype(f32) + from_below.astype(f32) + from_above.astype(f32)).astype(bf16)
    q_rows = rows // 8
    g_below, g_above = shift_narrow(own, 1), shift_narrow(own, -1)
    grads_here = tie(grads_here, own)
    up_pair = weigh(
        mine_wide, slots, width, turned_two, turned_two_other, grads_here, grads_other, 1
    )
    g_below, g_above, up_pair, down_moved = tie((g_below, g_above, up_pair, down_moved))
    g_far = (shift_narrow(g_below[:q_rows], 1), shift_narrow(g_above[q_rows:], -1))
    ffn = partial_rows("partial_down", mine_narrow, tie(hidden, g_below)[None], [w_down])
    down_sends = down_steps.settle(down_moved)
    g_far, ffn, down_sends = tie((g_far, ffn, down_sends))
    grad_middle, turned_attn, grad_context, gain_two_grad = middle_back(
        mine_narrow, (own, g_above, g_far, g_below), middle, scale_two, cotangent,
        gain_two, w_out,
    )

    ffn_own, ffn_above, ffn_far_a, ffn_far_b, ffn_below = ffn
    ffn_up, ffn_down = shift_narrow(ffn_far_a, 1), shift_narrow(ffn_far_b, -1)
    grad_context, gate_moved = tie((grad_context, gate_moved), ffn_up, ffn_down)
    down_steps.sends = tie(down_sends, gate_moved)
    down_moved = down_steps.exchange()
    query_lin_grad, send, keep = attend_back(
        info, queries, grad_context, context, start, lse, cosine, sine, k_pieces, v_pieces
    )
    ffn_to = pass_on(ffn_above, ffn_below, ffn_up, ffn_down)
    ffn_from_below, ffn_from_above = shift_narrow(ffn_to[0], 1), shift_narrow(ffn_to[1], -1)
    query_lin_grad, send, keep, down_moved = tie(
        (query_lin_grad, send, keep, down_moved), ffn_from_below, ffn_from_above
    )
    turned_attn = tie(turned_attn, send)
    turned_attn_other = swap_core(turned_attn)
    down_steps.settle(down_moved)
    down_steps.rest()
    out_rows = lax.dynamic_slice_in_dim(middle, narrow_index * (rows // 4), rows // 4, 0)
    out_rows = (
        out_rows + ffn_own.astype(f32) + ffn_from_below.astype(f32) + ffn_from_above.astype(f32)
    ).astype(bf16)

    ql_below, ql_above = shift_narrow(query_lin_grad, 1), shift_narrow(query_lin_grad, -1)
    key_value = add_rounded(keep, swap_core(send))
    ql_far = (shift_narrow(ql_below[:half], 1), shift_narrow(ql_above[half:], -1))
    spread = (2,) * len(chip_bits) + key_value.shape[2:]
    key_part = xor_scatter(key_value[0].reshape(spread), chip_bits, low_chip)
    value_part = xor_scatter(key_value[1].reshape(spread), chip_bits, chip_bits)
    n_narrow = lax.axis_size("narrow")
    pair = jnp.concatenate([key_part, value_part], axis=1)
    pair, ql_far, up_sends, gate_moved = tie((pair, ql_far, up_pair[0], gate_moved))
    up_steps = Halving((up_sends, up_pair[1]), orders)
    up_moved = up_steps.exchange()
    partner = lax.ppermute(pair, "narrow", [(i, i ^ 1) for i in range(n_narrow)])
    query_mine = jnp.concatenate([query_above, query_below, query_far_a, query_far_b], axis=0)
    query_other = swap_core(query_mine)
    gate_steps.settle(gate_moved)
    gate_moved = gate_steps.exchange()
    pair = add_rounded(pair, partner)
    cross = lax.ppermute(pair, "narrow", [(i, n_narrow - 1 - i) for i in range(n_narrow)])
    cross, query_other, turned_attn_other, up_moved = tie(
        (cross, query_other, turned_attn_other, up_moved)
    )
    late, bias = late_grads(head_s, query_lin_grad, pair, cross, cosine, sine)
    late_other = swap_core(late)
    up_sends = up_steps.settle(up_moved)
    late_other, up_sends, gate_moved = tie((late_other, up_sends, gate_moved))
    up_steps.sends = up_sends
    up_moved = up_steps.exchange()
    late_pair = weigh_late(
        mine_wide, slots, turned_attn, turned_attn_other, turned_two, turned_two_other,
        turned_one, turned_one_other, late, late_other,
    )
    late_steps = Halving(late_pair, orders)
    late_moved = late_steps.exchange()
    late, out_rows = tie((late, out_rows), late_pair)
    o_below, o_above = shift_narrow(out_rows, 1), shift_narrow(out_rows, -1)
    grad_hidden_in, vectors = project_back(
        core_s, hidden_in, late, (ql_above, ql_far, ql_below), w_query, query_mine, query_other,
        key_projection, value_projection, gain_one, grad_middle, gain_two_grad, bias,
    )
    late_moved, vectors = tie((late_moved, vectors))
    late_steps.settle(late_moved)
    late_steps.rest()

    for bit in bits[::-1]:
        vectors = vectors + swap_wide(vectors, bit)
    vectors = vectors[0]

    def own_part(first, size):
        return lax.dynamic_slice_in_dim(vectors, first + wide_index * (size // n_wide), size // n_wide)

    bias_at = 2 * width
    query_bias = vectors[bias_at : bias_at + n_query].reshape(heads, n_wide, -1)
    query_bias = lax.dynamic_index_in_dim(query_bias, wide_index, 1, keepdims=False)

    o_far = (shift_narrow(o_below[:q_rows], 1), shift_narrow(o_above[q_rows:], -1))
    output = in_rows(mine_narrow, (out_rows, o_above, o_far, o_below))

    gate_steps.settle(gate_moved)
    gate_steps.rest()
    up_steps.settle(up_moved)
    up_steps.rest()
    n_hidden = w_down.shape[0]
    (down_sum,) = finish(down_steps.terms, n_hidden)
    (gate_sum,) = finish(gate_steps.terms, n_hidden)
    (up_sum,) = finish(up_steps.terms, n_hidden)
    (late_sum,) = finish(late_steps.terms, late_steps.terms[0][0].shape[3])
    return (
        output,
        grad_hidden_in,
        own_part(0, width),
        late_sum[:, n_query : 2 * n_query],
        query_bias,
        late_sum[:, 2 * n_query : 2 * n_query + kv_width],
        own_part(bias_at + n_query, kv_width),
        late_sum[:, 2 * n_query + kv_width :],
        own_part(bias_at + n_query + kv_width, kv_width),
        late_sum[:, :n_query].T,
        own_part(width, width),
        gate_sum,
        up_sum,
        down_sum.T,
    )


def solution(mesh):
    placed = (
        P("wide", None),
        P("wide", None),
        P(),
        P("wide"),
        P(),
        P(None, "narrow"),
        P("narrow"),
        P(),
        P(),
        P(),
        P(),
        P("narrow", None),
        P(),
        P(None, "narrow"),
        P(None, "narrow"),
        P("narrow", None),
    )
    return jax.shard_map(
        on_device,
        mesh=mesh,
        in_specs=placed,
        out_specs=(
            P("wide", None),
            P("wide", None),
            P("wide"),
            P("wide", "narrow"),
            P("narrow", "wide"),
            P("wide", None),
            P("wide"),
            P("wide", None),
            P("wide"),
            P("narrow", "wide"),
            P("wide"),
            P("wide", "narrow"),
            P("wide", "narrow"),
            P("narrow", "wide"),
        ),
        check_vma=False,
    )
```

```python
import functools
import math

import jax
import jax.numpy as jnp
from jax import lax
from jax.experimental import pallas as pl
from jax.experimental.pallas import tpu as pltpu
from jax.sharding import PartitionSpec as P

QUERY_HEADS = 12
KEY_VALUE_HEADS = 2
HEAD_SIZE = 128
FLAG_ROWS = 16

eps = 1e-06
big_negative = -1e30
score_scale = 1.0 / math.sqrt(HEAD_SIZE)
log2_scale = score_scale * math.log2(math.e)

bf16 = jnp.bfloat16
f32 = jnp.float32
ANY = pl.BlockSpec(memory_space=pl.ANY)
VMEM = pl.BlockSpec(memory_space=pltpu.VMEM)
SMEM = pl.BlockSpec(memory_space=pltpu.SMEM)


def dot(a, b, dims=((1,), (0,))):
    return lax.dot_general(a, b, (dims, ((), ())), preferred_element_type=f32)


NT = ((1,), (1,))
TN = ((0,), (0,))


def swap_wide(array, bit):
    n = lax.axis_size("wide")
    return lax.ppermute(array, "wide", [(i, i ^ bit) for i in range(n)])


def shift_narrow(array, by):
    n = lax.axis_size("narrow")
    return lax.ppermute(array, "narrow", [(i, (i + by) % n) for i in range(n)])


def ring_gather(block):
    half = block.shape[0] // 2
    below = shift_narrow(block, 1)
    above = shift_narrow(block, -1)
    far_a = shift_narrow(below[:half], 1)
    far_b = shift_narrow(above[half:], -1)
    return [block, above, jnp.concatenate([far_a, far_b], axis=0), below]


def ring_scatter(parts):
    half = parts[0].shape[0] // 2
    add = lambda a, b: (a.astype(f32) + b.astype(f32)).astype(bf16)
    up = shift_narrow(parts[2][:half], 1)
    down = shift_narrow(parts[2][half:], -1)
    to_above = jnp.concatenate([add(parts[1][:half], up), parts[1][half:]], axis=0)
    to_below = jnp.concatenate([parts[3][:half], add(parts[3][half:], down)], axis=0)
    from_below = shift_narrow(to_above, 1)
    from_above = shift_narrow(to_below, -1)
    return parts[0].astype(f32) + from_below.astype(f32) + from_above.astype(f32)


def xor_gather(block, bits):
    slots, held = [0], [block[None]]
    pieces = [((0,), block[None])]
    for bit in bits:
        payload = held[0] if len(held) == 1 else jnp.concatenate(held, axis=0)
        received = swap_wide(payload, bit)
        new = [s ^ bit for s in slots]
        pieces.append((tuple(new), received))
        slots, held = slots + new, [payload, received]
    return pieces


def add_rounded(a, b):
    return (a.astype(f32) + b.astype(f32)).astype(bf16)


def xor_scatter(array, bits, order):
    bits = list(bits)
    for bit in order:
        axis = bits.index(bit)
        keep = lax.index_in_dim(array, 0, axis, keepdims=False)
        send = lax.index_in_dim(array, 1, axis, keepdims=False)
        array = add_rounded(keep, swap_wide(send, bit))
        bits.remove(bit)
    return array


def tie(values, *gates):
    return lax.optimization_barrier((values, gates))[0]


class Halving:
    def __init__(self, pair, orders):
        self.sends, keeps = pair
        self.terms = [[k] for k in keeps]
        self.views = [[k] for k in keeps]
        self.orders = [list(o) for o in orders]

    def exchange(self):
        return [swap_wide(s, order.pop(0)) for s, order in zip(self.sends, self.orders)]

    def settle(self, received):
        for part in range(2):
            self.terms[part].append(received[part])
            self.views[part].append(received[part])
        if not self.orders[0]:
            return None
        n = self.views[0][0].shape[1]
        total = lambda terms: sum(t.astype(f32) for t in terms).astype(bf16)
        self.sends = [
            total([t[:, 1::2] for t in self.views[0]]),
            total([t[:, n // 2 :] for t in self.views[1]]),
        ]
        self.views = [
            [t[:, ::2] for t in self.views[0]],
            [t[:, : n // 2] for t in self.views[1]],
        ]
        return self.sends

    def rest(self):
        while self.orders[0]:
            self.settle(self.exchange())


def as_row(vector):
    return vector[...].astype(f32).reshape(1, -1)


def rope(value, cosine, signed_sine):
    return value * cosine + pltpu.roll(value, HEAD_SIZE // 2, 1) * signed_sine


def front_kernel(head, x, gain, wk, wv, bk, bv, cosine, sine, flags, acts_out, k_out, v_out):
    rows = x.shape[0]
    of_head = lambda b: jnp.where(
        head[0] == 0, as_row(b)[:, :HEAD_SIZE], as_row(b)[:, HEAD_SIZE:]
    )
    xf = x[...].astype(f32)
    scale = lax.rsqrt(jnp.mean(xf * xf, axis=1, keepdims=True) + eps)
    acts = (xf * scale * as_row(gain)).astype(bf16)
    acts_out[...] = acts
    key = dot(acts, wk[...]) + of_head(bk)
    k_out[:rows, :] = rope(key, cosine[...], sine[...]).astype(bf16)
    k_out[rows:, :] = flags[...]
    v_out[...] = (dot(acts, wv[...]) + of_head(bv)).astype(bf16)


def front(head, x, gain, wk, wv, bk, bv, cosine, sine, flags):
    rows, width = x.shape
    whole = lambda *shape: pl.BlockSpec(shape, lambda i, h: (0,) * len(shape))
    column = lambda r: pl.BlockSpec((r, HEAD_SIZE), lambda i, h: (0, h[0]))
    return pl.pallas_call(
        front_kernel,
        name="front",
        grid_spec=pltpu.PrefetchScalarGridSpec(
            num_scalar_prefetch=1,
            grid=(1,),
            in_specs=[
                whole(rows, width),
                whole(width),
                column(width),
                column(width),
                whole(*bk.shape),
                whole(*bv.shape),
                whole(rows, HEAD_SIZE),
                whole(rows, HEAD_SIZE),
                whole(FLAG_ROWS, HEAD_SIZE),
            ],
            out_specs=[
                whole(rows, width),
                whole(rows + FLAG_ROWS, HEAD_SIZE),
                whole(rows, HEAD_SIZE),
            ],
        ),
        out_shape=[
            jax.ShapeDtypeStruct((rows, width), bf16),
            jax.ShapeDtypeStruct((rows + FLAG_ROWS, HEAD_SIZE), bf16),
            jax.ShapeDtypeStruct((rows, HEAD_SIZE), bf16),
        ],
    )(head, x, gain, wk, wv, bk, bv, cosine, sine, flags)


def query_kernel(acts, cot, w, b, cosine, sine, out, turned):
    lin = dot(acts[...], w[...]) + as_row(b)
    for h in range(out.shape[1] // HEAD_SIZE):
        cols = slice(h * HEAD_SIZE, (h + 1) * HEAD_SIZE)
        out[:, cols] = rope(lin[:, cols], cosine[...], sine[...]).astype(bf16)
    turned[0] = jnp.transpose(cot[...])
    turned[1] = jnp.transpose(acts[...])


def project_queries(acts, cot, w, b, cosine, sine):
    rows, width = acts.shape
    return pl.pallas_call(
        query_kernel,
        name="queries",
        in_specs=[VMEM] * 6,
        out_specs=[VMEM, VMEM],
        out_shape=[
            jax.ShapeDtypeStruct((rows, w.shape[1]), bf16),
            jax.ShapeDtypeStruct((2, width, rows), bf16),
        ],
    )(acts, cot, w, b, cosine, sine)


def load_pieces(k_refs, v_refs, k_slots, v_slots, kbuf, vbuf, sem):
    copies = []
    for which, refs, slots, buf in ((0, k_refs, k_slots, kbuf), (1, v_refs, v_slots, vbuf)):
        for ref, names in zip(refs, slots):
            for at, slot in enumerate(names):
                copies.append(
                    pltpu.make_async_copy(ref.at[at], buf.at[slot], sem.at[which, slot])
                )
    for copy in copies:
        copy.start()
    return copies


def key_codes(kbuf, slot, half, base, chunk):
    rows = kbuf.shape[1] - FLAG_ROWS
    per = chunk // HEAD_SIZE
    flags = jnp.transpose(kbuf[slot, rows:, :].astype(f32))
    columns = []
    for c in range(per):
        first = flags[:, c : c + 1]
        second = flags[:, per + c : per + c + 1]
        columns.append(jnp.where(half == 1, second, first))
    column = jnp.concatenate(columns, axis=0)
    index = base + lax.broadcasted_iota(jnp.int32, (chunk, 1), 0)
    return jnp.where(column > 0, index, -1)


def visible(codes, start, diagonal):
    seen = codes >= start
    if diagonal:
        shape = (codes.shape[0], start.shape[1])
        row = lax.broadcasted_iota(jnp.int32, shape, 0)
        col = lax.broadcasted_iota(jnp.int32, shape, 1)
        seen = (seen & (row < col)) | (row == col)
    return seen


def first_chunk(info, rows, chunk):
    base = info[0] * rows
    end = first = jnp.int32(0)
    for s in range(1, info.shape[0]):
        end = end + info[s]
        first = jnp.where(end <= base, end, first)
    return first // chunk


def forward_kernel(k_slots, v_slots, info, q, start, *refs):
    nk, nv = len(k_slots), len(v_slots)
    k_refs, v_refs = refs[:nk], refs[nk : nk + nv]
    out, lse, kbuf, vbuf, sem, acc_s, m_s, l_s = refs[nk + nv :]
    rows = q.shape[0]
    heads = q.shape[1] // HEAD_SIZE
    chunk = rows // 2
    own = info[0]
    copies = load_pieces(k_refs, v_refs, k_slots, v_slots, kbuf, vbuf, sem)
    for copy in copies:
        copy.wait()

    def tile(h, k, v, codes, lo, n, diagonal):
        qh = q[lo : lo + n, h * HEAD_SIZE : (h + 1) * HEAD_SIZE]
        s = dot(k, qh, NT) * log2_scale
        s = jnp.where(visible(codes, start[:, lo : lo + n], diagonal), s, big_negative)
        peak = jnp.max(s, axis=0, keepdims=True)
        cols = slice(lo, lo + n)
        if diagonal:
            p = jnp.exp2(s - peak)
            m_s[h : h + 1, cols] = peak
            l_s[h : h + 1, cols] = jnp.sum(p, axis=0, keepdims=True)
            acc_s[h, :, cols] = dot(v, p.astype(bf16), TN)
        else:
            old = m_s[h : h + 1, cols]
            new = jnp.maximum(old, peak)
            alpha = jnp.exp2(old - new)
            p = jnp.exp2(s - new)
            m_s[h : h + 1, cols] = new
            l_s[h : h + 1, cols] = alpha * l_s[h : h + 1, cols] + jnp.sum(p, axis=0, keepdims=True)
            acc_s[h, :, cols] = alpha * acc_s[h, :, cols] + dot(v, p.astype(bf16), TN)

    base = own * rows
    for half in (1, 0):
        k = kbuf[0, half * chunk : (half + 1) * chunk, :]
        v = vbuf[0, half * chunk : (half + 1) * chunk, :]
        codes = key_codes(kbuf, 0, half, base + half * chunk, chunk)
        for h in range(heads):
            tile(h, k, v, codes, half * chunk, chunk, True)
            if half == 0:
                tile(h, k, v, codes, chunk, chunk, False)

    def step(c, carry):
        block, half = c // 2, c % 2
        slot = lax.bitwise_xor(block, own)
        at = pl.multiple_of(half * chunk, chunk)
        k = kbuf[slot, pl.ds(at, chunk), :]
        v = vbuf[slot, pl.ds(at, chunk), :]
        codes = key_codes(kbuf, slot, half, c * chunk, chunk)
        for h in range(heads):
            tile(h, k, v, codes, 0, rows, False)
        return carry

    lax.fori_loop(first_chunk(info, rows, chunk), own * 2, step, 0)
    lse[...] = jnp.zeros_like(lse)
    for h in range(heads):
        total = l_s[h : h + 1, :]
        lse[h : h + 1, :] = m_s[h : h + 1, :] + jnp.log2(total)
        o = acc_s[h] * (1.0 / total)
        out[:, h * HEAD_SIZE : (h + 1) * HEAD_SIZE] = jnp.transpose(o).astype(bf16)


def attend(info, q, start, k_pieces, v_pieces):
    rows, width = q.shape
    heads = width // HEAD_SIZE
    slots = sum(len(s) for s, _ in k_pieces)
    return pl.pallas_call(
        functools.partial(
            forward_kernel, [s for s, _ in k_pieces], [s for s, _ in v_pieces]
        ),
        name="attend",
        in_specs=[SMEM, VMEM, VMEM] + [ANY] * (len(k_pieces) + len(v_pieces)),
        out_specs=[VMEM, VMEM],
        out_shape=[
            jax.ShapeDtypeStruct((rows, width), bf16),
            jax.ShapeDtypeStruct((8, rows), f32),
        ],
        scratch_shapes=[
            pltpu.VMEM((slots, rows + FLAG_ROWS, HEAD_SIZE), bf16),
            pltpu.VMEM((slots, rows, HEAD_SIZE), bf16),
            pltpu.SemaphoreType.DMA((2, slots)),
            pltpu.VMEM((heads, HEAD_SIZE, rows), f32),
            pltpu.VMEM((8, rows), f32),
            pltpu.VMEM((8, rows), f32),
        ],
    )(info, q, start, *[a for _, a in k_pieces], *[a for _, a in v_pieces])


def backward_kernel(k_slots, v_slots, info, q, do, ctx, start, lse, cosine, sine, *refs):
    nk, nv = len(k_slots), len(v_slots)
    k_refs, v_refs = refs[:nk], refs[nk : nk + nv]
    dq_out, send, keep, kbuf, vbuf, sem, dq_s, delta_s = refs[nk + nv :]
    rows = q.shape[0]
    heads = q.shape[1] // HEAD_SIZE
    chunk = rows // 2
    own = info[0]
    copies = load_pieces(k_refs, v_refs, k_slots, v_slots, kbuf, vbuf, sem)
    send[...] = jnp.zeros_like(send)
    keep[...] = jnp.zeros_like(keep)
    for h in range(heads):
        cols = slice(h * HEAD_SIZE, (h + 1) * HEAD_SIZE)
        both = do[:, cols].astype(f32) * ctx[:, cols].astype(f32)
        delta_s[h : h + 1, :] = jnp.sum(jnp.transpose(both), axis=0, keepdims=True)
        dq_s[h] = jnp.zeros((HEAD_SIZE, rows), f32)
    for copy in copies:
        copy.wait()

    def tile(h, k, v, codes, lo, n, diagonal):
        cols = slice(lo, lo + n)
        qh = q[cols, h * HEAD_SIZE : (h + 1) * HEAD_SIZE]
        doh = do[cols, h * HEAD_SIZE : (h + 1) * HEAD_SIZE]
        s = dot(k, qh, NT) * log2_scale - lse[h : h + 1, cols]
        s = jnp.where(visible(codes, start[:, cols], diagonal), s, big_negative)
        p = jnp.exp2(s)
        dv = dot(p.astype(bf16), doh)
        ds = (p * (dot(v, doh, NT) - delta_s[h : h + 1, cols])).astype(bf16)
        dk = dot(ds, qh)
        dq_s[h, :, cols] = dq_s[h, :, cols] + dot(k, ds, TN)
        return dk, dv

    def both(h, k, v, codes, spans):
        dk = dv = None
        for lo, n, diagonal in spans:
            a, b = tile(h, k, v, codes, lo, n, diagonal)
            dk, dv = (a, b) if dk is None else (dk + a, dv + b)
        return dk, dv

    def all_heads(k, v, codes, spans):
        dk = dv = None
        for h in range(heads):
            a, b = both(h, k, v, codes, spans)
            dk, dv = (a, b) if dk is None else (dk + a, dv + b)
        return (dk * score_scale).astype(bf16), dv.astype(bf16)

    base = own * rows
    for half in (1, 0):
        span = slice(half * chunk, (half + 1) * chunk)
        codes = key_codes(kbuf, 0, half, base + half * chunk, chunk)
        spans = [(chunk, chunk, True)] if half else [(0, chunk, True), (chunk, chunk, False)]
        dk, dv = all_heads(kbuf[0, span, :], vbuf[0, span, :], codes, spans)
        keep[0, 0, span, :] = dk
        keep[1, 0, span, :] = dv

    def step(c, carry):
        block, half = c // 2, c % 2
        slot = lax.bitwise_xor(block, own)
        at = pl.multiple_of(half * chunk, chunk)
        k = kbuf[slot, pl.ds(at, chunk), :]
        v = vbuf[slot, pl.ds(at, chunk), :]
        codes = key_codes(kbuf, slot, half, c * chunk, chunk)
        dk, dv = all_heads(k, v, codes, [(0, rows, False)])

        @pl.when(slot % 2 == 0)
        def _():
            keep[0, slot // 2, pl.ds(at, chunk), :] = dk
            keep[1, slot // 2, pl.ds(at, chunk), :] = dv

        @pl.when(slot % 2 == 1)
        def _():
            send[0, slot // 2, pl.ds(at, chunk), :] = dk
            send[1, slot // 2, pl.ds(at, chunk), :] = dv

        return carry

    lax.fori_loop(first_chunk(info, rows, chunk), own * 2, step, 0)
    for h in range(heads):
        g = jnp.transpose(dq_s[h]) * score_scale
        back = g * cosine[...] - pltpu.roll(g, HEAD_SIZE // 2, 1) * sine[...]
        dq_out[:, h * HEAD_SIZE : (h + 1) * HEAD_SIZE] = back.astype(bf16)


def attend_back(info, q, do, ctx, start, lse, cosine, sine, k_pieces, v_pieces):
    rows, width = q.shape
    heads = width // HEAD_SIZE
    slots = sum(len(s) for s, _ in k_pieces)
    half = jax.ShapeDtypeStruct((2, slots // 2, rows, HEAD_SIZE), bf16)
    return pl.pallas_call(
        functools.partial(
            backward_kernel, [s for s, _ in k_pieces], [s for s, _ in v_pieces]
        ),
        name="attend_back",
        in_specs=[SMEM] + [VMEM] * 7 + [ANY] * (len(k_pieces) + len(v_pieces)),
        out_specs=[VMEM] * 3,
        out_shape=[jax.ShapeDtypeStruct((rows, width), bf16), half, half],
        scratch_shapes=[
            pltpu.VMEM((slots, rows + FLAG_ROWS, HEAD_SIZE), bf16),
            pltpu.VMEM((slots, rows, HEAD_SIZE), bf16),
            pltpu.SemaphoreType.DMA((2, slots)),
            pltpu.VMEM((heads, HEAD_SIZE, rows), f32),
            pltpu.VMEM((8, rows), f32),
        ],
    )(
        info, q, do, ctx, start, lse, cosine, sine,
        *[a for _, a in k_pieces], *[a for _, a in v_pieces],
    )


def whole(shape):
    return pl.BlockSpec(shape, lambda *_: (0,) * len(shape))


def struct(shape, dtype):
    return jax.ShapeDtypeStruct(shape, dtype)


def project_out_kernel(
    core, x, own, above, fa, fb, below, w_own, mine, other, gain, middle, acts, turned, scale
):
    n = w_own.shape[0]
    width = x.shape[1]
    far = jnp.where(pl.program_id(0) == 0, fa[...].astype(f32), fb[...].astype(f32)).astype(bf16)
    part = lambda m: (
        dot(above[...], m[:n, :]) + dot(below[...], m[n : 2 * n, :]) + dot(far, m[2 * n :, :])
    )
    a, b = part(mine), part(other)
    first = core[0] == 0
    out = dot(own[...], w_own[...]) + jnp.concatenate(
        [jnp.where(first, a, b), jnp.where(first, b, a)], axis=1
    )
    mid = x[...].astype(f32) + out
    r = lax.rsqrt(jnp.mean(mid * mid, axis=1, keepdims=True) + eps)
    middle[...] = mid
    scale[...] = r
    normed = mid * r * as_row(gain)
    acts[...] = normed.astype(bf16)
    turned[:width, :] = jnp.transpose(normed.astype(bf16))
    turned[width:, :] = jnp.transpose(own[...])


def project_out(core, x, pieces, w_own, mine, other, gain):
    rows, width = x.shape
    n = w_own.shape[0]
    half = rows // 2
    own, above, (fa, fb), below = pieces
    block = lambda c: pl.BlockSpec((half, c), lambda i, s: (i, 0))
    return pl.pallas_call(
        project_out_kernel,
        name="project_out",
        grid_spec=pltpu.PrefetchScalarGridSpec(
            num_scalar_prefetch=1,
            grid=(2,),
            in_specs=[
                block(width), block(n), block(n), whole((half, n)), whole((half, n)), block(n),
                whole(w_own.shape), whole(mine.shape), whole(other.shape), whole(gain.shape),
            ],
            out_specs=[
                block(width), block(width),
                pl.BlockSpec((width + n, half), lambda i, s: (0, i)),
                block(1),
            ],
        ),
        out_shape=[
            struct((rows, width), f32), struct((rows, width), bf16),
            struct((width + n, rows), bf16), struct((rows, 1), f32),
        ],
    )(core, x, own, above, fa, fb, below, w_own, mine, other, gain)


def feed_kernel(n, acts, cot, wg, wu, wd, hidden, grads):
    tile = wg.shape[0]
    part = min(256, tile)
    for lo in range(0, tile, part):
        cols = slice(lo, lo + part)
        gate = dot(acts[...], wg[cols, :], NT)
        up = dot(acts[...], wu[cols, :], NT)
        g = dot(cot[...], wd[cols, :], NT)
        sig = 1.0 / (1.0 + jnp.exp(-gate))
        silu = gate * sig
        column = pl.program_id(0) * tile + lo + lax.broadcasted_iota(jnp.int32, (1, part), 1)
        keep = lambda v: jnp.where(column < n, v, 0.0).astype(bf16)
        hidden[:, cols] = keep(silu * up)
        grads[0, :, cols] = keep(g * up * (sig * (1.0 + gate * (1.0 - sig))))
        grads[1, :, cols] = keep(g * silu)


def feed(acts, cot, wg, wu, wd, tile=768):
    rows, width = acts.shape
    n = wg.shape[0]
    steps = pl.cdiv(n, tile)
    w_spec = pl.BlockSpec((tile, width), lambda j: (j, 0))
    return pl.pallas_call(
        functools.partial(feed_kernel, n),
        name="feed",
        grid=(steps,),
        in_specs=[whole((rows, width)), whole((rows, width)), w_spec, w_spec, w_spec],
        out_specs=[
            pl.BlockSpec((rows, tile), lambda j: (0, j)),
            pl.BlockSpec((2, rows, tile), lambda j: (0, 0, j)),
        ],
        out_shape=[struct((rows, steps * tile), bf16), struct((2, rows, steps * tile), bf16)],
    )(acts, cot, wg, wu, wd)


def assemble_kernel(plan, chip, *refs):
    out = refs[-1]
    n = out.shape[0] // 3
    block = n // plan[0]
    for ref, (names, first) in zip(refs, plan[1]):
        rows = ref.shape[1]
        for at, name in enumerate(names):
            source = lax.bitwise_xor(chip[0], name)
            done = 0
            while done < rows:
                piece, inside = divmod(first + done, block)
                size = min(rows - done, block - inside)
                to = pl.multiple_of(piece * n + source * block + inside, 16)
                out[pl.ds(to, size), :] = ref[at, done : done + size, :]
                done += size


def assemble(chip, chips, parts):
    one = sum({first: a.shape[1] for _, first, a in parts}.values())
    plan = (chips, [(names, first) for names, first, _ in parts])
    return pl.pallas_call(
        functools.partial(assemble_kernel, plan),
        name="assemble",
        in_specs=[SMEM] + [VMEM] * len(parts),
        out_specs=VMEM,
        out_shape=struct((chips * one, parts[0][2].shape[2]), bf16),
    )(chip, *[a for _, _, a in parts])


def partial_kernel(mine, a, *refs):
    n = a.shape[0]
    ws, outs, acc = refs[:n], refs[n:-1], refs[-1]
    inner = ws[0].shape[0]
    total = None
    for k in range(n):
        g = dot(a[k, :, :inner], ws[k][...])
        total = g if total is None else total + g
    acc[...] = total
    block = acc.shape[0] // 4
    own, above, far_a, far_b, below = outs

    def take(k, first, size):
        at = ((mine[0] + k) % 4) * block + first
        return acc[pl.ds(pl.multiple_of(at, size), size), :].astype(bf16)

    own[...] = take(0, 0, block)
    above[...] = take(1, 0, block)
    far_a[...] = take(2, 0, block // 2)
    far_b[...] = take(2, block // 2, block // 2)
    below[...] = take(3, 0, block)


def partial_rows(name, mine, a, ws, tile=512):
    n, rows, _ = a.shape
    inner, width = ws[0].shape
    sizes = [rows // 4, rows // 4, rows // 8, rows // 8, rows // 4]
    return pl.pallas_call(
        partial_kernel,
        name=name,
        grid_spec=pltpu.PrefetchScalarGridSpec(
            num_scalar_prefetch=1,
            grid=(width // tile,),
            in_specs=[whole(a.shape)]
            + [pl.BlockSpec((inner, tile), lambda j, s: (0, j))] * n,
            out_specs=[pl.BlockSpec((r, tile), lambda j, s: (0, j)) for r in sizes],
            scratch_shapes=[pltpu.VMEM((rows, tile), f32)],
        ),
        out_shape=[struct((r, width), bf16) for r in sizes],
    )(mine, a, *ws)


def pass_on_kernel(above, below, up, down, to_above, to_below):
    half = up.shape[0]
    to_above[:half, :] = (above[:half, :].astype(f32) + up[...].astype(f32)).astype(bf16)
    to_above[half:, :] = above[half:, :]
    to_below[:half, :] = below[:half, :]
    to_below[half:, :] = (below[half:, :].astype(f32) + down[...].astype(f32)).astype(bf16)


def pass_on(above, below, up, down):
    return pl.pallas_call(
        pass_on_kernel,
        name="pass_on",
        in_specs=[VMEM] * 4,
        out_specs=[VMEM] * 2,
        out_shape=[struct(above.shape, bf16)] * 2,
    )(above, below, up, down)


def weigh_kernel(slots, half, mine, a_own, a_other, b_own, b_other, *refs):
    send_a, keep_a, send_b, keep_b, lhs = refs
    rows = a_own.shape[1]
    block = 2 * half

    @pl.when(pl.program_id(0) == 0)
    def _():
        for s in range(slots):
            at = pl.multiple_of(lax.bitwise_xor(mine[0], 2 * s) * block, 16)
            lhs[s * block : (s + 1) * block, :rows] = a_own[pl.ds(at, block), :]
            lhs[s * block : (s + 1) * block, rows:] = a_other[pl.ds(at, block), :]

    g = dot(lhs[:, :rows], b_own[0]) + dot(lhs[:, rows:], b_other[0])
    place_slots(g, slots, half, 0, send_a, keep_a, send_b, keep_b)


def place_slots(g, slots, half, group, send_a, keep_a, send_b, keep_b):
    cols = slice(0, g.shape[1])
    for s in range(slots):
        first = g[2 * s * half : (2 * s + 1) * half].astype(bf16)
        second = g[(2 * s + 1) * half : (2 * s + 2) * half].astype(bf16)
        (send_a if s % 2 else keep_a)[group, s // 2, :, cols] = first
        (send_b if s >= slots // 2 else keep_b)[group, s % (slots // 2), :, cols] = second


def weigh(mine, slots, width, a_own, a_other, b_own, b_other, group=0, tile=768):
    rows = a_own.shape[-1]
    n = b_own.shape[2]
    if a_own.ndim == 3:
        a_spec = pl.BlockSpec((None, width, rows), lambda j, s: (0, 0, 0))
    else:
        a_spec = pl.BlockSpec((width, rows), lambda j, s: (0, 0))
    half = width // slots // 4
    b_spec = pl.BlockSpec((1, rows, tile), lambda j, s: (group, 0, j))
    out = pl.BlockSpec((1, slots // 2, half, tile), lambda j, s: (0, 0, 0, j))
    outs = pl.pallas_call(
        functools.partial(weigh_kernel, slots, half),
        name="weigh",
        grid_spec=pltpu.PrefetchScalarGridSpec(
            num_scalar_prefetch=1,
            grid=(pl.cdiv(n, tile),),
            in_specs=[a_spec, a_spec, b_spec, b_spec],
            out_specs=[out] * 4,
            scratch_shapes=[pltpu.VMEM((width // 2, 2 * rows), bf16)],
        ),
        out_shape=[struct((1, slots // 2, half, n), bf16)] * 4,
    )(mine, a_own, a_other, b_own, b_other)
    return [outs[0], outs[2]], [outs[1], outs[3]]


def weigh_late_kernel(
    slots, half, mine, t_own, t_other, c_own, c_other, a_own, a_other, b_own, b_other, *refs
):
    send_a, keep_a, send_b, keep_b = refs
    block = 2 * half

    def gather(ref):
        pieces = []
        for s in range(slots):
            at = pl.multiple_of(lax.bitwise_xor(mine[0], 2 * s) * block, 16)
            pieces.append(ref[pl.ds(at, block), :])
        return jnp.concatenate(pieces, axis=0)

    n = c_own.shape[0]
    g = dot(gather(t_own), c_own[...], NT) + dot(gather(t_other), c_other[...], NT)
    late = dot(gather(a_own), b_own[...]) + dot(gather(a_other), b_other[...])
    g = jnp.concatenate([g, late], axis=1)
    place_slots(g, slots, half, 0, send_a, keep_a, send_b, keep_b)


def weigh_late(mine, slots, t_own, t_other, c_own, c_other, a_own, a_other, b_own, b_other):
    width, rows = t_own.shape
    n = c_own.shape[0] - width
    half = width // slots // 4
    total = n + b_own.shape[1]
    t_spec = whole((width, rows))
    c_spec = pl.BlockSpec((n, rows), lambda i, s: (width // n, 0))
    a_spec = pl.BlockSpec((None, width, rows), lambda i, s: (1, 0, 0))
    b_spec = whole(b_own.shape)
    shape = (1, slots // 2, half, total)
    outs = pl.pallas_call(
        functools.partial(weigh_late_kernel, slots, half),
        name="weigh_late",
        grid_spec=pltpu.PrefetchScalarGridSpec(
            num_scalar_prefetch=1,
            grid=(1,),
            in_specs=[t_spec, t_spec, c_spec, c_spec, a_spec, a_spec, b_spec, b_spec],
            out_specs=[whole(shape)] * 4,
        ),
        out_shape=[struct(shape, bf16)] * 4,
    )(mine, t_own, t_other, c_own, c_other, a_own, a_other, b_own, b_other)
    return [outs[0], outs[2]], [outs[1], outs[3]]


def finish_kernel(n, *refs):
    terms, outs = refs[: 2 * n], refs[2 * n :]
    half = terms[0].shape[2]
    for g, out in enumerate(outs):
        for part in range(2):
            total = None
            for t in terms[part * n : (part + 1) * n]:
                value = t[g, 0, :, : out.shape[1]].astype(f32)
                total = value if total is None else total + value
            out[part * half : (part + 1) * half, :] = total


def finish(terms, columns):
    flat = terms[0] + terms[1]
    groups, _, half, n = flat[0].shape
    return pl.pallas_call(
        functools.partial(finish_kernel, len(terms[0])),
        name="finish",
        grid=(1,),
        in_specs=[whole((groups, 1, half, n))] * len(flat),
        out_specs=[whole((2 * half, columns))] * groups,
        out_shape=[struct((2 * half, columns), f32)] * groups,
    )(*flat)


def middle_back_kernel(
    mine, own, above, fa, fb, below, middle, scale, cot, gain, w_out,
    grad_middle, turned, grad_context, gain_grad, g_s,
):
    k = pl.program_id(0)
    half = fa.shape[0]
    for at, ref in ((0, own), (1, above), (3, below)):
        @pl.when(k == at)
        def _():
            g_s[...] = ref[...].astype(f32)

    @pl.when(k == 2)
    def _():
        g_s[:half, :] = fa[...].astype(f32)
        g_s[half:, :] = fb[...].astype(f32)

    g = g_s[...]
    r = scale[...]
    n2 = middle[...] * r
    u2 = g * as_row(gain)
    gm = cot[...].astype(f32) + r * (u2 - n2 * jnp.mean(u2 * n2, axis=1, keepdims=True))
    part = jnp.sum(g * n2, axis=0, keepdims=True)

    @pl.when(k == 0)
    def _():
        gain_grad[...] = part

    @pl.when(k > 0)
    def _():
        gain_grad[...] = gain_grad[...] + part

    grad_middle[...] = gm
    turned[...] = jnp.transpose(gm.astype(bf16))
    grad_context[...] = dot(gm.astype(bf16), w_out[...], NT).astype(bf16)


def middle_back(mine, pieces, middle, scale, cot, gain, w_out):
    rows, width = middle.shape
    block = rows // 4
    own, above, (fa, fb), below = pieces
    at = lambda c: pl.BlockSpec((block, c), lambda k, s: ((s[0] + k) % 4, 0))
    n = w_out.shape[0]
    return pl.pallas_call(
        middle_back_kernel,
        name="middle_back",
        grid_spec=pltpu.PrefetchScalarGridSpec(
            num_scalar_prefetch=1,
            grid=(4,),
            in_specs=[
                whole((block, width)), whole((block, width)),
                whole((block // 2, width)), whole((block // 2, width)), whole((block, width)),
                at(width), at(1), at(width), whole(gain.shape), whole(w_out.shape),
            ],
            out_specs=[
                at(width),
                pl.BlockSpec((width, block), lambda k, s: (0, (s[0] + k) % 4)),
                at(n),
                whole((1, width)),
            ],
            scratch_shapes=[pltpu.VMEM((block, width), f32)],
        ),
        out_shape=[
            struct((rows, width), f32), struct((width, rows), bf16),
            struct((rows, n), bf16), struct((1, width), f32),
        ],
    )(mine, own, above, fa, fb, below, middle, scale, cot, gain, w_out)


def in_rows_kernel(mine, own, above, fa, fb, below, out):
    block = own.shape[0]
    at = lambda k: pl.ds(pl.multiple_of((mine[0] + k) % 4 * block, block), block)
    out[at(0), :] = own[...]
    out[at(1), :] = above[...]
    out[at(2), :] = jnp.concatenate([fa[...], fb[...]], axis=0)
    out[at(3), :] = below[...]


def in_rows(mine, pieces):
    own, above, (fa, fb), below = pieces
    rows, width = own.shape
    return pl.pallas_call(
        in_rows_kernel,
        name="in_rows",
        in_specs=[SMEM] + [VMEM] * 5,
        out_specs=VMEM,
        out_shape=struct((4 * rows, width), bf16),
    )(mine, own, above, fa, fb, below)


def late_kernel(head, q, pair, cross, cosine, sine, late, bias):
    rows, n = q.shape
    kv = KEY_VALUE_HEADS * HEAD_SIZE

    def lin(ref):
        g = ref[:, :HEAD_SIZE].astype(f32)
        key = g * cosine[...] - pltpu.roll(g, HEAD_SIZE // 2, 1) * sine[...]
        return key, ref[:, HEAD_SIZE:].astype(f32)

    (own_k, own_v), (other_k, other_v) = lin(pair), lin(cross)
    first = head[0] == 0
    late[:, :n] = q[...]
    columns = [
        jnp.where(first, own_k, other_k), jnp.where(first, other_k, own_k),
        jnp.where(first, own_v, other_v), jnp.where(first, other_v, own_v),
    ]
    for c, value in enumerate(columns):
        late[:, n + c * HEAD_SIZE : n + (c + 1) * HEAD_SIZE] = value.astype(bf16)
    bias[...] = jnp.sum(late[...].astype(f32), axis=0, keepdims=True)


def late_grads(head, q, pair, cross, cosine, sine):
    rows, n = q.shape
    total = n + 2 * KEY_VALUE_HEADS * HEAD_SIZE
    return pl.pallas_call(
        late_kernel,
        name="late_grads",
        in_specs=[SMEM] + [VMEM] * 5,
        out_specs=[VMEM] * 2,
        out_shape=[struct((rows, total), bf16), struct((1, total), f32)],
    )(head, q, pair, cross, cosine, sine)


def project_back_kernel(
    core, x, late, above, fa, fb, below, w_own, mine, other, wk, wv, gain, grad_middle,
    gain_two_grad, bias, out, vectors,
):
    i = pl.program_id(0)
    n = w_own.shape[1]
    kv = wk.shape[1]
    far = jnp.where(i == 0, fa[...].astype(f32), fb[...].astype(f32)).astype(bf16)
    part = lambda m: (
        dot(above[...], m[:n, :]) + dot(below[...], m[n : 2 * n, :]) + dot(far, m[2 * n :, :])
    )
    a, b = part(mine), part(other)
    first = core[0] == 0
    g = jnp.concatenate([jnp.where(first, a, b), jnp.where(first, b, a)], axis=1)
    g = g + dot(late[:, :n], w_own[...], NT)
    g = g + dot(late[:, n : n + kv], wk[...], NT) + dot(late[:, n + kv :], wv[...], NT)
    xf = x[...].astype(f32)
    r = lax.rsqrt(jnp.mean(xf * xf, axis=1, keepdims=True) + eps)
    n1 = xf * r
    u1 = g * as_row(gain)
    out[...] = (
        grad_middle[...] + r * (u1 - n1 * jnp.mean(u1 * n1, axis=1, keepdims=True))
    ).astype(bf16)
    total = jnp.sum(g * n1, axis=0, keepdims=True)
    width = x.shape[1]

    @pl.when(i == 0)
    def _():
        vectors[:, :width] = total
        vectors[:, width : 2 * width] = gain_two_grad[...]
        vectors[:, 2 * width :] = bias[...]

    @pl.when(i > 0)
    def _():
        vectors[:, :width] = vectors[:, :width] + total


def project_back(
    core, x, late, pieces, w_own, mine, other, wk, wv, gain, grad_middle, gain_two_grad, bias
):
    rows, width = x.shape
    n = w_own.shape[1]
    half = rows // 2
    above, (fa, fb), below = pieces
    block = lambda c: pl.BlockSpec((half, c), lambda i, s: (i, 0))
    return pl.pallas_call(
        project_back_kernel,
        name="project_back",
        grid_spec=pltpu.PrefetchScalarGridSpec(
            num_scalar_prefetch=1,
            grid=(2,),
            in_specs=[
                block(width), block(late.shape[1]), block(n), whole((half, n)), whole((half, n)),
                block(n), whole(w_own.shape), whole(mine.shape), whole(other.shape),
                whole(wk.shape), whole(wv.shape), whole(gain.shape), block(width),
                whole(gain_two_grad.shape), whole(bias.shape),
            ],
            out_specs=[block(width), whole((1, 2 * width + bias.shape[1]))],
        ),
        out_shape=[struct((rows, width), bf16), struct((1, 2 * width + bias.shape[1]), f32)],
    )(
        core, x, late, above, fa, fb, below, w_own, mine, other, wk, wv, gain, grad_middle,
        gain_two_grad, bias,
    )


def place_tokens(index, lengths):
    ends = jnp.cumsum(lengths)
    before = (ends[None, :] <= index[:, None]).astype(jnp.int32)
    return index - jnp.sum(before * lengths[None, :], axis=1)


def on_device(
    hidden_in,
    cotangent,
    lengths,
    valid,
    gain_one,
    w_query,
    b_query,
    key_projection,
    key_bias_vector,
    value_projection,
    value_bias_vector,
    w_out,
    gain_two,
    w_gate,
    w_up,
    w_down,
):
    rows, width = hidden_in.shape
    n_wide = lax.axis_size("wide")
    wide_index = lax.axis_index("wide")
    narrow_index = lax.axis_index("narrow")
    heads = w_query.shape[1] // HEAD_SIZE
    n_query = heads * HEAD_SIZE
    kv_width = KEY_VALUE_HEADS * HEAD_SIZE
    head = narrow_index * heads // (QUERY_HEADS // KEY_VALUE_HEADS)
    bits = [1 << b for b in reversed(range(n_wide.bit_length() - 1))]
    chip_bits = bits[:-1]
    up_first, down_first = bits, chip_bits[::-1] + [1]
    low_chip = chip_bits[::-1]
    slots = n_wide // 2
    core = wide_index % 2
    base = wide_index * rows
    as_scalar = lambda v: v.astype(jnp.int32).reshape(1)
    mine_wide, mine_narrow, core_s, head_s = map(
        as_scalar, (wide_index, narrow_index, core, head)
    )
    swap_core = lambda v: swap_wide(v, 1)

    token_index = base + jnp.arange(rows, dtype=jnp.int32)
    positions = place_tokens(token_index, lengths)
    start = (token_index - positions)[None, :]
    info = jnp.concatenate([mine_wide, lengths])
    freqs = 10000.0 ** (-(jnp.arange(HEAD_SIZE // 2, dtype=f32) * 2.0) / HEAD_SIZE)
    angles = positions.astype(f32)[:, None] * freqs[None, :]
    cos_half, sin_half = jnp.cos(angles), jnp.sin(angles)
    cosine = jnp.concatenate([cos_half, cos_half], axis=1)
    sine = jnp.concatenate([-sin_half, sin_half], axis=1)

    flags = jnp.pad(
        valid.astype(bf16).reshape(rows // HEAD_SIZE, HEAD_SIZE),
        ((0, FLAG_ROWS - rows // HEAD_SIZE), (0, 0)),
    )
    acts_one, key_own, value_own = front(
        head_s,
        hidden_in,
        gain_one,
        key_projection,
        value_projection,
        key_bias_vector,
        value_bias_vector,
        cosine,
        sine,
        flags,
    )

    col = width // 2
    n_half = n_query // 2
    half_query = lax.dynamic_slice_in_dim(w_query, core * col, col, 0).T
    spread_out = n_query // slots % 32 == 0
    if spread_out:
        quarter = n_query // slots
        half_out = lax.dynamic_slice(
            w_out, (wide_index // 2 * quarter, core * col), (quarter, col)
        )
    else:
        quarter = n_query
        half_out = lax.dynamic_slice_in_dim(w_out, core * col, col, 1)
    out_below, out_above = shift_narrow(half_out, 1), shift_narrow(half_out, -1)

    k_slots, keys = [(0,)], [key_own[None]]
    v_slots, values = [(0,)], [value_own[None]]
    join = lambda pieces: pieces[0] if len(pieces) == 1 else jnp.concatenate(pieces, axis=0)
    queries = turned_one = None
    for step, (k_bit, v_bit) in enumerate(zip(up_first, down_first)):
        k_send, v_send = join(keys), join(values)
        if step + 1 == len(up_first):
            k_send, v_send, queries, half_query, fetched = tie(
                (k_send, v_send, queries, half_query, fetched)
            )
        for names, pieces, send, bit in (
            (k_slots, keys, k_send, k_bit), (v_slots, values, v_send, v_bit)
        ):
            pieces.append(swap_wide(send, bit))
            names.append(tuple(s ^ bit for group in names for s in group))
        if step == 0:
            acts_late, out_below, out_above = tie(
                (acts_one, out_below, out_above), keys[1], values[1]
            )
            out_far_a = shift_narrow(out_below[: quarter // 2], 1)
            out_far_b = shift_narrow(out_above[quarter // 2 :], -1)
            fetched = jnp.concatenate([out_above, out_below, out_far_a, out_far_b], axis=0)
            queries, turned_one = project_queries(
                acts_late, cotangent, w_query, b_query, cosine, sine
            )
    k_pieces, v_pieces = list(zip(k_slots, keys)), list(zip(v_slots, values))
    fetched = tie(fetched, keys[-1], values[-1])
    context, lse = attend(info, queries, start, k_pieces, v_pieces)
    if spread_out:
        cut_at = fetched.shape[0] // 2
        parts = []
        moving = [[((0,), fetched[None, :cut_at])], [((0,), fetched[None, cut_at:])]]
        spread_steps = list(zip(low_chip, chip_bits))
        for step, bits_ in enumerate(spread_steps):
            for part, bit in enumerate(bits_):
                payload = join([a for _, a in moving[part]])
                if step:
                    payload = tie(payload, context)
                names = [s ^ (bit >> 1) for group, _ in moving[part] for s in group]
                moving[part].append((tuple(names), swap_wide(payload, bit)))
        for part, first in ((0, 0), (1, cut_at)):
            parts += [(names, first, a) for names, a in moving[part]]

    half = rows // 2
    ctx_below, ctx_above = shift_narrow(context, 1), shift_narrow(context, -1)
    out_mine = fetched
    if spread_out:
        arrays, ctx_below, ctx_above = tie(([a for _, _, a in parts], ctx_below, ctx_above))
        parts = [(names, first, a) for (names, first, _), a in zip(parts, arrays)]
        out_mine = assemble(as_scalar(wide_index // 2), slots, parts)
    out_other = swap_core(out_mine)
    ctx_far = (shift_narrow(ctx_below[:half], 1), shift_narrow(ctx_above[half:], -1))
    turned_one_other = swap_core(turned_one)
    ctx_far, half_query = tie((ctx_far, half_query), turned_one_other, out_other)
    w_gate_t, w_up_t = w_gate.T, w_up.T
    middle, acts_two, turned_two, scale_two = project_out(
        core_s, hidden_in, (context, ctx_above, ctx_far, ctx_below),
        w_out, out_mine, out_other, gain_two,
    )

    query_below, query_above = shift_narrow(half_query, 1), shift_narrow(half_query, -1)
    hidden, grads = feed(acts_two, cotangent, w_gate_t, w_up_t, w_down)
    turned_two_other = swap_core(turned_two)
    (hidden, grads), query_below, query_above = tie(
        ((hidden, grads), query_below, query_above), turned_two_other
    )
    hidden_other = swap_core(hidden)
    query_far_a = shift_narrow(query_below[:n_half], 1)
    query_far_b = shift_narrow(query_above[n_half:], -1)
    own, above, far_a, far_b, below = partial_rows(
        "partial_back", mine_narrow, grads, [w_gate_t, w_up_t]
    )
    (own, above, far_a, far_b, below), hidden = tie(
        ((own, above, far_a, far_b, below), hidden), hidden_other, query_far_a, query_far_b
    )
    up, down = shift_narrow(far_a, 1), shift_narrow(far_b, -1)
    down_pair = weigh(
        mine_wide, slots, width, turned_one, turned_one_other, hidden[None], hidden_other[None]
    )
    grads_other = swap_core(grads)
    up, down, down_pair = tie((up, down, down_pair))
    orders = (low_chip, chip_bits)
    down_steps = Halving(down_pair, orders)
    down_moved = down_steps.exchange()
    to_above, to_below = pass_on(above, below, up, down)
    from_below, from_above = shift_narrow(to_above, 1), shift_narrow(to_below, -1)
    grads_here = tie(grads, to_above, to_below, grads_other)
    gate_pair = weigh(
        mine_wide, slots, width, turned_two, turned_two_other, grads_here, grads_other, 0
    )
    from_below, from_above, gate_pair = tie((from_below, from_above, gate_pair))
    gate_steps = Halving(gate_pair, orders)
    gate_moved = gate_steps.exchange()
    own = (own.astype(f32) + from_below.astype(f32) + from_above.astype(f32)).astype(bf16)
    q_rows = rows // 8
    g_below, g_above = shift_narrow(own, 1), shift_narrow(own, -1)
    grads_here = tie(grads_here, own)
    up_pair = weigh(
        mine_wide, slots, width, turned_two, turned_two_other, grads_here, grads_other, 1
    )
    g_below, g_above, up_pair, down_moved = tie((g_below, g_above, up_pair, down_moved))
    g_far = (shift_narrow(g_below[:q_rows], 1), shift_narrow(g_above[q_rows:], -1))
    ffn = partial_rows("partial_down", mine_narrow, tie(hidden, g_below)[None], [w_down])
    down_sends = down_steps.settle(down_moved)
    g_far, ffn, down_sends = tie((g_far, ffn, down_sends))
    grad_middle, turned_attn, grad_context, gain_two_grad = middle_back(
        mine_narrow, (own, g_above, g_far, g_below), middle, scale_two, cotangent,
        gain_two, w_out,
    )

    ffn_own, ffn_above, ffn_far_a, ffn_far_b, ffn_below = ffn
    ffn_up, ffn_down = shift_narrow(ffn_far_a, 1), shift_narrow(ffn_far_b, -1)
    grad_context, gate_moved = tie((grad_context, gate_moved))
    down_steps.sends = tie(down_sends, gate_moved)
    down_moved = down_steps.exchange()
    query_lin_grad, send, keep = attend_back(
        info, queries, grad_context, context, start, lse, cosine, sine, k_pieces, v_pieces
    )
    query_lin_grad, send, keep, down_moved, ffn_up, ffn_down = tie(
        (query_lin_grad, send, keep, down_moved, ffn_up, ffn_down)
    )
    turned_attn = tie(turned_attn, send)
    turned_attn_other = swap_core(turned_attn)
    down_steps.settle(down_moved)
    down_steps.rest()
    ql_below, ql_above = shift_narrow(query_lin_grad, 1), shift_narrow(query_lin_grad, -1)
    key_value = add_rounded(keep, swap_core(send))
    ql_far = (shift_narrow(ql_below[:half], 1), shift_narrow(ql_above[half:], -1))
    spread = (2,) * len(chip_bits) + key_value.shape[2:]
    key_part = xor_scatter(key_value[0].reshape(spread), chip_bits, low_chip)
    value_part = xor_scatter(key_value[1].reshape(spread), chip_bits, chip_bits)
    n_narrow = lax.axis_size("narrow")
    pair = jnp.concatenate([key_part, value_part], axis=1)
    pair, ql_far, up_sends, gate_moved = tie((pair, ql_far, up_pair[0], gate_moved))
    up_steps = Halving((up_sends, up_pair[1]), orders)
    up_moved = up_steps.exchange()
    partner = lax.ppermute(pair, "narrow", [(i, i ^ 1) for i in range(n_narrow)])
    query_mine = jnp.concatenate([query_above, query_below, query_far_a, query_far_b], axis=0)
    query_other = swap_core(query_mine)
    gate_steps.settle(gate_moved)
    gate_moved = gate_steps.exchange()
    pair = add_rounded(pair, partner)
    cross = lax.ppermute(pair, "narrow", [(i, n_narrow - 1 - i) for i in range(n_narrow)])
    cross, query_other, turned_attn_other, up_moved = tie(
        (cross, query_other, turned_attn_other, up_moved)
    )
    ffn_up = tie(ffn_up, cross)
    ffn_to = pass_on(ffn_above, ffn_below, ffn_up, ffn_down)
    ffn_from_below, ffn_from_above = shift_narrow(ffn_to[0], 1), shift_narrow(ffn_to[1], -1)
    late, bias = late_grads(head_s, query_lin_grad, pair, cross, cosine, sine)
    late_other = swap_core(late)
    up_sends = up_steps.settle(up_moved)
    late_other, up_sends, gate_moved = tie((late_other, up_sends, gate_moved))
    up_steps.sends = up_sends
    up_moved = up_steps.exchange()
    late_pair = weigh_late(
        mine_wide, slots, turned_attn, turned_attn_other, turned_two, turned_two_other,
        turned_one, turned_one_other, late, late_other,
    )
    late_pair, up_moved = tie((late_pair, up_moved))
    late_steps = Halving(late_pair, orders)
    late_moved = late_steps.exchange()
    late, ffn_from_below, ffn_from_above = tie((late, ffn_from_below, ffn_from_above), late_pair)
    out_rows = lax.dynamic_slice_in_dim(middle, narrow_index * (rows // 4), rows // 4, 0)
    out_rows = (
        out_rows + ffn_own.astype(f32) + ffn_from_below.astype(f32) + ffn_from_above.astype(f32)
    ).astype(bf16)
    o_below, o_above = shift_narrow(out_rows, 1), shift_narrow(out_rows, -1)
    grad_hidden_in, vectors = project_back(
        core_s, hidden_in, late, (ql_above, ql_far, ql_below), w_query, query_mine, query_other,
        key_projection, value_projection, gain_one, grad_middle, gain_two_grad, bias,
    )
    late_moved, vectors, o_below, o_above = tie((late_moved, vectors, o_below, o_above))
    late_steps.settle(late_moved)
    late_steps.rest()

    for bit in bits[::-1]:
        vectors = vectors + swap_wide(vectors, bit)
    vectors = vectors[0]

    def own_part(first, size):
        return lax.dynamic_slice_in_dim(vectors, first + wide_index * (size // n_wide), size // n_wide)

    bias_at = 2 * width
    query_bias = vectors[bias_at : bias_at + n_query].reshape(heads, n_wide, -1)
    query_bias = lax.dynamic_index_in_dim(query_bias, wide_index, 1, keepdims=False)

    o_far = (shift_narrow(o_below[:q_rows], 1), shift_narrow(o_above[q_rows:], -1))
    output = in_rows(mine_narrow, (out_rows, o_above, o_far, o_below))

    gate_steps.settle(gate_moved)
    gate_steps.rest()
    up_steps.settle(up_moved)
    up_steps.rest()
    n_hidden = w_down.shape[0]
    (down_sum,) = finish(down_steps.terms, n_hidden)
    (gate_sum,) = finish(gate_steps.terms, n_hidden)
    (up_sum,) = finish(up_steps.terms, n_hidden)
    (late_sum,) = finish(late_steps.terms, late_steps.terms[0][0].shape[3])
    return (
        output,
        grad_hidden_in,
        own_part(0, width),
        late_sum[:, n_query : 2 * n_query],
        query_bias,
        late_sum[:, 2 * n_query : 2 * n_query + kv_width],
        own_part(bias_at + n_query, kv_width),
        late_sum[:, 2 * n_query + kv_width :],
        own_part(bias_at + n_query + kv_width, kv_width),
        late_sum[:, :n_query].T,
        own_part(width, width),
        gate_sum,
        up_sum,
        down_sum.T,
    )


def solution(mesh):
    placed = (
        P("wide", None),
        P("wide", None),
        P(),
        P("wide"),
        P(),
        P(None, "narrow"),
        P("narrow"),
        P(),
        P(),
        P(),
        P(),
        P("narrow", None),
        P(),
        P(None, "narrow"),
        P(None, "narrow"),
        P("narrow", None),
    )
    return jax.shard_map(
        on_device,
        mesh=mesh,
        in_specs=placed,
        out_specs=(
            P("wide", None),
            P("wide", None),
            P("wide"),
            P("wide", "narrow"),
            P("narrow", "wide"),
            P("wide", None),
            P("wide"),
            P("wide", None),
            P("wide"),
            P("narrow", "wide"),
            P("wide"),
            P("wide", "narrow"),
            P("wide", "narrow"),
            P("narrow", "wide"),
        ),
        check_vma=False,
    )
```

```python
import functools
import math

import jax
import jax.numpy as jnp
from jax import lax
from jax.experimental import pallas as pl
from jax.experimental.pallas import tpu as pltpu
from jax.sharding import PartitionSpec as P

QUERY_HEADS = 12
KEY_VALUE_HEADS = 2
HEAD_SIZE = 128
FLAG_ROWS = 16

eps = 1e-06
big_negative = -1e30
score_scale = 1.0 / math.sqrt(HEAD_SIZE)
log2_scale = score_scale * math.log2(math.e)

bf16 = jnp.bfloat16
f32 = jnp.float32
ANY = pl.BlockSpec(memory_space=pl.ANY)
VMEM = pl.BlockSpec(memory_space=pltpu.VMEM)
SMEM = pl.BlockSpec(memory_space=pltpu.SMEM)


def dot(a, b, dims=((1,), (0,))):
    return lax.dot_general(a, b, (dims, ((), ())), preferred_element_type=f32)


NT = ((1,), (1,))
TN = ((0,), (0,))


def swap_wide(array, bit):
    n = lax.axis_size("wide")
    return lax.ppermute(array, "wide", [(i, i ^ bit) for i in range(n)])


def shift_narrow(array, by):
    n = lax.axis_size("narrow")
    return lax.ppermute(array, "narrow", [(i, (i + by) % n) for i in range(n)])


def ring_gather(block):
    half = block.shape[0] // 2
    below = shift_narrow(block, 1)
    above = shift_narrow(block, -1)
    far_a = shift_narrow(below[:half], 1)
    far_b = shift_narrow(above[half:], -1)
    return [block, above, jnp.concatenate([far_a, far_b], axis=0), below]


def ring_scatter(parts):
    half = parts[0].shape[0] // 2
    add = lambda a, b: (a.astype(f32) + b.astype(f32)).astype(bf16)
    up = shift_narrow(parts[2][:half], 1)
    down = shift_narrow(parts[2][half:], -1)
    to_above = jnp.concatenate([add(parts[1][:half], up), parts[1][half:]], axis=0)
    to_below = jnp.concatenate([parts[3][:half], add(parts[3][half:], down)], axis=0)
    from_below = shift_narrow(to_above, 1)
    from_above = shift_narrow(to_below, -1)
    return parts[0].astype(f32) + from_below.astype(f32) + from_above.astype(f32)


def xor_gather(block, bits):
    slots, held = [0], [block[None]]
    pieces = [((0,), block[None])]
    for bit in bits:
        payload = held[0] if len(held) == 1 else jnp.concatenate(held, axis=0)
        received = swap_wide(payload, bit)
        new = [s ^ bit for s in slots]
        pieces.append((tuple(new), received))
        slots, held = slots + new, [payload, received]
    return pieces


def add_rounded(a, b):
    return (a.astype(f32) + b.astype(f32)).astype(bf16)


def xor_scatter(array, bits, order):
    bits = list(bits)
    for bit in order:
        axis = bits.index(bit)
        keep = lax.index_in_dim(array, 0, axis, keepdims=False)
        send = lax.index_in_dim(array, 1, axis, keepdims=False)
        array = add_rounded(keep, swap_wide(send, bit))
        bits.remove(bit)
    return array


def tie(values, *gates):
    return lax.optimization_barrier((values, gates))[0]


class Halving:
    def __init__(self, pair, orders):
        self.sends, keeps = pair
        self.terms = [[k] for k in keeps]
        self.views = [[k] for k in keeps]
        self.orders = [list(o) for o in orders]

    def exchange(self):
        return [swap_wide(s, order.pop(0)) for s, order in zip(self.sends, self.orders)]

    def settle(self, received):
        for part in range(2):
            self.terms[part].append(received[part])
            self.views[part].append(received[part])
        if not self.orders[0]:
            return None
        n = self.views[0][0].shape[1]
        total = lambda terms: sum(t.astype(f32) for t in terms).astype(bf16)
        self.sends = [
            total([t[:, 1::2] for t in self.views[0]]),
            total([t[:, n // 2 :] for t in self.views[1]]),
        ]
        self.views = [
            [t[:, ::2] for t in self.views[0]],
            [t[:, : n // 2] for t in self.views[1]],
        ]
        return self.sends

    def rest(self):
        while self.orders[0]:
            self.settle(self.exchange())


def as_row(vector):
    return vector[...].astype(f32).reshape(1, -1)


def rope(value, cosine, signed_sine):
    return value * cosine + pltpu.roll(value, HEAD_SIZE // 2, 1) * signed_sine


def front_kernel(head, x, gain, wk, wv, bk, bv, cosine, sine, flags, acts_out, k_out, v_out):
    rows = x.shape[0]
    of_head = lambda b: jnp.where(
        head[0] == 0, as_row(b)[:, :HEAD_SIZE], as_row(b)[:, HEAD_SIZE:]
    )
    xf = x[...].astype(f32)
    scale = lax.rsqrt(jnp.mean(xf * xf, axis=1, keepdims=True) + eps)
    acts = (xf * scale * as_row(gain)).astype(bf16)
    acts_out[...] = acts
    key = dot(acts, wk[...]) + of_head(bk)
    k_out[:rows, :] = rope(key, cosine[...], sine[...]).astype(bf16)
    k_out[rows:, :] = flags[...]
    v_out[...] = (dot(acts, wv[...]) + of_head(bv)).astype(bf16)


def front(head, x, gain, wk, wv, bk, bv, cosine, sine, flags):
    rows, width = x.shape
    whole = lambda *shape: pl.BlockSpec(shape, lambda i, h: (0,) * len(shape))
    column = lambda r: pl.BlockSpec((r, HEAD_SIZE), lambda i, h: (0, h[0]))
    return pl.pallas_call(
        front_kernel,
        name="front",
        grid_spec=pltpu.PrefetchScalarGridSpec(
            num_scalar_prefetch=1,
            grid=(1,),
            in_specs=[
                whole(rows, width),
                whole(width),
                column(width),
                column(width),
                whole(*bk.shape),
                whole(*bv.shape),
                whole(rows, HEAD_SIZE),
                whole(rows, HEAD_SIZE),
                whole(FLAG_ROWS, HEAD_SIZE),
            ],
            out_specs=[
                whole(rows, width),
                whole(rows + FLAG_ROWS, HEAD_SIZE),
                whole(rows, HEAD_SIZE),
            ],
        ),
        out_shape=[
            jax.ShapeDtypeStruct((rows, width), bf16),
            jax.ShapeDtypeStruct((rows + FLAG_ROWS, HEAD_SIZE), bf16),
            jax.ShapeDtypeStruct((rows, HEAD_SIZE), bf16),
        ],
    )(head, x, gain, wk, wv, bk, bv, cosine, sine, flags)


def query_kernel(acts, cot, w, b, cosine, sine, out, turned):
    lin = dot(acts[...], w[...]) + as_row(b)
    for h in range(out.shape[1] // HEAD_SIZE):
        cols = slice(h * HEAD_SIZE, (h + 1) * HEAD_SIZE)
        out[:, cols] = rope(lin[:, cols], cosine[...], sine[...]).astype(bf16)
    turned[0] = jnp.transpose(cot[...])
    turned[1] = jnp.transpose(acts[...])


def project_queries(acts, cot, w, b, cosine, sine):
    rows, width = acts.shape
    return pl.pallas_call(
        query_kernel,
        name="queries",
        in_specs=[VMEM] * 6,
        out_specs=[VMEM, VMEM],
        out_shape=[
            jax.ShapeDtypeStruct((rows, w.shape[1]), bf16),
            jax.ShapeDtypeStruct((2, width, rows), bf16),
        ],
    )(acts, cot, w, b, cosine, sine)


def load_pieces(k_refs, v_refs, k_slots, v_slots, kbuf, vbuf, sem):
    copies = []
    for which, refs, slots, buf in ((0, k_refs, k_slots, kbuf), (1, v_refs, v_slots, vbuf)):
        for ref, names in zip(refs, slots):
            for at, slot in enumerate(names):
                copies.append(
                    pltpu.make_async_copy(ref.at[at], buf.at[slot], sem.at[which, slot])
                )
    for copy in copies:
        copy.start()
    return copies


def key_codes(kbuf, slot, half, base, chunk):
    rows = kbuf.shape[1] - FLAG_ROWS
    per = chunk // HEAD_SIZE
    flags = jnp.transpose(kbuf[slot, rows:, :].astype(f32))
    columns = []
    for c in range(per):
        first = flags[:, c : c + 1]
        second = flags[:, per + c : per + c + 1]
        columns.append(jnp.where(half == 1, second, first))
    column = jnp.concatenate(columns, axis=0)
    index = base + lax.broadcasted_iota(jnp.int32, (chunk, 1), 0)
    return jnp.where(column > 0, index, -1)


def visible(codes, start, diagonal):
    seen = codes >= start
    if diagonal:
        shape = (codes.shape[0], start.shape[1])
        row = lax.broadcasted_iota(jnp.int32, shape, 0)
        col = lax.broadcasted_iota(jnp.int32, shape, 1)
        seen = (seen & (row < col)) | (row == col)
    return seen


def first_chunk(info, rows, chunk):
    base = info[0] * rows
    end = first = jnp.int32(0)
    for s in range(1, info.shape[0]):
        end = end + info[s]
        first = jnp.where(end <= base, end, first)
    return first // chunk


def forward_kernel(k_slots, v_slots, info, q, start, *refs):
    nk, nv = len(k_slots), len(v_slots)
    k_refs, v_refs = refs[:nk], refs[nk : nk + nv]
    out, lse, kbuf, vbuf, sem, acc_s, m_s, l_s = refs[nk + nv :]
    rows = q.shape[0]
    heads = q.shape[1] // HEAD_SIZE
    chunk = rows // 2
    own = info[0]
    copies = load_pieces(k_refs, v_refs, k_slots, v_slots, kbuf, vbuf, sem)
    for copy in copies:
        copy.wait()

    def tile(h, k, v, codes, lo, n, diagonal):
        qh = q[lo : lo + n, h * HEAD_SIZE : (h + 1) * HEAD_SIZE]
        s = dot(k, qh, NT) * log2_scale
        s = jnp.where(visible(codes, start[:, lo : lo + n], diagonal), s, big_negative)
        peak = jnp.max(s, axis=0, keepdims=True)
        cols = slice(lo, lo + n)
        if diagonal:
            p = jnp.exp2(s - peak)
            m_s[h : h + 1, cols] = peak
            l_s[h : h + 1, cols] = jnp.sum(p, axis=0, keepdims=True)
            acc_s[h, :, cols] = dot(v, p.astype(bf16), TN)
        else:
            old = m_s[h : h + 1, cols]
            new = jnp.maximum(old, peak)
            alpha = jnp.exp2(old - new)
            p = jnp.exp2(s - new)
            m_s[h : h + 1, cols] = new
            l_s[h : h + 1, cols] = alpha * l_s[h : h + 1, cols] + jnp.sum(p, axis=0, keepdims=True)
            acc_s[h, :, cols] = alpha * acc_s[h, :, cols] + dot(v, p.astype(bf16), TN)

    base = own * rows
    for half in (1, 0):
        k = kbuf[0, half * chunk : (half + 1) * chunk, :]
        v = vbuf[0, half * chunk : (half + 1) * chunk, :]
        codes = key_codes(kbuf, 0, half, base + half * chunk, chunk)
        for h in range(heads):
            tile(h, k, v, codes, half * chunk, chunk, True)
            if half == 0:
                tile(h, k, v, codes, chunk, chunk, False)

    def step(c, carry):
        block, half = c // 2, c % 2
        slot = lax.bitwise_xor(block, own)
        at = pl.multiple_of(half * chunk, chunk)
        k = kbuf[slot, pl.ds(at, chunk), :]
        v = vbuf[slot, pl.ds(at, chunk), :]
        codes = key_codes(kbuf, slot, half, c * chunk, chunk)
        for h in range(heads):
            tile(h, k, v, codes, 0, rows, False)
        return carry

    lax.fori_loop(first_chunk(info, rows, chunk), own * 2, step, 0)
    lse[...] = jnp.zeros_like(lse)
    for h in range(heads):
        total = l_s[h : h + 1, :]
        lse[h : h + 1, :] = m_s[h : h + 1, :] + jnp.log2(total)
        o = acc_s[h] * (1.0 / total)
        out[:, h * HEAD_SIZE : (h + 1) * HEAD_SIZE] = jnp.transpose(o).astype(bf16)


def attend(info, q, start, k_pieces, v_pieces):
    rows, width = q.shape
    heads = width // HEAD_SIZE
    slots = sum(len(s) for s, _ in k_pieces)
    return pl.pallas_call(
        functools.partial(
            forward_kernel, [s for s, _ in k_pieces], [s for s, _ in v_pieces]
        ),
        name="attend",
        in_specs=[SMEM, VMEM, VMEM] + [ANY] * (len(k_pieces) + len(v_pieces)),
        out_specs=[VMEM, VMEM],
        out_shape=[
            jax.ShapeDtypeStruct((rows, width), bf16),
            jax.ShapeDtypeStruct((8, rows), f32),
        ],
        scratch_shapes=[
            pltpu.VMEM((slots, rows + FLAG_ROWS, HEAD_SIZE), bf16),
            pltpu.VMEM((slots, rows, HEAD_SIZE), bf16),
            pltpu.SemaphoreType.DMA((2, slots)),
            pltpu.VMEM((heads, HEAD_SIZE, rows), f32),
            pltpu.VMEM((8, rows), f32),
            pltpu.VMEM((8, rows), f32),
        ],
    )(info, q, start, *[a for _, a in k_pieces], *[a for _, a in v_pieces])


def backward_kernel(k_slots, v_slots, info, q, do, ctx, start, lse, cosine, sine, *refs):
    nk, nv = len(k_slots), len(v_slots)
    k_refs, v_refs = refs[:nk], refs[nk : nk + nv]
    dq_out, send, keep, kbuf, vbuf, sem, dq_s, delta_s = refs[nk + nv :]
    rows = q.shape[0]
    heads = q.shape[1] // HEAD_SIZE
    chunk = rows // 2
    own = info[0]
    copies = load_pieces(k_refs, v_refs, k_slots, v_slots, kbuf, vbuf, sem)
    send[...] = jnp.zeros_like(send)
    keep[...] = jnp.zeros_like(keep)
    for h in range(heads):
        cols = slice(h * HEAD_SIZE, (h + 1) * HEAD_SIZE)
        both = do[:, cols].astype(f32) * ctx[:, cols].astype(f32)
        delta_s[h : h + 1, :] = jnp.sum(jnp.transpose(both), axis=0, keepdims=True)
        dq_s[h] = jnp.zeros((HEAD_SIZE, rows), f32)
    for copy in copies:
        copy.wait()

    def tile(h, k, v, codes, lo, n, diagonal):
        cols = slice(lo, lo + n)
        qh = q[cols, h * HEAD_SIZE : (h + 1) * HEAD_SIZE]
        doh = do[cols, h * HEAD_SIZE : (h + 1) * HEAD_SIZE]
        s = dot(k, qh, NT) * log2_scale - lse[h : h + 1, cols]
        s = jnp.where(visible(codes, start[:, cols], diagonal), s, big_negative)
        p = jnp.exp2(s)
        dv = dot(p.astype(bf16), doh)
        ds = (p * (dot(v, doh, NT) - delta_s[h : h + 1, cols])).astype(bf16)
        dk = dot(ds, qh)
        dq_s[h, :, cols] = dq_s[h, :, cols] + dot(k, ds, TN)
        return dk, dv

    def both(h, k, v, codes, spans):
        dk = dv = None
        for lo, n, diagonal in spans:
            a, b = tile(h, k, v, codes, lo, n, diagonal)
            dk, dv = (a, b) if dk is None else (dk + a, dv + b)
        return dk, dv

    def all_heads(k, v, codes, spans):
        dk = dv = None
        for h in range(heads):
            a, b = both(h, k, v, codes, spans)
            dk, dv = (a, b) if dk is None else (dk + a, dv + b)
        return (dk * score_scale).astype(bf16), dv.astype(bf16)

    base = own * rows
    for half in (1, 0):
        span = slice(half * chunk, (half + 1) * chunk)
        codes = key_codes(kbuf, 0, half, base + half * chunk, chunk)
        spans = [(chunk, chunk, True)] if half else [(0, chunk, True), (chunk, chunk, False)]
        dk, dv = all_heads(kbuf[0, span, :], vbuf[0, span, :], codes, spans)
        keep[0, 0, span, :] = dk
        keep[1, 0, span, :] = dv

    def step(c, carry):
        block, half = c // 2, c % 2
        slot = lax.bitwise_xor(block, own)
        at = pl.multiple_of(half * chunk, chunk)
        k = kbuf[slot, pl.ds(at, chunk), :]
        v = vbuf[slot, pl.ds(at, chunk), :]
        codes = key_codes(kbuf, slot, half, c * chunk, chunk)
        dk, dv = all_heads(k, v, codes, [(0, rows, False)])

        @pl.when(slot % 2 == 0)
        def _():
            keep[0, slot // 2, pl.ds(at, chunk), :] = dk
            keep[1, slot // 2, pl.ds(at, chunk), :] = dv

        @pl.when(slot % 2 == 1)
        def _():
            send[0, slot // 2, pl.ds(at, chunk), :] = dk
            send[1, slot // 2, pl.ds(at, chunk), :] = dv

        return carry

    lax.fori_loop(first_chunk(info, rows, chunk), own * 2, step, 0)
    for h in range(heads):
        g = jnp.transpose(dq_s[h]) * score_scale
        back = g * cosine[...] - pltpu.roll(g, HEAD_SIZE // 2, 1) * sine[...]
        dq_out[:, h * HEAD_SIZE : (h + 1) * HEAD_SIZE] = back.astype(bf16)


def attend_back(info, q, do, ctx, start, lse, cosine, sine, k_pieces, v_pieces):
    rows, width = q.shape
    heads = width // HEAD_SIZE
    slots = sum(len(s) for s, _ in k_pieces)
    half = jax.ShapeDtypeStruct((2, slots // 2, rows, HEAD_SIZE), bf16)
    return pl.pallas_call(
        functools.partial(
            backward_kernel, [s for s, _ in k_pieces], [s for s, _ in v_pieces]
        ),
        name="attend_back",
        in_specs=[SMEM] + [VMEM] * 7 + [ANY] * (len(k_pieces) + len(v_pieces)),
        out_specs=[VMEM] * 3,
        out_shape=[jax.ShapeDtypeStruct((rows, width), bf16), half, half],
        scratch_shapes=[
            pltpu.VMEM((slots, rows + FLAG_ROWS, HEAD_SIZE), bf16),
            pltpu.VMEM((slots, rows, HEAD_SIZE), bf16),
            pltpu.SemaphoreType.DMA((2, slots)),
            pltpu.VMEM((heads, HEAD_SIZE, rows), f32),
            pltpu.VMEM((8, rows), f32),
        ],
    )(
        info, q, do, ctx, start, lse, cosine, sine,
        *[a for _, a in k_pieces], *[a for _, a in v_pieces],
    )


def whole(shape):
    return pl.BlockSpec(shape, lambda *_: (0,) * len(shape))


def struct(shape, dtype):
    return jax.ShapeDtypeStruct(shape, dtype)


def project_out_kernel(
    core, x, own, above, fa, fb, below, w_own, mine, other, gain, middle, acts, turned, scale
):
    n = w_own.shape[0]
    width = x.shape[1]
    far = jnp.where(pl.program_id(0) == 0, fa[...].astype(f32), fb[...].astype(f32)).astype(bf16)
    part = lambda m: (
        dot(above[...], m[:n, :]) + dot(below[...], m[n : 2 * n, :]) + dot(far, m[2 * n :, :])
    )
    a, b = part(mine), part(other)
    first = core[0] == 0
    out = dot(own[...], w_own[...]) + jnp.concatenate(
        [jnp.where(first, a, b), jnp.where(first, b, a)], axis=1
    )
    mid = x[...].astype(f32) + out
    r = lax.rsqrt(jnp.mean(mid * mid, axis=1, keepdims=True) + eps)
    middle[...] = mid
    scale[...] = r
    normed = mid * r * as_row(gain)
    acts[...] = normed.astype(bf16)
    turned[:width, :] = jnp.transpose(normed.astype(bf16))
    turned[width:, :] = jnp.transpose(own[...])


def project_out(core, x, pieces, w_own, mine, other, gain):
    rows, width = x.shape
    n = w_own.shape[0]
    half = rows // 2
    own, above, (fa, fb), below = pieces
    block = lambda c: pl.BlockSpec((half, c), lambda i, s: (i, 0))
    return pl.pallas_call(
        project_out_kernel,
        name="project_out",
        grid_spec=pltpu.PrefetchScalarGridSpec(
            num_scalar_prefetch=1,
            grid=(2,),
            in_specs=[
                block(width), block(n), block(n), whole((half, n)), whole((half, n)), block(n),
                whole(w_own.shape), whole(mine.shape), whole(other.shape), whole(gain.shape),
            ],
            out_specs=[
                block(width), block(width),
                pl.BlockSpec((width + n, half), lambda i, s: (0, i)),
                block(1),
            ],
        ),
        out_shape=[
            struct((rows, width), f32), struct((rows, width), bf16),
            struct((width + n, rows), bf16), struct((rows, 1), f32),
        ],
    )(core, x, own, above, fa, fb, below, w_own, mine, other, gain)


def ring_blocks(acc, mine, outs):
    block = acc.shape[0] // 4
    own, above, far_a, far_b, below = outs

    def take(k, first, size):
        at = ((mine[0] + k) % 4) * block + first
        return acc[pl.ds(pl.multiple_of(at, size), size), :].astype(bf16)

    own[...] = take(0, 0, block)
    above[...] = take(1, 0, block)
    far_a[...] = take(2, 0, block // 2)
    far_b[...] = take(2, block // 2, block // 2)
    below[...] = take(3, 0, block)


def block_sizes(rows):
    return [rows // 4, rows // 4, rows // 8, rows // 8, rows // 4]


def feed_kernel(n, mine, acts, cot, wg, wu, wd, hidden, grads, *refs):
    outs, acc = refs[:-1], refs[-1]
    j = pl.program_id(0)
    tile = wg.shape[0]
    part = min(256, tile)
    for lo in range(0, tile, part):
        cols = slice(lo, lo + part)
        gate = dot(acts[...], wg[cols, :], NT)
        up = dot(acts[...], wu[cols, :], NT)
        g = dot(cot[...], wd[cols, :], NT)
        sig = 1.0 / (1.0 + jnp.exp(-gate))
        silu = gate * sig
        column = j * tile + lo + lax.broadcasted_iota(jnp.int32, (1, part), 1)
        keep = lambda v: jnp.where(column < n, v, 0.0).astype(bf16)
        hidden[:, cols] = keep(silu * up)
        grads[0, :, cols] = keep(g * up * (sig * (1.0 + gate * (1.0 - sig))))
        grads[1, :, cols] = keep(g * silu)
    back = lambda k: dot(grads[0, :, :k], wg[:k, :]) + dot(grads[1, :, :k], wu[:k, :])
    steps = pl.cdiv(n, tile)

    @pl.when(j == 0)
    def _():
        acc[...] = back(min(n, tile))

    if steps > 2:
        @pl.when((j > 0) & (j < steps - 1))
        def _():
            acc[...] = acc[...] + back(tile)

    if steps > 1:
        @pl.when(j == steps - 1)
        def _():
            acc[...] = acc[...] + back(n - (steps - 1) * tile)

    @pl.when(j == steps - 1)
    def _():
        ring_blocks(acc, mine, outs)


def feed(mine, acts, cot, wg, wu, wd, tile=768):
    rows, width = acts.shape
    n = wg.shape[0]
    steps = pl.cdiv(n, tile)
    w_spec = pl.BlockSpec((tile, width), lambda j, s: (j, 0))
    sizes = block_sizes(rows)
    outs = pl.pallas_call(
        functools.partial(feed_kernel, n),
        name="feed",
        grid_spec=pltpu.PrefetchScalarGridSpec(
            num_scalar_prefetch=1,
            grid=(steps,),
            in_specs=[whole((rows, width)), whole((rows, width)), w_spec, w_spec, w_spec],
            out_specs=[
                pl.BlockSpec((rows, tile), lambda j, s: (0, j)),
                pl.BlockSpec((2, rows, tile), lambda j, s: (0, 0, j)),
            ]
            + [whole((r, width)) for r in sizes],
            scratch_shapes=[pltpu.VMEM((rows, width), f32)],
        ),
        out_shape=[struct((rows, steps * tile), bf16), struct((2, rows, steps * tile), bf16)]
        + [struct((r, width), bf16) for r in sizes],
    )(mine, acts, cot, wg, wu, wd)
    return outs[0], outs[1], outs[2:]


def stack_kernel(*refs):
    done = 0
    for ref in refs[:-1]:
        refs[-1][done : done + ref.shape[0], :] = ref[...]
        done += ref.shape[0]


def stack(arrays):
    rows = sum(a.shape[0] for a in arrays)
    return pl.pallas_call(
        stack_kernel,
        name="stack",
        in_specs=[VMEM] * len(arrays),
        out_specs=VMEM,
        out_shape=struct((rows, arrays[0].shape[1]), bf16),
    )(*arrays)


def assemble_kernel(plan, chip, *refs):
    out = refs[-1]
    n = out.shape[0] // 3
    block = n // plan[0]
    for ref, (names, first) in zip(refs, plan[1]):
        rows = ref.shape[1]
        for at, name in enumerate(names):
            source = lax.bitwise_xor(chip[0], name)
            done = 0
            while done < rows:
                piece, inside = divmod(first + done, block)
                size = min(rows - done, block - inside)
                to = pl.multiple_of(piece * n + source * block + inside, 16)
                out[pl.ds(to, size), :] = ref[at, done : done + size, :]
                done += size


def assemble(chip, chips, parts):
    one = sum({first: a.shape[1] for _, first, a in parts}.values())
    plan = (chips, [(names, first) for names, first, _ in parts])
    return pl.pallas_call(
        functools.partial(assemble_kernel, plan),
        name="assemble",
        in_specs=[SMEM] + [VMEM] * len(parts),
        out_specs=VMEM,
        out_shape=struct((chips * one, parts[0][2].shape[2]), bf16),
    )(chip, *[a for _, _, a in parts])


def partial_kernel(mine, a, w, *refs):
    refs[-1][...] = dot(a[:, : w.shape[0]], w[...])
    ring_blocks(refs[-1], mine, refs[:-1])


def partial_rows(mine, a, w, tile=512):
    rows, columns = a.shape
    inner, width = w.shape
    sizes = block_sizes(rows)
    return pl.pallas_call(
        partial_kernel,
        name="partial_down",
        grid_spec=pltpu.PrefetchScalarGridSpec(
            num_scalar_prefetch=1,
            grid=(width // tile,),
            in_specs=[whole(a.shape), pl.BlockSpec((inner, tile), lambda j, s: (0, j))],
            out_specs=[pl.BlockSpec((r, tile), lambda j, s: (0, j)) for r in sizes],
            scratch_shapes=[pltpu.VMEM((rows, tile), f32)],
        ),
        out_shape=[struct((r, width), bf16) for r in sizes],
    )(mine, a, w)


def pass_on_kernel(above, below, up, down, to_above, to_below):
    half = up.shape[0]
    to_above[:half, :] = (above[:half, :].astype(f32) + up[...].astype(f32)).astype(bf16)
    to_above[half:, :] = above[half:, :]
    to_below[:half, :] = below[:half, :]
    to_below[half:, :] = (below[half:, :].astype(f32) + down[...].astype(f32)).astype(bf16)


def pass_on(above, below, up, down):
    return pl.pallas_call(
        pass_on_kernel,
        name="pass_on",
        in_specs=[VMEM] * 4,
        out_specs=[VMEM] * 2,
        out_shape=[struct(above.shape, bf16)] * 2,
    )(above, below, up, down)


def weigh_kernel(slots, half, mine, a_own, a_other, b_own, b_other, *refs):
    send_a, keep_a, send_b, keep_b, lhs = refs
    rows = a_own.shape[1]
    block = 2 * half

    @pl.when(pl.program_id(0) == 0)
    def _():
        for s in range(slots):
            at = pl.multiple_of(lax.bitwise_xor(mine[0], 2 * s) * block, 16)
            lhs[s * block : (s + 1) * block, :rows] = a_own[pl.ds(at, block), :]
            lhs[s * block : (s + 1) * block, rows:] = a_other[pl.ds(at, block), :]

    g = dot(lhs[:, :rows], b_own[0]) + dot(lhs[:, rows:], b_other[0])
    place_slots(g, slots, half, 0, send_a, keep_a, send_b, keep_b)


def place_slots(g, slots, half, group, send_a, keep_a, send_b, keep_b):
    cols = slice(0, g.shape[1])
    for s in range(slots):
        first = g[2 * s * half : (2 * s + 1) * half].astype(bf16)
        second = g[(2 * s + 1) * half : (2 * s + 2) * half].astype(bf16)
        (send_a if s % 2 else keep_a)[group, s // 2, :, cols] = first
        (send_b if s >= slots // 2 else keep_b)[group, s % (slots // 2), :, cols] = second


def weigh(mine, slots, width, a_own, a_other, b_own, b_other, group=0, tile=768):
    rows = a_own.shape[-1]
    n = b_own.shape[2]
    if a_own.ndim == 3:
        a_spec = pl.BlockSpec((None, width, rows), lambda j, s: (0, 0, 0))
    else:
        a_spec = pl.BlockSpec((width, rows), lambda j, s: (0, 0))
    half = width // slots // 4
    b_spec = pl.BlockSpec((1, rows, tile), lambda j, s: (group, 0, j))
    out = pl.BlockSpec((1, slots // 2, half, tile), lambda j, s: (0, 0, 0, j))
    outs = pl.pallas_call(
        functools.partial(weigh_kernel, slots, half),
        name="weigh",
        grid_spec=pltpu.PrefetchScalarGridSpec(
            num_scalar_prefetch=1,
            grid=(pl.cdiv(n, tile),),
            in_specs=[a_spec, a_spec, b_spec, b_spec],
            out_specs=[out] * 4,
            scratch_shapes=[pltpu.VMEM((width // 2, 2 * rows), bf16)],
        ),
        out_shape=[struct((1, slots // 2, half, n), bf16)] * 4,
    )(mine, a_own, a_other, b_own, b_other)
    return [outs[0], outs[2]], [outs[1], outs[3]]


def weigh_late_kernel(
    slots, half, mine, t_own, t_other, c_own, c_other, a_own, a_other, b_own, b_other, *refs
):
    send_a, keep_a, send_b, keep_b = refs
    block = 2 * half

    def gather(ref):
        pieces = []
        for s in range(slots):
            at = pl.multiple_of(lax.bitwise_xor(mine[0], 2 * s) * block, 16)
            pieces.append(ref[pl.ds(at, block), :])
        return jnp.concatenate(pieces, axis=0)

    n = c_own.shape[0]
    g = dot(gather(t_own), c_own[...], NT) + dot(gather(t_other), c_other[...], NT)
    late = dot(gather(a_own), b_own[...]) + dot(gather(a_other), b_other[...])
    g = jnp.concatenate([g, late], axis=1)
    place_slots(g, slots, half, 0, send_a, keep_a, send_b, keep_b)


def weigh_late(mine, slots, t_own, t_other, c_own, c_other, a_own, a_other, b_own, b_other):
    width, rows = t_own.shape
    n = c_own.shape[0] - width
    half = width // slots // 4
    total = n + b_own.shape[1]
    t_spec = whole((width, rows))
    c_spec = pl.BlockSpec((n, rows), lambda i, s: (width // n, 0))
    a_spec = pl.BlockSpec((None, width, rows), lambda i, s: (1, 0, 0))
    b_spec = whole(b_own.shape)
    shape = (1, slots // 2, half, total)
    outs = pl.pallas_call(
        functools.partial(weigh_late_kernel, slots, half),
        name="weigh_late",
        grid_spec=pltpu.PrefetchScalarGridSpec(
            num_scalar_prefetch=1,
            grid=(1,),
            in_specs=[t_spec, t_spec, c_spec, c_spec, a_spec, a_spec, b_spec, b_spec],
            out_specs=[whole(shape)] * 4,
        ),
        out_shape=[struct(shape, bf16)] * 4,
    )(mine, t_own, t_other, c_own, c_other, a_own, a_other, b_own, b_other)
    return [outs[0], outs[2]], [outs[1], outs[3]]


def finish_kernel(n, *refs):
    terms, outs = refs[: 2 * n], refs[2 * n :]
    half = terms[0].shape[2]
    for g, out in enumerate(outs):
        for part in range(2):
            total = None
            for t in terms[part * n : (part + 1) * n]:
                value = t[g, 0, :, : out.shape[1]].astype(f32)
                total = value if total is None else total + value
            out[part * half : (part + 1) * half, :] = total


def finish(terms, columns):
    flat = terms[0] + terms[1]
    groups, _, half, n = flat[0].shape
    return pl.pallas_call(
        functools.partial(finish_kernel, len(terms[0])),
        name="finish",
        grid=(1,),
        in_specs=[whole((groups, 1, half, n))] * len(flat),
        out_specs=[whole((2 * half, columns))] * groups,
        out_shape=[struct((2 * half, columns), f32)] * groups,
    )(*flat)


def middle_back_kernel(
    mine, own, above, fa, fb, below, middle, scale, cot, gain, w_out,
    grad_middle, turned, grad_context, gain_grad, g_s,
):
    k = pl.program_id(0)
    half = fa.shape[0]
    for at, ref in ((0, own), (1, above), (3, below)):
        @pl.when(k == at)
        def _():
            g_s[...] = ref[...].astype(f32)

    @pl.when(k == 2)
    def _():
        g_s[:half, :] = fa[...].astype(f32)
        g_s[half:, :] = fb[...].astype(f32)

    g = g_s[...]
    r = scale[...]
    n2 = middle[...] * r
    u2 = g * as_row(gain)
    gm = cot[...].astype(f32) + r * (u2 - n2 * jnp.mean(u2 * n2, axis=1, keepdims=True))
    part = jnp.sum(g * n2, axis=0, keepdims=True)

    @pl.when(k == 0)
    def _():
        gain_grad[...] = part

    @pl.when(k > 0)
    def _():
        gain_grad[...] = gain_grad[...] + part

    grad_middle[...] = gm
    turned[...] = jnp.transpose(gm.astype(bf16))
    grad_context[...] = dot(gm.astype(bf16), w_out[...], NT).astype(bf16)


def middle_back(mine, pieces, middle, scale, cot, gain, w_out):
    rows, width = middle.shape
    block = rows // 4
    own, above, (fa, fb), below = pieces
    at = lambda c: pl.BlockSpec((block, c), lambda k, s: ((s[0] + k) % 4, 0))
    n = w_out.shape[0]
    return pl.pallas_call(
        middle_back_kernel,
        name="middle_back",
        grid_spec=pltpu.PrefetchScalarGridSpec(
            num_scalar_prefetch=1,
            grid=(4,),
            in_specs=[
                whole((block, width)), whole((block, width)),
                whole((block // 2, width)), whole((block // 2, width)), whole((block, width)),
                at(width), at(1), at(width), whole(gain.shape), whole(w_out.shape),
            ],
            out_specs=[
                at(width),
                pl.BlockSpec((width, block), lambda k, s: (0, (s[0] + k) % 4)),
                at(n),
                whole((1, width)),
            ],
            scratch_shapes=[pltpu.VMEM((block, width), f32)],
        ),
        out_shape=[
            struct((rows, width), f32), struct((width, rows), bf16),
            struct((rows, n), bf16), struct((1, width), f32),
        ],
    )(mine, own, above, fa, fb, below, middle, scale, cot, gain, w_out)


def in_rows_kernel(mine, own, above, fa, fb, below, out):
    block = own.shape[0]
    at = lambda k: pl.ds(pl.multiple_of((mine[0] + k) % 4 * block, block), block)
    out[at(0), :] = own[...]
    out[at(1), :] = above[...]
    out[at(2), :] = jnp.concatenate([fa[...], fb[...]], axis=0)
    out[at(3), :] = below[...]


def in_rows(mine, pieces):
    own, above, (fa, fb), below = pieces
    rows, width = own.shape
    return pl.pallas_call(
        in_rows_kernel,
        name="in_rows",
        in_specs=[SMEM] + [VMEM] * 5,
        out_specs=VMEM,
        out_shape=struct((4 * rows, width), bf16),
    )(mine, own, above, fa, fb, below)


def late_kernel(head, q, pair, cross, cosine, sine, late, bias):
    rows, n = q.shape
    kv = KEY_VALUE_HEADS * HEAD_SIZE

    def lin(ref):
        g = ref[:, :HEAD_SIZE].astype(f32)
        key = g * cosine[...] - pltpu.roll(g, HEAD_SIZE // 2, 1) * sine[...]
        return key, ref[:, HEAD_SIZE:].astype(f32)

    (own_k, own_v), (other_k, other_v) = lin(pair), lin(cross)
    first = head[0] == 0
    late[:, :n] = q[...]
    columns = [
        jnp.where(first, own_k, other_k), jnp.where(first, other_k, own_k),
        jnp.where(first, own_v, other_v), jnp.where(first, other_v, own_v),
    ]
    for c, value in enumerate(columns):
        late[:, n + c * HEAD_SIZE : n + (c + 1) * HEAD_SIZE] = value.astype(bf16)
    bias[...] = jnp.sum(late[...].astype(f32), axis=0, keepdims=True)


def late_grads(head, q, pair, cross, cosine, sine):
    rows, n = q.shape
    total = n + 2 * KEY_VALUE_HEADS * HEAD_SIZE
    return pl.pallas_call(
        late_kernel,
        name="late_grads",
        in_specs=[SMEM] + [VMEM] * 5,
        out_specs=[VMEM] * 2,
        out_shape=[struct((rows, total), bf16), struct((1, total), f32)],
    )(head, q, pair, cross, cosine, sine)


def project_back_kernel(
    core, x, late, above, fa, fb, below, w_own, mine, other, wk, wv, gain, grad_middle,
    gain_two_grad, bias, out, vectors,
):
    i = pl.program_id(0)
    n = w_own.shape[1]
    kv = wk.shape[1]
    far = jnp.where(i == 0, fa[...].astype(f32), fb[...].astype(f32)).astype(bf16)
    part = lambda m: (
        dot(above[...], m[:n, :]) + dot(below[...], m[n : 2 * n, :]) + dot(far, m[2 * n :, :])
    )
    a, b = part(mine), part(other)
    first = core[0] == 0
    g = jnp.concatenate([jnp.where(first, a, b), jnp.where(first, b, a)], axis=1)
    g = g + dot(late[:, :n], w_own[...], NT)
    g = g + dot(late[:, n : n + kv], wk[...], NT) + dot(late[:, n + kv :], wv[...], NT)
    xf = x[...].astype(f32)
    r = lax.rsqrt(jnp.mean(xf * xf, axis=1, keepdims=True) + eps)
    n1 = xf * r
    u1 = g * as_row(gain)
    out[...] = (
        grad_middle[...] + r * (u1 - n1 * jnp.mean(u1 * n1, axis=1, keepdims=True))
    ).astype(bf16)
    total = jnp.sum(g * n1, axis=0, keepdims=True)
    width = x.shape[1]

    @pl.when(i == 0)
    def _():
        vectors[:, :width] = total
        vectors[:, width : 2 * width] = gain_two_grad[...]
        vectors[:, 2 * width :] = bias[...]

    @pl.when(i > 0)
    def _():
        vectors[:, :width] = vectors[:, :width] + total


def project_back(
    core, x, late, pieces, w_own, mine, other, wk, wv, gain, grad_middle, gain_two_grad, bias
):
    rows, width = x.shape
    n = w_own.shape[1]
    half = rows // 2
    above, (fa, fb), below = pieces
    block = lambda c: pl.BlockSpec((half, c), lambda i, s: (i, 0))
    return pl.pallas_call(
        project_back_kernel,
        name="project_back",
        grid_spec=pltpu.PrefetchScalarGridSpec(
            num_scalar_prefetch=1,
            grid=(2,),
            in_specs=[
                block(width), block(late.shape[1]), block(n), whole((half, n)), whole((half, n)),
                block(n), whole(w_own.shape), whole(mine.shape), whole(other.shape),
                whole(wk.shape), whole(wv.shape), whole(gain.shape), block(width),
                whole(gain_two_grad.shape), whole(bias.shape),
            ],
            out_specs=[block(width), whole((1, 2 * width + bias.shape[1]))],
        ),
        out_shape=[struct((rows, width), bf16), struct((1, 2 * width + bias.shape[1]), f32)],
    )(
        core, x, late, above, fa, fb, below, w_own, mine, other, wk, wv, gain, grad_middle,
        gain_two_grad, bias,
    )


class Spread:
    def __init__(self, share, low_chip, chip_bits, split):
        self.share = share
        self.half = share.shape[0] // 2
        self.steps = list(zip(low_chip, chip_bits)) if split else []
        self.near = [shift_narrow(share, 1), shift_narrow(share, -1)]

    def fetch_far(self):
        below, above = self.near
        self.far = [shift_narrow(below[: self.half], 1), shift_narrow(above[self.half :], -1)]

    def collect(self):
        below, above = self.near
        fetched = stack([above, below] + self.far)
        self.cut = fetched.shape[0] // 2 if self.steps else fetched.shape[0]
        self.names = [[(0,)], [(0,)]]
        self.arrays = [[fetched[None, : self.cut]], [fetched[None, self.cut :]]]

    def hop(self):
        if not self.steps:
            return
        for part, bit in enumerate(self.steps.pop(0)):
            held = self.arrays[part]
            payload = held[0] if len(held) == 1 else jnp.concatenate(held, axis=0)
            names = tuple(s ^ (bit >> 1) for group in self.names[part] for s in group)
            self.names[part].append(names)
            held.append(swap_wide(payload, bit))

    def whole(self, chip, chips):
        while self.steps:
            self.hop()
        if self.cut == 6 * self.half:
            return self.arrays[0][0][0]
        parts = []
        for part, first in ((0, 0), (1, self.cut)):
            for names, array in zip(self.names[part], self.arrays[part]):
                parts.append((names, first, array))
        return assemble(chip, chips, parts)


def place_tokens(index, lengths):
    ends = jnp.cumsum(lengths)
    before = (ends[None, :] <= index[:, None]).astype(jnp.int32)
    return index - jnp.sum(before * lengths[None, :], axis=1)


def on_device(
    hidden_in,
    cotangent,
    lengths,
    valid,
    gain_one,
    w_query,
    b_query,
    key_projection,
    key_bias_vector,
    value_projection,
    value_bias_vector,
    w_out,
    gain_two,
    w_gate,
    w_up,
    w_down,
):
    rows, width = hidden_in.shape
    n_wide = lax.axis_size("wide")
    wide_index = lax.axis_index("wide")
    narrow_index = lax.axis_index("narrow")
    heads = w_query.shape[1] // HEAD_SIZE
    n_query = heads * HEAD_SIZE
    kv_width = KEY_VALUE_HEADS * HEAD_SIZE
    head = narrow_index * heads // (QUERY_HEADS // KEY_VALUE_HEADS)
    bits = [1 << b for b in reversed(range(n_wide.bit_length() - 1))]
    chip_bits = bits[:-1]
    up_first, down_first = bits, chip_bits[::-1] + [1]
    low_chip = chip_bits[::-1]
    slots = n_wide // 2
    core = wide_index % 2
    base = wide_index * rows
    as_scalar = lambda v: v.astype(jnp.int32).reshape(1)
    mine_wide, mine_narrow, core_s, head_s = map(
        as_scalar, (wide_index, narrow_index, core, head)
    )
    swap_core = lambda v: swap_wide(v, 1)

    token_index = base + jnp.arange(rows, dtype=jnp.int32)
    positions = place_tokens(token_index, lengths)
    start = (token_index - positions)[None, :]
    info = jnp.concatenate([mine_wide, lengths])
    freqs = 10000.0 ** (-(jnp.arange(HEAD_SIZE // 2, dtype=f32) * 2.0) / HEAD_SIZE)
    angles = positions.astype(f32)[:, None] * freqs[None, :]
    cos_half, sin_half = jnp.cos(angles), jnp.sin(angles)
    cosine = jnp.concatenate([cos_half, cos_half], axis=1)
    sine = jnp.concatenate([-sin_half, sin_half], axis=1)

    flags = jnp.pad(
        valid.astype(bf16).reshape(rows // HEAD_SIZE, HEAD_SIZE),
        ((0, FLAG_ROWS - rows // HEAD_SIZE), (0, 0)),
    )
    acts_one, key_own, value_own = front(
        head_s,
        hidden_in,
        gain_one,
        key_projection,
        value_projection,
        key_bias_vector,
        value_bias_vector,
        cosine,
        sine,
        flags,
    )

    col = width // 2
    n_half = n_query // 2
    split = n_query // slots % 32 == 0
    share = n_query // slots if split else n_query
    at = wide_index // 2 * share if split else 0
    half_query = lax.dynamic_slice_in_dim(w_query, core * col, col, 0).T
    half_out = lax.dynamic_slice(w_out, (at, core * col), (share, col))
    out_weights = Spread(half_out, low_chip, chip_bits, split)

    k_slots, keys = [(0,)], [key_own[None]]
    v_slots, values = [(0,)], [value_own[None]]
    join = lambda pieces: pieces[0] if len(pieces) == 1 else jnp.concatenate(pieces, axis=0)
    queries = turned_one = None
    for step, (k_bit, v_bit) in enumerate(zip(up_first, down_first)):
        k_send, v_send = join(keys), join(values)
        if step + 1 == len(up_first):
            k_send, v_send, queries, half_query, out_weights.arrays = tie(
                (k_send, v_send, queries, half_query, out_weights.arrays)
            )
        for names, pieces, send, bit in (
            (k_slots, keys, k_send, k_bit), (v_slots, values, v_send, v_bit)
        ):
            pieces.append(swap_wide(send, bit))
            names.append(tuple(s ^ bit for group in names for s in group))
        if step == 0:
            acts_late, out_weights.near = tie((acts_one, out_weights.near), keys[1], values[1])
            out_weights.fetch_far()
            out_weights.collect()
            queries, turned_one = project_queries(
                acts_late, cotangent, w_query, b_query, cosine, sine
            )
    k_pieces, v_pieces = list(zip(k_slots, keys)), list(zip(v_slots, values))
    out_weights.arrays = tie(out_weights.arrays, keys[-1], values[-1])
    out_weights.hop()
    context, lse = attend(info, queries, start, k_pieces, v_pieces)
    out_weights.arrays = tie(out_weights.arrays, context)
    out_weights.hop()

    half = rows // 2
    ctx_below, ctx_above = shift_narrow(context, 1), shift_narrow(context, -1)
    out_mine = out_weights.whole(as_scalar(wide_index // 2), slots)
    out_mine, ctx_below, ctx_above = tie((out_mine, ctx_below, ctx_above))
    out_other = swap_core(out_mine)
    ctx_far = (shift_narrow(ctx_below[:half], 1), shift_narrow(ctx_above[half:], -1))
    turned_one_other = swap_core(turned_one)
    ctx_far, half_query = tie((ctx_far, half_query), turned_one_other, out_other)
    w_gate_t, w_up_t = w_gate.T, w_up.T
    middle, acts_two, turned_two, scale_two = project_out(
        core_s, hidden_in, (context, ctx_above, ctx_far, ctx_below),
        w_out, out_mine, out_other, gain_two,
    )

    query_weights = Spread(half_query, low_chip, chip_bits, False)
    hidden, grads, blocks = feed(
        mine_narrow, acts_two, cotangent, w_gate_t, w_up_t, w_down
    )
    turned_two_other = swap_core(tie(turned_two, acts_two))
    (hidden, grads, blocks), query_weights.near = tie(
        ((hidden, grads, blocks), query_weights.near), turned_two_other
    )
    own, above, far_a, far_b, below = blocks
    up, down = shift_narrow(far_a, 1), shift_narrow(far_b, -1)
    hidden_other = swap_core(hidden)
    ffn = partial_rows(mine_narrow, hidden, w_down)
    up, down, ffn, hidden_other = tie((up, down, ffn, hidden_other))
    grads_other = swap_core(tie(grads, up, down))
    to_above, to_below = pass_on(above, below, up, down)
    from_below, from_above = shift_narrow(to_above, 1), shift_narrow(to_below, -1)
    hidden_here = tie(hidden, to_above, to_below)
    down_pair = weigh(
        mine_wide, slots, width, turned_one, turned_one_other, hidden_here[None],
        hidden_other[None],
    )
    from_below, from_above, grads, grads_other, down_pair = tie(
        (from_below, from_above, grads, grads_other, down_pair)
    )
    orders = (low_chip, chip_bits)
    down_steps = Halving(down_pair, orders)
    down_moved = down_steps.exchange()
    own = (own.astype(f32) + from_below.astype(f32) + from_above.astype(f32)).astype(bf16)
    q_rows = rows // 8
    g_below, g_above = shift_narrow(own, 1), shift_narrow(own, -1)
    grads_here = tie(grads, own)
    gate_pair, up_pair = [
        weigh(mine_wide, slots, width, turned_two, turned_two_other, grads_here, grads_other, k)
        for k in range(2)
    ]
    g_below, g_above, gate_pair, up_pair, down_moved = tie(
        (g_below, g_above, gate_pair, up_pair, down_moved)
    )
    gate_steps = Halving(gate_pair, orders)
    gate_moved = gate_steps.exchange()
    g_far = (shift_narrow(g_below[:q_rows], 1), shift_narrow(g_above[q_rows:], -1))
    down_sends = down_steps.settle(down_moved)
    g_far, down_sends = tie((g_far, down_sends))
    grad_middle, turned_attn, grad_context, gain_two_grad = middle_back(
        mine_narrow, (own, g_above, g_far, g_below), middle, scale_two, cotangent,
        gain_two, w_out,
    )

    ffn_own, ffn_above, ffn_far_a, ffn_far_b, ffn_below = ffn
    ffn_far_a, ffn_far_b = tie((ffn_far_a, ffn_far_b), g_far)
    ffn_up, ffn_down = shift_narrow(ffn_far_a, 1), shift_narrow(ffn_far_b, -1)
    ffn_to = pass_on(ffn_above, ffn_below, ffn_up, ffn_down)
    grad_context, ffn_to, gate_moved = tie((grad_context, ffn_to, gate_moved))
    ffn_from_below, ffn_from_above = shift_narrow(ffn_to[0], 1), shift_narrow(ffn_to[1], -1)
    down_steps.sends = tie(down_sends, gate_moved)
    down_moved = down_steps.exchange()
    query_lin_grad, send, keep = attend_back(
        info, queries, grad_context, context, start, lse, cosine, sine, k_pieces, v_pieces
    )
    query_lin_grad, send, keep, down_moved, ffn_from_below, ffn_from_above = tie(
        (query_lin_grad, send, keep, down_moved, ffn_from_below, ffn_from_above)
    )
    turned_attn = tie(turned_attn, send)
    turned_attn_other = swap_core(turned_attn)
    down_steps.settle(down_moved)
    down_steps.rest()
    ql_below, ql_above = shift_narrow(query_lin_grad, 1), shift_narrow(query_lin_grad, -1)
    send_other, turned_attn_other = tie((swap_core(send), turned_attn_other))
    key_value = add_rounded(keep, send_other)
    ql_far = (shift_narrow(ql_below[:half], 1), shift_narrow(ql_above[half:], -1))
    spread = (2,) * len(chip_bits) + key_value.shape[2:]
    key_part = xor_scatter(key_value[0].reshape(spread), chip_bits, low_chip)
    value_part = xor_scatter(key_value[1].reshape(spread), chip_bits, chip_bits)
    n_narrow = lax.axis_size("narrow")
    pair = jnp.concatenate([key_part, value_part], axis=1)
    n_hidden = w_down.shape[0]
    (down_sum,) = finish(down_steps.terms, n_hidden)
    pair, ql_far, up_sends, gate_moved, down_sum = tie(
        (pair, ql_far, up_pair[0], gate_moved, down_sum)
    )
    up_steps = Halving((up_sends, up_pair[1]), orders)
    up_moved = up_steps.exchange()
    partner = lax.ppermute(pair, "narrow", [(i, i ^ 1) for i in range(n_narrow)])
    gate_steps.settle(gate_moved)
    gate_moved = gate_steps.exchange()
    pair = add_rounded(pair, partner)
    cross = lax.ppermute(pair, "narrow", [(i, n_narrow - 1 - i) for i in range(n_narrow)])
    cross, up_moved, query_weights.near = tie((cross, up_moved, query_weights.near))
    query_weights.fetch_far()
    late, bias = late_grads(head_s, query_lin_grad, pair, cross, cosine, sine)
    late_other = swap_core(late)
    up_sends = up_steps.settle(up_moved)
    late_other, up_sends, gate_moved = tie((late_other, up_sends, gate_moved))
    up_steps.sends = up_sends
    up_moved = up_steps.exchange()
    late_pair = weigh_late(
        mine_wide, slots, turned_attn, turned_attn_other, turned_two, turned_two_other,
        turned_one, turned_one_other, late, late_other,
    )
    late_pair, up_moved, query_weights.far = tie((late_pair, up_moved, query_weights.far))
    query_weights.collect()
    query_mine = query_weights.whole(as_scalar(wide_index // 2), slots)
    query_other = swap_core(query_mine)
    late_steps = Halving(late_pair, orders)
    late_moved = late_steps.exchange()
    late, ffn_from_below, ffn_from_above = tie((late, ffn_from_below, ffn_from_above), late_pair)
    out_rows = lax.dynamic_slice_in_dim(middle, narrow_index * (rows // 4), rows // 4, 0)
    out_rows = (
        out_rows + ffn_own.astype(f32) + ffn_from_below.astype(f32) + ffn_from_above.astype(f32)
    ).astype(bf16)
    o_below, o_above = shift_narrow(out_rows, 1), shift_narrow(out_rows, -1)
    grad_hidden_in, vectors = project_back(
        core_s, hidden_in, late, (ql_above, ql_far, ql_below), w_query, query_mine, query_other,
        key_projection, value_projection, gain_one, grad_middle, gain_two_grad, bias,
    )
    gate_steps.settle(gate_moved)
    gate_steps.rest()
    (gate_sum,) = finish(gate_steps.terms, n_hidden)
    late_moved, vectors, o_below, o_above, gate_sum = tie(
        (late_moved, vectors, o_below, o_above, gate_sum)
    )
    late_steps.settle(late_moved)
    late_steps.rest()

    for bit in bits[::-1]:
        vectors = vectors + swap_wide(vectors, bit)
    vectors = vectors[0]

    def own_part(first, size):
        return lax.dynamic_slice_in_dim(vectors, first + wide_index * (size // n_wide), size // n_wide)

    bias_at = 2 * width
    query_bias = vectors[bias_at : bias_at + n_query].reshape(heads, n_wide, -1)
    query_bias = lax.dynamic_index_in_dim(query_bias, wide_index, 1, keepdims=False)

    o_far = (shift_narrow(o_below[:q_rows], 1), shift_narrow(o_above[q_rows:], -1))
    output = in_rows(mine_narrow, (out_rows, o_above, o_far, o_below))

    up_steps.settle(up_moved)
    up_steps.rest()
    (up_sum,) = finish(up_steps.terms, n_hidden)
    (late_sum,) = finish(late_steps.terms, late_steps.terms[0][0].shape[3])
    return (
        output,
        grad_hidden_in,
        own_part(0, width),
        late_sum[:, n_query : 2 * n_query],
        query_bias,
        late_sum[:, 2 * n_query : 2 * n_query + kv_width],
        own_part(bias_at + n_query, kv_width),
        late_sum[:, 2 * n_query + kv_width :],
        own_part(bias_at + n_query + kv_width, kv_width),
        late_sum[:, :n_query].T,
        own_part(width, width),
        gate_sum,
        up_sum,
        down_sum.T,
    )


def solution(mesh):
    placed = (
        P("wide", None),
        P("wide", None),
        P(),
        P("wide"),
        P(),
        P(None, "narrow"),
        P("narrow"),
        P(),
        P(),
        P(),
        P(),
        P("narrow", None),
        P(),
        P(None, "narrow"),
        P(None, "narrow"),
        P("narrow", None),
    )
    return jax.shard_map(
        on_device,
        mesh=mesh,
        in_specs=placed,
        out_specs=(
            P("wide", None),
            P("wide", None),
            P("wide"),
            P("wide", "narrow"),
            P("narrow", "wide"),
            P("wide", None),
            P("wide"),
            P("wide", None),
            P("wide"),
            P("narrow", "wide"),
            P("wide"),
            P("wide", "narrow"),
            P("wide", "narrow"),
            P("narrow", "wide"),
        ),
        check_vma=False,
    )
```

```python
import functools
import math

import jax
import jax.numpy as jnp
from jax import lax
from jax.experimental import pallas as pl
from jax.experimental.pallas import tpu as pltpu
from jax.sharding import PartitionSpec as P

QUERY_HEADS = 12
KEY_VALUE_HEADS = 2
HEAD_SIZE = 128
FLAG_ROWS = 16

eps = 1e-06
big_negative = -1e30
score_scale = 1.0 / math.sqrt(HEAD_SIZE)
log2_scale = score_scale * math.log2(math.e)

bf16 = jnp.bfloat16
f32 = jnp.float32
ANY = pl.BlockSpec(memory_space=pl.ANY)
VMEM = pl.BlockSpec(memory_space=pltpu.VMEM)
SMEM = pl.BlockSpec(memory_space=pltpu.SMEM)


def dot(a, b, dims=((1,), (0,))):
    return lax.dot_general(a, b, (dims, ((), ())), preferred_element_type=f32)


NT = ((1,), (1,))
TN = ((0,), (0,))


def swap_wide(array, bit):
    n = lax.axis_size("wide")
    return lax.ppermute(array, "wide", [(i, i ^ bit) for i in range(n)])


def shift_narrow(array, by):
    n = lax.axis_size("narrow")
    return lax.ppermute(array, "narrow", [(i, (i + by) % n) for i in range(n)])


def ring_gather(block):
    half = block.shape[0] // 2
    below = shift_narrow(block, 1)
    above = shift_narrow(block, -1)
    far_a = shift_narrow(below[:half], 1)
    far_b = shift_narrow(above[half:], -1)
    return [block, above, jnp.concatenate([far_a, far_b], axis=0), below]


def ring_scatter(parts):
    half = parts[0].shape[0] // 2
    add = lambda a, b: (a.astype(f32) + b.astype(f32)).astype(bf16)
    up = shift_narrow(parts[2][:half], 1)
    down = shift_narrow(parts[2][half:], -1)
    to_above = jnp.concatenate([add(parts[1][:half], up), parts[1][half:]], axis=0)
    to_below = jnp.concatenate([parts[3][:half], add(parts[3][half:], down)], axis=0)
    from_below = shift_narrow(to_above, 1)
    from_above = shift_narrow(to_below, -1)
    return parts[0].astype(f32) + from_below.astype(f32) + from_above.astype(f32)


def xor_gather(block, bits):
    slots, held = [0], [block[None]]
    pieces = [((0,), block[None])]
    for bit in bits:
        payload = held[0] if len(held) == 1 else jnp.concatenate(held, axis=0)
        received = swap_wide(payload, bit)
        new = [s ^ bit for s in slots]
        pieces.append((tuple(new), received))
        slots, held = slots + new, [payload, received]
    return pieces


def add_rounded(a, b):
    return (a.astype(f32) + b.astype(f32)).astype(bf16)


def xor_scatter(array, bits, order):
    bits = list(bits)
    for bit in order:
        axis = bits.index(bit)
        keep = lax.index_in_dim(array, 0, axis, keepdims=False)
        send = lax.index_in_dim(array, 1, axis, keepdims=False)
        array = add_rounded(keep, swap_wide(send, bit))
        bits.remove(bit)
    return array


def tie(values, *gates):
    return lax.optimization_barrier((values, gates))[0]


class Halving:
    def __init__(self, pair, orders):
        self.sends, keeps = pair
        self.terms = [[k] for k in keeps]
        self.views = [[k] for k in keeps]
        self.orders = [list(o) for o in orders]

    def exchange(self):
        return [swap_wide(s, order.pop(0)) for s, order in zip(self.sends, self.orders)]

    def settle(self, received):
        for part in range(2):
            self.terms[part].append(received[part])
            self.views[part].append(received[part])
        if not self.orders[0]:
            return None
        n = self.views[0][0].shape[1]
        total = lambda terms: sum(t.astype(f32) for t in terms).astype(bf16)
        self.sends = [
            total([t[:, 1::2] for t in self.views[0]]),
            total([t[:, n // 2 :] for t in self.views[1]]),
        ]
        self.views = [
            [t[:, ::2] for t in self.views[0]],
            [t[:, : n // 2] for t in self.views[1]],
        ]
        return self.sends

    def rest(self):
        while self.orders[0]:
            self.settle(self.exchange())


def as_row(vector):
    return vector[...].astype(f32).reshape(1, -1)


def rope(value, cosine, signed_sine):
    return value * cosine + pltpu.roll(value, HEAD_SIZE // 2, 1) * signed_sine


def front_kernel(head, x, gain, wk, wv, bk, bv, cosine, sine, flags, acts_out, k_out, v_out):
    rows = x.shape[0]
    of_head = lambda b: jnp.where(
        head[0] == 0, as_row(b)[:, :HEAD_SIZE], as_row(b)[:, HEAD_SIZE:]
    )
    xf = x[...].astype(f32)
    scale = lax.rsqrt(jnp.mean(xf * xf, axis=1, keepdims=True) + eps)
    acts = (xf * scale * as_row(gain)).astype(bf16)
    acts_out[...] = acts
    key = dot(acts, wk[...]) + of_head(bk)
    k_out[:rows, :] = rope(key, cosine[...], sine[...]).astype(bf16)
    k_out[rows:, :] = flags[...]
    v_out[...] = (dot(acts, wv[...]) + of_head(bv)).astype(bf16)


def front(head, x, gain, wk, wv, bk, bv, cosine, sine, flags):
    rows, width = x.shape
    whole = lambda *shape: pl.BlockSpec(shape, lambda i, h: (0,) * len(shape))
    column = lambda r: pl.BlockSpec((r, HEAD_SIZE), lambda i, h: (0, h[0]))
    return pl.pallas_call(
        front_kernel,
        name="front",
        grid_spec=pltpu.PrefetchScalarGridSpec(
            num_scalar_prefetch=1,
            grid=(1,),
            in_specs=[
                whole(rows, width),
                whole(width),
                column(width),
                column(width),
                whole(*bk.shape),
                whole(*bv.shape),
                whole(rows, HEAD_SIZE),
                whole(rows, HEAD_SIZE),
                whole(FLAG_ROWS, HEAD_SIZE),
            ],
            out_specs=[
                whole(rows, width),
                whole(rows + FLAG_ROWS, HEAD_SIZE),
                whole(rows, HEAD_SIZE),
            ],
        ),
        out_shape=[
            jax.ShapeDtypeStruct((rows, width), bf16),
            jax.ShapeDtypeStruct((rows + FLAG_ROWS, HEAD_SIZE), bf16),
            jax.ShapeDtypeStruct((rows, HEAD_SIZE), bf16),
        ],
    )(head, x, gain, wk, wv, bk, bv, cosine, sine, flags)


def query_kernel(acts, cot, w, b, cosine, sine, out, turned):
    lin = dot(acts[...], w[...]) + as_row(b)
    for h in range(out.shape[1] // HEAD_SIZE):
        cols = slice(h * HEAD_SIZE, (h + 1) * HEAD_SIZE)
        out[:, cols] = rope(lin[:, cols], cosine[...], sine[...]).astype(bf16)
    turned[0] = jnp.transpose(cot[...])
    turned[1] = jnp.transpose(acts[...])


def project_queries(acts, cot, w, b, cosine, sine):
    rows, width = acts.shape
    return pl.pallas_call(
        query_kernel,
        name="queries",
        in_specs=[VMEM] * 6,
        out_specs=[VMEM, VMEM],
        out_shape=[
            jax.ShapeDtypeStruct((rows, w.shape[1]), bf16),
            jax.ShapeDtypeStruct((2, width, rows), bf16),
        ],
    )(acts, cot, w, b, cosine, sine)


def load_pieces(k_refs, v_refs, k_slots, v_slots, kbuf, vbuf, sem):
    copies = []
    for which, refs, slots, buf in ((0, k_refs, k_slots, kbuf), (1, v_refs, v_slots, vbuf)):
        for ref, names in zip(refs, slots):
            for at, slot in enumerate(names):
                copies.append(
                    pltpu.make_async_copy(ref.at[at], buf.at[slot], sem.at[which, slot])
                )
    for copy in copies:
        copy.start()
    return copies


def key_codes(kbuf, slot, half, base, chunk):
    rows = kbuf.shape[1] - FLAG_ROWS
    per = chunk // HEAD_SIZE
    flags = jnp.transpose(kbuf[slot, rows:, :].astype(f32))
    columns = []
    for c in range(per):
        first = flags[:, c : c + 1]
        second = flags[:, per + c : per + c + 1]
        columns.append(jnp.where(half == 1, second, first))
    column = jnp.concatenate(columns, axis=0)
    index = base + lax.broadcasted_iota(jnp.int32, (chunk, 1), 0)
    return jnp.where(column > 0, index, -1)


def visible(codes, start, diagonal):
    seen = codes >= start
    if diagonal:
        shape = (codes.shape[0], start.shape[1])
        row = lax.broadcasted_iota(jnp.int32, shape, 0)
        col = lax.broadcasted_iota(jnp.int32, shape, 1)
        seen = (seen & (row < col)) | (row == col)
    return seen


def first_chunk(info, rows, chunk):
    base = info[0] * rows
    end = first = jnp.int32(0)
    for s in range(1, info.shape[0]):
        end = end + info[s]
        first = jnp.where(end <= base, end, first)
    return first // chunk


def forward_kernel(k_slots, v_slots, info, q, start, *refs):
    nk, nv = len(k_slots), len(v_slots)
    k_refs, v_refs = refs[:nk], refs[nk : nk + nv]
    out, lse, kbuf, vbuf, sem, acc_s, m_s, l_s = refs[nk + nv :]
    rows = q.shape[0]
    heads = q.shape[1] // HEAD_SIZE
    chunk = rows // 2
    own = info[0]
    copies = load_pieces(k_refs, v_refs, k_slots, v_slots, kbuf, vbuf, sem)
    for copy in copies:
        copy.wait()

    def tile(h, k, v, codes, lo, n, diagonal):
        qh = q[lo : lo + n, h * HEAD_SIZE : (h + 1) * HEAD_SIZE]
        s = dot(k, qh, NT) * log2_scale
        s = jnp.where(visible(codes, start[:, lo : lo + n], diagonal), s, big_negative)
        peak = jnp.max(s, axis=0, keepdims=True)
        cols = slice(lo, lo + n)
        if diagonal:
            p = jnp.exp2(s - peak)
            m_s[h : h + 1, cols] = peak
            l_s[h : h + 1, cols] = jnp.sum(p, axis=0, keepdims=True)
            acc_s[h, :, cols] = dot(v, p.astype(bf16), TN)
        else:
            old = m_s[h : h + 1, cols]
            new = jnp.maximum(old, peak)
            alpha = jnp.exp2(old - new)
            p = jnp.exp2(s - new)
            m_s[h : h + 1, cols] = new
            l_s[h : h + 1, cols] = alpha * l_s[h : h + 1, cols] + jnp.sum(p, axis=0, keepdims=True)
            acc_s[h, :, cols] = alpha * acc_s[h, :, cols] + dot(v, p.astype(bf16), TN)

    base = own * rows
    for half in (1, 0):
        k = kbuf[0, half * chunk : (half + 1) * chunk, :]
        v = vbuf[0, half * chunk : (half + 1) * chunk, :]
        codes = key_codes(kbuf, 0, half, base + half * chunk, chunk)
        for h in range(heads):
            tile(h, k, v, codes, half * chunk, chunk, True)
            if half == 0:
                tile(h, k, v, codes, chunk, chunk, False)

    def step(c, carry):
        block, half = c // 2, c % 2
        slot = lax.bitwise_xor(block, own)
        at = pl.multiple_of(half * chunk, chunk)
        k = kbuf[slot, pl.ds(at, chunk), :]
        v = vbuf[slot, pl.ds(at, chunk), :]
        codes = key_codes(kbuf, slot, half, c * chunk, chunk)
        for h in range(heads):
            tile(h, k, v, codes, 0, rows, False)
        return carry

    lax.fori_loop(first_chunk(info, rows, chunk), own * 2, step, 0)
    lse[...] = jnp.zeros_like(lse)
    for h in range(heads):
        total = l_s[h : h + 1, :]
        lse[h : h + 1, :] = m_s[h : h + 1, :] + jnp.log2(total)
        o = acc_s[h] * (1.0 / total)
        out[:, h * HEAD_SIZE : (h + 1) * HEAD_SIZE] = jnp.transpose(o).astype(bf16)


def attend(info, q, start, k_pieces, v_pieces):
    rows, width = q.shape
    heads = width // HEAD_SIZE
    slots = sum(len(s) for s, _ in k_pieces)
    return pl.pallas_call(
        functools.partial(
            forward_kernel, [s for s, _ in k_pieces], [s for s, _ in v_pieces]
        ),
        name="attend",
        in_specs=[SMEM, VMEM, VMEM] + [ANY] * (len(k_pieces) + len(v_pieces)),
        out_specs=[VMEM, VMEM],
        out_shape=[
            jax.ShapeDtypeStruct((rows, width), bf16),
            jax.ShapeDtypeStruct((8, rows), f32),
        ],
        scratch_shapes=[
            pltpu.VMEM((slots, rows + FLAG_ROWS, HEAD_SIZE), bf16),
            pltpu.VMEM((slots, rows, HEAD_SIZE), bf16),
            pltpu.SemaphoreType.DMA((2, slots)),
            pltpu.VMEM((heads, HEAD_SIZE, rows), f32),
            pltpu.VMEM((8, rows), f32),
            pltpu.VMEM((8, rows), f32),
        ],
    )(info, q, start, *[a for _, a in k_pieces], *[a for _, a in v_pieces])


def backward_kernel(k_slots, v_slots, info, q, do, ctx, start, lse, cosine, sine, *refs):
    nk, nv = len(k_slots), len(v_slots)
    k_refs, v_refs = refs[:nk], refs[nk : nk + nv]
    dq_out, send, keep, kbuf, vbuf, sem, dq_s, delta_s = refs[nk + nv :]
    rows = q.shape[0]
    heads = q.shape[1] // HEAD_SIZE
    chunk = rows // 2
    own = info[0]
    copies = load_pieces(k_refs, v_refs, k_slots, v_slots, kbuf, vbuf, sem)
    send[...] = jnp.zeros_like(send)
    keep[...] = jnp.zeros_like(keep)
    for h in range(heads):
        cols = slice(h * HEAD_SIZE, (h + 1) * HEAD_SIZE)
        both = do[:, cols].astype(f32) * ctx[:, cols].astype(f32)
        delta_s[h : h + 1, :] = jnp.sum(jnp.transpose(both), axis=0, keepdims=True)
        dq_s[h] = jnp.zeros((HEAD_SIZE, rows), f32)
    for copy in copies:
        copy.wait()

    def tile(h, k, v, codes, lo, n, diagonal):
        cols = slice(lo, lo + n)
        qh = q[cols, h * HEAD_SIZE : (h + 1) * HEAD_SIZE]
        doh = do[cols, h * HEAD_SIZE : (h + 1) * HEAD_SIZE]
        s = dot(k, qh, NT) * log2_scale - lse[h : h + 1, cols]
        s = jnp.where(visible(codes, start[:, cols], diagonal), s, big_negative)
        p = jnp.exp2(s)
        dv = dot(p.astype(bf16), doh)
        ds = (p * (dot(v, doh, NT) - delta_s[h : h + 1, cols])).astype(bf16)
        dk = dot(ds, qh)
        dq_s[h, :, cols] = dq_s[h, :, cols] + dot(k, ds, TN)
        return dk, dv

    def both(h, k, v, codes, spans):
        dk = dv = None
        for lo, n, diagonal in spans:
            a, b = tile(h, k, v, codes, lo, n, diagonal)
            dk, dv = (a, b) if dk is None else (dk + a, dv + b)
        return dk, dv

    def all_heads(k, v, codes, spans):
        dk = dv = None
        for h in range(heads):
            a, b = both(h, k, v, codes, spans)
            dk, dv = (a, b) if dk is None else (dk + a, dv + b)
        return (dk * score_scale).astype(bf16), dv.astype(bf16)

    base = own * rows
    for half in (1, 0):
        span = slice(half * chunk, (half + 1) * chunk)
        codes = key_codes(kbuf, 0, half, base + half * chunk, chunk)
        spans = [(chunk, chunk, True)] if half else [(0, chunk, True), (chunk, chunk, False)]
        dk, dv = all_heads(kbuf[0, span, :], vbuf[0, span, :], codes, spans)
        keep[0, 0, span, :] = dk
        keep[1, 0, span, :] = dv

    def step(c, carry):
        block, half = c // 2, c % 2
        slot = lax.bitwise_xor(block, own)
        at = pl.multiple_of(half * chunk, chunk)
        k = kbuf[slot, pl.ds(at, chunk), :]
        v = vbuf[slot, pl.ds(at, chunk), :]
        codes = key_codes(kbuf, slot, half, c * chunk, chunk)
        dk, dv = all_heads(k, v, codes, [(0, rows, False)])

        @pl.when(slot % 2 == 0)
        def _():
            keep[0, slot // 2, pl.ds(at, chunk), :] = dk
            keep[1, slot // 2, pl.ds(at, chunk), :] = dv

        @pl.when(slot % 2 == 1)
        def _():
            send[0, slot // 2, pl.ds(at, chunk), :] = dk
            send[1, slot // 2, pl.ds(at, chunk), :] = dv

        return carry

    lax.fori_loop(first_chunk(info, rows, chunk), own * 2, step, 0)
    for h in range(heads):
        g = jnp.transpose(dq_s[h]) * score_scale
        back = g * cosine[...] - pltpu.roll(g, HEAD_SIZE // 2, 1) * sine[...]
        dq_out[:, h * HEAD_SIZE : (h + 1) * HEAD_SIZE] = back.astype(bf16)


def attend_back(info, q, do, ctx, start, lse, cosine, sine, k_pieces, v_pieces):
    rows, width = q.shape
    heads = width // HEAD_SIZE
    slots = sum(len(s) for s, _ in k_pieces)
    half = jax.ShapeDtypeStruct((2, slots // 2, rows, HEAD_SIZE), bf16)
    return pl.pallas_call(
        functools.partial(
            backward_kernel, [s for s, _ in k_pieces], [s for s, _ in v_pieces]
        ),
        name="attend_back",
        in_specs=[SMEM] + [VMEM] * 7 + [ANY] * (len(k_pieces) + len(v_pieces)),
        out_specs=[VMEM] * 3,
        out_shape=[jax.ShapeDtypeStruct((rows, width), bf16), half, half],
        scratch_shapes=[
            pltpu.VMEM((slots, rows + FLAG_ROWS, HEAD_SIZE), bf16),
            pltpu.VMEM((slots, rows, HEAD_SIZE), bf16),
            pltpu.SemaphoreType.DMA((2, slots)),
            pltpu.VMEM((heads, HEAD_SIZE, rows), f32),
            pltpu.VMEM((8, rows), f32),
        ],
    )(
        info, q, do, ctx, start, lse, cosine, sine,
        *[a for _, a in k_pieces], *[a for _, a in v_pieces],
    )


def whole(shape):
    return pl.BlockSpec(shape, lambda *_: (0,) * len(shape))


def struct(shape, dtype):
    return jax.ShapeDtypeStruct(shape, dtype)


def project_out_kernel(
    core, x, own, above, fa, fb, below, w_own, mine, other, gain, middle, acts, turned, scale
):
    n = w_own.shape[0]
    width = x.shape[1]
    far = jnp.where(pl.program_id(0) == 0, fa[...].astype(f32), fb[...].astype(f32)).astype(bf16)
    part = lambda m: (
        dot(above[...], m[:n, :]) + dot(below[...], m[n : 2 * n, :]) + dot(far, m[2 * n :, :])
    )
    a, b = part(mine), part(other)
    first = core[0] == 0
    out = dot(own[...], w_own[...]) + jnp.concatenate(
        [jnp.where(first, a, b), jnp.where(first, b, a)], axis=1
    )
    mid = x[...].astype(f32) + out
    r = lax.rsqrt(jnp.mean(mid * mid, axis=1, keepdims=True) + eps)
    middle[...] = mid
    scale[...] = r
    normed = mid * r * as_row(gain)
    acts[...] = normed.astype(bf16)
    turned[:width, :] = jnp.transpose(normed.astype(bf16))
    turned[width:, :] = jnp.transpose(own[...])


def project_out(core, x, pieces, w_own, mine, other, gain):
    rows, width = x.shape
    n = w_own.shape[0]
    half = rows // 2
    own, above, (fa, fb), below = pieces
    block = lambda c: pl.BlockSpec((half, c), lambda i, s: (i, 0))
    return pl.pallas_call(
        project_out_kernel,
        name="project_out",
        grid_spec=pltpu.PrefetchScalarGridSpec(
            num_scalar_prefetch=1,
            grid=(2,),
            in_specs=[
                block(width), block(n), block(n), whole((half, n)), whole((half, n)), block(n),
                whole(w_own.shape), whole(mine.shape), whole(other.shape), whole(gain.shape),
            ],
            out_specs=[
                block(width), block(width),
                pl.BlockSpec((width + n, half), lambda i, s: (0, i)),
                block(1),
            ],
        ),
        out_shape=[
            struct((rows, width), f32), struct((rows, width), bf16),
            struct((width + n, rows), bf16), struct((rows, 1), f32),
        ],
    )(core, x, own, above, fa, fb, below, w_own, mine, other, gain)


def ring_blocks(acc, mine, outs):
    block = acc.shape[0] // 4
    own, above, far_a, far_b, below = outs

    def take(k, first, size):
        at = ((mine[0] + k) % 4) * block + first
        return acc[pl.ds(pl.multiple_of(at, size), size), :].astype(bf16)

    own[...] = take(0, 0, block)
    above[...] = take(1, 0, block)
    far_a[...] = take(2, 0, block // 2)
    far_b[...] = take(2, block // 2, block // 2)
    below[...] = take(3, 0, block)


def block_sizes(rows):
    return [rows // 4, rows // 4, rows // 8, rows // 8, rows // 4]


def feed_kernel(n, mine, acts, cot, wg, wu, wd, hidden, grads, *refs):
    outs, acc = refs[:-1], refs[-1]
    j = pl.program_id(0)
    tile = wg.shape[0]
    part = min(256, tile)
    for lo in range(0, tile, part):
        cols = slice(lo, lo + part)
        gate = dot(acts[...], wg[cols, :], NT)
        up = dot(acts[...], wu[cols, :], NT)
        g = dot(cot[...], wd[cols, :], NT)
        sig = 1.0 / (1.0 + jnp.exp(-gate))
        silu = gate * sig
        column = j * tile + lo + lax.broadcasted_iota(jnp.int32, (1, part), 1)
        keep = lambda v: jnp.where(column < n, v, 0.0).astype(bf16)
        hidden[:, cols] = keep(silu * up)
        grads[0, :, cols] = keep(g * up * (sig * (1.0 + gate * (1.0 - sig))))
        grads[1, :, cols] = keep(g * silu)
    back = lambda k: dot(grads[0, :, :k], wg[:k, :]) + dot(grads[1, :, :k], wu[:k, :])
    steps = pl.cdiv(n, tile)

    @pl.when(j == 0)
    def _():
        acc[...] = back(min(n, tile))

    if steps > 2:
        @pl.when((j > 0) & (j < steps - 1))
        def _():
            acc[...] = acc[...] + back(tile)

    if steps > 1:
        @pl.when(j == steps - 1)
        def _():
            acc[...] = acc[...] + back(n - (steps - 1) * tile)

    @pl.when(j == steps - 1)
    def _():
        ring_blocks(acc, mine, outs)


def feed(mine, acts, cot, wg, wu, wd, tile=768):
    rows, width = acts.shape
    n = wg.shape[0]
    steps = pl.cdiv(n, tile)
    w_spec = pl.BlockSpec((tile, width), lambda j, s: (j, 0))
    sizes = block_sizes(rows)
    outs = pl.pallas_call(
        functools.partial(feed_kernel, n),
        name="feed",
        grid_spec=pltpu.PrefetchScalarGridSpec(
            num_scalar_prefetch=1,
            grid=(steps,),
            in_specs=[whole((rows, width)), whole((rows, width)), w_spec, w_spec, w_spec],
            out_specs=[
                pl.BlockSpec((rows, tile), lambda j, s: (0, j)),
                pl.BlockSpec((2, rows, tile), lambda j, s: (0, 0, j)),
            ]
            + [whole((r, width)) for r in sizes],
            scratch_shapes=[pltpu.VMEM((rows, width), f32)],
        ),
        out_shape=[struct((rows, steps * tile), bf16), struct((2, rows, steps * tile), bf16)]
        + [struct((r, width), bf16) for r in sizes],
    )(mine, acts, cot, wg, wu, wd)
    return outs[0], outs[1], outs[2:]


def stack_kernel(cut, *refs):
    ins, outs = refs[:-2], refs[-2:]
    done = 0
    for ref in ins:
        rows = ref.shape[0]
        head = min(max(cut - done, 0), rows)
        if head:
            outs[0][done : done + head, :] = ref[:head, :]
        if head < rows:
            at = done + head - cut
            outs[1][at : at + rows - head, :] = ref[head:, :]
        done += rows


def stack(arrays, cut):
    rows = sum(a.shape[0] for a in arrays)
    width = arrays[0].shape[1]
    return pl.pallas_call(
        functools.partial(stack_kernel, cut),
        name="stack",
        in_specs=[VMEM] * len(arrays),
        out_specs=[VMEM] * 2,
        out_shape=[struct((cut, width), bf16), struct((rows - cut, width), bf16)],
    )(*arrays)


def assemble_kernel(plan, chip, *refs):
    out = refs[-1]
    n = out.shape[0] // 3
    block = n // plan[0]
    for ref, (names, first) in zip(refs, plan[1]):
        rows = ref.shape[1]
        for at, name in enumerate(names):
            source = lax.bitwise_xor(chip[0], name)
            done = 0
            while done < rows:
                piece, inside = divmod(first + done, block)
                size = min(rows - done, block - inside)
                to = pl.multiple_of(piece * n + source * block + inside, 16)
                out[pl.ds(to, size), :] = ref[at, done : done + size, :]
                done += size


def assemble(chip, chips, parts):
    one = sum({first: a.shape[1] for _, first, a in parts}.values())
    plan = (chips, [(names, first) for names, first, _ in parts])
    return pl.pallas_call(
        functools.partial(assemble_kernel, plan),
        name="assemble",
        in_specs=[SMEM] + [VMEM] * len(parts),
        out_specs=VMEM,
        out_shape=struct((chips * one, parts[0][2].shape[2]), bf16),
    )(chip, *[a for _, _, a in parts])


def partial_kernel(mine, a, w, *refs):
    refs[-1][...] = dot(a[:, : w.shape[0]], w[...])
    ring_blocks(refs[-1], mine, refs[:-1])


def partial_rows(mine, a, w, tile=512):
    rows, columns = a.shape
    inner, width = w.shape
    sizes = block_sizes(rows)
    return pl.pallas_call(
        partial_kernel,
        name="partial_down",
        grid_spec=pltpu.PrefetchScalarGridSpec(
            num_scalar_prefetch=1,
            grid=(width // tile,),
            in_specs=[whole(a.shape), pl.BlockSpec((inner, tile), lambda j, s: (0, j))],
            out_specs=[pl.BlockSpec((r, tile), lambda j, s: (0, j)) for r in sizes],
            scratch_shapes=[pltpu.VMEM((rows, tile), f32)],
        ),
        out_shape=[struct((r, width), bf16) for r in sizes],
    )(mine, a, w)


def pass_on_kernel(above, below, up, down, to_above, to_below):
    half = up.shape[0]
    to_above[:half, :] = (above[:half, :].astype(f32) + up[...].astype(f32)).astype(bf16)
    to_above[half:, :] = above[half:, :]
    to_below[:half, :] = below[:half, :]
    to_below[half:, :] = (below[half:, :].astype(f32) + down[...].astype(f32)).astype(bf16)


def pass_on(above, below, up, down):
    return pl.pallas_call(
        pass_on_kernel,
        name="pass_on",
        in_specs=[VMEM] * 4,
        out_specs=[VMEM] * 2,
        out_shape=[struct(above.shape, bf16)] * 2,
    )(above, below, up, down)


def weigh_kernel(slots, half, mine, a_own, a_other, b_own, b_other, *refs):
    send_a, keep_a, send_b, keep_b, lhs = refs
    rows = a_own.shape[1]
    block = 2 * half

    @pl.when(pl.program_id(0) == 0)
    def _():
        for s in range(slots):
            at = pl.multiple_of(lax.bitwise_xor(mine[0], 2 * s) * block, 16)
            lhs[s * block : (s + 1) * block, :rows] = a_own[pl.ds(at, block), :]
            lhs[s * block : (s + 1) * block, rows:] = a_other[pl.ds(at, block), :]

    g = dot(lhs[:, :rows], b_own[0]) + dot(lhs[:, rows:], b_other[0])
    place_slots(g, slots, half, 0, send_a, keep_a, send_b, keep_b)


def place_slots(g, slots, half, group, send_a, keep_a, send_b, keep_b):
    cols = slice(0, g.shape[1])
    for s in range(slots):
        first = g[2 * s * half : (2 * s + 1) * half].astype(bf16)
        second = g[(2 * s + 1) * half : (2 * s + 2) * half].astype(bf16)
        (send_a if s % 2 else keep_a)[group, s // 2, :, cols] = first
        (send_b if s >= slots // 2 else keep_b)[group, s % (slots // 2), :, cols] = second


def weigh(mine, slots, width, a_own, a_other, b_own, b_other, group=0, tile=768):
    rows = a_own.shape[-1]
    n = b_own.shape[2]
    if a_own.ndim == 3:
        a_spec = pl.BlockSpec((None, width, rows), lambda j, s: (0, 0, 0))
    else:
        a_spec = pl.BlockSpec((width, rows), lambda j, s: (0, 0))
    half = width // slots // 4
    b_spec = pl.BlockSpec((1, rows, tile), lambda j, s: (group, 0, j))
    out = pl.BlockSpec((1, slots // 2, half, tile), lambda j, s: (0, 0, 0, j))
    outs = pl.pallas_call(
        functools.partial(weigh_kernel, slots, half),
        name="weigh",
        grid_spec=pltpu.PrefetchScalarGridSpec(
            num_scalar_prefetch=1,
            grid=(pl.cdiv(n, tile),),
            in_specs=[a_spec, a_spec, b_spec, b_spec],
            out_specs=[out] * 4,
            scratch_shapes=[pltpu.VMEM((width // 2, 2 * rows), bf16)],
        ),
        out_shape=[struct((1, slots // 2, half, n), bf16)] * 4,
    )(mine, a_own, a_other, b_own, b_other)
    return [outs[0], outs[2]], [outs[1], outs[3]]


def weigh_late_kernel(
    slots, half, mine, t_own, t_other, c_own, c_other, a_own, a_other, b_own, b_other, *refs
):
    send_a, keep_a, send_b, keep_b = refs
    block = 2 * half

    def gather(ref):
        pieces = []
        for s in range(slots):
            at = pl.multiple_of(lax.bitwise_xor(mine[0], 2 * s) * block, 16)
            pieces.append(ref[pl.ds(at, block), :])
        return jnp.concatenate(pieces, axis=0)

    n = c_own.shape[0]
    g = dot(gather(t_own), c_own[...], NT) + dot(gather(t_other), c_other[...], NT)
    late = dot(gather(a_own), b_own[...]) + dot(gather(a_other), b_other[...])
    g = jnp.concatenate([g, late], axis=1)
    place_slots(g, slots, half, 0, send_a, keep_a, send_b, keep_b)


def weigh_late(mine, slots, t_own, t_other, c_own, c_other, a_own, a_other, b_own, b_other):
    width, rows = t_own.shape
    n = c_own.shape[0] - width
    half = width // slots // 4
    total = n + b_own.shape[1]
    t_spec = whole((width, rows))
    c_spec = pl.BlockSpec((n, rows), lambda i, s: (width // n, 0))
    a_spec = pl.BlockSpec((None, width, rows), lambda i, s: (1, 0, 0))
    b_spec = whole(b_own.shape)
    shape = (1, slots // 2, half, total)
    outs = pl.pallas_call(
        functools.partial(weigh_late_kernel, slots, half),
        name="weigh_late",
        grid_spec=pltpu.PrefetchScalarGridSpec(
            num_scalar_prefetch=1,
            grid=(1,),
            in_specs=[t_spec, t_spec, c_spec, c_spec, a_spec, a_spec, b_spec, b_spec],
            out_specs=[whole(shape)] * 4,
        ),
        out_shape=[struct(shape, bf16)] * 4,
    )(mine, t_own, t_other, c_own, c_other, a_own, a_other, b_own, b_other)
    return [outs[0], outs[2]], [outs[1], outs[3]]


def finish_kernel(n, *refs):
    terms, outs = refs[: 2 * n], refs[2 * n :]
    half = terms[0].shape[2]
    for g, out in enumerate(outs):
        for part in range(2):
            total = None
            for t in terms[part * n : (part + 1) * n]:
                value = t[g, 0, :, : out.shape[1]].astype(f32)
                total = value if total is None else total + value
            out[part * half : (part + 1) * half, :] = total


def finish(terms, columns):
    flat = terms[0] + terms[1]
    groups, _, half, n = flat[0].shape
    return pl.pallas_call(
        functools.partial(finish_kernel, len(terms[0])),
        name="finish",
        grid=(1,),
        in_specs=[whole((groups, 1, half, n))] * len(flat),
        out_specs=[whole((2 * half, columns))] * groups,
        out_shape=[struct((2 * half, columns), f32)] * groups,
    )(*flat)


def middle_back_kernel(
    mine, own, above, fa, fb, below, middle, scale, cot, gain, w_out,
    grad_middle, turned, grad_context, gain_grad, g_s,
):
    k = pl.program_id(0)
    half = fa.shape[0]
    for at, ref in ((0, own), (1, above), (3, below)):
        @pl.when(k == at)
        def _():
            g_s[...] = ref[...].astype(f32)

    @pl.when(k == 2)
    def _():
        g_s[:half, :] = fa[...].astype(f32)
        g_s[half:, :] = fb[...].astype(f32)

    g = g_s[...]
    r = scale[...]
    n2 = middle[...] * r
    u2 = g * as_row(gain)
    gm = cot[...].astype(f32) + r * (u2 - n2 * jnp.mean(u2 * n2, axis=1, keepdims=True))
    part = jnp.sum(g * n2, axis=0, keepdims=True)

    @pl.when(k == 0)
    def _():
        gain_grad[...] = part

    @pl.when(k > 0)
    def _():
        gain_grad[...] = gain_grad[...] + part

    grad_middle[...] = gm
    turned[...] = jnp.transpose(gm.astype(bf16))
    grad_context[...] = dot(gm.astype(bf16), w_out[...], NT).astype(bf16)


def middle_back(mine, pieces, middle, scale, cot, gain, w_out):
    rows, width = middle.shape
    block = rows // 4
    own, above, (fa, fb), below = pieces
    at = lambda c: pl.BlockSpec((block, c), lambda k, s: ((s[0] + k) % 4, 0))
    n = w_out.shape[0]
    return pl.pallas_call(
        middle_back_kernel,
        name="middle_back",
        grid_spec=pltpu.PrefetchScalarGridSpec(
            num_scalar_prefetch=1,
            grid=(4,),
            in_specs=[
                whole((block, width)), whole((block, width)),
                whole((block // 2, width)), whole((block // 2, width)), whole((block, width)),
                at(width), at(1), at(width), whole(gain.shape), whole(w_out.shape),
            ],
            out_specs=[
                at(width),
                pl.BlockSpec((width, block), lambda k, s: (0, (s[0] + k) % 4)),
                at(n),
                whole((1, width)),
            ],
            scratch_shapes=[pltpu.VMEM((block, width), f32)],
        ),
        out_shape=[
            struct((rows, width), f32), struct((width, rows), bf16),
            struct((rows, n), bf16), struct((1, width), f32),
        ],
    )(mine, own, above, fa, fb, below, middle, scale, cot, gain, w_out)


def in_rows_kernel(mine, own, above, fa, fb, below, out):
    block = own.shape[0]
    at = lambda k: pl.ds(pl.multiple_of((mine[0] + k) % 4 * block, block), block)
    out[at(0), :] = own[...]
    out[at(1), :] = above[...]
    out[at(2), :] = jnp.concatenate([fa[...], fb[...]], axis=0)
    out[at(3), :] = below[...]


def in_rows(mine, pieces):
    own, above, (fa, fb), below = pieces
    rows, width = own.shape
    return pl.pallas_call(
        in_rows_kernel,
        name="in_rows",
        in_specs=[SMEM] + [VMEM] * 5,
        out_specs=VMEM,
        out_shape=struct((4 * rows, width), bf16),
    )(mine, own, above, fa, fb, below)


def late_kernel(head, q, pair, cross, cosine, sine, late, bias):
    rows, n = q.shape
    kv = KEY_VALUE_HEADS * HEAD_SIZE

    def lin(ref):
        g = ref[:, :HEAD_SIZE].astype(f32)
        key = g * cosine[...] - pltpu.roll(g, HEAD_SIZE // 2, 1) * sine[...]
        return key, ref[:, HEAD_SIZE:].astype(f32)

    (own_k, own_v), (other_k, other_v) = lin(pair), lin(cross)
    first = head[0] == 0
    late[:, :n] = q[...]
    columns = [
        jnp.where(first, own_k, other_k), jnp.where(first, other_k, own_k),
        jnp.where(first, own_v, other_v), jnp.where(first, other_v, own_v),
    ]
    for c, value in enumerate(columns):
        late[:, n + c * HEAD_SIZE : n + (c + 1) * HEAD_SIZE] = value.astype(bf16)
    bias[...] = jnp.sum(late[...].astype(f32), axis=0, keepdims=True)


def late_grads(head, q, pair, cross, cosine, sine):
    rows, n = q.shape
    total = n + 2 * KEY_VALUE_HEADS * HEAD_SIZE
    return pl.pallas_call(
        late_kernel,
        name="late_grads",
        in_specs=[SMEM] + [VMEM] * 5,
        out_specs=[VMEM] * 2,
        out_shape=[struct((rows, total), bf16), struct((1, total), f32)],
    )(head, q, pair, cross, cosine, sine)


def project_back_kernel(
    core, x, late, above, fa, fb, below, w_own, mine, other, wk, wv, gain, grad_middle,
    gain_two_grad, bias, out, vectors,
):
    i = pl.program_id(0)
    n = w_own.shape[1]
    kv = wk.shape[1]
    far = jnp.where(i == 0, fa[...].astype(f32), fb[...].astype(f32)).astype(bf16)
    part = lambda m: (
        dot(above[...], m[:n, :]) + dot(below[...], m[n : 2 * n, :]) + dot(far, m[2 * n :, :])
    )
    a, b = part(mine), part(other)
    first = core[0] == 0
    g = jnp.concatenate([jnp.where(first, a, b), jnp.where(first, b, a)], axis=1)
    g = g + dot(late[:, :n], w_own[...], NT)
    g = g + dot(late[:, n : n + kv], wk[...], NT) + dot(late[:, n + kv :], wv[...], NT)
    xf = x[...].astype(f32)
    r = lax.rsqrt(jnp.mean(xf * xf, axis=1, keepdims=True) + eps)
    n1 = xf * r
    u1 = g * as_row(gain)
    out[...] = (
        grad_middle[...] + r * (u1 - n1 * jnp.mean(u1 * n1, axis=1, keepdims=True))
    ).astype(bf16)
    total = jnp.sum(g * n1, axis=0, keepdims=True)
    width = x.shape[1]

    @pl.when(i == 0)
    def _():
        vectors[:, :width] = total
        vectors[:, width : 2 * width] = gain_two_grad[...]
        vectors[:, 2 * width :] = bias[...]

    @pl.when(i > 0)
    def _():
        vectors[:, :width] = vectors[:, :width] + total


def project_back(
    core, x, late, pieces, w_own, mine, other, wk, wv, gain, grad_middle, gain_two_grad, bias
):
    rows, width = x.shape
    n = w_own.shape[1]
    half = rows // 2
    above, (fa, fb), below = pieces
    block = lambda c: pl.BlockSpec((half, c), lambda i, s: (i, 0))
    return pl.pallas_call(
        project_back_kernel,
        name="project_back",
        grid_spec=pltpu.PrefetchScalarGridSpec(
            num_scalar_prefetch=1,
            grid=(2,),
            in_specs=[
                block(width), block(late.shape[1]), block(n), whole((half, n)), whole((half, n)),
                block(n), whole(w_own.shape), whole(mine.shape), whole(other.shape),
                whole(wk.shape), whole(wv.shape), whole(gain.shape), block(width),
                whole(gain_two_grad.shape), whole(bias.shape),
            ],
            out_specs=[block(width), whole((1, 2 * width + bias.shape[1]))],
        ),
        out_shape=[struct((rows, width), bf16), struct((1, 2 * width + bias.shape[1]), f32)],
    )(
        core, x, late, above, fa, fb, below, w_own, mine, other, wk, wv, gain, grad_middle,
        gain_two_grad, bias,
    )


class Spread:
    def __init__(self, share, low_chip, chip_bits, split):
        self.share = share
        self.half = share.shape[0] // 2
        self.steps = list(zip(low_chip, chip_bits)) if split else []
        self.near = [shift_narrow(share, 1), shift_narrow(share, -1)]

    def fetch_far(self):
        below, above = self.near
        self.far = [shift_narrow(below[: self.half], 1), shift_narrow(above[self.half :], -1)]

    def collect(self):
        below, above = self.near
        pieces = [above, below] + self.far
        if not self.steps:
            self.rows = jnp.concatenate(pieces, axis=0)
            return
        self.cut = 3 * self.half
        self.names = [[(0,)], [(0,)]]
        self.arrays = [[part[None]] for part in stack(pieces, self.cut)]

    def hop(self):
        if not self.steps:
            return
        for part, bit in enumerate(self.steps.pop(0)):
            held = self.arrays[part]
            payload = held[0] if len(held) == 1 else jnp.concatenate(held, axis=0)
            names = tuple(s ^ (bit >> 1) for group in self.names[part] for s in group)
            self.names[part].append(names)
            held.append(swap_wide(payload, bit))

    def whole(self, chip, chips):
        if not hasattr(self, "arrays"):
            return self.rows
        while self.steps:
            self.hop()
        parts = []
        for part, first in ((0, 0), (1, self.cut)):
            for names, array in zip(self.names[part], self.arrays[part]):
                parts.append((names, first, array))
        return assemble(chip, chips, parts)


def place_tokens(index, lengths):
    ends = jnp.cumsum(lengths)
    before = (ends[None, :] <= index[:, None]).astype(jnp.int32)
    return index - jnp.sum(before * lengths[None, :], axis=1)


def on_device(
    hidden_in,
    cotangent,
    lengths,
    valid,
    gain_one,
    w_query,
    b_query,
    key_projection,
    key_bias_vector,
    value_projection,
    value_bias_vector,
    w_out,
    gain_two,
    w_gate,
    w_up,
    w_down,
):
    rows, width = hidden_in.shape
    n_wide = lax.axis_size("wide")
    wide_index = lax.axis_index("wide")
    narrow_index = lax.axis_index("narrow")
    heads = w_query.shape[1] // HEAD_SIZE
    n_query = heads * HEAD_SIZE
    kv_width = KEY_VALUE_HEADS * HEAD_SIZE
    head = narrow_index * heads // (QUERY_HEADS // KEY_VALUE_HEADS)
    bits = [1 << b for b in reversed(range(n_wide.bit_length() - 1))]
    chip_bits = bits[:-1]
    up_first, down_first = bits, chip_bits[::-1] + [1]
    low_chip = chip_bits[::-1]
    slots = n_wide // 2
    core = wide_index % 2
    base = wide_index * rows
    as_scalar = lambda v: v.astype(jnp.int32).reshape(1)
    mine_wide, mine_narrow, core_s, head_s = map(
        as_scalar, (wide_index, narrow_index, core, head)
    )
    swap_core = lambda v: swap_wide(v, 1)

    token_index = base + jnp.arange(rows, dtype=jnp.int32)
    positions = place_tokens(token_index, lengths)
    start = (token_index - positions)[None, :]
    info = jnp.concatenate([mine_wide, lengths])
    freqs = 10000.0 ** (-(jnp.arange(HEAD_SIZE // 2, dtype=f32) * 2.0) / HEAD_SIZE)
    angles = positions.astype(f32)[:, None] * freqs[None, :]
    cos_half, sin_half = jnp.cos(angles), jnp.sin(angles)
    cosine = jnp.concatenate([cos_half, cos_half], axis=1)
    sine = jnp.concatenate([-sin_half, sin_half], axis=1)

    flags = jnp.pad(
        valid.astype(bf16).reshape(rows // HEAD_SIZE, HEAD_SIZE),
        ((0, FLAG_ROWS - rows // HEAD_SIZE), (0, 0)),
    )
    acts_one, key_own, value_own = front(
        head_s,
        hidden_in,
        gain_one,
        key_projection,
        value_projection,
        key_bias_vector,
        value_bias_vector,
        cosine,
        sine,
        flags,
    )

    col = width // 2
    n_half = n_query // 2
    split = n_query // slots % 32 == 0
    share = n_query // slots if split else n_query
    at = wide_index // 2 * share if split else 0
    half_query = lax.dynamic_slice_in_dim(w_query, core * col, col, 0).T
    half_out = lax.dynamic_slice(w_out, (at, core * col), (share, col))
    out_weights = Spread(half_out, low_chip, chip_bits, split)

    k_slots, keys = [(0,)], [key_own[None]]
    v_slots, values = [(0,)], [value_own[None]]
    join = lambda pieces: pieces[0] if len(pieces) == 1 else jnp.concatenate(pieces, axis=0)
    queries = turned_one = None
    for step, (k_bit, v_bit) in enumerate(zip(up_first, down_first)):
        k_send, v_send = join(keys), join(values)
        if step + 1 == len(up_first):
            k_send, v_send, queries, half_query, out_weights.far = tie(
                (k_send, v_send, queries, half_query, out_weights.far)
            )
            out_weights.collect()
            out_weights.hop()
        for names, pieces, send, bit in (
            (k_slots, keys, k_send, k_bit), (v_slots, values, v_send, v_bit)
        ):
            pieces.append(swap_wide(send, bit))
            names.append(tuple(s ^ bit for group in names for s in group))
        if step == 0:
            acts_late, out_weights.near = tie((acts_one, out_weights.near), keys[1], values[1])
            out_weights.fetch_far()
            queries, turned_one = project_queries(
                acts_late, cotangent, w_query, b_query, cosine, sine
            )
    k_pieces, v_pieces = list(zip(k_slots, keys)), list(zip(v_slots, values))
    out_weights.hop()
    context, lse = attend(info, queries, start, k_pieces, v_pieces)
    if split:
        context, out_weights.arrays = tie((context, out_weights.arrays))

    half = rows // 2
    ctx_below, ctx_above = shift_narrow(context, 1), shift_narrow(context, -1)
    out_mine = out_weights.whole(as_scalar(wide_index // 2), slots)
    out_mine, ctx_below, ctx_above = tie((out_mine, ctx_below, ctx_above))
    out_other = swap_core(out_mine)
    ctx_far = (shift_narrow(ctx_below[:half], 1), shift_narrow(ctx_above[half:], -1))
    turned_one_other = swap_core(turned_one)
    ctx_far, half_query = tie((ctx_far, half_query), turned_one_other, out_other)
    w_gate_t, w_up_t = w_gate.T, w_up.T
    middle, acts_two, turned_two, scale_two = project_out(
        core_s, hidden_in, (context, ctx_above, ctx_far, ctx_below),
        w_out, out_mine, out_other, gain_two,
    )

    query_weights = Spread(half_query, low_chip, chip_bits, False)
    hidden, grads, blocks = feed(
        mine_narrow, acts_two, cotangent, w_gate_t, w_up_t, w_down
    )
    turned_two_other = swap_core(tie(turned_two, acts_two))
    (hidden, grads, blocks), query_weights.near = tie(
        ((hidden, grads, blocks), query_weights.near), turned_two_other
    )
    own, above, far_a, far_b, below = blocks
    up, down = shift_narrow(far_a, 1), shift_narrow(far_b, -1)
    hidden_other = swap_core(hidden)
    up, down, hidden_other = tie((up, down, hidden_other))
    grads_other = swap_core(tie(grads, up, down))
    to_above, to_below = pass_on(above, below, up, down)
    from_below, from_above = shift_narrow(to_above, 1), shift_narrow(to_below, -1)
    hidden_here = tie(hidden, to_above, to_below)
    down_pair = weigh(
        mine_wide, slots, width, turned_one, turned_one_other, hidden_here[None],
        hidden_other[None],
    )
    ffn = partial_rows(mine_narrow, hidden_here, w_down)
    from_below, from_above, grads, grads_other, down_pair, ffn = tie(
        (from_below, from_above, grads, grads_other, down_pair, ffn)
    )
    orders = (low_chip, chip_bits)
    down_steps = Halving(down_pair, orders)
    down_moved = down_steps.exchange()
    own = (own.astype(f32) + from_below.astype(f32) + from_above.astype(f32)).astype(bf16)
    q_rows = rows // 8
    g_below, g_above = shift_narrow(own, 1), shift_narrow(own, -1)
    grads_here = tie(grads, own)
    gate_pair, up_pair = [
        weigh(mine_wide, slots, width, turned_two, turned_two_other, grads_here, grads_other, k)
        for k in range(2)
    ]
    g_below, g_above, gate_pair, up_pair, down_moved = tie(
        (g_below, g_above, gate_pair, up_pair, down_moved)
    )
    gate_steps = Halving(gate_pair, orders)
    gate_moved = gate_steps.exchange()
    g_far = (shift_narrow(g_below[:q_rows], 1), shift_narrow(g_above[q_rows:], -1))
    down_sends = down_steps.settle(down_moved)
    g_far, down_sends = tie((g_far, down_sends))
    grad_middle, turned_attn, grad_context, gain_two_grad = middle_back(
        mine_narrow, (own, g_above, g_far, g_below), middle, scale_two, cotangent,
        gain_two, w_out,
    )

    ffn_own, ffn_above, ffn_far_a, ffn_far_b, ffn_below = ffn
    ffn_far_a, ffn_far_b = tie((ffn_far_a, ffn_far_b), g_far)
    ffn_up, ffn_down = shift_narrow(ffn_far_a, 1), shift_narrow(ffn_far_b, -1)
    ffn_to = pass_on(ffn_above, ffn_below, ffn_up, ffn_down)
    grad_context, ffn_to, gate_moved = tie((grad_context, ffn_to, gate_moved))
    ffn_from_below, ffn_from_above = shift_narrow(ffn_to[0], 1), shift_narrow(ffn_to[1], -1)
    up_steps = Halving(tie(up_pair, gate_moved), orders)
    up_moved = up_steps.exchange()
    query_lin_grad, send, keep = attend_back(
        info, queries, grad_context, context, start, lse, cosine, sine, k_pieces, v_pieces
    )
    query_lin_grad, send, keep, up_moved, ffn_from_below, ffn_from_above = tie(
        (query_lin_grad, send, keep, up_moved, ffn_from_below, ffn_from_above)
    )
    turned_attn = tie(turned_attn, send)
    turned_attn_other = swap_core(turned_attn)
    ql_below, ql_above = shift_narrow(query_lin_grad, 1), shift_narrow(query_lin_grad, -1)
    send_other, turned_attn_other = tie((swap_core(send), turned_attn_other))
    key_value = add_rounded(keep, send_other)
    ql_far = (shift_narrow(ql_below[:half], 1), shift_narrow(ql_above[half:], -1))
    spread = (2,) * len(chip_bits) + key_value.shape[2:]
    key_part = xor_scatter(key_value[0].reshape(spread), chip_bits, low_chip)
    value_part = xor_scatter(key_value[1].reshape(spread), chip_bits, chip_bits)
    n_narrow = lax.axis_size("narrow")
    pair = jnp.concatenate([key_part, value_part], axis=1)
    pair, ql_far, down_steps.sends, gate_moved = tie((pair, ql_far, down_sends, gate_moved))
    down_moved = down_steps.exchange()
    partner = lax.ppermute(pair, "narrow", [(i, i ^ 1) for i in range(n_narrow)])
    gate_steps.settle(gate_moved)
    gate_moved = gate_steps.exchange()
    pair = add_rounded(pair, partner)
    cross = lax.ppermute(pair, "narrow", [(i, n_narrow - 1 - i) for i in range(n_narrow)])
    cross, query_weights.near, gate_moved, down_moved = tie(
        (cross, query_weights.near, gate_moved, down_moved)
    )
    query_weights.fetch_far()
    late, bias = late_grads(head_s, query_lin_grad, pair, cross, cosine, sine)
    late_other = swap_core(late)
    up_sends = up_steps.settle(up_moved)
    late_other, up_sends = tie((late_other, up_sends))
    down_steps.settle(down_moved)
    down_steps.rest()
    n_hidden = w_down.shape[0]
    up_steps.sends = up_sends
    up_moved = up_steps.exchange()
    late_pair = weigh_late(
        mine_wide, slots, turned_attn, turned_attn_other, turned_two, turned_two_other,
        turned_one, turned_one_other, late, late_other,
    )
    late_pair, up_moved = tie((late_pair, up_moved))
    query_weights.far = tie(query_weights.far, late_pair)
    query_weights.collect()
    query_mine = query_weights.whole(as_scalar(wide_index // 2), slots)
    query_other = swap_core(query_mine)
    late_steps = Halving(late_pair, orders)
    late_moved = late_steps.exchange()
    late, ffn_from_below, ffn_from_above = tie((late, ffn_from_below, ffn_from_above), late_pair)
    out_rows = lax.dynamic_slice_in_dim(middle, narrow_index * (rows // 4), rows // 4, 0)
    out_rows = (
        out_rows + ffn_own.astype(f32) + ffn_from_below.astype(f32) + ffn_from_above.astype(f32)
    ).astype(bf16)
    o_below, o_above = shift_narrow(out_rows, 1), shift_narrow(out_rows, -1)
    grad_hidden_in, vectors = project_back(
        core_s, hidden_in, late, (ql_above, ql_far, ql_below), w_query, query_mine, query_other,
        key_projection, value_projection, gain_one, grad_middle, gain_two_grad, bias,
    )
    gate_steps.settle(gate_moved)
    gate_steps.rest()
    late_moved, vectors, o_below, o_above = tie((late_moved, vectors, o_below, o_above))
    (gate_sum,) = finish(tie(gate_steps.terms, vectors), n_hidden)
    (down_sum,) = finish(tie(down_steps.terms, vectors), n_hidden)
    late_steps.settle(late_moved)
    late_steps.rest()

    for bit in bits[::-1]:
        vectors = vectors + swap_wide(vectors, bit)
    vectors = vectors[0]

    def own_part(first, size):
        return lax.dynamic_slice_in_dim(vectors, first + wide_index * (size // n_wide), size // n_wide)

    bias_at = 2 * width
    query_bias = vectors[bias_at : bias_at + n_query].reshape(heads, n_wide, -1)
    query_bias = lax.dynamic_index_in_dim(query_bias, wide_index, 1, keepdims=False)

    o_far = (shift_narrow(o_below[:q_rows], 1), shift_narrow(o_above[q_rows:], -1))
    output = in_rows(mine_narrow, (out_rows, o_above, o_far, o_below))

    up_steps.settle(up_moved)
    up_steps.rest()
    (up_sum,) = finish(up_steps.terms, n_hidden)
    (late_sum,) = finish(late_steps.terms, late_steps.terms[0][0].shape[3])
    return (
        output,
        grad_hidden_in,
        own_part(0, width),
        late_sum[:, n_query : 2 * n_query],
        query_bias,
        late_sum[:, 2 * n_query : 2 * n_query + kv_width],
        own_part(bias_at + n_query, kv_width),
        late_sum[:, 2 * n_query + kv_width :],
        own_part(bias_at + n_query + kv_width, kv_width),
        late_sum[:, :n_query].T,
        own_part(width, width),
        gate_sum,
        up_sum,
        down_sum.T,
    )


def solution(mesh):
    placed = (
        P("wide", None),
        P("wide", None),
        P(),
        P("wide"),
        P(),
        P(None, "narrow"),
        P("narrow"),
        P(),
        P(),
        P(),
        P(),
        P("narrow", None),
        P(),
        P(None, "narrow"),
        P(None, "narrow"),
        P("narrow", None),
    )
    return jax.shard_map(
        on_device,
        mesh=mesh,
        in_specs=placed,
        out_specs=(
            P("wide", None),
            P("wide", None),
            P("wide"),
            P("wide", "narrow"),
            P("narrow", "wide"),
            P("wide", None),
            P("wide"),
            P("wide", None),
            P("wide"),
            P("narrow", "wide"),
            P("wide"),
            P("wide", "narrow"),
            P("wide", "narrow"),
            P("narrow", "wide"),
        ),
        check_vma=False,
    )
```

```python
import functools
import math

import jax
import jax.numpy as jnp
from jax import lax
from jax.experimental import pallas as pl
from jax.experimental.pallas import tpu as pltpu
from jax.sharding import PartitionSpec as P

QUERY_HEADS = 12
KEY_VALUE_HEADS = 2
HEAD_SIZE = 128
FLAG_ROWS = 16

eps = 1e-06
big_negative = -1e30
score_scale = 1.0 / math.sqrt(HEAD_SIZE)
log2_scale = score_scale * math.log2(math.e)

bf16 = jnp.bfloat16
f32 = jnp.float32
ANY = pl.BlockSpec(memory_space=pl.ANY)
VMEM = pl.BlockSpec(memory_space=pltpu.VMEM)
SMEM = pl.BlockSpec(memory_space=pltpu.SMEM)


def dot(a, b, dims=((1,), (0,))):
    return lax.dot_general(a, b, (dims, ((), ())), preferred_element_type=f32)


NT = ((1,), (1,))
TN = ((0,), (0,))


def swap_wide(array, bit):
    n = lax.axis_size("wide")
    return lax.ppermute(array, "wide", [(i, i ^ bit) for i in range(n)])


def shift_narrow(array, by):
    n = lax.axis_size("narrow")
    return lax.ppermute(array, "narrow", [(i, (i + by) % n) for i in range(n)])


def ring_gather(block):
    half = block.shape[0] // 2
    below = shift_narrow(block, 1)
    above = shift_narrow(block, -1)
    far_a = shift_narrow(below[:half], 1)
    far_b = shift_narrow(above[half:], -1)
    return [block, above, jnp.concatenate([far_a, far_b], axis=0), below]


def ring_scatter(parts):
    half = parts[0].shape[0] // 2
    add = lambda a, b: (a.astype(f32) + b.astype(f32)).astype(bf16)
    up = shift_narrow(parts[2][:half], 1)
    down = shift_narrow(parts[2][half:], -1)
    to_above = jnp.concatenate([add(parts[1][:half], up), parts[1][half:]], axis=0)
    to_below = jnp.concatenate([parts[3][:half], add(parts[3][half:], down)], axis=0)
    from_below = shift_narrow(to_above, 1)
    from_above = shift_narrow(to_below, -1)
    return parts[0].astype(f32) + from_below.astype(f32) + from_above.astype(f32)


def add_rounded(a, b):
    return (a.astype(f32) + b.astype(f32)).astype(bf16)


def xor_scatter(array, bits, order):
    bits = list(bits)
    for bit in order:
        axis = bits.index(bit)
        keep = lax.index_in_dim(array, 0, axis, keepdims=False)
        send = lax.index_in_dim(array, 1, axis, keepdims=False)
        array = add_rounded(keep, swap_wide(send, bit))
        bits.remove(bit)
    return array


def tie(values, *gates):
    return lax.optimization_barrier((values, gates))[0]


class Halving:
    def __init__(self, pair, orders):
        self.sends, keeps = pair
        self.terms = [[k] for k in keeps]
        self.views = [[k] for k in keeps]
        self.orders = [list(o) for o in orders]

    def exchange(self):
        return [swap_wide(s, order.pop(0)) for s, order in zip(self.sends, self.orders)]

    def settle(self, received):
        for part in range(2):
            self.terms[part].append(received[part])
            self.views[part].append(received[part])
        if not self.orders[0]:
            return None
        n = self.views[0][0].shape[1]
        total = lambda terms: sum(t.astype(f32) for t in terms).astype(bf16)
        self.sends = [
            total([t[:, 1::2] for t in self.views[0]]),
            total([t[:, n // 2 :] for t in self.views[1]]),
        ]
        self.views = [
            [t[:, ::2] for t in self.views[0]],
            [t[:, : n // 2] for t in self.views[1]],
        ]
        return self.sends

    def rest(self):
        while self.orders[0]:
            self.settle(self.exchange())


def as_row(vector):
    return vector[...].astype(f32).reshape(1, -1)


def rope(value, cosine, signed_sine):
    return value * cosine + pltpu.roll(value, HEAD_SIZE // 2, 1) * signed_sine


def front_kernel(head, x, gain, wk, wv, bk, bv, cosine, sine, flags, acts_out, kv_out):
    rows = x.shape[0]
    of_head = lambda b: jnp.where(
        head[0] == 0, as_row(b)[:, :HEAD_SIZE], as_row(b)[:, HEAD_SIZE:]
    )
    xf = x[...].astype(f32)
    scale = lax.rsqrt(jnp.mean(xf * xf, axis=1, keepdims=True) + eps)
    acts = (xf * scale * as_row(gain)).astype(bf16)
    acts_out[...] = acts
    key = dot(acts, wk[...]) + of_head(bk)
    kv_out[:rows, :] = rope(key, cosine[...], sine[...]).astype(bf16)
    kv_out[rows : rows + FLAG_ROWS, :] = flags[...]
    kv_out[rows + FLAG_ROWS :, :] = (dot(acts, wv[...]) + of_head(bv)).astype(bf16)


def front(head, x, gain, wk, wv, bk, bv, cosine, sine, flags):
    rows, width = x.shape
    whole = lambda *shape: pl.BlockSpec(shape, lambda i, h: (0,) * len(shape))
    column = lambda r: pl.BlockSpec((r, HEAD_SIZE), lambda i, h: (0, h[0]))
    return pl.pallas_call(
        front_kernel,
        name="front",
        grid_spec=pltpu.PrefetchScalarGridSpec(
            num_scalar_prefetch=1,
            grid=(1,),
            in_specs=[
                whole(rows, width),
                whole(width),
                column(width),
                column(width),
                whole(*bk.shape),
                whole(*bv.shape),
                whole(rows, HEAD_SIZE),
                whole(rows, HEAD_SIZE),
                whole(FLAG_ROWS, HEAD_SIZE),
            ],
            out_specs=[
                whole(rows, width),
                whole(2 * rows + FLAG_ROWS, HEAD_SIZE),
            ],
        ),
        out_shape=[
            jax.ShapeDtypeStruct((rows, width), bf16),
            jax.ShapeDtypeStruct((2 * rows + FLAG_ROWS, HEAD_SIZE), bf16),
        ],
    )(head, x, gain, wk, wv, bk, bv, cosine, sine, flags)


def query_kernel(acts, cot, w, b, cosine, sine, out, turned):
    lin = dot(acts[...], w[...]) + as_row(b)
    for h in range(out.shape[1] // HEAD_SIZE):
        cols = slice(h * HEAD_SIZE, (h + 1) * HEAD_SIZE)
        out[:, cols] = rope(lin[:, cols], cosine[...], sine[...]).astype(bf16)
    turned[0] = jnp.transpose(cot[...])
    turned[1] = jnp.transpose(acts[...])


def project_queries(acts, cot, w, b, cosine, sine):
    rows, width = acts.shape
    return pl.pallas_call(
        query_kernel,
        name="queries",
        in_specs=[VMEM] * 6,
        out_specs=[VMEM, VMEM],
        out_shape=[
            jax.ShapeDtypeStruct((rows, w.shape[1]), bf16),
            jax.ShapeDtypeStruct((2, width, rows), bf16),
        ],
    )(acts, cot, w, b, cosine, sine)


def load_pieces(refs, slots, kbuf, vbuf, sem):
    copies = []
    keys, values = kbuf.shape[1], vbuf.shape[1]
    for ref, names in zip(refs, slots):
        for at, slot in enumerate(names):
            k_part = ref.at[at, pl.ds(0, keys)]
            v_part = ref.at[at, pl.ds(keys, values)]
            copies.append(pltpu.make_async_copy(k_part, kbuf.at[slot], sem.at[0, slot]))
            copies.append(pltpu.make_async_copy(v_part, vbuf.at[slot], sem.at[1, slot]))
    for copy in copies:
        copy.start()
    return copies


def key_codes(kbuf, slot, half, base, chunk):
    rows = kbuf.shape[1] - FLAG_ROWS
    per = chunk // HEAD_SIZE
    flags = jnp.transpose(kbuf[slot, rows:, :].astype(f32))
    columns = []
    for c in range(per):
        first = flags[:, c : c + 1]
        second = flags[:, per + c : per + c + 1]
        columns.append(jnp.where(half == 1, second, first))
    column = jnp.concatenate(columns, axis=0)
    index = base + lax.broadcasted_iota(jnp.int32, (chunk, 1), 0)
    return jnp.where(column > 0, index, -1)


def visible(codes, start, diagonal):
    seen = codes >= start
    if diagonal:
        shape = (codes.shape[0], start.shape[1])
        row = lax.broadcasted_iota(jnp.int32, shape, 0)
        col = lax.broadcasted_iota(jnp.int32, shape, 1)
        seen = (seen & (row < col)) | (row == col)
    return seen


def first_chunk(info, rows, chunk):
    base = info[0] * rows
    end = first = jnp.int32(0)
    for s in range(1, info.shape[0]):
        end = end + info[s]
        first = jnp.where(end <= base, end, first)
    return first // chunk


def forward_kernel(slots, info, q, start, *refs):
    kv_refs, refs = refs[: len(slots)], refs[len(slots) :]
    out, lse, kbuf, vbuf, sem, acc_s, m_s, l_s = refs
    rows = q.shape[0]
    heads = q.shape[1] // HEAD_SIZE
    chunk = rows // 2
    own = info[0]
    copies = load_pieces(kv_refs, slots, kbuf, vbuf, sem)
    for copy in copies:
        copy.wait()

    def tile(h, k, v, codes, lo, n, diagonal):
        qh = q[lo : lo + n, h * HEAD_SIZE : (h + 1) * HEAD_SIZE]
        s = dot(k, qh, NT) * log2_scale
        s = jnp.where(visible(codes, start[:, lo : lo + n], diagonal), s, big_negative)
        peak = jnp.max(s, axis=0, keepdims=True)
        cols = slice(lo, lo + n)
        if diagonal:
            p = jnp.exp2(s - peak)
            m_s[h : h + 1, cols] = peak
            l_s[h : h + 1, cols] = jnp.sum(p, axis=0, keepdims=True)
            acc_s[h, :, cols] = dot(v, p.astype(bf16), TN)
        else:
            old = m_s[h : h + 1, cols]
            new = jnp.maximum(old, peak)
            alpha = jnp.exp2(old - new)
            p = jnp.exp2(s - new)
            m_s[h : h + 1, cols] = new
            l_s[h : h + 1, cols] = alpha * l_s[h : h + 1, cols] + jnp.sum(p, axis=0, keepdims=True)
            acc_s[h, :, cols] = alpha * acc_s[h, :, cols] + dot(v, p.astype(bf16), TN)

    base = own * rows
    for half in (1, 0):
        k = kbuf[0, half * chunk : (half + 1) * chunk, :]
        v = vbuf[0, half * chunk : (half + 1) * chunk, :]
        codes = key_codes(kbuf, 0, half, base + half * chunk, chunk)
        for h in range(heads):
            tile(h, k, v, codes, half * chunk, chunk, True)
            if half == 0:
                tile(h, k, v, codes, chunk, chunk, False)

    def step(c, carry):
        block, half = c // 2, c % 2
        slot = lax.bitwise_xor(block, own)
        at = pl.multiple_of(half * chunk, chunk)
        k = kbuf[slot, pl.ds(at, chunk), :]
        v = vbuf[slot, pl.ds(at, chunk), :]
        codes = key_codes(kbuf, slot, half, c * chunk, chunk)
        for h in range(heads):
            tile(h, k, v, codes, 0, rows, False)
        return carry

    lax.fori_loop(first_chunk(info, rows, chunk), own * 2, step, 0)
    lse[...] = jnp.zeros_like(lse)
    for h in range(heads):
        total = l_s[h : h + 1, :]
        lse[h : h + 1, :] = m_s[h : h + 1, :] + jnp.log2(total)
        o = acc_s[h] * (1.0 / total)
        out[:, h * HEAD_SIZE : (h + 1) * HEAD_SIZE] = jnp.transpose(o).astype(bf16)


def attend(info, q, start, kv_pieces):
    rows, width = q.shape
    heads = width // HEAD_SIZE
    slots = sum(len(s) for s, _ in kv_pieces)
    return pl.pallas_call(
        functools.partial(forward_kernel, [s for s, _ in kv_pieces]),
        name="attend",
        in_specs=[SMEM, VMEM, VMEM] + [ANY] * len(kv_pieces),
        out_specs=[VMEM, VMEM],
        out_shape=[
            jax.ShapeDtypeStruct((rows, width), bf16),
            jax.ShapeDtypeStruct((8, rows), f32),
        ],
        scratch_shapes=[
            pltpu.VMEM((slots, rows + FLAG_ROWS, HEAD_SIZE), bf16),
            pltpu.VMEM((slots, rows, HEAD_SIZE), bf16),
            pltpu.SemaphoreType.DMA((2, slots)),
            pltpu.VMEM((heads, HEAD_SIZE, rows), f32),
            pltpu.VMEM((8, rows), f32),
            pltpu.VMEM((8, rows), f32),
        ],
    )(info, q, start, *[a for _, a in kv_pieces])


def backward_kernel(slots, info, q, do, ctx, start, lse, cosine, sine, *refs):
    kv_refs, refs = refs[: len(slots)], refs[len(slots) :]
    dq_out, send, keep, kbuf, vbuf, sem, dq_s, delta_s = refs
    rows = q.shape[0]
    heads = q.shape[1] // HEAD_SIZE
    chunk = rows // 2
    own = info[0]
    copies = load_pieces(kv_refs, slots, kbuf, vbuf, sem)
    send[...] = jnp.zeros_like(send)
    keep[...] = jnp.zeros_like(keep)
    for h in range(heads):
        cols = slice(h * HEAD_SIZE, (h + 1) * HEAD_SIZE)
        both = do[:, cols].astype(f32) * ctx[:, cols].astype(f32)
        delta_s[h : h + 1, :] = jnp.sum(jnp.transpose(both), axis=0, keepdims=True)
        dq_s[h] = jnp.zeros((HEAD_SIZE, rows), f32)
    for copy in copies:
        copy.wait()

    def tile(h, k, v, codes, lo, n, diagonal):
        cols = slice(lo, lo + n)
        qh = q[cols, h * HEAD_SIZE : (h + 1) * HEAD_SIZE]
        doh = do[cols, h * HEAD_SIZE : (h + 1) * HEAD_SIZE]
        s = dot(k, qh, NT) * log2_scale - lse[h : h + 1, cols]
        s = jnp.where(visible(codes, start[:, cols], diagonal), s, big_negative)
        p = jnp.exp2(s)
        dv = dot(p.astype(bf16), doh)
        ds = (p * (dot(v, doh, NT) - delta_s[h : h + 1, cols])).astype(bf16)
        dk = dot(ds, qh)
        dq_s[h, :, cols] = dq_s[h, :, cols] + dot(k, ds, TN)
        return dk, dv

    def both(h, k, v, codes, spans):
        dk = dv = None
        for lo, n, diagonal in spans:
            a, b = tile(h, k, v, codes, lo, n, diagonal)
            dk, dv = (a, b) if dk is None else (dk + a, dv + b)
        return dk, dv

    def all_heads(k, v, codes, spans):
        dk = dv = None
        for h in range(heads):
            a, b = both(h, k, v, codes, spans)
            dk, dv = (a, b) if dk is None else (dk + a, dv + b)
        return (dk * score_scale).astype(bf16), dv.astype(bf16)

    base = own * rows
    for half in (1, 0):
        span = slice(half * chunk, (half + 1) * chunk)
        codes = key_codes(kbuf, 0, half, base + half * chunk, chunk)
        spans = [(chunk, chunk, True)] if half else [(0, chunk, True), (chunk, chunk, False)]
        dk, dv = all_heads(kbuf[0, span, :], vbuf[0, span, :], codes, spans)
        keep[0, 0, span, :] = dk
        keep[1, 0, span, :] = dv

    def step(c, carry):
        block, half = c // 2, c % 2
        slot = lax.bitwise_xor(block, own)
        at = pl.multiple_of(half * chunk, chunk)
        k = kbuf[slot, pl.ds(at, chunk), :]
        v = vbuf[slot, pl.ds(at, chunk), :]
        codes = key_codes(kbuf, slot, half, c * chunk, chunk)
        dk, dv = all_heads(k, v, codes, [(0, rows, False)])

        @pl.when(slot % 2 == 0)
        def _():
            keep[0, slot // 2, pl.ds(at, chunk), :] = dk
            keep[1, slot // 2, pl.ds(at, chunk), :] = dv

        @pl.when(slot % 2 == 1)
        def _():
            send[0, slot // 2, pl.ds(at, chunk), :] = dk
            send[1, slot // 2, pl.ds(at, chunk), :] = dv

        return carry

    lax.fori_loop(first_chunk(info, rows, chunk), own * 2, step, 0)
    for h in range(heads):
        g = jnp.transpose(dq_s[h]) * score_scale
        back = g * cosine[...] - pltpu.roll(g, HEAD_SIZE // 2, 1) * sine[...]
        dq_out[:, h * HEAD_SIZE : (h + 1) * HEAD_SIZE] = back.astype(bf16)


def attend_back(info, q, do, ctx, start, lse, cosine, sine, kv_pieces):
    rows, width = q.shape
    heads = width // HEAD_SIZE
    slots = sum(len(s) for s, _ in kv_pieces)
    half = jax.ShapeDtypeStruct((2, slots // 2, rows, HEAD_SIZE), bf16)
    return pl.pallas_call(
        functools.partial(backward_kernel, [s for s, _ in kv_pieces]),
        name="attend_back",
        in_specs=[SMEM] + [VMEM] * 7 + [ANY] * len(kv_pieces),
        out_specs=[VMEM] * 3,
        out_shape=[jax.ShapeDtypeStruct((rows, width), bf16), half, half],
        scratch_shapes=[
            pltpu.VMEM((slots, rows + FLAG_ROWS, HEAD_SIZE), bf16),
            pltpu.VMEM((slots, rows, HEAD_SIZE), bf16),
            pltpu.SemaphoreType.DMA((2, slots)),
            pltpu.VMEM((heads, HEAD_SIZE, rows), f32),
            pltpu.VMEM((8, rows), f32),
        ],
    )(
        info, q, do, ctx, start, lse, cosine, sine,
        *[a for _, a in kv_pieces],
    )


def whole(shape):
    return pl.BlockSpec(shape, lambda *_: (0,) * len(shape))


def struct(shape, dtype):
    return jax.ShapeDtypeStruct(shape, dtype)


def project_out_kernel(
    core, x, own, above, fa, fb, below, w_own, mine, other, gain, middle, acts, turned, scale
):
    n = w_own.shape[0]
    width = x.shape[1]
    far = jnp.where(pl.program_id(0) == 0, fa[...].astype(f32), fb[...].astype(f32)).astype(bf16)
    part = lambda m: (
        dot(above[...], m[:n, :]) + dot(below[...], m[n : 2 * n, :]) + dot(far, m[2 * n :, :])
    )
    a, b = part(mine), part(other)
    first = core[0] == 0
    out = dot(own[...], w_own[...]) + jnp.concatenate(
        [jnp.where(first, a, b), jnp.where(first, b, a)], axis=1
    )
    mid = x[...].astype(f32) + out
    r = lax.rsqrt(jnp.mean(mid * mid, axis=1, keepdims=True) + eps)
    middle[...] = mid
    scale[...] = r
    normed = mid * r * as_row(gain)
    acts[...] = normed.astype(bf16)
    turned[:width, :] = jnp.transpose(normed.astype(bf16))
    turned[width:, :] = jnp.transpose(own[...])


def project_out(core, x, pieces, w_own, mine, other, gain):
    rows, width = x.shape
    n = w_own.shape[0]
    half = rows // 2
    own, above, (fa, fb), below = pieces
    block = lambda c: pl.BlockSpec((half, c), lambda i, s: (i, 0))
    return pl.pallas_call(
        project_out_kernel,
        name="project_out",
        grid_spec=pltpu.PrefetchScalarGridSpec(
            num_scalar_prefetch=1,
            grid=(2,),
            in_specs=[
                block(width), block(n), block(n), whole((half, n)), whole((half, n)), block(n),
                whole(w_own.shape), whole(mine.shape), whole(other.shape), whole(gain.shape),
            ],
            out_specs=[
                block(width), block(width),
                pl.BlockSpec((width + n, half), lambda i, s: (0, i)),
                block(1),
            ],
        ),
        out_shape=[
            struct((rows, width), f32), struct((rows, width), bf16),
            struct((width + n, rows), bf16), struct((rows, 1), f32),
        ],
    )(core, x, own, above, fa, fb, below, w_own, mine, other, gain)


def ring_blocks(acc, mine, outs):
    block = acc.shape[0] // 4
    own, above, far_a, far_b, below = outs

    def take(k, first, size):
        at = ((mine[0] + k) % 4) * block + first
        return acc[pl.ds(pl.multiple_of(at, size), size), :].astype(bf16)

    own[...] = take(0, 0, block)
    above[...] = take(1, 0, block)
    far_a[...] = take(2, 0, block // 2)
    far_b[...] = take(2, block // 2, block // 2)
    below[...] = take(3, 0, block)


def block_sizes(rows):
    return [rows // 4, rows // 4, rows // 8, rows // 8, rows // 4]


def feed_kernel(n, mine, acts, cot, wg, wu, wd, hidden, grads, *refs):
    outs, acc = refs[:-1], refs[-1]
    j = pl.program_id(0)
    tile = wg.shape[0]
    part = min(256, tile)
    for lo in range(0, tile, part):
        cols = slice(lo, lo + part)
        gate = dot(acts[...], wg[cols, :], NT)
        up = dot(acts[...], wu[cols, :], NT)
        g = dot(cot[...], wd[cols, :], NT)
        sig = 1.0 / (1.0 + jnp.exp(-gate))
        silu = gate * sig
        column = j * tile + lo + lax.broadcasted_iota(jnp.int32, (1, part), 1)
        keep = lambda v: jnp.where(column < n, v, 0.0).astype(bf16)
        hidden[:, cols] = keep(silu * up)
        grads[0, :, cols] = keep(g * up * (sig * (1.0 + gate * (1.0 - sig))))
        grads[1, :, cols] = keep(g * silu)
    back = lambda k: dot(grads[0, :, :k], wg[:k, :]) + dot(grads[1, :, :k], wu[:k, :])
    steps = pl.cdiv(n, tile)

    @pl.when(j == 0)
    def _():
        acc[...] = back(min(n, tile))

    if steps > 2:
        @pl.when((j > 0) & (j < steps - 1))
        def _():
            acc[...] = acc[...] + back(tile)

    if steps > 1:
        @pl.when(j == steps - 1)
        def _():
            acc[...] = acc[...] + back(n - (steps - 1) * tile)

    @pl.when(j == steps - 1)
    def _():
        ring_blocks(acc, mine, outs)


def feed(mine, acts, cot, wg, wu, wd, tile=768):
    rows, width = acts.shape
    n = wg.shape[0]
    steps = pl.cdiv(n, tile)
    w_spec = pl.BlockSpec((tile, width), lambda j, s: (j, 0))
    sizes = block_sizes(rows)
    outs = pl.pallas_call(
        functools.partial(feed_kernel, n),
        name="feed",
        grid_spec=pltpu.PrefetchScalarGridSpec(
            num_scalar_prefetch=1,
            grid=(steps,),
            in_specs=[whole((rows, width)), whole((rows, width)), w_spec, w_spec, w_spec],
            out_specs=[
                pl.BlockSpec((rows, tile), lambda j, s: (0, j)),
                pl.BlockSpec((2, rows, tile), lambda j, s: (0, 0, j)),
            ]
            + [whole((r, width)) for r in sizes],
            scratch_shapes=[pltpu.VMEM((rows, width), f32)],
        ),
        out_shape=[struct((rows, steps * tile), bf16), struct((2, rows, steps * tile), bf16)]
        + [struct((r, width), bf16) for r in sizes],
    )(mine, acts, cot, wg, wu, wd)
    return outs[0], outs[1], outs[2:]


def stack_kernel(cut, *refs):
    count = 1 if cut is None else 2
    ins, outs = refs[:-count], refs[-count:]
    cut = outs[0].shape[0]
    done = 0
    for ref in ins:
        rows = ref.shape[0]
        head = min(max(cut - done, 0), rows)
        if head:
            outs[0][done : done + head, :] = ref[:head, :]
        if head < rows:
            at = done + head - cut
            outs[1][at : at + rows - head, :] = ref[head:, :]
        done += rows


def stack(arrays, cut):
    rows = sum(a.shape[0] for a in arrays)
    width = arrays[0].shape[1]
    sizes = [cut, rows - cut] if cut < rows else [rows]
    return pl.pallas_call(
        functools.partial(stack_kernel, cut if cut < rows else None),
        name="stack",
        in_specs=[VMEM] * len(arrays),
        out_specs=[VMEM] * len(sizes),
        out_shape=[struct((size, width), bf16) for size in sizes],
    )(*arrays)


def assemble_kernel(plan, chip, *refs):
    out = refs[-1]
    n = out.shape[0] // 3
    block = n // plan[0]
    for ref, (names, first) in zip(refs, plan[1]):
        rows = ref.shape[1]
        for at, name in enumerate(names):
            source = lax.bitwise_xor(chip[0], name)
            done = 0
            while done < rows:
                piece, inside = divmod(first + done, block)
                size = min(rows - done, block - inside)
                to = pl.multiple_of(piece * n + source * block + inside, 16)
                out[pl.ds(to, size), :] = ref[at, done : done + size, :]
                done += size


def assemble(chip, chips, parts):
    one = sum({first: a.shape[1] for _, first, a in parts}.values())
    plan = (chips, [(names, first) for names, first, _ in parts])
    return pl.pallas_call(
        functools.partial(assemble_kernel, plan),
        name="assemble",
        in_specs=[SMEM] + [VMEM] * len(parts),
        out_specs=VMEM,
        out_shape=struct((chips * one, parts[0][2].shape[2]), bf16),
    )(chip, *[a for _, _, a in parts])


def partial_kernel(mine, a, w, *refs):
    refs[-1][...] = dot(a[:, : w.shape[0]], w[...])
    ring_blocks(refs[-1], mine, refs[:-1])


def partial_rows(mine, a, w, tile=512):
    rows, columns = a.shape
    inner, width = w.shape
    sizes = block_sizes(rows)
    return pl.pallas_call(
        partial_kernel,
        name="partial_down",
        grid_spec=pltpu.PrefetchScalarGridSpec(
            num_scalar_prefetch=1,
            grid=(width // tile,),
            in_specs=[whole(a.shape), pl.BlockSpec((inner, tile), lambda j, s: (0, j))],
            out_specs=[pl.BlockSpec((r, tile), lambda j, s: (0, j)) for r in sizes],
            scratch_shapes=[pltpu.VMEM((rows, tile), f32)],
        ),
        out_shape=[struct((r, width), bf16) for r in sizes],
    )(mine, a, w)


def pass_on_kernel(above, below, up, down, to_above, to_below):
    half = up.shape[0]
    to_above[:half, :] = (above[:half, :].astype(f32) + up[...].astype(f32)).astype(bf16)
    to_above[half:, :] = above[half:, :]
    to_below[:half, :] = below[:half, :]
    to_below[half:, :] = (below[half:, :].astype(f32) + down[...].astype(f32)).astype(bf16)


def pass_on(above, below, up, down):
    return pl.pallas_call(
        pass_on_kernel,
        name="pass_on",
        in_specs=[VMEM] * 4,
        out_specs=[VMEM] * 2,
        out_shape=[struct(above.shape, bf16)] * 2,
    )(above, below, up, down)


def weigh_kernel(slots, half, mine, a_own, a_other, b_own, b_other, *refs):
    send_a, keep_a, send_b, keep_b, lhs = refs
    rows = a_own.shape[1]
    block = 2 * half

    @pl.when(pl.program_id(0) == 0)
    def _():
        for s in range(slots):
            at = pl.multiple_of(lax.bitwise_xor(mine[0], 2 * s) * block, 16)
            lhs[s * block : (s + 1) * block, :rows] = a_own[pl.ds(at, block), :]
            lhs[s * block : (s + 1) * block, rows:] = a_other[pl.ds(at, block), :]

    g = dot(lhs[:, :rows], b_own[0]) + dot(lhs[:, rows:], b_other[0])
    place_slots(g, slots, half, 0, send_a, keep_a, send_b, keep_b)


def place_slots(g, slots, half, group, send_a, keep_a, send_b, keep_b):
    cols = slice(0, g.shape[1])
    for s in range(slots):
        first = g[2 * s * half : (2 * s + 1) * half].astype(bf16)
        second = g[(2 * s + 1) * half : (2 * s + 2) * half].astype(bf16)
        (send_a if s % 2 else keep_a)[group, s // 2, :, cols] = first
        (send_b if s >= slots // 2 else keep_b)[group, s % (slots // 2), :, cols] = second


def weigh(mine, slots, width, a_own, a_other, b_own, b_other, group=0, tile=768):
    rows = a_own.shape[-1]
    n = b_own.shape[2]
    if a_own.ndim == 3:
        a_spec = pl.BlockSpec((None, width, rows), lambda j, s: (0, 0, 0))
    else:
        a_spec = pl.BlockSpec((width, rows), lambda j, s: (0, 0))
    half = width // slots // 4
    b_spec = pl.BlockSpec((1, rows, tile), lambda j, s: (group, 0, j))
    out = pl.BlockSpec((1, slots // 2, half, tile), lambda j, s: (0, 0, 0, j))
    outs = pl.pallas_call(
        functools.partial(weigh_kernel, slots, half),
        name="weigh",
        grid_spec=pltpu.PrefetchScalarGridSpec(
            num_scalar_prefetch=1,
            grid=(pl.cdiv(n, tile),),
            in_specs=[a_spec, a_spec, b_spec, b_spec],
            out_specs=[out] * 4,
            scratch_shapes=[pltpu.VMEM((width // 2, 2 * rows), bf16)],
        ),
        out_shape=[struct((1, slots // 2, half, n), bf16)] * 4,
    )(mine, a_own, a_other, b_own, b_other)
    return [outs[0], outs[2]], [outs[1], outs[3]]


def weigh_late_kernel(
    slots, half, mine, t_own, t_other, c_own, c_other, a_own, a_other, b_own, b_other, *refs
):
    send_a, keep_a, send_b, keep_b = refs
    block = 2 * half

    def gather(ref):
        pieces = []
        for s in range(slots):
            at = pl.multiple_of(lax.bitwise_xor(mine[0], 2 * s) * block, 16)
            pieces.append(ref[pl.ds(at, block), :])
        return jnp.concatenate(pieces, axis=0)

    n = c_own.shape[0]
    g = dot(gather(t_own), c_own[...], NT) + dot(gather(t_other), c_other[...], NT)
    late = dot(gather(a_own), b_own[...]) + dot(gather(a_other), b_other[...])
    g = jnp.concatenate([g, late], axis=1)
    place_slots(g, slots, half, 0, send_a, keep_a, send_b, keep_b)


def weigh_late(mine, slots, t_own, t_other, c_own, c_other, a_own, a_other, b_own, b_other):
    width, rows = t_own.shape
    n = c_own.shape[0] - width
    half = width // slots // 4
    total = n + b_own.shape[1]
    t_spec = whole((width, rows))
    c_spec = pl.BlockSpec((n, rows), lambda i, s: (width // n, 0))
    a_spec = pl.BlockSpec((None, width, rows), lambda i, s: (1, 0, 0))
    b_spec = whole(b_own.shape)
    shape = (1, slots // 2, half, total)
    outs = pl.pallas_call(
        functools.partial(weigh_late_kernel, slots, half),
        name="weigh_late",
        grid_spec=pltpu.PrefetchScalarGridSpec(
            num_scalar_prefetch=1,
            grid=(1,),
            in_specs=[t_spec, t_spec, c_spec, c_spec, a_spec, a_spec, b_spec, b_spec],
            out_specs=[whole(shape)] * 4,
        ),
        out_shape=[struct(shape, bf16)] * 4,
    )(mine, t_own, t_other, c_own, c_other, a_own, a_other, b_own, b_other)
    return [outs[0], outs[2]], [outs[1], outs[3]]


def total_of(refs, cols):
    total = None
    for t in refs:
        value = t[0, 0, :, cols].astype(f32)
        total = value if total is None else total + value
    return total


def finish_kernel(n, *refs):
    out = refs[-1]
    half = out.shape[0] // 2
    for part in range(2):
        total = total_of(refs[part * n : (part + 1) * n], slice(None))
        out[part * half : (part + 1) * half, :] = total


def finish(terms, columns, tile=768):
    flat = terms[0] + terms[1]
    half = flat[0].shape[2]
    return pl.pallas_call(
        functools.partial(finish_kernel, len(terms[0])),
        name="finish",
        grid=(pl.cdiv(columns, tile),),
        in_specs=[pl.BlockSpec((1, 1, half, tile), lambda j: (0, 0, 0, j))] * len(flat),
        out_specs=pl.BlockSpec((2 * half, tile), lambda j: (0, j)),
        out_shape=struct((2 * half, columns), f32),
    )(*flat)


def finish_late_kernel(n, count, *refs):
    terms, outs = refs[:-count], refs[-count:]
    half = outs[0].shape[0] // 2
    for part in range(2):
        at = 0
        for out in outs:
            cols = slice(at, at + out.shape[1])
            total = total_of(terms[part * n : (part + 1) * n], cols)
            out[part * half : (part + 1) * half, :] = total
            at += out.shape[1]


def finish_late(terms, sizes):
    flat = terms[0] + terms[1]
    _, _, half, columns = flat[0].shape
    return pl.pallas_call(
        functools.partial(finish_late_kernel, len(terms[0]), len(sizes)),
        name="finish_late",
        grid=(1,),
        in_specs=[whole((1, 1, half, columns))] * len(flat),
        out_specs=[whole((2 * half, size)) for size in sizes],
        out_shape=[struct((2 * half, size), f32) for size in sizes],
    )(*flat)


def middle_back_kernel(
    mine, own, above, fa, fb, below, middle, scale, cot, gain, w_out,
    grad_middle, turned, grad_context, gain_grad, g_s,
):
    k = pl.program_id(0)
    half = fa.shape[0]
    for at, ref in ((0, own), (1, above), (3, below)):
        @pl.when(k == at)
        def _():
            g_s[...] = ref[...].astype(f32)

    @pl.when(k == 2)
    def _():
        g_s[:half, :] = fa[...].astype(f32)
        g_s[half:, :] = fb[...].astype(f32)

    g = g_s[...]
    r = scale[...]
    n2 = middle[...] * r
    u2 = g * as_row(gain)
    gm = cot[...].astype(f32) + r * (u2 - n2 * jnp.mean(u2 * n2, axis=1, keepdims=True))
    part = jnp.sum(g * n2, axis=0, keepdims=True)

    @pl.when(k == 0)
    def _():
        gain_grad[...] = part

    @pl.when(k > 0)
    def _():
        gain_grad[...] = gain_grad[...] + part

    grad_middle[...] = gm
    turned[...] = jnp.transpose(gm.astype(bf16))
    grad_context[...] = dot(gm.astype(bf16), w_out[...], NT).astype(bf16)


def middle_back(mine, pieces, middle, scale, cot, gain, w_out):
    rows, width = middle.shape
    block = rows // 4
    own, above, (fa, fb), below = pieces
    at = lambda c: pl.BlockSpec((block, c), lambda k, s: ((s[0] + k) % 4, 0))
    n = w_out.shape[0]
    return pl.pallas_call(
        middle_back_kernel,
        name="middle_back",
        grid_spec=pltpu.PrefetchScalarGridSpec(
            num_scalar_prefetch=1,
            grid=(4,),
            in_specs=[
                whole((block, width)), whole((block, width)),
                whole((block // 2, width)), whole((block // 2, width)), whole((block, width)),
                at(width), at(1), at(width), whole(gain.shape), whole(w_out.shape),
            ],
            out_specs=[
                at(width),
                pl.BlockSpec((width, block), lambda k, s: (0, (s[0] + k) % 4)),
                at(n),
                whole((1, width)),
            ],
            scratch_shapes=[pltpu.VMEM((block, width), f32)],
        ),
        out_shape=[
            struct((rows, width), f32), struct((width, rows), bf16),
            struct((rows, n), bf16), struct((1, width), f32),
        ],
    )(mine, own, above, fa, fb, below, middle, scale, cot, gain, w_out)


def in_rows_kernel(mine, own, above, fa, fb, below, out):
    block = own.shape[0]
    at = lambda k: pl.ds(pl.multiple_of((mine[0] + k) % 4 * block, block), block)
    out[at(0), :] = own[...]
    out[at(1), :] = above[...]
    out[at(2), :] = jnp.concatenate([fa[...], fb[...]], axis=0)
    out[at(3), :] = below[...]


def in_rows(mine, pieces):
    own, above, (fa, fb), below = pieces
    rows, width = own.shape
    return pl.pallas_call(
        in_rows_kernel,
        name="in_rows",
        in_specs=[SMEM] + [VMEM] * 5,
        out_specs=VMEM,
        out_shape=struct((4 * rows, width), bf16),
    )(mine, own, above, fa, fb, below)


def late_kernel(head, q, pair, cross, cosine, sine, late, bias):
    rows, n = q.shape
    kv = KEY_VALUE_HEADS * HEAD_SIZE

    def lin(ref):
        g = ref[:, :HEAD_SIZE].astype(f32)
        key = g * cosine[...] - pltpu.roll(g, HEAD_SIZE // 2, 1) * sine[...]
        return key, ref[:, HEAD_SIZE:].astype(f32)

    (own_k, own_v), (other_k, other_v) = lin(pair), lin(cross)
    first = head[0] == 0
    late[:, :n] = q[...]
    columns = [
        jnp.where(first, own_k, other_k), jnp.where(first, other_k, own_k),
        jnp.where(first, own_v, other_v), jnp.where(first, other_v, own_v),
    ]
    for c, value in enumerate(columns):
        late[:, n + c * HEAD_SIZE : n + (c + 1) * HEAD_SIZE] = value.astype(bf16)
    bias[...] = jnp.sum(late[...].astype(f32), axis=0, keepdims=True)


def late_grads(head, q, pair, cross, cosine, sine):
    rows, n = q.shape
    total = n + 2 * KEY_VALUE_HEADS * HEAD_SIZE
    return pl.pallas_call(
        late_kernel,
        name="late_grads",
        in_specs=[SMEM] + [VMEM] * 5,
        out_specs=[VMEM] * 2,
        out_shape=[struct((rows, total), bf16), struct((1, total), f32)],
    )(head, q, pair, cross, cosine, sine)


def project_back_kernel(
    core, x, late, above, fa, fb, below, w_own, mine, other, wk, wv, gain, grad_middle,
    gain_two_grad, bias, out, vectors,
):
    i = pl.program_id(0)
    n = w_own.shape[1]
    kv = wk.shape[1]
    far = jnp.where(i == 0, fa[...].astype(f32), fb[...].astype(f32)).astype(bf16)
    part = lambda m: (
        dot(above[...], m[:n, :]) + dot(below[...], m[n : 2 * n, :]) + dot(far, m[2 * n :, :])
    )
    a, b = part(mine), part(other)
    first = core[0] == 0
    g = jnp.concatenate([jnp.where(first, a, b), jnp.where(first, b, a)], axis=1)
    g = g + dot(late[:, :n], w_own[...], NT)
    g = g + dot(late[:, n : n + kv], wk[...], NT) + dot(late[:, n + kv :], wv[...], NT)
    xf = x[...].astype(f32)
    r = lax.rsqrt(jnp.mean(xf * xf, axis=1, keepdims=True) + eps)
    n1 = xf * r
    u1 = g * as_row(gain)
    out[...] = (
        grad_middle[...] + r * (u1 - n1 * jnp.mean(u1 * n1, axis=1, keepdims=True))
    ).astype(bf16)
    total = jnp.sum(g * n1, axis=0, keepdims=True)
    width = x.shape[1]

    @pl.when(i == 0)
    def _():
        vectors[:, :width] = total
        vectors[:, width : 2 * width] = gain_two_grad[...]
        vectors[:, 2 * width :] = bias[...]

    @pl.when(i > 0)
    def _():
        vectors[:, :width] = vectors[:, :width] + total


def project_back(
    core, x, late, pieces, w_own, mine, other, wk, wv, gain, grad_middle, gain_two_grad, bias
):
    rows, width = x.shape
    n = w_own.shape[1]
    half = rows // 2
    above, (fa, fb), below = pieces
    block = lambda c: pl.BlockSpec((half, c), lambda i, s: (i, 0))
    return pl.pallas_call(
        project_back_kernel,
        name="project_back",
        grid_spec=pltpu.PrefetchScalarGridSpec(
            num_scalar_prefetch=1,
            grid=(2,),
            in_specs=[
                block(width), block(late.shape[1]), block(n), whole((half, n)), whole((half, n)),
                block(n), whole(w_own.shape), whole(mine.shape), whole(other.shape),
                whole(wk.shape), whole(wv.shape), whole(gain.shape), block(width),
                whole(gain_two_grad.shape), whole(bias.shape),
            ],
            out_specs=[block(width), whole((1, 2 * width + bias.shape[1]))],
        ),
        out_shape=[struct((rows, width), bf16), struct((1, 2 * width + bias.shape[1]), f32)],
    )(
        core, x, late, above, fa, fb, below, w_own, mine, other, wk, wv, gain, grad_middle,
        gain_two_grad, bias,
    )


class Spread:
    def __init__(self, share, orders):
        self.share = share
        self.half = share.shape[0] // 2
        self.orders = [list(o) for o in orders]
        self.near = [shift_narrow(share, 1), shift_narrow(share, -1)]

    def fetch_far(self):
        below, above = self.near
        self.far = [shift_narrow(below[: self.half], 1), shift_narrow(above[self.half :], -1)]

    def collect(self):
        below, above = self.near
        pieces = [above, below] + self.far
        if not self.orders:
            self.rows = jnp.concatenate(pieces, axis=0)
            return
        rows = 6 * self.half
        self.cut = rows // len(self.orders)
        self.names = [[(0,)] for _ in self.orders]
        self.arrays = [[part[None]] for part in stack(pieces, self.cut)]

    def hop(self):
        if not self.orders or not self.orders[0]:
            return
        for part, order in enumerate(self.orders):
            bit = order.pop(0)
            held = self.arrays[part]
            payload = held[0] if len(held) == 1 else jnp.concatenate(held, axis=0)
            names = tuple(s ^ (bit >> 1) for group in self.names[part] for s in group)
            self.names[part].append(names)
            held.append(swap_wide(payload, bit))

    def whole(self, chip, chips):
        if not hasattr(self, "arrays"):
            return self.rows
        while self.orders[0]:
            self.hop()
        parts = []
        for part in range(len(self.orders)):
            for names, array in zip(self.names[part], self.arrays[part]):
                parts.append((names, part * self.cut, array))
        return assemble(chip, chips, parts)


def place_tokens(index, lengths):
    ends = jnp.cumsum(lengths)
    before = (ends[None, :] <= index[:, None]).astype(jnp.int32)
    return index - jnp.sum(before * lengths[None, :], axis=1)


def on_device(
    hidden_in,
    cotangent,
    lengths,
    valid,
    gain_one,
    w_query,
    b_query,
    key_projection,
    key_bias_vector,
    value_projection,
    value_bias_vector,
    w_out,
    gain_two,
    w_gate,
    w_up,
    w_down,
):
    rows, width = hidden_in.shape
    n_wide = lax.axis_size("wide")
    wide_index = lax.axis_index("wide")
    narrow_index = lax.axis_index("narrow")
    heads = w_query.shape[1] // HEAD_SIZE
    n_query = heads * HEAD_SIZE
    kv_width = KEY_VALUE_HEADS * HEAD_SIZE
    head = narrow_index * heads // (QUERY_HEADS // KEY_VALUE_HEADS)
    bits = [1 << b for b in reversed(range(n_wide.bit_length() - 1))]
    chip_bits = bits[:-1]
    low_chip = chip_bits[::-1]
    slots = n_wide // 2
    core = wide_index % 2
    base = wide_index * rows
    as_scalar = lambda v: v.astype(jnp.int32).reshape(1)
    mine_wide, mine_narrow, core_s, head_s = map(
        as_scalar, (wide_index, narrow_index, core, head)
    )
    swap_core = lambda v: swap_wide(v, 1)

    token_index = base + jnp.arange(rows, dtype=jnp.int32)
    positions = place_tokens(token_index, lengths)
    start = (token_index - positions)[None, :]
    info = jnp.concatenate([mine_wide, lengths])
    freqs = 10000.0 ** (-(jnp.arange(HEAD_SIZE // 2, dtype=f32) * 2.0) / HEAD_SIZE)
    angles = positions.astype(f32)[:, None] * freqs[None, :]
    cos_half, sin_half = jnp.cos(angles), jnp.sin(angles)
    cosine = jnp.concatenate([cos_half, cos_half], axis=1)
    sine = jnp.concatenate([-sin_half, sin_half], axis=1)

    flags = jnp.pad(
        valid.astype(bf16).reshape(rows // HEAD_SIZE, HEAD_SIZE),
        ((0, FLAG_ROWS - rows // HEAD_SIZE), (0, 0)),
    )
    acts_one, kv_own = front(
        head_s,
        hidden_in,
        gain_one,
        key_projection,
        value_projection,
        key_bias_vector,
        value_bias_vector,
        cosine,
        sine,
        flags,
    )

    col = width // 2
    n_half = n_query // 2
    split = n_query // slots % 32 == 0
    share = n_query // slots if split else n_query
    at = wide_index // 2 * share if split else 0
    pair_split = n_query // 2 % 32 == 0
    half_at = wide_index // 2 % 2
    query_share = n_query // 2 if pair_split else n_query
    half_query = lax.dynamic_slice(
        w_query, (core * col, half_at * query_share if pair_split else 0), (col, query_share)
    ).T
    half_out = lax.dynamic_slice(w_out, (at, core * col), (share, col))
    out_weights = Spread(half_out, [low_chip, chip_bits] if split else [])

    kv_slots, kv_arrays = [(0,)], [kv_own[None]]
    for step, bit in enumerate(bits):
        send = kv_arrays[0] if step == 0 else jnp.concatenate(kv_arrays, axis=0)
        if step == 1:
            send, out_weights.near = tie((send, out_weights.near))
            out_weights.fetch_far()
        if step + 1 == len(bits):
            send, queries, half_query, out_weights.far = tie(
                (send, queries, half_query, out_weights.far)
            )
            out_weights.collect()
            out_weights.hop()
        kv_arrays.append(swap_wide(send, bit))
        kv_slots.append(tuple(s ^ bit for group in kv_slots for s in group))
        if step == 0:
            acts_late = tie(acts_one, kv_arrays[1])
            queries, turned_one = project_queries(
                acts_late, cotangent, w_query, b_query, cosine, sine
            )
    kv_pieces = list(zip(kv_slots, kv_arrays))
    out_weights.hop()
    context, lse = attend(info, queries, start, kv_pieces)
    if split:
        context, out_weights.arrays = tie((context, out_weights.arrays))

    half = rows // 2
    ctx_below, ctx_above = shift_narrow(context, 1), shift_narrow(context, -1)
    out_mine = out_weights.whole(as_scalar(wide_index // 2), slots)
    out_mine, ctx_below, ctx_above = tie((out_mine, ctx_below, ctx_above))
    out_other = swap_core(out_mine)
    ctx_far = (shift_narrow(ctx_below[:half], 1), shift_narrow(ctx_above[half:], -1))
    turned_one_other = swap_core(turned_one)
    ctx_far, half_query = tie((ctx_far, half_query), turned_one_other, out_other)
    w_gate_t, w_up_t = w_gate.T, w_up.T
    middle, acts_two, turned_two, scale_two = project_out(
        core_s, hidden_in, (context, ctx_above, ctx_far, ctx_below),
        w_out, out_mine, out_other, gain_two,
    )

    query_weights = Spread(half_query, [[2]] if pair_split else [])
    acts_two, query_weights.near = tie((acts_two, query_weights.near))
    query_weights.fetch_far()
    hidden, grads, blocks = feed(
        mine_narrow, acts_two, cotangent, w_gate_t, w_up_t, w_down
    )
    turned_two_other = swap_core(tie(turned_two, acts_two))
    (hidden, grads, blocks), query_weights.far = tie(
        ((hidden, grads, blocks), query_weights.far), turned_two_other
    )
    own, above, far_a, far_b, below = blocks
    up, down = shift_narrow(far_a, 1), shift_narrow(far_b, -1)
    hidden_other = swap_core(hidden)
    up, down, hidden_other = tie((up, down, hidden_other))
    grads_other = swap_core(tie(grads, up, down))
    to_above, to_below = pass_on(above, below, up, down)
    from_below, from_above = shift_narrow(to_above, 1), shift_narrow(to_below, -1)
    hidden_here, query_weights.far = tie((hidden, query_weights.far), to_above, to_below)
    query_weights.collect()
    query_weights.hop()
    down_pair = weigh(
        mine_wide, slots, width, turned_one, turned_one_other, hidden_here[None],
        hidden_other[None],
    )
    ffn = partial_rows(mine_narrow, hidden_here, w_down)
    from_below, from_above, grads, grads_other, down_pair, ffn = tie(
        (from_below, from_above, grads, grads_other, down_pair, ffn)
    )
    orders = (low_chip, chip_bits)
    down_steps = Halving(down_pair, orders)
    down_moved = down_steps.exchange()
    own = (own.astype(f32) + from_below.astype(f32) + from_above.astype(f32)).astype(bf16)
    q_rows = rows // 8
    g_below, g_above = shift_narrow(own, 1), shift_narrow(own, -1)
    grads_here = tie(grads, own)
    gate_pair, up_pair = [
        weigh(mine_wide, slots, width, turned_two, turned_two_other, grads_here, grads_other, k)
        for k in range(2)
    ]
    query_mine = query_weights.whole(as_scalar(half_at), 2)
    g_below, g_above, gate_pair, up_pair, down_moved, query_mine = tie(
        (g_below, g_above, gate_pair, up_pair, down_moved, query_mine)
    )
    query_other = swap_core(query_mine)
    gate_steps = Halving(gate_pair, orders)
    gate_moved = gate_steps.exchange()
    g_far = (shift_narrow(g_below[:q_rows], 1), shift_narrow(g_above[q_rows:], -1))
    down_sends = down_steps.settle(down_moved)
    g_far, down_sends, query_other = tie((g_far, down_sends, query_other))
    grad_middle, turned_attn, grad_context, gain_two_grad = middle_back(
        mine_narrow, (own, g_above, g_far, g_below), middle, scale_two, cotangent,
        gain_two, w_out,
    )

    ffn_own, ffn_above, ffn_far_a, ffn_far_b, ffn_below = ffn
    ffn_far_a, ffn_far_b = tie((ffn_far_a, ffn_far_b), g_far)
    ffn_up, ffn_down = shift_narrow(ffn_far_a, 1), shift_narrow(ffn_far_b, -1)
    ffn_to = pass_on(ffn_above, ffn_below, ffn_up, ffn_down)
    grad_context, ffn_to, gate_moved = tie((grad_context, ffn_to, gate_moved))
    ffn_from_below, ffn_from_above = shift_narrow(ffn_to[0], 1), shift_narrow(ffn_to[1], -1)
    up_steps = Halving(tie(up_pair, gate_moved), orders)
    up_moved = up_steps.exchange()
    query_lin_grad, send, keep = attend_back(
        info, queries, grad_context, context, start, lse, cosine, sine, kv_pieces
    )
    query_lin_grad, send, keep, up_moved, ffn_from_below, ffn_from_above = tie(
        (query_lin_grad, send, keep, up_moved, ffn_from_below, ffn_from_above)
    )
    turned_attn = tie(turned_attn, send)
    turned_attn_other = swap_core(turned_attn)
    ql_below, ql_above = shift_narrow(query_lin_grad, 1), shift_narrow(query_lin_grad, -1)
    send_other, turned_attn_other = tie((swap_core(send), turned_attn_other))
    key_value = add_rounded(keep, send_other)
    spread = (2,) * len(chip_bits) + key_value.shape[2:]
    key_part = xor_scatter(key_value[0].reshape(spread), chip_bits, low_chip)
    value_part = xor_scatter(key_value[1].reshape(spread), chip_bits, chip_bits)
    n_narrow = lax.axis_size("narrow")
    pair = jnp.concatenate([key_part, value_part], axis=1)
    pair, ql_below, ql_above, down_steps.sends, gate_moved = tie(
        (pair, ql_below, ql_above, down_sends, gate_moved)
    )
    down_moved = down_steps.exchange()
    partner = lax.ppermute(pair, "narrow", [(i, i ^ 1) for i in range(n_narrow)])
    gate_steps.settle(gate_moved)
    gate_moved = gate_steps.exchange()
    pair = add_rounded(pair, partner)
    cross = lax.ppermute(pair, "narrow", [(i, n_narrow - 1 - i) for i in range(n_narrow)])
    cross, ql_below, ql_above, gate_moved, down_moved = tie(
        (cross, ql_below, ql_above, gate_moved, down_moved)
    )
    ql_far = (shift_narrow(ql_below[:half], 1), shift_narrow(ql_above[half:], -1))
    late, bias = late_grads(head_s, query_lin_grad, pair, cross, cosine, sine)
    late_other = swap_core(late)
    up_sends = up_steps.settle(up_moved)
    late_other, up_sends = tie((late_other, up_sends))
    down_steps.settle(down_moved)
    down_steps.rest()
    n_hidden = w_down.shape[0]
    up_steps.sends = up_sends
    up_moved = up_steps.exchange()
    late_pair = weigh_late(
        mine_wide, slots, turned_attn, turned_attn_other, turned_two, turned_two_other,
        turned_one, turned_one_other, late, late_other,
    )
    late_pair, up_moved, ql_far = tie((late_pair, up_moved, ql_far))
    late_steps = Halving(late_pair, orders)
    late_moved = late_steps.exchange()
    late, ffn_from_below, ffn_from_above = tie((late, ffn_from_below, ffn_from_above), late_pair)
    out_rows = lax.dynamic_slice_in_dim(middle, narrow_index * (rows // 4), rows // 4, 0)
    out_rows = (
        out_rows + ffn_own.astype(f32) + ffn_from_below.astype(f32) + ffn_from_above.astype(f32)
    ).astype(bf16)
    o_below, o_above = shift_narrow(out_rows, 1), shift_narrow(out_rows, -1)
    grad_hidden_in, vectors = project_back(
        core_s, hidden_in, late, (ql_above, ql_far, ql_below), w_query, query_mine, query_other,
        key_projection, value_projection, gain_one, grad_middle, gain_two_grad, bias,
    )
    gate_steps.settle(gate_moved)
    gate_steps.rest()
    late_moved, vectors = tie((late_moved, vectors))
    gate_sum = finish(tie(gate_steps.terms, vectors), n_hidden)
    down_sum = finish(tie(down_steps.terms, vectors), n_hidden)
    late_steps.settle(late_moved)
    late_steps.rest()

    for bit in bits[::-1]:
        vectors = vectors + swap_wide(vectors, bit)
    vectors = vectors[0]

    def own_part(first, size):
        return lax.dynamic_slice_in_dim(vectors, first + wide_index * (size // n_wide), size // n_wide)

    bias_at = 2 * width
    query_bias = vectors[bias_at : bias_at + n_query].reshape(heads, n_wide, -1)
    query_bias = lax.dynamic_index_in_dim(query_bias, wide_index, 1, keepdims=False)

    o_far = (shift_narrow(o_below[:q_rows], 1), shift_narrow(o_above[q_rows:], -1))
    output = in_rows(mine_narrow, (out_rows, o_above, o_far, o_below))

    up_steps.settle(up_moved)
    up_steps.rest()
    up_sum = finish(up_steps.terms, n_hidden)
    out_sum, query_sum, key_sum, value_sum = finish_late(
        late_steps.terms, [n_query, n_query, kv_width, kv_width]
    )
    return (
        output,
        grad_hidden_in,
        own_part(0, width),
        query_sum,
        query_bias,
        key_sum,
        own_part(bias_at + n_query, kv_width),
        value_sum,
        own_part(bias_at + n_query + kv_width, kv_width),
        out_sum.T,
        own_part(width, width),
        gate_sum,
        up_sum,
        down_sum.T,
    )


def solution(mesh):
    placed = (
        P("wide", None),
        P("wide", None),
        P(),
        P("wide"),
        P(),
        P(None, "narrow"),
        P("narrow"),
        P(),
        P(),
        P(),
        P(),
        P("narrow", None),
        P(),
        P(None, "narrow"),
        P(None, "narrow"),
        P("narrow", None),
    )
    return jax.shard_map(
        on_device,
        mesh=mesh,
        in_specs=placed,
        out_specs=(
            P("wide", None),
            P("wide", None),
            P("wide"),
            P("wide", "narrow"),
            P("narrow", "wide"),
            P("wide", None),
            P("wide"),
            P("wide", None),
            P("wide"),
            P("narrow", "wide"),
            P("wide"),
            P("wide", "narrow"),
            P("wide", "narrow"),
            P("narrow", "wide"),
        ),
        check_vma=False,
    )
```

```python
import functools
import math

import jax
import jax.numpy as jnp
from jax import lax
from jax.experimental import pallas as pl
from jax.experimental.pallas import tpu as pltpu
from jax.sharding import PartitionSpec as P

QUERY_HEADS = 12
KEY_VALUE_HEADS = 2
HEAD_SIZE = 128
FLAG_ROWS = 16

eps = 1e-06
big_negative = -1e30
score_scale = 1.0 / math.sqrt(HEAD_SIZE)
log2_scale = score_scale * math.log2(math.e)

bf16 = jnp.bfloat16
f32 = jnp.float32
ANY = pl.BlockSpec(memory_space=pl.ANY)
VMEM = pl.BlockSpec(memory_space=pltpu.VMEM)
SMEM = pl.BlockSpec(memory_space=pltpu.SMEM)


def dot(a, b, dims=((1,), (0,))):
    return lax.dot_general(a, b, (dims, ((), ())), preferred_element_type=f32)


NT = ((1,), (1,))
TN = ((0,), (0,))


def swap_wide(array, bit):
    n = lax.axis_size("wide")
    return lax.ppermute(array, "wide", [(i, i ^ bit) for i in range(n)])


def shift_narrow(array, by):
    n = lax.axis_size("narrow")
    return lax.ppermute(array, "narrow", [(i, (i + by) % n) for i in range(n)])


def ring_gather(block):
    half = block.shape[0] // 2
    below = shift_narrow(block, 1)
    above = shift_narrow(block, -1)
    far_a = shift_narrow(below[:half], 1)
    far_b = shift_narrow(above[half:], -1)
    return [block, above, jnp.concatenate([far_a, far_b], axis=0), below]


def ring_scatter(parts):
    half = parts[0].shape[0] // 2
    add = lambda a, b: (a.astype(f32) + b.astype(f32)).astype(bf16)
    up = shift_narrow(parts[2][:half], 1)
    down = shift_narrow(parts[2][half:], -1)
    to_above = jnp.concatenate([add(parts[1][:half], up), parts[1][half:]], axis=0)
    to_below = jnp.concatenate([parts[3][:half], add(parts[3][half:], down)], axis=0)
    from_below = shift_narrow(to_above, 1)
    from_above = shift_narrow(to_below, -1)
    return parts[0].astype(f32) + from_below.astype(f32) + from_above.astype(f32)


def add_rounded(a, b):
    return (a.astype(f32) + b.astype(f32)).astype(bf16)


def xor_scatter(array, bits, order):
    bits = list(bits)
    for bit in order:
        axis = bits.index(bit)
        keep = lax.index_in_dim(array, 0, axis, keepdims=False)
        send = lax.index_in_dim(array, 1, axis, keepdims=False)
        array = add_rounded(keep, swap_wide(send, bit))
        bits.remove(bit)
    return array


def tie(values, *gates):
    return lax.optimization_barrier((values, gates))[0]


class Halving:
    def __init__(self, pair, orders):
        self.sends, keeps = pair
        self.terms = [[k] for k in keeps]
        self.views = [[k] for k in keeps]
        self.orders = [list(o) for o in orders]

    def exchange(self):
        return [swap_wide(s, order.pop(0)) for s, order in zip(self.sends, self.orders)]

    def settle(self, received):
        for part in range(2):
            self.terms[part].append(received[part])
            self.views[part].append(received[part])
        if not self.orders[0]:
            return None
        n = self.views[0][0].shape[1]
        total = lambda terms: sum(t.astype(f32) for t in terms).astype(bf16)
        self.sends = [
            total([t[:, 1::2] for t in self.views[0]]),
            total([t[:, n // 2 :] for t in self.views[1]]),
        ]
        self.views = [
            [t[:, ::2] for t in self.views[0]],
            [t[:, : n // 2] for t in self.views[1]],
        ]
        return self.sends

    def rest(self):
        while self.orders[0]:
            self.settle(self.exchange())


def as_row(vector):
    return vector[...].astype(f32).reshape(1, -1)


def rope(value, cosine, signed_sine):
    return value * cosine + pltpu.roll(value, HEAD_SIZE // 2, 1) * signed_sine


def front_kernel(head, x, gain, wk, wv, bk, bv, cosine, sine, flags, acts_out, kv_out):
    rows = x.shape[0]
    of_head = lambda b: jnp.where(
        head[0] == 0, as_row(b)[:, :HEAD_SIZE], as_row(b)[:, HEAD_SIZE:]
    )
    xf = x[...].astype(f32)
    scale = lax.rsqrt(jnp.mean(xf * xf, axis=1, keepdims=True) + eps)
    acts = (xf * scale * as_row(gain)).astype(bf16)
    acts_out[...] = acts
    key = dot(acts, wk[...]) + of_head(bk)
    kv_out[:rows, :] = rope(key, cosine[...], sine[...]).astype(bf16)
    kv_out[rows : rows + FLAG_ROWS, :] = flags[...]
    kv_out[rows + FLAG_ROWS :, :] = (dot(acts, wv[...]) + of_head(bv)).astype(bf16)


def front(head, x, gain, wk, wv, bk, bv, cosine, sine, flags):
    rows, width = x.shape
    whole = lambda *shape: pl.BlockSpec(shape, lambda i, h: (0,) * len(shape))
    column = lambda r: pl.BlockSpec((r, HEAD_SIZE), lambda i, h: (0, h[0]))
    return pl.pallas_call(
        front_kernel,
        name="front",
        grid_spec=pltpu.PrefetchScalarGridSpec(
            num_scalar_prefetch=1,
            grid=(1,),
            in_specs=[
                whole(rows, width),
                whole(width),
                column(width),
                column(width),
                whole(*bk.shape),
                whole(*bv.shape),
                whole(rows, HEAD_SIZE),
                whole(rows, HEAD_SIZE),
                whole(FLAG_ROWS, HEAD_SIZE),
            ],
            out_specs=[
                whole(rows, width),
                whole(2 * rows + FLAG_ROWS, HEAD_SIZE),
            ],
        ),
        out_shape=[
            jax.ShapeDtypeStruct((rows, width), bf16),
            jax.ShapeDtypeStruct((2 * rows + FLAG_ROWS, HEAD_SIZE), bf16),
        ],
    )(head, x, gain, wk, wv, bk, bv, cosine, sine, flags)


def query_kernel(acts, cot, w, b, cosine, sine, out, turned):
    lin = dot(acts[...], w[...]) + as_row(b)
    for h in range(out.shape[1] // HEAD_SIZE):
        cols = slice(h * HEAD_SIZE, (h + 1) * HEAD_SIZE)
        out[:, cols] = rope(lin[:, cols], cosine[...], sine[...]).astype(bf16)
    turned[0] = jnp.transpose(cot[...])
    turned[1] = jnp.transpose(acts[...])


def project_queries(acts, cot, w, b, cosine, sine):
    rows, width = acts.shape
    return pl.pallas_call(
        query_kernel,
        name="queries",
        in_specs=[VMEM] * 6,
        out_specs=[VMEM, VMEM],
        out_shape=[
            jax.ShapeDtypeStruct((rows, w.shape[1]), bf16),
            jax.ShapeDtypeStruct((2, width, rows), bf16),
        ],
    )(acts, cot, w, b, cosine, sine)


def load_pieces(refs, slots, kbuf, vbuf, sem):
    copies = []
    keys, values = kbuf.shape[1], vbuf.shape[1]
    for ref, names in zip(refs, slots):
        for at, slot in enumerate(names):
            k_part = ref.at[at, pl.ds(0, keys)]
            v_part = ref.at[at, pl.ds(keys, values)]
            copies.append(pltpu.make_async_copy(k_part, kbuf.at[slot], sem.at[0, slot]))
            copies.append(pltpu.make_async_copy(v_part, vbuf.at[slot], sem.at[1, slot]))
    for copy in copies:
        copy.start()
    return copies


def key_codes(kbuf, slot, half, base, chunk):
    rows = kbuf.shape[1] - FLAG_ROWS
    per = chunk // HEAD_SIZE
    flags = jnp.transpose(kbuf[slot, rows:, :].astype(f32))
    columns = []
    for c in range(per):
        first = flags[:, c : c + 1]
        second = flags[:, per + c : per + c + 1]
        columns.append(jnp.where(half == 1, second, first))
    column = jnp.concatenate(columns, axis=0)
    index = base + lax.broadcasted_iota(jnp.int32, (chunk, 1), 0)
    return jnp.where(column > 0, index, -1)


def visible(codes, start, diagonal):
    seen = codes >= start
    if diagonal:
        shape = (codes.shape[0], start.shape[1])
        row = lax.broadcasted_iota(jnp.int32, shape, 0)
        col = lax.broadcasted_iota(jnp.int32, shape, 1)
        seen = (seen & (row < col)) | (row == col)
    return seen


def first_chunk(info, rows, chunk):
    base = info[0] * rows
    end = first = jnp.int32(0)
    for s in range(1, info.shape[0]):
        end = end + info[s]
        first = jnp.where(end <= base, end, first)
    return first // chunk


def forward_kernel(slots, info, q, start, *refs):
    kv_refs, refs = refs[: len(slots)], refs[len(slots) :]
    out, lse, kbuf, vbuf, sem, acc_s, m_s, l_s = refs
    rows = q.shape[0]
    heads = q.shape[1] // HEAD_SIZE
    chunk = rows // 2
    own = info[0]
    copies = load_pieces(kv_refs, slots, kbuf, vbuf, sem)
    for copy in copies:
        copy.wait()

    def tile(h, k, v, codes, lo, n, diagonal):
        qh = q[lo : lo + n, h * HEAD_SIZE : (h + 1) * HEAD_SIZE]
        s = dot(k, qh, NT) * log2_scale
        s = jnp.where(visible(codes, start[:, lo : lo + n], diagonal), s, big_negative)
        peak = jnp.max(s, axis=0, keepdims=True)
        cols = slice(lo, lo + n)
        if diagonal:
            p = jnp.exp2(s - peak)
            m_s[h : h + 1, cols] = peak
            l_s[h : h + 1, cols] = jnp.sum(p, axis=0, keepdims=True)
            acc_s[h, :, cols] = dot(v, p.astype(bf16), TN)
        else:
            old = m_s[h : h + 1, cols]
            new = jnp.maximum(old, peak)
            alpha = jnp.exp2(old - new)
            p = jnp.exp2(s - new)
            m_s[h : h + 1, cols] = new
            l_s[h : h + 1, cols] = alpha * l_s[h : h + 1, cols] + jnp.sum(p, axis=0, keepdims=True)
            acc_s[h, :, cols] = alpha * acc_s[h, :, cols] + dot(v, p.astype(bf16), TN)

    base = own * rows
    for half in (1, 0):
        k = kbuf[0, half * chunk : (half + 1) * chunk, :]
        v = vbuf[0, half * chunk : (half + 1) * chunk, :]
        codes = key_codes(kbuf, 0, half, base + half * chunk, chunk)
        for h in range(heads):
            tile(h, k, v, codes, half * chunk, chunk, True)
            if half == 0:
                tile(h, k, v, codes, chunk, chunk, False)

    def step(c, carry):
        block, half = c // 2, c % 2
        slot = lax.bitwise_xor(block, own)
        at = pl.multiple_of(half * chunk, chunk)
        k = kbuf[slot, pl.ds(at, chunk), :]
        v = vbuf[slot, pl.ds(at, chunk), :]
        codes = key_codes(kbuf, slot, half, c * chunk, chunk)
        for h in range(heads):
            tile(h, k, v, codes, 0, rows, False)
        return carry

    lax.fori_loop(first_chunk(info, rows, chunk), own * 2, step, 0)
    lse[...] = jnp.zeros_like(lse)
    for h in range(heads):
        total = l_s[h : h + 1, :]
        lse[h : h + 1, :] = m_s[h : h + 1, :] + jnp.log2(total)
        o = acc_s[h] * (1.0 / total)
        out[:, h * HEAD_SIZE : (h + 1) * HEAD_SIZE] = jnp.transpose(o).astype(bf16)


def attend(info, q, start, kv_pieces):
    rows, width = q.shape
    heads = width // HEAD_SIZE
    slots = sum(len(s) for s, _ in kv_pieces)
    return pl.pallas_call(
        functools.partial(forward_kernel, [s for s, _ in kv_pieces]),
        name="attend",
        in_specs=[SMEM, VMEM, VMEM] + [ANY] * len(kv_pieces),
        out_specs=[VMEM, VMEM],
        out_shape=[
            jax.ShapeDtypeStruct((rows, width), bf16),
            jax.ShapeDtypeStruct((8, rows), f32),
        ],
        scratch_shapes=[
            pltpu.VMEM((slots, rows + FLAG_ROWS, HEAD_SIZE), bf16),
            pltpu.VMEM((slots, rows, HEAD_SIZE), bf16),
            pltpu.SemaphoreType.DMA((2, slots)),
            pltpu.VMEM((heads, HEAD_SIZE, rows), f32),
            pltpu.VMEM((8, rows), f32),
            pltpu.VMEM((8, rows), f32),
        ],
    )(info, q, start, *[a for _, a in kv_pieces])


def backward_kernel(slots, info, q, do, ctx, start, lse, cosine, sine, *refs):
    kv_refs, refs = refs[: len(slots)], refs[len(slots) :]
    dq_out, send, keep, kbuf, vbuf, sem, dq_s, delta_s = refs
    rows = q.shape[0]
    heads = q.shape[1] // HEAD_SIZE
    chunk = rows // 2
    own = info[0]
    copies = load_pieces(kv_refs, slots, kbuf, vbuf, sem)
    send[...] = jnp.zeros_like(send)
    keep[...] = jnp.zeros_like(keep)
    for h in range(heads):
        cols = slice(h * HEAD_SIZE, (h + 1) * HEAD_SIZE)
        both = do[:, cols].astype(f32) * ctx[:, cols].astype(f32)
        delta_s[h : h + 1, :] = jnp.sum(jnp.transpose(both), axis=0, keepdims=True)
        dq_s[h] = jnp.zeros((HEAD_SIZE, rows), f32)
    for copy in copies:
        copy.wait()

    def tile(h, k, v, codes, lo, n, diagonal):
        cols = slice(lo, lo + n)
        qh = q[cols, h * HEAD_SIZE : (h + 1) * HEAD_SIZE]
        doh = do[cols, h * HEAD_SIZE : (h + 1) * HEAD_SIZE]
        s = dot(k, qh, NT) * log2_scale - lse[h : h + 1, cols]
        s = jnp.where(visible(codes, start[:, cols], diagonal), s, big_negative)
        p = jnp.exp2(s)
        dv = dot(p.astype(bf16), doh)
        ds = (p * (dot(v, doh, NT) - delta_s[h : h + 1, cols])).astype(bf16)
        dk = dot(ds, qh)
        dq_s[h, :, cols] = dq_s[h, :, cols] + dot(k, ds, TN)
        return dk, dv

    def both(h, k, v, codes, spans):
        dk = dv = None
        for lo, n, diagonal in spans:
            a, b = tile(h, k, v, codes, lo, n, diagonal)
            dk, dv = (a, b) if dk is None else (dk + a, dv + b)
        return dk, dv

    def all_heads(k, v, codes, spans):
        dk = dv = None
        for h in range(heads):
            a, b = both(h, k, v, codes, spans)
            dk, dv = (a, b) if dk is None else (dk + a, dv + b)
        return (dk * score_scale).astype(bf16), dv.astype(bf16)

    base = own * rows
    for half in (1, 0):
        span = slice(half * chunk, (half + 1) * chunk)
        codes = key_codes(kbuf, 0, half, base + half * chunk, chunk)
        spans = [(chunk, chunk, True)] if half else [(0, chunk, True), (chunk, chunk, False)]
        dk, dv = all_heads(kbuf[0, span, :], vbuf[0, span, :], codes, spans)
        keep[0, 0, span, :] = dk
        keep[1, 0, span, :] = dv

    def step(c, carry):
        block, half = c // 2, c % 2
        slot = lax.bitwise_xor(block, own)
        at = pl.multiple_of(half * chunk, chunk)
        k = kbuf[slot, pl.ds(at, chunk), :]
        v = vbuf[slot, pl.ds(at, chunk), :]
        codes = key_codes(kbuf, slot, half, c * chunk, chunk)
        dk, dv = all_heads(k, v, codes, [(0, rows, False)])

        @pl.when(slot % 2 == 0)
        def _():
            keep[0, slot // 2, pl.ds(at, chunk), :] = dk
            keep[1, slot // 2, pl.ds(at, chunk), :] = dv

        @pl.when(slot % 2 == 1)
        def _():
            send[0, slot // 2, pl.ds(at, chunk), :] = dk
            send[1, slot // 2, pl.ds(at, chunk), :] = dv

        return carry

    lax.fori_loop(first_chunk(info, rows, chunk), own * 2, step, 0)
    for h in range(heads):
        g = jnp.transpose(dq_s[h]) * score_scale
        back = g * cosine[...] - pltpu.roll(g, HEAD_SIZE // 2, 1) * sine[...]
        dq_out[:, h * HEAD_SIZE : (h + 1) * HEAD_SIZE] = back.astype(bf16)


def attend_back(info, q, do, ctx, start, lse, cosine, sine, kv_pieces):
    rows, width = q.shape
    heads = width // HEAD_SIZE
    slots = sum(len(s) for s, _ in kv_pieces)
    half = jax.ShapeDtypeStruct((2, slots // 2, rows, HEAD_SIZE), bf16)
    return pl.pallas_call(
        functools.partial(backward_kernel, [s for s, _ in kv_pieces]),
        name="attend_back",
        in_specs=[SMEM] + [VMEM] * 7 + [ANY] * len(kv_pieces),
        out_specs=[VMEM] * 3,
        out_shape=[jax.ShapeDtypeStruct((rows, width), bf16), half, half],
        scratch_shapes=[
            pltpu.VMEM((slots, rows + FLAG_ROWS, HEAD_SIZE), bf16),
            pltpu.VMEM((slots, rows, HEAD_SIZE), bf16),
            pltpu.SemaphoreType.DMA((2, slots)),
            pltpu.VMEM((heads, HEAD_SIZE, rows), f32),
            pltpu.VMEM((8, rows), f32),
        ],
    )(
        info, q, do, ctx, start, lse, cosine, sine,
        *[a for _, a in kv_pieces],
    )


def whole(shape):
    return pl.BlockSpec(shape, lambda *_: (0,) * len(shape))


def struct(shape, dtype):
    return jax.ShapeDtypeStruct(shape, dtype)


def project_out_kernel(
    core, x, own, above, fa, fb, below, w_own, mine, other, gain, middle, acts, turned, scale
):
    n = w_own.shape[0]
    width = x.shape[1]
    far = jnp.where(pl.program_id(0) == 0, fa[...].astype(f32), fb[...].astype(f32)).astype(bf16)
    part = lambda m: (
        dot(above[...], m[:n, :]) + dot(below[...], m[n : 2 * n, :]) + dot(far, m[2 * n :, :])
    )
    a, b = part(mine), part(other)
    first = core[0] == 0
    out = dot(own[...], w_own[...]) + jnp.concatenate(
        [jnp.where(first, a, b), jnp.where(first, b, a)], axis=1
    )
    mid = x[...].astype(f32) + out
    r = lax.rsqrt(jnp.mean(mid * mid, axis=1, keepdims=True) + eps)
    middle[...] = mid
    scale[...] = r
    normed = mid * r * as_row(gain)
    acts[...] = normed.astype(bf16)
    turned[:width, :] = jnp.transpose(normed.astype(bf16))
    turned[width:, :] = jnp.transpose(own[...])


def project_out(core, x, pieces, w_own, mine, other, gain):
    rows, width = x.shape
    n = w_own.shape[0]
    half = rows // 2
    own, above, (fa, fb), below = pieces
    block = lambda c: pl.BlockSpec((half, c), lambda i, s: (i, 0))
    return pl.pallas_call(
        project_out_kernel,
        name="project_out",
        grid_spec=pltpu.PrefetchScalarGridSpec(
            num_scalar_prefetch=1,
            grid=(2,),
            in_specs=[
                block(width), block(n), block(n), whole((half, n)), whole((half, n)), block(n),
                whole(w_own.shape), whole(mine.shape), whole(other.shape), whole(gain.shape),
            ],
            out_specs=[
                block(width), block(width),
                pl.BlockSpec((width + n, half), lambda i, s: (0, i)),
                block(1),
            ],
        ),
        out_shape=[
            struct((rows, width), f32), struct((rows, width), bf16),
            struct((width + n, rows), bf16), struct((rows, 1), f32),
        ],
    )(core, x, own, above, fa, fb, below, w_own, mine, other, gain)


def ring_blocks(acc, mine, outs):
    block = acc.shape[0] // 4
    own, above, far_a, far_b, below = outs

    def take(k, first, size):
        at = ((mine[0] + k) % 4) * block + first
        return acc[pl.ds(pl.multiple_of(at, size), size), :].astype(bf16)

    own[...] = take(0, 0, block)
    above[...] = take(1, 0, block)
    far_a[...] = take(2, 0, block // 2)
    far_b[...] = take(2, block // 2, block // 2)
    below[...] = take(3, 0, block)


def block_sizes(rows):
    return [rows // 4, rows // 4, rows // 8, rows // 8, rows // 4]


def feed_kernel(n, mine, acts, cot, wg, wu, wd, hidden, grads, *refs):
    outs, acc = refs[:-1], refs[-1]
    j = pl.program_id(0)
    tile = wg.shape[0]
    part = min(256, tile)
    for lo in range(0, tile, part):
        cols = slice(lo, lo + part)
        gate = dot(acts[...], wg[cols, :], NT)
        up = dot(acts[...], wu[cols, :], NT)
        g = dot(cot[...], wd[cols, :], NT)
        sig = 1.0 / (1.0 + jnp.exp(-gate))
        silu = gate * sig
        column = j * tile + lo + lax.broadcasted_iota(jnp.int32, (1, part), 1)
        keep = lambda v: jnp.where(column < n, v, 0.0).astype(bf16)
        hidden[:, cols] = keep(silu * up)
        grads[0, :, cols] = keep(g * up * (sig * (1.0 + gate * (1.0 - sig))))
        grads[1, :, cols] = keep(g * silu)
    back = lambda k: dot(grads[0, :, :k], wg[:k, :]) + dot(grads[1, :, :k], wu[:k, :])
    steps = pl.cdiv(n, tile)

    @pl.when(j == 0)
    def _():
        acc[...] = back(min(n, tile))

    if steps > 2:
        @pl.when((j > 0) & (j < steps - 1))
        def _():
            acc[...] = acc[...] + back(tile)

    if steps > 1:
        @pl.when(j == steps - 1)
        def _():
            acc[...] = acc[...] + back(n - (steps - 1) * tile)

    @pl.when(j == steps - 1)
    def _():
        ring_blocks(acc, mine, outs)


def feed(mine, acts, cot, wg, wu, wd, tile=768):
    rows, width = acts.shape
    n = wg.shape[0]
    steps = pl.cdiv(n, tile)
    w_spec = pl.BlockSpec((tile, width), lambda j, s: (j, 0))
    sizes = block_sizes(rows)
    outs = pl.pallas_call(
        functools.partial(feed_kernel, n),
        name="feed",
        grid_spec=pltpu.PrefetchScalarGridSpec(
            num_scalar_prefetch=1,
            grid=(steps,),
            in_specs=[whole((rows, width)), whole((rows, width)), w_spec, w_spec, w_spec],
            out_specs=[
                pl.BlockSpec((rows, tile), lambda j, s: (0, j)),
                pl.BlockSpec((2, rows, tile), lambda j, s: (0, 0, j)),
            ]
            + [whole((r, width)) for r in sizes],
            scratch_shapes=[pltpu.VMEM((rows, width), f32)],
        ),
        out_shape=[struct((rows, steps * tile), bf16), struct((2, rows, steps * tile), bf16)]
        + [struct((r, width), bf16) for r in sizes],
    )(mine, acts, cot, wg, wu, wd)
    return outs[0], outs[1], outs[2:]


def stack_kernel(cut, *refs):
    count = 1 if cut is None else 2
    ins, outs = refs[:-count], refs[-count:]
    cut = outs[0].shape[0]
    done = 0
    for ref in ins:
        rows = ref.shape[0]
        head = min(max(cut - done, 0), rows)
        if head:
            outs[0][done : done + head, :] = ref[:head, :]
        if head < rows:
            at = done + head - cut
            outs[1][at : at + rows - head, :] = ref[head:, :]
        done += rows


def stack(arrays, cut):
    rows = sum(a.shape[0] for a in arrays)
    width = arrays[0].shape[1]
    sizes = [cut, rows - cut] if cut < rows else [rows]
    return pl.pallas_call(
        functools.partial(stack_kernel, cut if cut < rows else None),
        name="stack",
        in_specs=[VMEM] * len(arrays),
        out_specs=[VMEM] * len(sizes),
        out_shape=[struct((size, width), bf16) for size in sizes],
    )(*arrays)


def assemble_kernel(plan, chip, *refs):
    out = refs[-1]
    n = out.shape[0] // 3
    block = n // plan[0]
    for ref, (names, first) in zip(refs, plan[1]):
        rows = ref.shape[1]
        for at, name in enumerate(names):
            source = lax.bitwise_xor(chip[0], name)
            done = 0
            while done < rows:
                piece, inside = divmod(first + done, block)
                size = min(rows - done, block - inside)
                to = pl.multiple_of(piece * n + source * block + inside, 16)
                out[pl.ds(to, size), :] = ref[at, done : done + size, :]
                done += size


def assemble(chip, chips, parts):
    one = sum({first: a.shape[1] for _, first, a in parts}.values())
    plan = (chips, [(names, first) for names, first, _ in parts])
    return pl.pallas_call(
        functools.partial(assemble_kernel, plan),
        name="assemble",
        in_specs=[SMEM] + [VMEM] * len(parts),
        out_specs=VMEM,
        out_shape=struct((chips * one, parts[0][2].shape[2]), bf16),
    )(chip, *[a for _, _, a in parts])


def partial_kernel(mine, a, w, *refs):
    refs[-1][...] = dot(a[:, : w.shape[0]], w[...])
    ring_blocks(refs[-1], mine, refs[:-1])


def partial_rows(mine, a, w, tile=512):
    rows, columns = a.shape
    inner, width = w.shape
    sizes = block_sizes(rows)
    return pl.pallas_call(
        partial_kernel,
        name="partial_down",
        grid_spec=pltpu.PrefetchScalarGridSpec(
            num_scalar_prefetch=1,
            grid=(width // tile,),
            in_specs=[whole(a.shape), pl.BlockSpec((inner, tile), lambda j, s: (0, j))],
            out_specs=[pl.BlockSpec((r, tile), lambda j, s: (0, j)) for r in sizes],
            scratch_shapes=[pltpu.VMEM((rows, tile), f32)],
        ),
        out_shape=[struct((r, width), bf16) for r in sizes],
    )(mine, a, w)


def pass_on_kernel(above, below, up, down, to_above, to_below):
    half = up.shape[0]
    to_above[:half, :] = (above[:half, :].astype(f32) + up[...].astype(f32)).astype(bf16)
    to_above[half:, :] = above[half:, :]
    to_below[:half, :] = below[:half, :]
    to_below[half:, :] = (below[half:, :].astype(f32) + down[...].astype(f32)).astype(bf16)


def pass_on(above, below, up, down):
    return pl.pallas_call(
        pass_on_kernel,
        name="pass_on",
        in_specs=[VMEM] * 4,
        out_specs=[VMEM] * 2,
        out_shape=[struct(above.shape, bf16)] * 2,
    )(above, below, up, down)


def weigh_kernel(slots, half, mine, a_own, a_other, b_own, b_other, *refs):
    send_a, keep_a, send_b, keep_b, lhs = refs
    rows = a_own.shape[1]
    block = 2 * half

    @pl.when(pl.program_id(0) == 0)
    def _():
        for s in range(slots):
            at = pl.multiple_of(lax.bitwise_xor(mine[0], 2 * s) * block, 16)
            lhs[s * block : (s + 1) * block, :rows] = a_own[pl.ds(at, block), :]
            lhs[s * block : (s + 1) * block, rows:] = a_other[pl.ds(at, block), :]

    g = dot(lhs[:, :rows], b_own[0]) + dot(lhs[:, rows:], b_other[0])
    place_slots(g, slots, half, 0, send_a, keep_a, send_b, keep_b)


def place_slots(g, slots, half, group, send_a, keep_a, send_b, keep_b):
    cols = slice(0, g.shape[1])
    for s in range(slots):
        first = g[2 * s * half : (2 * s + 1) * half].astype(bf16)
        second = g[(2 * s + 1) * half : (2 * s + 2) * half].astype(bf16)
        (send_a if s % 2 else keep_a)[group, s // 2, :, cols] = first
        (send_b if s >= slots // 2 else keep_b)[group, s % (slots // 2), :, cols] = second


def weigh(mine, slots, width, a_own, a_other, b_own, b_other, group=0, tile=768):
    rows = a_own.shape[-1]
    n = b_own.shape[2]
    if a_own.ndim == 3:
        a_spec = pl.BlockSpec((None, width, rows), lambda j, s: (0, 0, 0))
    else:
        a_spec = pl.BlockSpec((width, rows), lambda j, s: (0, 0))
    half = width // slots // 4
    b_spec = pl.BlockSpec((1, rows, tile), lambda j, s: (group, 0, j))
    out = pl.BlockSpec((1, slots // 2, half, tile), lambda j, s: (0, 0, 0, j))
    outs = pl.pallas_call(
        functools.partial(weigh_kernel, slots, half),
        name="weigh",
        grid_spec=pltpu.PrefetchScalarGridSpec(
            num_scalar_prefetch=1,
            grid=(pl.cdiv(n, tile),),
            in_specs=[a_spec, a_spec, b_spec, b_spec],
            out_specs=[out] * 4,
            scratch_shapes=[pltpu.VMEM((width // 2, 2 * rows), bf16)],
        ),
        out_shape=[struct((1, slots // 2, half, n), bf16)] * 4,
    )(mine, a_own, a_other, b_own, b_other)
    return [outs[0], outs[2]], [outs[1], outs[3]]


def weigh_late_kernel(
    slots, half, mine, t_own, t_other, c_own, c_other, a_own, a_other, b_own, b_other, *refs
):
    send_a, keep_a, send_b, keep_b = refs
    block = 2 * half

    def gather(ref):
        pieces = []
        for s in range(slots):
            at = pl.multiple_of(lax.bitwise_xor(mine[0], 2 * s) * block, 16)
            pieces.append(ref[pl.ds(at, block), :])
        return jnp.concatenate(pieces, axis=0)

    n = c_own.shape[0]
    g = dot(gather(t_own), c_own[...], NT) + dot(gather(t_other), c_other[...], NT)
    late = dot(gather(a_own), b_own[...]) + dot(gather(a_other), b_other[...])
    g = jnp.concatenate([g, late], axis=1)
    place_slots(g, slots, half, 0, send_a, keep_a, send_b, keep_b)


def weigh_late(mine, slots, t_own, t_other, c_own, c_other, a_own, a_other, b_own, b_other):
    width, rows = t_own.shape
    n = c_own.shape[0] - width
    half = width // slots // 4
    total = n + b_own.shape[1]
    t_spec = whole((width, rows))
    c_spec = pl.BlockSpec((n, rows), lambda i, s: (width // n, 0))
    a_spec = pl.BlockSpec((None, width, rows), lambda i, s: (1, 0, 0))
    b_spec = whole(b_own.shape)
    shape = (1, slots // 2, half, total)
    outs = pl.pallas_call(
        functools.partial(weigh_late_kernel, slots, half),
        name="weigh_late",
        grid_spec=pltpu.PrefetchScalarGridSpec(
            num_scalar_prefetch=1,
            grid=(1,),
            in_specs=[t_spec, t_spec, c_spec, c_spec, a_spec, a_spec, b_spec, b_spec],
            out_specs=[whole(shape)] * 4,
        ),
        out_shape=[struct(shape, bf16)] * 4,
    )(mine, t_own, t_other, c_own, c_other, a_own, a_other, b_own, b_other)
    return [outs[0], outs[2]], [outs[1], outs[3]]


def total_of(refs, cols):
    total = None
    for t in refs:
        value = t[0, 0, :, cols].astype(f32)
        total = value if total is None else total + value
    return total


def finish_kernel(n, *refs):
    out = refs[-1]
    half = out.shape[0] // 2
    for part in range(2):
        total = total_of(refs[part * n : (part + 1) * n], slice(0, out.shape[1]))
        out[part * half : (part + 1) * half, :] = total


def finish(terms, columns):
    flat = terms[0] + terms[1]
    _, _, half, width = flat[0][0].shape
    at = lambda g: pl.BlockSpec((1, 1, half, width), lambda i: (g, 0, 0, 0))
    return pl.pallas_call(
        functools.partial(finish_kernel, len(terms[0])),
        name="finish",
        grid=(1,),
        in_specs=[at(g) for _, g in flat],
        out_specs=whole((2 * half, columns)),
        out_shape=struct((2 * half, columns), f32),
    )(*[a for a, _ in flat])


def finish_late_kernel(n, count, *refs):
    terms, outs = refs[:-count], refs[-count:]
    half = outs[0].shape[0] // 2
    for part in range(2):
        at = 0
        for out in outs:
            cols = slice(at, at + out.shape[1])
            total = total_of(terms[part * n : (part + 1) * n], cols)
            out[part * half : (part + 1) * half, :] = total
            at += out.shape[1]


def finish_late(terms, sizes):
    flat = terms[0] + terms[1]
    _, _, half, columns = flat[0].shape
    return pl.pallas_call(
        functools.partial(finish_late_kernel, len(terms[0]), len(sizes)),
        name="finish_late",
        grid=(1,),
        in_specs=[whole((1, 1, half, columns))] * len(flat),
        out_specs=[whole((2 * half, size)) for size in sizes],
        out_shape=[struct((2 * half, size), f32) for size in sizes],
    )(*flat)


def middle_back_kernel(
    mine, own, above, fa, fb, below, middle, scale, cot, gain, w_out,
    grad_middle, turned, grad_context, gain_grad, g_s,
):
    k = pl.program_id(0)
    half = fa.shape[0]
    for at, ref in ((0, own), (1, above), (3, below)):
        @pl.when(k == at)
        def _():
            g_s[...] = ref[...].astype(f32)

    @pl.when(k == 2)
    def _():
        g_s[:half, :] = fa[...].astype(f32)
        g_s[half:, :] = fb[...].astype(f32)

    g = g_s[...]
    r = scale[...]
    n2 = middle[...] * r
    u2 = g * as_row(gain)
    gm = cot[...].astype(f32) + r * (u2 - n2 * jnp.mean(u2 * n2, axis=1, keepdims=True))
    part = jnp.sum(g * n2, axis=0, keepdims=True)

    @pl.when(k == 0)
    def _():
        gain_grad[...] = part

    @pl.when(k > 0)
    def _():
        gain_grad[...] = gain_grad[...] + part

    grad_middle[...] = gm
    turned[...] = jnp.transpose(gm.astype(bf16))
    grad_context[...] = dot(gm.astype(bf16), w_out[...], NT).astype(bf16)


def middle_back(mine, pieces, middle, scale, cot, gain, w_out):
    rows, width = middle.shape
    block = rows // 4
    own, above, (fa, fb), below = pieces
    at = lambda c: pl.BlockSpec((block, c), lambda k, s: ((s[0] + k) % 4, 0))
    n = w_out.shape[0]
    return pl.pallas_call(
        middle_back_kernel,
        name="middle_back",
        grid_spec=pltpu.PrefetchScalarGridSpec(
            num_scalar_prefetch=1,
            grid=(4,),
            in_specs=[
                whole((block, width)), whole((block, width)),
                whole((block // 2, width)), whole((block // 2, width)), whole((block, width)),
                at(width), at(1), at(width), whole(gain.shape), whole(w_out.shape),
            ],
            out_specs=[
                at(width),
                pl.BlockSpec((width, block), lambda k, s: (0, (s[0] + k) % 4)),
                at(n),
                whole((1, width)),
            ],
            scratch_shapes=[pltpu.VMEM((block, width), f32)],
        ),
        out_shape=[
            struct((rows, width), f32), struct((width, rows), bf16),
            struct((rows, n), bf16), struct((1, width), f32),
        ],
    )(mine, own, above, fa, fb, below, middle, scale, cot, gain, w_out)


def in_rows_kernel(mine, own, above, fa, fb, below, out):
    block = own.shape[0]
    at = lambda k: pl.ds(pl.multiple_of((mine[0] + k) % 4 * block, block), block)
    out[at(0), :] = own[...]
    out[at(1), :] = above[...]
    out[at(2), :] = jnp.concatenate([fa[...], fb[...]], axis=0)
    out[at(3), :] = below[...]


def in_rows(mine, pieces):
    own, above, (fa, fb), below = pieces
    rows, width = own.shape
    return pl.pallas_call(
        in_rows_kernel,
        name="in_rows",
        in_specs=[SMEM] + [VMEM] * 5,
        out_specs=VMEM,
        out_shape=struct((4 * rows, width), bf16),
    )(mine, own, above, fa, fb, below)


def late_kernel(head, q, pair, cross, cosine, sine, late, bias):
    rows, n = q.shape
    kv = KEY_VALUE_HEADS * HEAD_SIZE

    def lin(ref):
        g = ref[:, :HEAD_SIZE].astype(f32)
        key = g * cosine[...] - pltpu.roll(g, HEAD_SIZE // 2, 1) * sine[...]
        return key, ref[:, HEAD_SIZE:].astype(f32)

    (own_k, own_v), (other_k, other_v) = lin(pair), lin(cross)
    first = head[0] == 0
    late[:, :n] = q[...]
    columns = [
        jnp.where(first, own_k, other_k), jnp.where(first, other_k, own_k),
        jnp.where(first, own_v, other_v), jnp.where(first, other_v, own_v),
    ]
    for c, value in enumerate(columns):
        late[:, n + c * HEAD_SIZE : n + (c + 1) * HEAD_SIZE] = value.astype(bf16)
    bias[...] = jnp.sum(late[...].astype(f32), axis=0, keepdims=True)


def late_grads(head, q, pair, cross, cosine, sine):
    rows, n = q.shape
    total = n + 2 * KEY_VALUE_HEADS * HEAD_SIZE
    return pl.pallas_call(
        late_kernel,
        name="late_grads",
        in_specs=[SMEM] + [VMEM] * 5,
        out_specs=[VMEM] * 2,
        out_shape=[struct((rows, total), bf16), struct((1, total), f32)],
    )(head, q, pair, cross, cosine, sine)


def project_back_kernel(
    core, x, late, above, fa, fb, below, w_own, mine, other, wk, wv, gain, grad_middle,
    gain_two_grad, bias, out, vectors,
):
    i = pl.program_id(0)
    n = w_own.shape[1]
    kv = wk.shape[1]
    far = jnp.where(i == 0, fa[...].astype(f32), fb[...].astype(f32)).astype(bf16)
    part = lambda m: (
        dot(above[...], m[:n, :]) + dot(below[...], m[n : 2 * n, :]) + dot(far, m[2 * n :, :])
    )
    a, b = part(mine), part(other)
    first = core[0] == 0
    g = jnp.concatenate([jnp.where(first, a, b), jnp.where(first, b, a)], axis=1)
    g = g + dot(late[:, :n], w_own[...], NT)
    g = g + dot(late[:, n : n + kv], wk[...], NT) + dot(late[:, n + kv :], wv[...], NT)
    xf = x[...].astype(f32)
    r = lax.rsqrt(jnp.mean(xf * xf, axis=1, keepdims=True) + eps)
    n1 = xf * r
    u1 = g * as_row(gain)
    out[...] = (
        grad_middle[...] + r * (u1 - n1 * jnp.mean(u1 * n1, axis=1, keepdims=True))
    ).astype(bf16)
    total = jnp.sum(g * n1, axis=0, keepdims=True)
    width = x.shape[1]

    @pl.when(i == 0)
    def _():
        vectors[:, :width] = total
        vectors[:, width : 2 * width] = gain_two_grad[...]
        vectors[:, 2 * width :] = bias[...]

    @pl.when(i > 0)
    def _():
        vectors[:, :width] = vectors[:, :width] + total


def project_back(
    core, x, late, pieces, w_own, mine, other, wk, wv, gain, grad_middle, gain_two_grad, bias
):
    rows, width = x.shape
    n = w_own.shape[1]
    half = rows // 2
    above, (fa, fb), below = pieces
    block = lambda c: pl.BlockSpec((half, c), lambda i, s: (i, 0))
    return pl.pallas_call(
        project_back_kernel,
        name="project_back",
        grid_spec=pltpu.PrefetchScalarGridSpec(
            num_scalar_prefetch=1,
            grid=(2,),
            in_specs=[
                block(width), block(late.shape[1]), block(n), whole((half, n)), whole((half, n)),
                block(n), whole(w_own.shape), whole(mine.shape), whole(other.shape),
                whole(wk.shape), whole(wv.shape), whole(gain.shape), block(width),
                whole(gain_two_grad.shape), whole(bias.shape),
            ],
            out_specs=[block(width), whole((1, 2 * width + bias.shape[1]))],
        ),
        out_shape=[struct((rows, width), bf16), struct((1, 2 * width + bias.shape[1]), f32)],
    )(
        core, x, late, above, fa, fb, below, w_own, mine, other, wk, wv, gain, grad_middle,
        gain_two_grad, bias,
    )


class Spread:
    def __init__(self, share, orders):
        self.share = share
        self.half = share.shape[0] // 2
        self.orders = [list(o) for o in orders]
        self.near = [shift_narrow(share, 1), shift_narrow(share, -1)]

    def fetch_far(self):
        below, above = self.near
        self.far = [shift_narrow(below[: self.half], 1), shift_narrow(above[self.half :], -1)]

    def collect(self):
        below, above = self.near
        pieces = [above, below] + self.far
        if not self.orders:
            self.rows = jnp.concatenate(pieces, axis=0)
            return
        rows = 6 * self.half
        self.cut = rows // len(self.orders)
        self.names = [[(0,)] for _ in self.orders]
        self.arrays = [[part[None]] for part in stack(pieces, self.cut)]

    def hop(self):
        if not self.orders or not self.orders[0]:
            return
        for part, order in enumerate(self.orders):
            bit = order.pop(0)
            held = self.arrays[part]
            payload = held[0] if len(held) == 1 else jnp.concatenate(held, axis=0)
            names = tuple(s ^ (bit >> 1) for group in self.names[part] for s in group)
            self.names[part].append(names)
            held.append(swap_wide(payload, bit))

    def whole(self, chip, chips):
        if not hasattr(self, "arrays"):
            return self.rows
        while self.orders[0]:
            self.hop()
        parts = []
        for part in range(len(self.orders)):
            for names, array in zip(self.names[part], self.arrays[part]):
                parts.append((names, part * self.cut, array))
        return assemble(chip, chips, parts)


def join_kernel(*refs):
    ins, outs = refs[:-2], refs[-2:]
    for part, out in enumerate(outs):
        for g in range(out.shape[0]):
            a, b = ins[4 * g + 2 * part], ins[4 * g + 2 * part + 1]
            out[g, 0] = (a[0, 0].astype(f32) + b[0, 0].astype(f32)).astype(bf16)


def join_sends(steps):
    slots = steps[0].views[0][0].shape[1]
    if slots != 1 or len(steps[0].terms[0]) != 2:
        return [jnp.concatenate([s.sends[part] for s in steps], axis=0) for part in range(2)]
    flat = [t for s in steps for terms in s.terms for t in terms]
    _, _, rows, columns = flat[0].shape
    shape = (len(steps), 1, rows, columns)
    return pl.pallas_call(
        join_kernel,
        name="join",
        grid=(1,),
        in_specs=[pl.BlockSpec((1, 1, rows, columns), lambda i: (0, 1, 0, 0))] * len(flat),
        out_specs=[whole(shape)] * 2,
        out_shape=[struct(shape, bf16)] * 2,
    )(*flat)


def finish_joint(steps, received):
    for s in steps:
        for order in s.orders:
            order.pop(0)
    if not steps[0].orders[0]:
        return [
            [[(t, 0) for t in s.terms[part]] + [(received[part], g)] for part in range(2)]
            for g, s in enumerate(steps)
        ]
    for g, s in enumerate(steps):
        s.settle([r[g : g + 1] for r in received])
        s.rest()
    return [[[(t, 0) for t in terms] for terms in s.terms] for s in steps]


def place_tokens(index, lengths):
    ends = jnp.cumsum(lengths)
    before = (ends[None, :] <= index[:, None]).astype(jnp.int32)
    return index - jnp.sum(before * lengths[None, :], axis=1)


def on_device(
    hidden_in,
    cotangent,
    lengths,
    valid,
    gain_one,
    w_query,
    b_query,
    key_projection,
    key_bias_vector,
    value_projection,
    value_bias_vector,
    w_out,
    gain_two,
    w_gate,
    w_up,
    w_down,
):
    rows, width = hidden_in.shape
    n_wide = lax.axis_size("wide")
    wide_index = lax.axis_index("wide")
    narrow_index = lax.axis_index("narrow")
    heads = w_query.shape[1] // HEAD_SIZE
    n_query = heads * HEAD_SIZE
    kv_width = KEY_VALUE_HEADS * HEAD_SIZE
    head = narrow_index * heads // (QUERY_HEADS // KEY_VALUE_HEADS)
    bits = [1 << b for b in reversed(range(n_wide.bit_length() - 1))]
    chip_bits = bits[:-1]
    low_chip = chip_bits[::-1]
    slots = n_wide // 2
    core = wide_index % 2
    base = wide_index * rows
    as_scalar = lambda v: v.astype(jnp.int32).reshape(1)
    mine_wide, mine_narrow, core_s, head_s = map(
        as_scalar, (wide_index, narrow_index, core, head)
    )
    swap_core = lambda v: swap_wide(v, 1)

    token_index = base + jnp.arange(rows, dtype=jnp.int32)
    positions = place_tokens(token_index, lengths)
    start = (token_index - positions)[None, :]
    info = jnp.concatenate([mine_wide, lengths])
    freqs = 10000.0 ** (-(jnp.arange(HEAD_SIZE // 2, dtype=f32) * 2.0) / HEAD_SIZE)
    angles = positions.astype(f32)[:, None] * freqs[None, :]
    cos_half, sin_half = jnp.cos(angles), jnp.sin(angles)
    cosine = jnp.concatenate([cos_half, cos_half], axis=1)
    sine = jnp.concatenate([-sin_half, sin_half], axis=1)

    flags = jnp.pad(
        valid.astype(bf16).reshape(rows // HEAD_SIZE, HEAD_SIZE),
        ((0, FLAG_ROWS - rows // HEAD_SIZE), (0, 0)),
    )
    acts_one, kv_own = front(
        head_s,
        hidden_in,
        gain_one,
        key_projection,
        value_projection,
        key_bias_vector,
        value_bias_vector,
        cosine,
        sine,
        flags,
    )

    col = width // 2
    n_half = n_query // 2
    split = n_query // slots % 32 == 0
    share = n_query // slots if split else n_query
    at = wide_index // 2 * share if split else 0
    half_query = lax.dynamic_slice_in_dim(w_query, core * col, col, 0).T
    half_out = lax.dynamic_slice(w_out, (at, core * col), (share, col))
    out_weights = Spread(half_out, [low_chip, chip_bits] if split else [])

    kv_slots, kv_arrays = [(0,)], [kv_own[None]]
    for step, bit in enumerate(bits):
        send = kv_arrays[0] if step == 0 else jnp.concatenate(kv_arrays, axis=0)
        if step == 1:
            send, out_weights.near = tie((send, out_weights.near))
            out_weights.fetch_far()
        if step + 1 == len(bits):
            send, queries, half_query, out_weights.far = tie(
                (send, queries, half_query, out_weights.far)
            )
            out_weights.collect()
            out_weights.hop()
        kv_arrays.append(swap_wide(send, bit))
        kv_slots.append(tuple(s ^ bit for group in kv_slots for s in group))
        if step == 0:
            acts_late = tie(acts_one, kv_arrays[1])
            queries, turned_one = project_queries(
                acts_late, cotangent, w_query, b_query, cosine, sine
            )
    kv_pieces = list(zip(kv_slots, kv_arrays))
    context, lse = attend(info, queries, start, kv_pieces)
    if split:
        context, out_weights.arrays = tie((context, out_weights.arrays))

    half = rows // 2
    ctx_below, ctx_above = shift_narrow(context, 1), shift_narrow(context, -1)
    out_mine = out_weights.whole(as_scalar(wide_index // 2), slots)
    out_mine, ctx_below, ctx_above = tie((out_mine, ctx_below, ctx_above))
    out_other = swap_core(out_mine)
    ctx_far = (shift_narrow(ctx_below[:half], 1), shift_narrow(ctx_above[half:], -1))
    turned_one_other = swap_core(turned_one)
    ctx_far, half_query = tie((ctx_far, half_query), turned_one_other, out_other)
    w_gate_t, w_up_t = w_gate.T, w_up.T
    middle, acts_two, turned_two, scale_two = project_out(
        core_s, hidden_in, (context, ctx_above, ctx_far, ctx_below),
        w_out, out_mine, out_other, gain_two,
    )

    query_weights = Spread(half_query, [])
    hidden, grads, blocks = feed(
        mine_narrow, acts_two, cotangent, w_gate_t, w_up_t, w_down
    )
    turned_two_other = swap_core(tie(turned_two, acts_two))
    (hidden, grads, blocks), query_weights.near = tie(
        ((hidden, grads, blocks), query_weights.near), turned_two_other
    )
    own, above, far_a, far_b, below = blocks
    up, down = shift_narrow(far_a, 1), shift_narrow(far_b, -1)
    hidden_other = swap_core(hidden)
    up, down, hidden_other = tie((up, down, hidden_other))
    grads_other = swap_core(tie(grads, up, down))
    to_above, to_below = pass_on(above, below, up, down)
    from_below, from_above = shift_narrow(to_above, 1), shift_narrow(to_below, -1)
    hidden_here = tie(hidden, to_above, to_below)
    down_pair = weigh(
        mine_wide, slots, width, turned_one, turned_one_other, hidden_here[None],
        hidden_other[None],
    )
    ffn = partial_rows(mine_narrow, hidden_here, w_down)
    from_below, from_above, grads, grads_other, down_pair, ffn = tie(
        (from_below, from_above, grads, grads_other, down_pair, ffn)
    )
    orders = (low_chip, chip_bits)
    down_steps = Halving(down_pair, orders)
    down_moved = down_steps.exchange()
    own = (own.astype(f32) + from_below.astype(f32) + from_above.astype(f32)).astype(bf16)
    q_rows = rows // 8
    g_below, g_above = shift_narrow(own, 1), shift_narrow(own, -1)
    grads_here = tie(grads, own)
    gate_pair, up_pair = [
        weigh(mine_wide, slots, width, turned_two, turned_two_other, grads_here, grads_other, k)
        for k in range(2)
    ]
    g_below, g_above, gate_pair, up_pair, down_moved = tie(
        (g_below, g_above, gate_pair, up_pair, down_moved)
    )
    gate_steps = Halving(gate_pair, orders)
    gate_moved = gate_steps.exchange()
    g_far = (shift_narrow(g_below[:q_rows], 1), shift_narrow(g_above[q_rows:], -1))
    down_steps.settle(down_moved)
    g_far = tie(g_far)
    grad_middle, turned_attn, grad_context, gain_two_grad = middle_back(
        mine_narrow, (own, g_above, g_far, g_below), middle, scale_two, cotangent,
        gain_two, w_out,
    )

    ffn_own, ffn_above, ffn_far_a, ffn_far_b, ffn_below = ffn
    ffn_far_a, ffn_far_b = tie((ffn_far_a, ffn_far_b), g_far)
    ffn_up, ffn_down = shift_narrow(ffn_far_a, 1), shift_narrow(ffn_far_b, -1)
    ffn_to = pass_on(ffn_above, ffn_below, ffn_up, ffn_down)
    grad_context, ffn_to, gate_moved = tie((grad_context, ffn_to, gate_moved))
    ffn_from_below, ffn_from_above = shift_narrow(ffn_to[0], 1), shift_narrow(ffn_to[1], -1)
    up_steps = Halving(tie(up_pair, gate_moved), orders)
    up_moved = up_steps.exchange()
    query_lin_grad, send, keep = attend_back(
        info, queries, grad_context, context, start, lse, cosine, sine, kv_pieces
    )
    query_lin_grad, send, keep, up_moved, ffn_from_below, ffn_from_above = tie(
        (query_lin_grad, send, keep, up_moved, ffn_from_below, ffn_from_above)
    )
    turned_attn = tie(turned_attn, send)
    turned_attn_other = swap_core(turned_attn)
    ql_below, ql_above = shift_narrow(query_lin_grad, 1), shift_narrow(query_lin_grad, -1)
    send_other, turned_attn_other = tie((swap_core(send), turned_attn_other))
    key_value = add_rounded(keep, send_other)
    ql_far = (shift_narrow(ql_below[:half], 1), shift_narrow(ql_above[half:], -1))
    spread = (2,) * len(chip_bits) + key_value.shape[2:]
    key_part = xor_scatter(key_value[0].reshape(spread), chip_bits, low_chip)
    value_part = xor_scatter(key_value[1].reshape(spread), chip_bits, chip_bits)
    n_narrow = lax.axis_size("narrow")
    pair = jnp.concatenate([key_part, value_part], axis=1)
    gate_steps.settle(gate_moved)
    up_steps.settle(up_moved)
    feed_steps = [down_steps, gate_steps, up_steps]
    pair, ql_far, joint = tie((pair, ql_far, join_sends(feed_steps)))
    joint_moved = [swap_wide(s, order[0]) for s, order in zip(joint, down_steps.orders)]
    partner = lax.ppermute(pair, "narrow", [(i, i ^ 1) for i in range(n_narrow)])
    pair = add_rounded(pair, partner)
    cross = lax.ppermute(pair, "narrow", [(i, n_narrow - 1 - i) for i in range(n_narrow)])
    cross, query_weights.near = tie((cross, query_weights.near))
    query_weights.fetch_far()
    late, bias = late_grads(head_s, query_lin_grad, pair, cross, cosine, sine)
    late_other = swap_core(late)
    n_hidden = w_down.shape[0]
    late_pair = weigh_late(
        mine_wide, slots, turned_attn, turned_attn_other, turned_two, turned_two_other,
        turned_one, turned_one_other, late, late_other,
    )
    late_pair, joint_moved = tie((late_pair, joint_moved))
    late_steps = Halving(late_pair, orders)
    late_moved = late_steps.exchange()
    query_weights.far = tie(query_weights.far, late_pair)
    query_weights.collect()
    query_mine = query_weights.whole(None, 1)
    query_other = swap_core(query_mine)
    late, ffn_from_below, ffn_from_above = tie((late, ffn_from_below, ffn_from_above), late_pair)
    out_rows = lax.dynamic_slice_in_dim(middle, narrow_index * (rows // 4), rows // 4, 0)
    out_rows = (
        out_rows + ffn_own.astype(f32) + ffn_from_below.astype(f32) + ffn_from_above.astype(f32)
    ).astype(bf16)
    o_below, o_above = shift_narrow(out_rows, 1), shift_narrow(out_rows, -1)
    grad_hidden_in, vectors = project_back(
        core_s, hidden_in, late, (ql_above, ql_far, ql_below), w_query, query_mine, query_other,
        key_projection, value_projection, gain_one, grad_middle, gain_two_grad, bias,
    )
    late_moved, vectors = tie((late_moved, vectors))
    late_steps.settle(late_moved)
    late_steps.rest()
    for bit in bits[::-1]:
        vectors = vectors + swap_wide(vectors, bit)
        if bit == 1:
            vectors, o_below, o_above = tie((vectors, o_below, o_above))
        if bit == 2:
            joint_moved = tie(joint_moved, vectors)
    feed_terms = finish_joint(feed_steps, joint_moved)
    down_sum, gate_sum, up_sum = [finish(t, n_hidden) for t in feed_terms]

    vectors = vectors[0]

    def own_part(first, size):
        return lax.dynamic_slice_in_dim(vectors, first + wide_index * (size // n_wide), size // n_wide)

    bias_at = 2 * width
    query_bias = vectors[bias_at : bias_at + n_query].reshape(heads, n_wide, -1)
    query_bias = lax.dynamic_index_in_dim(query_bias, wide_index, 1, keepdims=False)

    o_far = (shift_narrow(o_below[:q_rows], 1), shift_narrow(o_above[q_rows:], -1))
    output = in_rows(mine_narrow, (out_rows, o_above, o_far, o_below))

    out_sum, query_sum, key_sum, value_sum = finish_late(
        late_steps.terms, [n_query, n_query, kv_width, kv_width]
    )
    return (
        output,
        grad_hidden_in,
        own_part(0, width),
        query_sum,
        query_bias,
        key_sum,
        own_part(bias_at + n_query, kv_width),
        value_sum,
        own_part(bias_at + n_query + kv_width, kv_width),
        out_sum.T,
        own_part(width, width),
        gate_sum,
        up_sum,
        down_sum.T,
    )


def solution(mesh):
    placed = (
        P("wide", None),
        P("wide", None),
        P(),
        P("wide"),
        P(),
        P(None, "narrow"),
        P("narrow"),
        P(),
        P(),
        P(),
        P(),
        P("narrow", None),
        P(),
        P(None, "narrow"),
        P(None, "narrow"),
        P("narrow", None),
    )
    return jax.shard_map(
        on_device,
        mesh=mesh,
        in_specs=placed,
        out_specs=(
            P("wide", None),
            P("wide", None),
            P("wide"),
            P("wide", "narrow"),
            P("narrow", "wide"),
            P("wide", None),
            P("wide"),
            P("wide", None),
            P("wide"),
            P("narrow", "wide"),
            P("wide"),
            P("wide", "narrow"),
            P("wide", "narrow"),
            P("narrow", "wide"),
        ),
        check_vma=False,
    )
```

```python
import functools
import math

import jax
import jax.numpy as jnp
from jax import lax
from jax.experimental import pallas as pl
from jax.experimental.pallas import tpu as pltpu
from jax.sharding import PartitionSpec as P

QUERY_HEADS = 12
KEY_VALUE_HEADS = 2
HEAD_SIZE = 128
FLAG_ROWS = 16

eps = 1e-06
big_negative = -1e30
score_scale = 1.0 / math.sqrt(HEAD_SIZE)
log2_scale = score_scale * math.log2(math.e)

bf16 = jnp.bfloat16
f32 = jnp.float32
ANY = pl.BlockSpec(memory_space=pl.ANY)
VMEM = pl.BlockSpec(memory_space=pltpu.VMEM)
SMEM = pl.BlockSpec(memory_space=pltpu.SMEM)


def dot(a, b, dims=((1,), (0,))):
    return lax.dot_general(a, b, (dims, ((), ())), preferred_element_type=f32)


NT = ((1,), (1,))
TN = ((0,), (0,))


def swap_wide(array, bit):
    n = lax.axis_size("wide")
    return lax.ppermute(array, "wide", [(i, i ^ bit) for i in range(n)])


def shift_narrow(array, by):
    n = lax.axis_size("narrow")
    return lax.ppermute(array, "narrow", [(i, (i + by) % n) for i in range(n)])


def ring_gather(block):
    half = block.shape[0] // 2
    below = shift_narrow(block, 1)
    above = shift_narrow(block, -1)
    far_a = shift_narrow(below[:half], 1)
    far_b = shift_narrow(above[half:], -1)
    return [block, above, jnp.concatenate([far_a, far_b], axis=0), below]


def ring_scatter(parts):
    half = parts[0].shape[0] // 2
    add = lambda a, b: (a.astype(f32) + b.astype(f32)).astype(bf16)
    up = shift_narrow(parts[2][:half], 1)
    down = shift_narrow(parts[2][half:], -1)
    to_above = jnp.concatenate([add(parts[1][:half], up), parts[1][half:]], axis=0)
    to_below = jnp.concatenate([parts[3][:half], add(parts[3][half:], down)], axis=0)
    from_below = shift_narrow(to_above, 1)
    from_above = shift_narrow(to_below, -1)
    return parts[0].astype(f32) + from_below.astype(f32) + from_above.astype(f32)


def add_rounded(a, b):
    return (a.astype(f32) + b.astype(f32)).astype(bf16)


def tie(values, *gates):
    return lax.optimization_barrier((values, gates))[0]


class Halving:
    def __init__(self, pair, orders):
        self.sends, keeps = pair
        self.terms = [[k] for k in keeps]
        self.views = [[k] for k in keeps]
        self.orders = [list(o) for o in orders]

    def exchange(self):
        return [swap_wide(s, order.pop(0)) for s, order in zip(self.sends, self.orders)]

    def settle(self, received):
        for part in range(2):
            self.terms[part].append(received[part])
            self.views[part].append(received[part])
        if not self.orders[0]:
            return None
        n = self.views[0][0].shape[1]
        total = lambda terms: sum(t.astype(f32) for t in terms).astype(bf16)
        self.sends = [
            total([t[:, 1::2] for t in self.views[0]]),
            total([t[:, n // 2 :] for t in self.views[1]]),
        ]
        self.views = [
            [t[:, ::2] for t in self.views[0]],
            [t[:, : n // 2] for t in self.views[1]],
        ]
        return self.sends

    def rest(self):
        while self.orders[0]:
            self.settle(self.exchange())


def as_row(vector):
    return vector[...].astype(f32).reshape(1, -1)


def rope(value, cosine, signed_sine):
    return value * cosine + pltpu.roll(value, HEAD_SIZE // 2, 1) * signed_sine


def front_kernel(head, x, gain, wk, wv, bk, bv, cosine, sine, flags, acts_out, kv_out):
    rows = x.shape[0]
    of_head = lambda b: jnp.where(
        head[0] == 0, as_row(b)[:, :HEAD_SIZE], as_row(b)[:, HEAD_SIZE:]
    )
    xf = x[...].astype(f32)
    scale = lax.rsqrt(jnp.mean(xf * xf, axis=1, keepdims=True) + eps)
    acts = (xf * scale * as_row(gain)).astype(bf16)
    acts_out[...] = acts
    key = dot(acts, wk[...]) + of_head(bk)
    kv_out[:rows, :] = rope(key, cosine[...], sine[...]).astype(bf16)
    kv_out[rows : rows + FLAG_ROWS, :] = flags[...]
    kv_out[rows + FLAG_ROWS :, :] = (dot(acts, wv[...]) + of_head(bv)).astype(bf16)


def front(head, x, gain, wk, wv, bk, bv, cosine, sine, flags):
    rows, width = x.shape
    whole = lambda *shape: pl.BlockSpec(shape, lambda i, h: (0,) * len(shape))
    column = lambda r: pl.BlockSpec((r, HEAD_SIZE), lambda i, h: (0, h[0]))
    return pl.pallas_call(
        front_kernel,
        name="front",
        grid_spec=pltpu.PrefetchScalarGridSpec(
            num_scalar_prefetch=1,
            grid=(1,),
            in_specs=[
                whole(rows, width),
                whole(width),
                column(width),
                column(width),
                whole(*bk.shape),
                whole(*bv.shape),
                whole(rows, HEAD_SIZE),
                whole(rows, HEAD_SIZE),
                whole(FLAG_ROWS, HEAD_SIZE),
            ],
            out_specs=[
                whole(rows, width),
                whole(2 * rows + FLAG_ROWS, HEAD_SIZE),
            ],
        ),
        out_shape=[
            jax.ShapeDtypeStruct((rows, width), bf16),
            jax.ShapeDtypeStruct((2 * rows + FLAG_ROWS, HEAD_SIZE), bf16),
        ],
    )(head, x, gain, wk, wv, bk, bv, cosine, sine, flags)


def query_kernel(acts, cot, w, b, cosine, sine, out, turned):
    lin = dot(acts[...], w[...]) + as_row(b)
    for h in range(out.shape[1] // HEAD_SIZE):
        cols = slice(h * HEAD_SIZE, (h + 1) * HEAD_SIZE)
        out[:, cols] = rope(lin[:, cols], cosine[...], sine[...]).astype(bf16)
    turned[0] = jnp.transpose(cot[...])
    turned[1] = jnp.transpose(acts[...])


def project_queries(acts, cot, w, b, cosine, sine):
    rows, width = acts.shape
    return pl.pallas_call(
        query_kernel,
        name="queries",
        in_specs=[VMEM] * 6,
        out_specs=[VMEM, VMEM],
        out_shape=[
            jax.ShapeDtypeStruct((rows, w.shape[1]), bf16),
            jax.ShapeDtypeStruct((2, width, rows), bf16),
        ],
    )(acts, cot, w, b, cosine, sine)


def load_pieces(refs, slots, kbuf, vbuf, sem):
    copies = []
    keys, values = kbuf.shape[1], vbuf.shape[1]
    for ref, names in zip(refs, slots):
        for at, slot in enumerate(names):
            k_part = ref.at[at, pl.ds(0, keys)]
            v_part = ref.at[at, pl.ds(keys, values)]
            copies.append(pltpu.make_async_copy(k_part, kbuf.at[slot], sem.at[0, slot]))
            copies.append(pltpu.make_async_copy(v_part, vbuf.at[slot], sem.at[1, slot]))
    for copy in copies:
        copy.start()
    return copies


def key_codes(kbuf, slot, half, base, chunk):
    rows = kbuf.shape[1] - FLAG_ROWS
    per = chunk // HEAD_SIZE
    flags = jnp.transpose(kbuf[slot, rows:, :].astype(f32))
    columns = []
    for c in range(per):
        first = flags[:, c : c + 1]
        second = flags[:, per + c : per + c + 1]
        columns.append(jnp.where(half == 1, second, first))
    column = jnp.concatenate(columns, axis=0)
    index = base + lax.broadcasted_iota(jnp.int32, (chunk, 1), 0)
    return jnp.where(column > 0, index, -1)


def visible(codes, start, diagonal):
    seen = codes >= start
    if diagonal:
        shape = (codes.shape[0], start.shape[1])
        row = lax.broadcasted_iota(jnp.int32, shape, 0)
        col = lax.broadcasted_iota(jnp.int32, shape, 1)
        seen = (seen & (row < col)) | (row == col)
    return seen


def first_chunk(info, rows, chunk):
    base = info[0] * rows
    end = first = jnp.int32(0)
    for s in range(1, info.shape[0]):
        end = end + info[s]
        first = jnp.where(end <= base, end, first)
    return first // chunk


def forward_kernel(slots, info, q, start, *refs):
    kv_refs, refs = refs[: len(slots)], refs[len(slots) :]
    out, lse, kbuf, vbuf, sem, acc_s, m_s, l_s = refs
    rows = q.shape[0]
    heads = q.shape[1] // HEAD_SIZE
    chunk = rows // 2
    own = info[0]
    copies = load_pieces(kv_refs, slots, kbuf, vbuf, sem)
    for copy in copies:
        copy.wait()

    def tile(h, k, v, codes, lo, n, diagonal):
        qh = q[lo : lo + n, h * HEAD_SIZE : (h + 1) * HEAD_SIZE]
        s = dot(k, qh, NT) * log2_scale
        s = jnp.where(visible(codes, start[:, lo : lo + n], diagonal), s, big_negative)
        peak = jnp.max(s, axis=0, keepdims=True)
        cols = slice(lo, lo + n)
        if diagonal:
            p = jnp.exp2(s - peak)
            m_s[h : h + 1, cols] = peak
            l_s[h : h + 1, cols] = jnp.sum(p, axis=0, keepdims=True)
            acc_s[h, :, cols] = dot(v, p.astype(bf16), TN)
        else:
            old = m_s[h : h + 1, cols]
            new = jnp.maximum(old, peak)
            alpha = jnp.exp2(old - new)
            p = jnp.exp2(s - new)
            m_s[h : h + 1, cols] = new
            l_s[h : h + 1, cols] = alpha * l_s[h : h + 1, cols] + jnp.sum(p, axis=0, keepdims=True)
            acc_s[h, :, cols] = alpha * acc_s[h, :, cols] + dot(v, p.astype(bf16), TN)

    base = own * rows
    for half in (1, 0):
        k = kbuf[0, half * chunk : (half + 1) * chunk, :]
        v = vbuf[0, half * chunk : (half + 1) * chunk, :]
        codes = key_codes(kbuf, 0, half, base + half * chunk, chunk)
        for h in range(heads):
            tile(h, k, v, codes, half * chunk, chunk, True)
            if half == 0:
                tile(h, k, v, codes, chunk, chunk, False)

    def step(c, carry):
        block, half = c // 2, c % 2
        slot = lax.bitwise_xor(block, own)
        at = pl.multiple_of(half * chunk, chunk)
        k = kbuf[slot, pl.ds(at, chunk), :]
        v = vbuf[slot, pl.ds(at, chunk), :]
        codes = key_codes(kbuf, slot, half, c * chunk, chunk)
        for h in range(heads):
            tile(h, k, v, codes, 0, rows, False)
        return carry

    lax.fori_loop(first_chunk(info, rows, chunk), own * 2, step, 0)
    lse[...] = jnp.zeros_like(lse)
    for h in range(heads):
        total = l_s[h : h + 1, :]
        lse[h : h + 1, :] = m_s[h : h + 1, :] + jnp.log2(total)
        o = acc_s[h] * (1.0 / total)
        out[:, h * HEAD_SIZE : (h + 1) * HEAD_SIZE] = jnp.transpose(o).astype(bf16)


def attend(info, q, start, kv_pieces):
    rows, width = q.shape
    heads = width // HEAD_SIZE
    slots = sum(len(s) for s, _ in kv_pieces)
    return pl.pallas_call(
        functools.partial(forward_kernel, [s for s, _ in kv_pieces]),
        name="attend",
        in_specs=[SMEM, VMEM, VMEM] + [ANY] * len(kv_pieces),
        out_specs=[VMEM, VMEM],
        out_shape=[
            jax.ShapeDtypeStruct((rows, width), bf16),
            jax.ShapeDtypeStruct((8, rows), f32),
        ],
        scratch_shapes=[
            pltpu.VMEM((slots, rows + FLAG_ROWS, HEAD_SIZE), bf16),
            pltpu.VMEM((slots, rows, HEAD_SIZE), bf16),
            pltpu.SemaphoreType.DMA((2, slots)),
            pltpu.VMEM((heads, HEAD_SIZE, rows), f32),
            pltpu.VMEM((8, rows), f32),
            pltpu.VMEM((8, rows), f32),
        ],
    )(info, q, start, *[a for _, a in kv_pieces])


def backward_kernel(slots, info, q, do, ctx, start, lse, cosine, sine, *refs):
    kv_refs, refs = refs[: len(slots)], refs[len(slots) :]
    dq_out, send, keep, kbuf, vbuf, sem, dq_s, delta_s = refs
    rows = q.shape[0]
    heads = q.shape[1] // HEAD_SIZE
    chunk = rows // 2
    own = info[0]
    copies = load_pieces(kv_refs, slots, kbuf, vbuf, sem)
    send[...] = jnp.zeros_like(send)
    keep[...] = jnp.zeros_like(keep)
    for h in range(heads):
        cols = slice(h * HEAD_SIZE, (h + 1) * HEAD_SIZE)
        both = do[:, cols].astype(f32) * ctx[:, cols].astype(f32)
        delta_s[h : h + 1, :] = jnp.sum(jnp.transpose(both), axis=0, keepdims=True)
        dq_s[h] = jnp.zeros((HEAD_SIZE, rows), f32)
    for copy in copies:
        copy.wait()

    def tile(h, k, v, codes, lo, n, diagonal):
        cols = slice(lo, lo + n)
        qh = q[cols, h * HEAD_SIZE : (h + 1) * HEAD_SIZE]
        doh = do[cols, h * HEAD_SIZE : (h + 1) * HEAD_SIZE]
        s = dot(k, qh, NT) * log2_scale - lse[h : h + 1, cols]
        s = jnp.where(visible(codes, start[:, cols], diagonal), s, big_negative)
        p = jnp.exp2(s)
        dv = dot(p.astype(bf16), doh)
        ds = (p * (dot(v, doh, NT) - delta_s[h : h + 1, cols])).astype(bf16)
        dk = dot(ds, qh)
        dq_s[h, :, cols] = dq_s[h, :, cols] + dot(k, ds, TN)
        return dk, dv

    def both(h, k, v, codes, spans):
        dk = dv = None
        for lo, n, diagonal in spans:
            a, b = tile(h, k, v, codes, lo, n, diagonal)
            dk, dv = (a, b) if dk is None else (dk + a, dv + b)
        return dk, dv

    def all_heads(k, v, codes, spans):
        dk = dv = None
        for h in range(heads):
            a, b = both(h, k, v, codes, spans)
            dk, dv = (a, b) if dk is None else (dk + a, dv + b)
        return (dk * score_scale).astype(bf16), dv.astype(bf16)

    base = own * rows
    for half in (1, 0):
        span = slice(half * chunk, (half + 1) * chunk)
        codes = key_codes(kbuf, 0, half, base + half * chunk, chunk)
        spans = [(chunk, chunk, True)] if half else [(0, chunk, True), (chunk, chunk, False)]
        dk, dv = all_heads(kbuf[0, span, :], vbuf[0, span, :], codes, spans)
        keep[0, 0, span, :] = dk
        keep[1, 0, span, :] = dv

    def step(c, carry):
        block, half = c // 2, c % 2
        slot = lax.bitwise_xor(block, own)
        at = pl.multiple_of(half * chunk, chunk)
        k = kbuf[slot, pl.ds(at, chunk), :]
        v = vbuf[slot, pl.ds(at, chunk), :]
        codes = key_codes(kbuf, slot, half, c * chunk, chunk)
        dk, dv = all_heads(k, v, codes, [(0, rows, False)])

        @pl.when(slot % 2 == 0)
        def _():
            keep[0, slot // 2, pl.ds(at, chunk), :] = dk
            keep[1, slot // 2, pl.ds(at, chunk), :] = dv

        @pl.when(slot % 2 == 1)
        def _():
            send[0, slot // 2, pl.ds(at, chunk), :] = dk
            send[1, slot // 2, pl.ds(at, chunk), :] = dv

        return carry

    lax.fori_loop(first_chunk(info, rows, chunk), own * 2, step, 0)
    for h in range(heads):
        g = jnp.transpose(dq_s[h]) * score_scale
        back = g * cosine[...] - pltpu.roll(g, HEAD_SIZE // 2, 1) * sine[...]
        dq_out[:, h * HEAD_SIZE : (h + 1) * HEAD_SIZE] = back.astype(bf16)


def attend_back(info, q, do, ctx, start, lse, cosine, sine, kv_pieces):
    rows, width = q.shape
    heads = width // HEAD_SIZE
    slots = sum(len(s) for s, _ in kv_pieces)
    half = jax.ShapeDtypeStruct((2, slots // 2, rows, HEAD_SIZE), bf16)
    return pl.pallas_call(
        functools.partial(backward_kernel, [s for s, _ in kv_pieces]),
        name="attend_back",
        in_specs=[SMEM] + [VMEM] * 7 + [ANY] * len(kv_pieces),
        out_specs=[VMEM] * 3,
        out_shape=[jax.ShapeDtypeStruct((rows, width), bf16), half, half],
        scratch_shapes=[
            pltpu.VMEM((slots, rows + FLAG_ROWS, HEAD_SIZE), bf16),
            pltpu.VMEM((slots, rows, HEAD_SIZE), bf16),
            pltpu.SemaphoreType.DMA((2, slots)),
            pltpu.VMEM((heads, HEAD_SIZE, rows), f32),
            pltpu.VMEM((8, rows), f32),
        ],
    )(
        info, q, do, ctx, start, lse, cosine, sine,
        *[a for _, a in kv_pieces],
    )


def whole(shape):
    return pl.BlockSpec(shape, lambda *_: (0,) * len(shape))


def struct(shape, dtype):
    return jax.ShapeDtypeStruct(shape, dtype)


def project_out_kernel(
    core, x, own, above, fa, fb, below, w_own, mine, other, gain, middle, acts, turned, scale
):
    n = w_own.shape[0]
    width = x.shape[1]
    far = jnp.where(pl.program_id(0) == 0, fa[...].astype(f32), fb[...].astype(f32)).astype(bf16)
    part = lambda m: (
        dot(above[...], m[:n, :]) + dot(below[...], m[n : 2 * n, :]) + dot(far, m[2 * n :, :])
    )
    a, b = part(mine), part(other)
    first = core[0] == 0
    out = dot(own[...], w_own[...]) + jnp.concatenate(
        [jnp.where(first, a, b), jnp.where(first, b, a)], axis=1
    )
    mid = x[...].astype(f32) + out
    r = lax.rsqrt(jnp.mean(mid * mid, axis=1, keepdims=True) + eps)
    middle[...] = mid
    scale[...] = r
    normed = mid * r * as_row(gain)
    acts[...] = normed.astype(bf16)
    turned[:width, :] = jnp.transpose(normed.astype(bf16))
    turned[width:, :] = jnp.transpose(own[...])


def project_out(core, x, pieces, w_own, mine, other, gain):
    rows, width = x.shape
    n = w_own.shape[0]
    half = rows // 2
    own, above, (fa, fb), below = pieces
    block = lambda c: pl.BlockSpec((half, c), lambda i, s: (i, 0))
    return pl.pallas_call(
        project_out_kernel,
        name="project_out",
        grid_spec=pltpu.PrefetchScalarGridSpec(
            num_scalar_prefetch=1,
            grid=(2,),
            in_specs=[
                block(width), block(n), block(n), whole((half, n)), whole((half, n)), block(n),
                whole(w_own.shape), whole(mine.shape), whole(other.shape), whole(gain.shape),
            ],
            out_specs=[
                block(width), block(width),
                pl.BlockSpec((width + n, half), lambda i, s: (0, i)),
                block(1),
            ],
        ),
        out_shape=[
            struct((rows, width), f32), struct((rows, width), bf16),
            struct((width + n, rows), bf16), struct((rows, 1), f32),
        ],
    )(core, x, own, above, fa, fb, below, w_own, mine, other, gain)


def ring_blocks(acc, mine, outs):
    block = acc.shape[0] // 4
    own, above, far_a, far_b, below = outs

    def take(k, first, size):
        at = ((mine[0] + k) % 4) * block + first
        return acc[pl.ds(pl.multiple_of(at, size), size), :].astype(bf16)

    own[...] = take(0, 0, block)
    above[...] = take(1, 0, block)
    far_a[...] = take(2, 0, block // 2)
    far_b[...] = take(2, block // 2, block // 2)
    below[...] = take(3, 0, block)


def block_sizes(rows):
    return [rows // 4, rows // 4, rows // 8, rows // 8, rows // 4]


def feed_kernel(n, mine, acts, cot, wg, wu, wd, hidden, grads, *refs):
    outs, acc = refs[:-1], refs[-1]
    j = pl.program_id(0)
    tile = wg.shape[0]
    part = min(256, tile)
    for lo in range(0, tile, part):
        cols = slice(lo, lo + part)
        gate = dot(acts[...], wg[cols, :], NT)
        up = dot(acts[...], wu[cols, :], NT)
        g = dot(cot[...], wd[cols, :], NT)
        sig = 1.0 / (1.0 + jnp.exp(-gate))
        silu = gate * sig
        column = j * tile + lo + lax.broadcasted_iota(jnp.int32, (1, part), 1)
        keep = lambda v: jnp.where(column < n, v, 0.0).astype(bf16)
        hidden[:, cols] = keep(silu * up)
        grads[0, :, cols] = keep(g * up * (sig * (1.0 + gate * (1.0 - sig))))
        grads[1, :, cols] = keep(g * silu)
    steps = pl.cdiv(n, tile)
    back = lambda k: dot(grads[0, :, :k], wg[:k, :]) + dot(grads[1, :, :k], wu[:k, :])

    @pl.when(j == 0)
    def _():
        acc[...] = jnp.zeros_like(acc)

    @pl.when(j < steps - 1)
    def _():
        acc[...] = acc[...] + back(tile)

    @pl.when(j == steps - 1)
    def _():
        acc[...] = acc[...] + back(n - (steps - 1) * tile)

    @pl.when(j == steps - 1)
    def _():
        ring_blocks(acc, mine, outs)


def feed(mine, acts, cot, wg, wu, wd, tile=768):
    rows, width = acts.shape
    n = wg.shape[0]
    steps = pl.cdiv(n, tile)
    w_spec = pl.BlockSpec((tile, width), lambda j, s: (j, 0))
    sizes = block_sizes(rows)
    outs = pl.pallas_call(
        functools.partial(feed_kernel, n),
        name="feed",
        grid_spec=pltpu.PrefetchScalarGridSpec(
            num_scalar_prefetch=1,
            grid=(steps,),
            in_specs=[whole((rows, width)), whole((rows, width)), w_spec, w_spec, w_spec],
            out_specs=[
                pl.BlockSpec((rows, tile), lambda j, s: (0, j)),
                pl.BlockSpec((2, rows, tile), lambda j, s: (0, 0, j)),
            ]
            + [whole((r, width)) for r in sizes],
            scratch_shapes=[pltpu.VMEM((rows, width), f32)],
        ),
        out_shape=[struct((rows, steps * tile), bf16), struct((2, rows, steps * tile), bf16)]
        + [struct((r, width), bf16) for r in sizes],
    )(mine, acts, cot, wg, wu, wd)
    return outs[0], outs[1], outs[2:]


def stack_kernel(cut, *refs):
    count = 1 if cut is None else 2
    ins, outs = refs[:-count], refs[-count:]
    cut = outs[0].shape[0]
    done = 0
    for ref in ins:
        rows = ref.shape[0]
        head = min(max(cut - done, 0), rows)
        if head:
            outs[0][done : done + head, :] = ref[:head, :]
        if head < rows:
            at = done + head - cut
            outs[1][at : at + rows - head, :] = ref[head:, :]
        done += rows


def stack(arrays, cut):
    rows = sum(a.shape[0] for a in arrays)
    width = arrays[0].shape[1]
    sizes = [cut, rows - cut] if cut < rows else [rows]
    return pl.pallas_call(
        functools.partial(stack_kernel, cut if cut < rows else None),
        name="stack",
        in_specs=[VMEM] * len(arrays),
        out_specs=[VMEM] * len(sizes),
        out_shape=[struct((size, width), bf16) for size in sizes],
    )(*arrays)


def assemble_kernel(plan, chip, *refs):
    out = refs[-1]
    n = out.shape[0] // 3
    block = n // plan[0]
    for ref, (names, first) in zip(refs, plan[1]):
        rows = ref.shape[1]
        for at, name in enumerate(names):
            source = lax.bitwise_xor(chip[0], name)
            done = 0
            while done < rows:
                piece, inside = divmod(first + done, block)
                size = min(rows - done, block - inside)
                to = pl.multiple_of(piece * n + source * block + inside, 16)
                out[pl.ds(to, size), :] = ref[at, done : done + size, :]
                done += size


def assemble(chip, chips, parts):
    one = sum({first: a.shape[1] for _, first, a in parts}.values())
    plan = (chips, [(names, first) for names, first, _ in parts])
    return pl.pallas_call(
        functools.partial(assemble_kernel, plan),
        name="assemble",
        in_specs=[SMEM] + [VMEM] * len(parts),
        out_specs=VMEM,
        out_shape=struct((chips * one, parts[0][2].shape[2]), bf16),
    )(chip, *[a for _, _, a in parts])


def partial_kernel(mine, a, w, *refs):
    refs[-1][...] = dot(a[:, : w.shape[0]], w[...])
    ring_blocks(refs[-1], mine, refs[:-1])


def partial_rows(mine, a, w, tile=512):
    rows, columns = a.shape
    inner, width = w.shape
    sizes = block_sizes(rows)
    return pl.pallas_call(
        partial_kernel,
        name="partial_down",
        grid_spec=pltpu.PrefetchScalarGridSpec(
            num_scalar_prefetch=1,
            grid=(width // tile,),
            in_specs=[whole(a.shape), pl.BlockSpec((inner, tile), lambda j, s: (0, j))],
            out_specs=[pl.BlockSpec((r, tile), lambda j, s: (0, j)) for r in sizes],
            scratch_shapes=[pltpu.VMEM((rows, tile), f32)],
        ),
        out_shape=[struct((r, width), bf16) for r in sizes],
    )(mine, a, w)


def pass_on_kernel(above, below, up, down, to_above, to_below):
    half = up.shape[0]
    to_above[:half, :] = (above[:half, :].astype(f32) + up[...].astype(f32)).astype(bf16)
    to_above[half:, :] = above[half:, :]
    to_below[:half, :] = below[:half, :]
    to_below[half:, :] = (below[half:, :].astype(f32) + down[...].astype(f32)).astype(bf16)


def pass_on(above, below, up, down):
    return pl.pallas_call(
        pass_on_kernel,
        name="pass_on",
        in_specs=[VMEM] * 4,
        out_specs=[VMEM] * 2,
        out_shape=[struct(above.shape, bf16)] * 2,
    )(above, below, up, down)


def weigh_kernel(slots, half, mine, a_own, a_other, b_own, b_other, *refs):
    send_a, keep_a, send_b, keep_b, lhs = refs
    rows = a_own.shape[1]
    block = 2 * half

    @pl.when(pl.program_id(0) == 0)
    def _():
        for s in range(slots):
            at = pl.multiple_of(lax.bitwise_xor(mine[0], 2 * s) * block, 16)
            lhs[s * block : (s + 1) * block, :rows] = a_own[pl.ds(at, block), :]
            lhs[s * block : (s + 1) * block, rows:] = a_other[pl.ds(at, block), :]

    g = dot(lhs[:, :rows], b_own[0]) + dot(lhs[:, rows:], b_other[0])
    place_slots(g, slots, half, 0, send_a, keep_a, send_b, keep_b)


def place_slots(g, slots, half, group, send_a, keep_a, send_b, keep_b):
    cols = slice(0, g.shape[1])
    for s in range(slots):
        first = g[2 * s * half : (2 * s + 1) * half].astype(bf16)
        second = g[(2 * s + 1) * half : (2 * s + 2) * half].astype(bf16)
        (send_a if s % 2 else keep_a)[group, s // 2, :, cols] = first
        (send_b if s >= slots // 2 else keep_b)[group, s % (slots // 2), :, cols] = second


def weigh(mine, slots, width, a_own, a_other, b_own, b_other, group=0, tile=768):
    rows = a_own.shape[-1]
    n = b_own.shape[2]
    if a_own.ndim == 3:
        a_spec = pl.BlockSpec((None, width, rows), lambda j, s: (0, 0, 0))
    else:
        a_spec = pl.BlockSpec((width, rows), lambda j, s: (0, 0))
    half = width // slots // 4
    b_spec = pl.BlockSpec((1, rows, tile), lambda j, s: (group, 0, j))
    out = pl.BlockSpec((1, slots // 2, half, tile), lambda j, s: (0, 0, 0, j))
    outs = pl.pallas_call(
        functools.partial(weigh_kernel, slots, half),
        name="weigh",
        grid_spec=pltpu.PrefetchScalarGridSpec(
            num_scalar_prefetch=1,
            grid=(pl.cdiv(n, tile),),
            in_specs=[a_spec, a_spec, b_spec, b_spec],
            out_specs=[out] * 4,
            scratch_shapes=[pltpu.VMEM((width // 2, 2 * rows), bf16)],
        ),
        out_shape=[struct((1, slots // 2, half, n), bf16)] * 4,
    )(mine, a_own, a_other, b_own, b_other)
    return [outs[0], outs[2]], [outs[1], outs[3]]


def weigh_late_kernel(
    slots, half, mine, t_own, t_other, c_own, c_other, a_own, a_other, b_own, b_other, *refs
):
    send_a, keep_a, send_b, keep_b = refs
    block = 2 * half

    def gather(ref):
        pieces = []
        for s in range(slots):
            at = pl.multiple_of(lax.bitwise_xor(mine[0], 2 * s) * block, 16)
            pieces.append(ref[pl.ds(at, block), :])
        return jnp.concatenate(pieces, axis=0)

    n = c_own.shape[0]
    g = dot(gather(t_own), c_own[...], NT) + dot(gather(t_other), c_other[...], NT)
    late = dot(gather(a_own), b_own[...]) + dot(gather(a_other), b_other[...])
    g = jnp.concatenate([g, late], axis=1)
    place_slots(g, slots, half, 0, send_a, keep_a, send_b, keep_b)


def weigh_late(mine, slots, t_own, t_other, c_own, c_other, a_own, a_other, b_own, b_other):
    width, rows = t_own.shape
    n = c_own.shape[0] - width
    half = width // slots // 4
    total = n + b_own.shape[1]
    t_spec = whole((width, rows))
    c_spec = pl.BlockSpec((n, rows), lambda i, s: (width // n, 0))
    a_spec = pl.BlockSpec((None, width, rows), lambda i, s: (1, 0, 0))
    b_spec = whole(b_own.shape)
    shape = (1, slots // 2, half, total)
    outs = pl.pallas_call(
        functools.partial(weigh_late_kernel, slots, half),
        name="weigh_late",
        grid_spec=pltpu.PrefetchScalarGridSpec(
            num_scalar_prefetch=1,
            grid=(1,),
            in_specs=[t_spec, t_spec, c_spec, c_spec, a_spec, a_spec, b_spec, b_spec],
            out_specs=[whole(shape)] * 4,
        ),
        out_shape=[struct(shape, bf16)] * 4,
    )(mine, t_own, t_other, c_own, c_other, a_own, a_other, b_own, b_other)
    return [outs[0], outs[2]], [outs[1], outs[3]]


def total_of(refs, cols):
    total = None
    for t in refs:
        value = t[0, 0, :, cols].astype(f32)
        total = value if total is None else total + value
    return total


def finish_kernel(n, *refs):
    outs = refs[2 * n * (len(refs) // (2 * n + 1)) :]
    for g, out in enumerate(outs):
        half = out.shape[0] // 2
        for part in range(2):
            first = (2 * g + part) * n
            total = total_of(refs[first : first + n], slice(0, out.shape[1]))
            out[part * half : (part + 1) * half, :] = total


def finish(all_terms, columns):
    flat = [t for terms in all_terms for part in terms for t in part]
    _, _, half, width = flat[0][0].shape
    at = lambda g: pl.BlockSpec((1, 1, half, width), lambda i: (g, 0, 0, 0))
    groups = len(all_terms)
    return pl.pallas_call(
        functools.partial(finish_kernel, len(all_terms[0][0])),
        name="finish",
        grid=(1,),
        in_specs=[at(g) for _, g in flat],
        out_specs=[whole((2 * half, columns))] * groups,
        out_shape=[struct((2 * half, columns), f32)] * groups,
    )(*[a for a, _ in flat])


def finish_late_kernel(n, count, *refs):
    terms, outs = refs[:-count], refs[-count:]
    half = outs[0].shape[0] // 2
    for part in range(2):
        at = 0
        for out in outs:
            cols = slice(at, at + out.shape[1])
            total = total_of(terms[part * n : (part + 1) * n], cols)
            out[part * half : (part + 1) * half, :] = total
            at += out.shape[1]


def finish_late(terms, sizes):
    flat = terms[0] + terms[1]
    _, _, half, columns = flat[0].shape
    return pl.pallas_call(
        functools.partial(finish_late_kernel, len(terms[0]), len(sizes)),
        name="finish_late",
        grid=(1,),
        in_specs=[whole((1, 1, half, columns))] * len(flat),
        out_specs=[whole((2 * half, size)) for size in sizes],
        out_shape=[struct((2 * half, size), f32) for size in sizes],
    )(*flat)


def middle_back_kernel(
    mine, own, above, fa, fb, below, middle, scale, cot, gain, w_out,
    grad_middle, turned, grad_context, gain_grad, g_s,
):
    k = pl.program_id(0)
    half = fa.shape[0]
    for at, ref in ((0, own), (1, above), (3, below)):
        @pl.when(k == at)
        def _():
            g_s[...] = ref[...].astype(f32)

    @pl.when(k == 2)
    def _():
        g_s[:half, :] = fa[...].astype(f32)
        g_s[half:, :] = fb[...].astype(f32)

    g = g_s[...]
    r = scale[...]
    n2 = middle[...] * r
    u2 = g * as_row(gain)
    gm = cot[...].astype(f32) + r * (u2 - n2 * jnp.mean(u2 * n2, axis=1, keepdims=True))
    part = jnp.sum(g * n2, axis=0, keepdims=True)

    @pl.when(k == 0)
    def _():
        gain_grad[...] = part

    @pl.when(k > 0)
    def _():
        gain_grad[...] = gain_grad[...] + part

    grad_middle[...] = gm
    turned[...] = jnp.transpose(gm.astype(bf16))
    grad_context[...] = dot(gm.astype(bf16), w_out[...], NT).astype(bf16)


def middle_back(mine, pieces, middle, scale, cot, gain, w_out):
    rows, width = middle.shape
    block = rows // 4
    own, above, (fa, fb), below = pieces
    at = lambda c: pl.BlockSpec((block, c), lambda k, s: ((s[0] + k) % 4, 0))
    n = w_out.shape[0]
    return pl.pallas_call(
        middle_back_kernel,
        name="middle_back",
        grid_spec=pltpu.PrefetchScalarGridSpec(
            num_scalar_prefetch=1,
            grid=(4,),
            in_specs=[
                whole((block, width)), whole((block, width)),
                whole((block // 2, width)), whole((block // 2, width)), whole((block, width)),
                at(width), at(1), at(width), whole(gain.shape), whole(w_out.shape),
            ],
            out_specs=[
                at(width),
                pl.BlockSpec((width, block), lambda k, s: (0, (s[0] + k) % 4)),
                at(n),
                whole((1, width)),
            ],
            scratch_shapes=[pltpu.VMEM((block, width), f32)],
        ),
        out_shape=[
            struct((rows, width), f32), struct((width, rows), bf16),
            struct((rows, n), bf16), struct((1, width), f32),
        ],
    )(mine, own, above, fa, fb, below, middle, scale, cot, gain, w_out)


def in_rows_kernel(mine, own, above, fa, fb, below, out):
    block = own.shape[0]
    at = lambda k: pl.ds(pl.multiple_of((mine[0] + k) % 4 * block, block), block)
    out[at(0), :] = own[...]
    out[at(1), :] = above[...]
    out[at(2), :] = jnp.concatenate([fa[...], fb[...]], axis=0)
    out[at(3), :] = below[...]


def in_rows(mine, pieces):
    own, above, (fa, fb), below = pieces
    rows, width = own.shape
    return pl.pallas_call(
        in_rows_kernel,
        name="in_rows",
        in_specs=[SMEM] + [VMEM] * 5,
        out_specs=VMEM,
        out_shape=struct((4 * rows, width), bf16),
    )(mine, own, above, fa, fb, below)


def late_kernel(head, q, pair, cross, cosine, sine, late, bias):
    rows, n = q.shape
    kv = KEY_VALUE_HEADS * HEAD_SIZE

    def lin(ref):
        g = ref[:, :HEAD_SIZE].astype(f32)
        key = g * cosine[...] - pltpu.roll(g, HEAD_SIZE // 2, 1) * sine[...]
        return key, ref[:, HEAD_SIZE:].astype(f32)

    (own_k, own_v), (other_k, other_v) = lin(pair), lin(cross)
    first = head[0] == 0
    late[:, :n] = q[...]
    columns = [
        jnp.where(first, own_k, other_k), jnp.where(first, other_k, own_k),
        jnp.where(first, own_v, other_v), jnp.where(first, other_v, own_v),
    ]
    for c, value in enumerate(columns):
        late[:, n + c * HEAD_SIZE : n + (c + 1) * HEAD_SIZE] = value.astype(bf16)
    bias[...] = jnp.sum(late[...].astype(f32), axis=0, keepdims=True)


def late_grads(head, q, pair, cross, cosine, sine):
    rows, n = q.shape
    total = n + 2 * KEY_VALUE_HEADS * HEAD_SIZE
    return pl.pallas_call(
        late_kernel,
        name="late_grads",
        in_specs=[SMEM] + [VMEM] * 5,
        out_specs=[VMEM] * 2,
        out_shape=[struct((rows, total), bf16), struct((1, total), f32)],
    )(head, q, pair, cross, cosine, sine)


def project_back_kernel(
    core, x, late, above, fa, fb, below, w_own, mine, other, wk, wv, gain, grad_middle,
    gain_two_grad, bias, out, vectors,
):
    i = pl.program_id(0)
    n = w_own.shape[1]
    kv = wk.shape[1]
    far = jnp.where(i == 0, fa[...].astype(f32), fb[...].astype(f32)).astype(bf16)
    part = lambda m: (
        dot(above[...], m[:n, :]) + dot(below[...], m[n : 2 * n, :]) + dot(far, m[2 * n :, :])
    )
    a, b = part(mine), part(other)
    first = core[0] == 0
    g = jnp.concatenate([jnp.where(first, a, b), jnp.where(first, b, a)], axis=1)
    g = g + dot(late[:, :n], w_own[...], NT)
    g = g + dot(late[:, n : n + kv], wk[...], NT) + dot(late[:, n + kv :], wv[...], NT)
    xf = x[...].astype(f32)
    r = lax.rsqrt(jnp.mean(xf * xf, axis=1, keepdims=True) + eps)
    n1 = xf * r
    u1 = g * as_row(gain)
    out[...] = (
        grad_middle[...] + r * (u1 - n1 * jnp.mean(u1 * n1, axis=1, keepdims=True))
    ).astype(bf16)
    total = jnp.sum(g * n1, axis=0, keepdims=True)
    width = x.shape[1]

    @pl.when(i == 0)
    def _():
        vectors[:, :width] = total
        vectors[:, width : 2 * width] = gain_two_grad[...]
        vectors[:, 2 * width :] = bias[...]

    @pl.when(i > 0)
    def _():
        vectors[:, :width] = vectors[:, :width] + total


def project_back(
    core, x, late, pieces, w_own, mine, other, wk, wv, gain, grad_middle, gain_two_grad, bias
):
    rows, width = x.shape
    n = w_own.shape[1]
    half = rows // 2
    above, (fa, fb), below = pieces
    block = lambda c: pl.BlockSpec((half, c), lambda i, s: (i, 0))
    return pl.pallas_call(
        project_back_kernel,
        name="project_back",
        grid_spec=pltpu.PrefetchScalarGridSpec(
            num_scalar_prefetch=1,
            grid=(2,),
            in_specs=[
                block(width), block(late.shape[1]), block(n), whole((half, n)), whole((half, n)),
                block(n), whole(w_own.shape), whole(mine.shape), whole(other.shape),
                whole(wk.shape), whole(wv.shape), whole(gain.shape), block(width),
                whole(gain_two_grad.shape), whole(bias.shape),
            ],
            out_specs=[block(width), whole((1, 2 * width + bias.shape[1]))],
        ),
        out_shape=[struct((rows, width), bf16), struct((1, 2 * width + bias.shape[1]), f32)],
    )(
        core, x, late, above, fa, fb, below, w_own, mine, other, wk, wv, gain, grad_middle,
        gain_two_grad, bias,
    )


class Spread:
    def __init__(self, share, orders):
        self.share = share
        self.half = share.shape[0] // 2
        self.orders = [list(o) for o in orders]
        self.near = [shift_narrow(share, 1), shift_narrow(share, -1)]

    def fetch_far(self):
        below, above = self.near
        self.far = [shift_narrow(below[: self.half], 1), shift_narrow(above[self.half :], -1)]

    def collect(self):
        below, above = self.near
        pieces = [above, below] + self.far
        if not self.orders:
            (self.rows,) = stack(pieces, 6 * self.half)
            return
        rows = 6 * self.half
        self.cut = rows // len(self.orders)
        self.names = [[(0,)] for _ in self.orders]
        self.arrays = [[part[None]] for part in stack(pieces, self.cut)]

    def hop(self):
        if not self.orders or not self.orders[0]:
            return
        for part, order in enumerate(self.orders):
            bit = order.pop(0)
            held = self.arrays[part]
            payload = held[0] if len(held) == 1 else jnp.concatenate(held, axis=0)
            names = tuple(s ^ (bit >> 1) for group in self.names[part] for s in group)
            self.names[part].append(names)
            held.append(swap_wide(payload, bit))

    def whole(self, chip, chips):
        if not hasattr(self, "arrays"):
            return self.rows
        while self.orders[0]:
            self.hop()
        parts = []
        for part in range(len(self.orders)):
            for names, array in zip(self.names[part], self.arrays[part]):
                parts.append((names, part * self.cut, array))
        return assemble(chip, chips, parts)


def join_kernel(*refs):
    ins, outs = refs[:-2], refs[-2:]
    for part, out in enumerate(outs):
        for g in range(out.shape[0]):
            a, b = ins[4 * g + 2 * part], ins[4 * g + 2 * part + 1]
            out[g, 0] = (a[0, 0].astype(f32) + b[0, 0].astype(f32)).astype(bf16)


def join_sends(steps):
    slots = steps[0].views[0][0].shape[1]
    if slots != 1 or len(steps[0].terms[0]) != 2:
        return [jnp.concatenate([s.sends[part] for s in steps], axis=0) for part in range(2)]
    flat = [t for s in steps for terms in s.terms for t in terms]
    _, _, rows, columns = flat[0].shape
    shape = (len(steps), 1, rows, columns)
    return pl.pallas_call(
        join_kernel,
        name="join",
        grid=(1,),
        in_specs=[pl.BlockSpec((1, 1, rows, columns), lambda i: (0, 1, 0, 0))] * len(flat),
        out_specs=[whole(shape)] * 2,
        out_shape=[struct(shape, bf16)] * 2,
    )(*flat)


def finish_joint(steps, received):
    for s in steps:
        for order in s.orders:
            order.pop(0)
    if not steps[0].orders[0]:
        return [
            [[(t, 0) for t in s.terms[part]] + [(received[part], g)] for part in range(2)]
            for g, s in enumerate(steps)
        ]
    for g, s in enumerate(steps):
        s.settle([r[g : g + 1] for r in received])
        s.rest()
    return [[[(t, 0) for t in terms] for terms in s.terms] for s in steps]


def place_tokens(index, lengths):
    ends = jnp.cumsum(lengths)
    before = (ends[None, :] <= index[:, None]).astype(jnp.int32)
    return index - jnp.sum(before * lengths[None, :], axis=1)


def on_device(
    hidden_in,
    cotangent,
    lengths,
    valid,
    gain_one,
    w_query,
    b_query,
    key_projection,
    key_bias_vector,
    value_projection,
    value_bias_vector,
    w_out,
    gain_two,
    w_gate,
    w_up,
    w_down,
):
    rows, width = hidden_in.shape
    n_wide = lax.axis_size("wide")
    wide_index = lax.axis_index("wide")
    narrow_index = lax.axis_index("narrow")
    heads = w_query.shape[1] // HEAD_SIZE
    n_query = heads * HEAD_SIZE
    kv_width = KEY_VALUE_HEADS * HEAD_SIZE
    head = narrow_index * heads // (QUERY_HEADS // KEY_VALUE_HEADS)
    bits = [1 << b for b in reversed(range(n_wide.bit_length() - 1))]
    chip_bits = bits[:-1]
    low_chip = chip_bits[::-1]
    slots = n_wide // 2
    core = wide_index % 2
    base = wide_index * rows
    as_scalar = lambda v: v.astype(jnp.int32).reshape(1)
    mine_wide, mine_narrow, core_s, head_s = map(
        as_scalar, (wide_index, narrow_index, core, head)
    )
    swap_core = lambda v: swap_wide(v, 1)

    token_index = base + jnp.arange(rows, dtype=jnp.int32)
    positions = place_tokens(token_index, lengths)
    start = (token_index - positions)[None, :]
    info = jnp.concatenate([mine_wide, lengths])
    freqs = 10000.0 ** (-(jnp.arange(HEAD_SIZE // 2, dtype=f32) * 2.0) / HEAD_SIZE)
    angles = positions.astype(f32)[:, None] * freqs[None, :]
    cos_half, sin_half = jnp.cos(angles), jnp.sin(angles)
    cosine = jnp.concatenate([cos_half, cos_half], axis=1)
    sine = jnp.concatenate([-sin_half, sin_half], axis=1)

    flags = jnp.pad(
        valid.astype(bf16).reshape(rows // HEAD_SIZE, HEAD_SIZE),
        ((0, FLAG_ROWS - rows // HEAD_SIZE), (0, 0)),
    )
    acts_one, kv_own = front(
        head_s,
        hidden_in,
        gain_one,
        key_projection,
        value_projection,
        key_bias_vector,
        value_bias_vector,
        cosine,
        sine,
        flags,
    )

    col = width // 2
    n_half = n_query // 2
    split = n_query // slots % 32 == 0
    share = n_query // slots if split else n_query
    at = wide_index // 2 * share if split else 0
    half_query = lax.dynamic_slice_in_dim(w_query, core * col, col, 0).T
    half_out = lax.dynamic_slice(w_out, (at, core * col), (share, col))
    out_weights = Spread(half_out, [low_chip, chip_bits] if split else [])

    kv_slots, kv_arrays = [(0,)], [kv_own[None]]
    for step, bit in enumerate(bits):
        send = kv_arrays[0] if step == 0 else jnp.concatenate(kv_arrays, axis=0)
        if step == 1:
            send, out_weights.near = tie((send, out_weights.near))
            out_weights.fetch_far()
        if step + 1 == len(bits):
            send, queries, half_query, out_weights.far = tie(
                (send, queries, half_query, out_weights.far)
            )
            out_weights.collect()
            out_weights.hop()
        kv_arrays.append(swap_wide(send, bit))
        kv_slots.append(tuple(s ^ bit for group in kv_slots for s in group))
        if step == 0:
            acts_late = tie(acts_one, kv_arrays[1])
            queries, turned_one = project_queries(
                acts_late, cotangent, w_query, b_query, cosine, sine
            )
    kv_pieces = list(zip(kv_slots, kv_arrays))
    context, lse = attend(info, queries, start, kv_pieces)
    if split:
        context, out_weights.arrays = tie((context, out_weights.arrays))

    half = rows // 2
    ctx_below, ctx_above = shift_narrow(context, 1), shift_narrow(context, -1)
    out_mine = out_weights.whole(as_scalar(wide_index // 2), slots)
    out_mine, ctx_below, ctx_above = tie((out_mine, ctx_below, ctx_above))
    out_other = swap_core(out_mine)
    ctx_far = (shift_narrow(ctx_below[:half], 1), shift_narrow(ctx_above[half:], -1))
    turned_one_other = swap_core(turned_one)
    ctx_far, half_query = tie((ctx_far, half_query), turned_one_other, out_other)
    w_gate_t, w_up_t = w_gate.T, w_up.T
    middle, acts_two, turned_two, scale_two = project_out(
        core_s, hidden_in, (context, ctx_above, ctx_far, ctx_below),
        w_out, out_mine, out_other, gain_two,
    )

    query_weights = Spread(half_query, [])
    hidden, grads, blocks = feed(
        mine_narrow, acts_two, cotangent, w_gate_t, w_up_t, w_down
    )
    turned_two_other = swap_core(tie(turned_two, acts_two))
    (hidden, grads, blocks), query_weights.near = tie(
        ((hidden, grads, blocks), query_weights.near), turned_two_other
    )
    own, above, far_a, far_b, below = blocks
    up, down = shift_narrow(far_a, 1), shift_narrow(far_b, -1)
    hidden_other = swap_core(hidden)
    up, down, hidden_other = tie((up, down, hidden_other))
    grads_other = swap_core(tie(grads, up, down))
    to_above, to_below = pass_on(above, below, up, down)
    from_below, from_above = shift_narrow(to_above, 1), shift_narrow(to_below, -1)
    hidden_here = tie(hidden, to_above, to_below)
    down_pair = weigh(
        mine_wide, slots, width, turned_one, turned_one_other, hidden_here[None],
        hidden_other[None],
    )
    ffn = partial_rows(mine_narrow, hidden_here, w_down)
    from_below, from_above, grads, grads_other, down_pair, ffn = tie(
        (from_below, from_above, grads, grads_other, down_pair, ffn)
    )
    orders = (low_chip, chip_bits)
    down_steps = Halving(down_pair, orders)
    down_moved = down_steps.exchange()
    own = (own.astype(f32) + from_below.astype(f32) + from_above.astype(f32)).astype(bf16)
    q_rows = rows // 8
    g_below, g_above = shift_narrow(own, 1), shift_narrow(own, -1)
    grads_here = tie(grads, own)
    gate_pair, up_pair = [
        weigh(mine_wide, slots, width, turned_two, turned_two_other, grads_here, grads_other, k)
        for k in range(2)
    ]
    g_below, g_above, gate_pair, up_pair, down_moved = tie(
        (g_below, g_above, gate_pair, up_pair, down_moved)
    )
    gate_steps = Halving(gate_pair, orders)
    gate_moved = gate_steps.exchange()
    g_far = (shift_narrow(g_below[:q_rows], 1), shift_narrow(g_above[q_rows:], -1))
    down_steps.settle(down_moved)
    g_far = tie(g_far)
    grad_middle, turned_attn, grad_context, gain_two_grad = middle_back(
        mine_narrow, (own, g_above, g_far, g_below), middle, scale_two, cotangent,
        gain_two, w_out,
    )

    ffn_own, ffn_above, ffn_far_a, ffn_far_b, ffn_below = ffn
    ffn_far_a, ffn_far_b = tie((ffn_far_a, ffn_far_b), g_far)
    ffn_up, ffn_down = shift_narrow(ffn_far_a, 1), shift_narrow(ffn_far_b, -1)
    ffn_to = pass_on(ffn_above, ffn_below, ffn_up, ffn_down)
    grad_context, ffn_to, gate_moved = tie((grad_context, ffn_to, gate_moved))
    ffn_from_below, ffn_from_above = shift_narrow(ffn_to[0], 1), shift_narrow(ffn_to[1], -1)
    up_steps = Halving(tie(up_pair, gate_moved), orders)
    up_moved = up_steps.exchange()
    query_lin_grad, send, keep = attend_back(
        info, queries, grad_context, context, start, lse, cosine, sine, kv_pieces
    )
    query_lin_grad, send, keep, up_moved, ffn_from_below, ffn_from_above = tie(
        (query_lin_grad, send, keep, up_moved, ffn_from_below, ffn_from_above)
    )
    turned_attn = tie(turned_attn, send)
    turned_attn_other = swap_core(turned_attn)
    send_other, turned_attn_other = tie((swap_core(send), turned_attn_other))
    key_value = add_rounded(keep, send_other)
    ql_below, ql_above = shift_narrow(query_lin_grad, 1), shift_narrow(query_lin_grad, -1)
    spread = (2,) * len(chip_bits) + key_value.shape[2:]
    parts, axes = list(key_value.reshape((2,) + spread)), [list(chip_bits), list(chip_bits)]
    for step, bits_ in enumerate(zip(low_chip, chip_bits)):
        moved = []
        for part, bit in enumerate(bits_):
            axis = axes[part].index(bit)
            axes[part].remove(bit)
            moved.append(swap_wide(lax.index_in_dim(parts[part], 1, axis, keepdims=False), bit))
            parts[part] = lax.index_in_dim(parts[part], 0, axis, keepdims=False)
        if step == 0:
            moved, ql_below, ql_above = tie((moved, ql_below, ql_above))
            ql_far = (shift_narrow(ql_below[:half], 1), shift_narrow(ql_above[half:], -1))
        parts = [add_rounded(p, m) for p, m in zip(parts, moved)]
    key_part, value_part = parts
    n_narrow = lax.axis_size("narrow")
    pair = jnp.concatenate([key_part, value_part], axis=1)
    gate_steps.settle(gate_moved)
    up_steps.settle(up_moved)
    feed_steps = [down_steps, gate_steps, up_steps]
    pair, ql_far, joint = tie((pair, ql_far, join_sends(feed_steps)))
    joint_moved = [swap_wide(s, order[0]) for s, order in zip(joint, down_steps.orders)]
    partner = lax.ppermute(pair, "narrow", [(i, i ^ 1) for i in range(n_narrow)])
    pair = add_rounded(pair, partner)
    cross = lax.ppermute(pair, "narrow", [(i, n_narrow - 1 - i) for i in range(n_narrow)])
    cross, query_weights.near = tie((cross, query_weights.near))
    query_weights.fetch_far()
    late, bias = late_grads(head_s, query_lin_grad, pair, cross, cosine, sine)
    late_other = swap_core(late)
    n_hidden = w_down.shape[0]
    late_pair = weigh_late(
        mine_wide, slots, turned_attn, turned_attn_other, turned_two, turned_two_other,
        turned_one, turned_one_other, late, late_other,
    )
    late_pair, joint_moved = tie((late_pair, joint_moved))
    late_steps = Halving(late_pair, orders)
    late_moved = late_steps.exchange()
    query_weights.far = tie(query_weights.far, late_pair)
    query_weights.collect()
    query_mine = query_weights.whole(None, 1)
    query_other = swap_core(query_mine)
    late, ffn_from_below, ffn_from_above = tie((late, ffn_from_below, ffn_from_above), late_pair)
    out_rows = lax.dynamic_slice_in_dim(middle, narrow_index * (rows // 4), rows // 4, 0)
    out_rows = (
        out_rows + ffn_own.astype(f32) + ffn_from_below.astype(f32) + ffn_from_above.astype(f32)
    ).astype(bf16)
    o_below, o_above = shift_narrow(out_rows, 1), shift_narrow(out_rows, -1)
    grad_hidden_in, vectors = project_back(
        core_s, hidden_in, late, (ql_above, ql_far, ql_below), w_query, query_mine, query_other,
        key_projection, value_projection, gain_one, grad_middle, gain_two_grad, bias,
    )
    late_moved, vectors = tie((late_moved, vectors))
    late_steps.settle(late_moved)
    late_steps.rest()
    for bit in bits[::-1]:
        vectors = vectors + swap_wide(vectors, bit)
        if bit == 1:
            vectors, o_below, o_above = tie((vectors, o_below, o_above))
        if bit == 2:
            joint_moved = tie(joint_moved, vectors)
    feed_terms = finish_joint(feed_steps, joint_moved)
    down_sum, gate_sum, up_sum = finish(feed_terms, n_hidden)

    vectors = vectors[0]

    def own_part(first, size):
        return lax.dynamic_slice_in_dim(vectors, first + wide_index * (size // n_wide), size // n_wide)

    bias_at = 2 * width
    query_bias = vectors[bias_at : bias_at + n_query].reshape(heads, n_wide, -1)
    query_bias = lax.dynamic_index_in_dim(query_bias, wide_index, 1, keepdims=False)

    o_far = (shift_narrow(o_below[:q_rows], 1), shift_narrow(o_above[q_rows:], -1))
    output = in_rows(mine_narrow, (out_rows, o_above, o_far, o_below))

    out_sum, query_sum, key_sum, value_sum = finish_late(
        late_steps.terms, [n_query, n_query, kv_width, kv_width]
    )
    return (
        output,
        grad_hidden_in,
        own_part(0, width),
        query_sum,
        query_bias,
        key_sum,
        own_part(bias_at + n_query, kv_width),
        value_sum,
        own_part(bias_at + n_query + kv_width, kv_width),
        out_sum.T,
        own_part(width, width),
        gate_sum,
        up_sum,
        down_sum.T,
    )


def solution(mesh):
    placed = (
        P("wide", None),
        P("wide", None),
        P(),
        P("wide"),
        P(),
        P(None, "narrow"),
        P("narrow"),
        P(),
        P(),
        P(),
        P(),
        P("narrow", None),
        P(),
        P(None, "narrow"),
        P(None, "narrow"),
        P("narrow", None),
    )
    return jax.shard_map(
        on_device,
        mesh=mesh,
        in_specs=placed,
        out_specs=(
            P("wide", None),
            P("wide", None),
            P("wide"),
            P("wide", "narrow"),
            P("narrow", "wide"),
            P("wide", None),
            P("wide"),
            P("wide", None),
            P("wide"),
            P("narrow", "wide"),
            P("wide"),
            P("wide", "narrow"),
            P("wide", "narrow"),
            P("narrow", "wide"),
        ),
        check_vma=False,
    )
```

```python
import functools
import math

import jax
import jax.numpy as jnp
from jax import lax
from jax.experimental import pallas as pl
from jax.experimental.pallas import tpu as pltpu
from jax.sharding import PartitionSpec as P

QUERY_HEADS = 12
KEY_VALUE_HEADS = 2
HEAD_SIZE = 128
FLAG_ROWS = 16

eps = 1e-06
big_negative = -1e30
score_scale = 1.0 / math.sqrt(HEAD_SIZE)
log2_scale = score_scale * math.log2(math.e)

bf16 = jnp.bfloat16
f32 = jnp.float32
ANY = pl.BlockSpec(memory_space=pl.ANY)
VMEM = pl.BlockSpec(memory_space=pltpu.VMEM)
SMEM = pl.BlockSpec(memory_space=pltpu.SMEM)


def dot(a, b, dims=((1,), (0,))):
    return lax.dot_general(a, b, (dims, ((), ())), preferred_element_type=f32)


NT = ((1,), (1,))
TN = ((0,), (0,))


def swap_wide(array, bit):
    n = lax.axis_size("wide")
    return lax.ppermute(array, "wide", [(i, i ^ bit) for i in range(n)])


def shift_narrow(array, by):
    n = lax.axis_size("narrow")
    return lax.ppermute(array, "narrow", [(i, (i + by) % n) for i in range(n)])


def ring_gather(block):
    half = block.shape[0] // 2
    below = shift_narrow(block, 1)
    above = shift_narrow(block, -1)
    far_a = shift_narrow(below[:half], 1)
    far_b = shift_narrow(above[half:], -1)
    return [block, above, jnp.concatenate([far_a, far_b], axis=0), below]


def ring_scatter(parts):
    half = parts[0].shape[0] // 2
    add = lambda a, b: (a.astype(f32) + b.astype(f32)).astype(bf16)
    up = shift_narrow(parts[2][:half], 1)
    down = shift_narrow(parts[2][half:], -1)
    to_above = jnp.concatenate([add(parts[1][:half], up), parts[1][half:]], axis=0)
    to_below = jnp.concatenate([parts[3][:half], add(parts[3][half:], down)], axis=0)
    from_below = shift_narrow(to_above, 1)
    from_above = shift_narrow(to_below, -1)
    return parts[0].astype(f32) + from_below.astype(f32) + from_above.astype(f32)


def add_rounded(a, b):
    return (a.astype(f32) + b.astype(f32)).astype(bf16)


def tie(values, *gates):
    return lax.optimization_barrier((values, gates))[0]


class Halving:
    def __init__(self, pair, orders):
        self.sends, keeps = pair
        self.terms = [[k] for k in keeps]
        self.views = [[k] for k in keeps]
        self.orders = [list(o) for o in orders]

    def exchange(self):
        return [swap_wide(s, order.pop(0)) for s, order in zip(self.sends, self.orders)]

    def settle(self, received):
        for part in range(2):
            self.terms[part].append(received[part])
            self.views[part].append(received[part])
        if not self.orders[0]:
            return None
        n = self.views[0][0].shape[1]
        total = lambda terms: sum(t.astype(f32) for t in terms).astype(bf16)
        self.sends = [
            total([t[:, 1::2] for t in self.views[0]]),
            total([t[:, n // 2 :] for t in self.views[1]]),
        ]
        self.views = [
            [t[:, ::2] for t in self.views[0]],
            [t[:, : n // 2] for t in self.views[1]],
        ]
        return self.sends

    def rest(self):
        while self.orders[0]:
            self.settle(self.exchange())


def as_row(vector):
    return vector[...].astype(f32).reshape(1, -1)


def rope(value, cosine, signed_sine):
    return value * cosine + pltpu.roll(value, HEAD_SIZE // 2, 1) * signed_sine


def front_kernel(head, x, gain, wk, wv, bk, bv, cosine, sine, flags, acts_out, kv_out):
    rows = x.shape[0]
    of_head = lambda b: jnp.where(
        head[0] == 0, as_row(b)[:, :HEAD_SIZE], as_row(b)[:, HEAD_SIZE:]
    )
    xf = x[...].astype(f32)
    scale = lax.rsqrt(jnp.mean(xf * xf, axis=1, keepdims=True) + eps)
    acts = (xf * scale * as_row(gain)).astype(bf16)
    acts_out[...] = acts
    key = dot(acts, wk[...]) + of_head(bk)
    kv_out[:rows, :] = rope(key, cosine[...], sine[...]).astype(bf16)
    kv_out[rows : rows + FLAG_ROWS, :] = flags[...]
    kv_out[rows + FLAG_ROWS :, :] = (dot(acts, wv[...]) + of_head(bv)).astype(bf16)


def front(head, x, gain, wk, wv, bk, bv, cosine, sine, flags):
    rows, width = x.shape
    whole = lambda *shape: pl.BlockSpec(shape, lambda i, h: (0,) * len(shape))
    column = lambda r: pl.BlockSpec((r, HEAD_SIZE), lambda i, h: (0, h[0]))
    return pl.pallas_call(
        front_kernel,
        name="front",
        grid_spec=pltpu.PrefetchScalarGridSpec(
            num_scalar_prefetch=1,
            grid=(1,),
            in_specs=[
                whole(rows, width),
                whole(width),
                column(width),
                column(width),
                whole(*bk.shape),
                whole(*bv.shape),
                whole(rows, HEAD_SIZE),
                whole(rows, HEAD_SIZE),
                whole(FLAG_ROWS, HEAD_SIZE),
            ],
            out_specs=[
                whole(rows, width),
                whole(2 * rows + FLAG_ROWS, HEAD_SIZE),
            ],
        ),
        out_shape=[
            jax.ShapeDtypeStruct((rows, width), bf16),
            jax.ShapeDtypeStruct((2 * rows + FLAG_ROWS, HEAD_SIZE), bf16),
        ],
    )(head, x, gain, wk, wv, bk, bv, cosine, sine, flags)


def query_kernel(acts, cot, w, b, cosine, sine, out, turned):
    lin = dot(acts[...], w[...]) + as_row(b)
    for h in range(out.shape[1] // HEAD_SIZE):
        cols = slice(h * HEAD_SIZE, (h + 1) * HEAD_SIZE)
        out[:, cols] = rope(lin[:, cols], cosine[...], sine[...]).astype(bf16)
    turned[0] = jnp.transpose(cot[...])
    turned[1] = jnp.transpose(acts[...])


def project_queries(acts, cot, w, b, cosine, sine):
    rows, width = acts.shape
    return pl.pallas_call(
        query_kernel,
        name="queries",
        in_specs=[VMEM] * 6,
        out_specs=[VMEM, VMEM],
        out_shape=[
            jax.ShapeDtypeStruct((rows, w.shape[1]), bf16),
            jax.ShapeDtypeStruct((2, width, rows), bf16),
        ],
    )(acts, cot, w, b, cosine, sine)


def load_pieces(refs, slots, kbuf, vbuf, sem):
    copies = []
    keys, values = kbuf.shape[1], vbuf.shape[1]
    for ref, names in zip(refs, slots):
        for at, slot in enumerate(names):
            k_part = ref.at[at, pl.ds(0, keys)]
            v_part = ref.at[at, pl.ds(keys, values)]
            copies.append(pltpu.make_async_copy(k_part, kbuf.at[slot], sem.at[0, slot]))
            copies.append(pltpu.make_async_copy(v_part, vbuf.at[slot], sem.at[1, slot]))
    for copy in copies:
        copy.start()
    return copies


def key_codes(kbuf, slot, half, base, chunk):
    rows = kbuf.shape[1] - FLAG_ROWS
    per = chunk // HEAD_SIZE
    flags = jnp.transpose(kbuf[slot, rows:, :].astype(f32))
    columns = []
    for c in range(per):
        first = flags[:, c : c + 1]
        second = flags[:, per + c : per + c + 1]
        columns.append(jnp.where(half == 1, second, first))
    column = jnp.concatenate(columns, axis=0)
    index = base + lax.broadcasted_iota(jnp.int32, (chunk, 1), 0)
    return jnp.where(column > 0, index, -1)


def visible(codes, start, diagonal):
    seen = codes >= start
    if diagonal:
        shape = (codes.shape[0], start.shape[1])
        row = lax.broadcasted_iota(jnp.int32, shape, 0)
        col = lax.broadcasted_iota(jnp.int32, shape, 1)
        seen = (seen & (row < col)) | (row == col)
    return seen


def first_chunk(info, rows, chunk):
    base = info[0] * rows
    end = first = jnp.int32(0)
    for s in range(1, info.shape[0]):
        end = end + info[s]
        first = jnp.where(end <= base, end, first)
    return first // chunk


def forward_kernel(slots, info, q, start, *refs):
    kv_refs, refs = refs[: len(slots)], refs[len(slots) :]
    out, lse, kbuf, vbuf, sem, acc_s, m_s, l_s = refs
    rows = q.shape[0]
    heads = q.shape[1] // HEAD_SIZE
    chunk = rows // 2
    own = info[0]
    copies = load_pieces(kv_refs, slots, kbuf, vbuf, sem)
    for copy in copies:
        copy.wait()

    def tile(h, k, v, codes, lo, n, diagonal):
        qh = q[lo : lo + n, h * HEAD_SIZE : (h + 1) * HEAD_SIZE]
        s = dot(k, qh, NT) * log2_scale
        s = jnp.where(visible(codes, start[:, lo : lo + n], diagonal), s, big_negative)
        peak = jnp.max(s, axis=0, keepdims=True)
        cols = slice(lo, lo + n)
        if diagonal:
            p = jnp.exp2(s - peak)
            m_s[h : h + 1, cols] = peak
            l_s[h : h + 1, cols] = jnp.sum(p, axis=0, keepdims=True)
            acc_s[h, :, cols] = dot(v, p.astype(bf16), TN)
        else:
            old = m_s[h : h + 1, cols]
            new = jnp.maximum(old, peak)
            alpha = jnp.exp2(old - new)
            p = jnp.exp2(s - new)
            m_s[h : h + 1, cols] = new
            l_s[h : h + 1, cols] = alpha * l_s[h : h + 1, cols] + jnp.sum(p, axis=0, keepdims=True)
            acc_s[h, :, cols] = alpha * acc_s[h, :, cols] + dot(v, p.astype(bf16), TN)

    base = own * rows
    for half in (1, 0):
        k = kbuf[0, half * chunk : (half + 1) * chunk, :]
        v = vbuf[0, half * chunk : (half + 1) * chunk, :]
        codes = key_codes(kbuf, 0, half, base + half * chunk, chunk)
        for h in range(heads):
            tile(h, k, v, codes, half * chunk, chunk, True)
            if half == 0:
                tile(h, k, v, codes, chunk, chunk, False)

    def step(c, carry):
        block, half = c // 2, c % 2
        slot = lax.bitwise_xor(block, own)
        at = pl.multiple_of(half * chunk, chunk)
        k = kbuf[slot, pl.ds(at, chunk), :]
        v = vbuf[slot, pl.ds(at, chunk), :]
        codes = key_codes(kbuf, slot, half, c * chunk, chunk)
        for h in range(heads):
            tile(h, k, v, codes, 0, rows, False)
        return carry

    lax.fori_loop(first_chunk(info, rows, chunk), own * 2, step, 0)
    lse[...] = jnp.zeros_like(lse)
    for h in range(heads):
        total = l_s[h : h + 1, :]
        lse[h : h + 1, :] = m_s[h : h + 1, :] + jnp.log2(total)
        o = acc_s[h] * (1.0 / total)
        out[:, h * HEAD_SIZE : (h + 1) * HEAD_SIZE] = jnp.transpose(o).astype(bf16)


def attend(info, q, start, kv_pieces):
    rows, width = q.shape
    heads = width // HEAD_SIZE
    slots = sum(len(s) for s, _ in kv_pieces)
    return pl.pallas_call(
        functools.partial(forward_kernel, [s for s, _ in kv_pieces]),
        name="attend",
        in_specs=[SMEM, VMEM, VMEM] + [ANY] * len(kv_pieces),
        out_specs=[VMEM, VMEM],
        out_shape=[
            jax.ShapeDtypeStruct((rows, width), bf16),
            jax.ShapeDtypeStruct((8, rows), f32),
        ],
        scratch_shapes=[
            pltpu.VMEM((slots, rows + FLAG_ROWS, HEAD_SIZE), bf16),
            pltpu.VMEM((slots, rows, HEAD_SIZE), bf16),
            pltpu.SemaphoreType.DMA((2, slots)),
            pltpu.VMEM((heads, HEAD_SIZE, rows), f32),
            pltpu.VMEM((8, rows), f32),
            pltpu.VMEM((8, rows), f32),
        ],
    )(info, q, start, *[a for _, a in kv_pieces])


def backward_kernel(slots, info, q, do, ctx, start, lse, cosine, sine, *refs):
    kv_refs, refs = refs[: len(slots)], refs[len(slots) :]
    dq_out, send, keep, kbuf, vbuf, sem, dq_s, delta_s = refs
    rows = q.shape[0]
    heads = q.shape[1] // HEAD_SIZE
    chunk = rows // 2
    own = info[0]
    copies = load_pieces(kv_refs, slots, kbuf, vbuf, sem)
    send[...] = jnp.zeros_like(send)
    keep[...] = jnp.zeros_like(keep)
    for h in range(heads):
        cols = slice(h * HEAD_SIZE, (h + 1) * HEAD_SIZE)
        both = do[:, cols].astype(f32) * ctx[:, cols].astype(f32)
        delta_s[h : h + 1, :] = jnp.sum(jnp.transpose(both), axis=0, keepdims=True)
        dq_s[h] = jnp.zeros((HEAD_SIZE, rows), f32)
    for copy in copies:
        copy.wait()

    def tile(h, k, v, codes, lo, n, diagonal):
        cols = slice(lo, lo + n)
        qh = q[cols, h * HEAD_SIZE : (h + 1) * HEAD_SIZE]
        doh = do[cols, h * HEAD_SIZE : (h + 1) * HEAD_SIZE]
        s = dot(k, qh, NT) * log2_scale - lse[h : h + 1, cols]
        s = jnp.where(visible(codes, start[:, cols], diagonal), s, big_negative)
        p = jnp.exp2(s)
        dv = dot(p.astype(bf16), doh)
        ds = (p * (dot(v, doh, NT) - delta_s[h : h + 1, cols])).astype(bf16)
        dk = dot(ds, qh)
        dq_s[h, :, cols] = dq_s[h, :, cols] + dot(k, ds, TN)
        return dk, dv

    def both(h, k, v, codes, spans):
        dk = dv = None
        for lo, n, diagonal in spans:
            a, b = tile(h, k, v, codes, lo, n, diagonal)
            dk, dv = (a, b) if dk is None else (dk + a, dv + b)
        return dk, dv

    def all_heads(k, v, codes, spans):
        dk = dv = None
        for h in range(heads):
            a, b = both(h, k, v, codes, spans)
            dk, dv = (a, b) if dk is None else (dk + a, dv + b)
        return (dk * score_scale).astype(bf16), dv.astype(bf16)

    base = own * rows
    for half in (1, 0):
        span = slice(half * chunk, (half + 1) * chunk)
        codes = key_codes(kbuf, 0, half, base + half * chunk, chunk)
        spans = [(chunk, chunk, True)] if half else [(0, chunk, True), (chunk, chunk, False)]
        dk, dv = all_heads(kbuf[0, span, :], vbuf[0, span, :], codes, spans)
        keep[0, 0, span, :] = dk
        keep[1, 0, span, :] = dv

    def step(c, carry):
        block, half = c // 2, c % 2
        slot = lax.bitwise_xor(block, own)
        at = pl.multiple_of(half * chunk, chunk)
        k = kbuf[slot, pl.ds(at, chunk), :]
        v = vbuf[slot, pl.ds(at, chunk), :]
        codes = key_codes(kbuf, slot, half, c * chunk, chunk)
        dk, dv = all_heads(k, v, codes, [(0, rows, False)])

        @pl.when(slot % 2 == 0)
        def _():
            keep[0, slot // 2, pl.ds(at, chunk), :] = dk
            keep[1, slot // 2, pl.ds(at, chunk), :] = dv

        @pl.when(slot % 2 == 1)
        def _():
            send[0, slot // 2, pl.ds(at, chunk), :] = dk
            send[1, slot // 2, pl.ds(at, chunk), :] = dv

        return carry

    lax.fori_loop(first_chunk(info, rows, chunk), own * 2, step, 0)
    for h in range(heads):
        g = jnp.transpose(dq_s[h]) * score_scale
        back = g * cosine[...] - pltpu.roll(g, HEAD_SIZE // 2, 1) * sine[...]
        dq_out[:, h * HEAD_SIZE : (h + 1) * HEAD_SIZE] = back.astype(bf16)


def attend_back(info, q, do, ctx, start, lse, cosine, sine, kv_pieces):
    rows, width = q.shape
    heads = width // HEAD_SIZE
    slots = sum(len(s) for s, _ in kv_pieces)
    half = jax.ShapeDtypeStruct((2, slots // 2, rows, HEAD_SIZE), bf16)
    return pl.pallas_call(
        functools.partial(backward_kernel, [s for s, _ in kv_pieces]),
        name="attend_back",
        in_specs=[SMEM] + [VMEM] * 7 + [ANY] * len(kv_pieces),
        out_specs=[VMEM] * 3,
        out_shape=[jax.ShapeDtypeStruct((rows, width), bf16), half, half],
        scratch_shapes=[
            pltpu.VMEM((slots, rows + FLAG_ROWS, HEAD_SIZE), bf16),
            pltpu.VMEM((slots, rows, HEAD_SIZE), bf16),
            pltpu.SemaphoreType.DMA((2, slots)),
            pltpu.VMEM((heads, HEAD_SIZE, rows), f32),
            pltpu.VMEM((8, rows), f32),
        ],
    )(
        info, q, do, ctx, start, lse, cosine, sine,
        *[a for _, a in kv_pieces],
    )


def whole(shape):
    return pl.BlockSpec(shape, lambda *_: (0,) * len(shape))


def struct(shape, dtype):
    return jax.ShapeDtypeStruct(shape, dtype)


def project_out_kernel(
    core, x, own, above, fa, fb, below, w_own, mine, other, gain, middle, acts, turned, scale
):
    n = w_own.shape[0]
    width = x.shape[1]
    far = jnp.where(pl.program_id(0) == 0, fa[...].astype(f32), fb[...].astype(f32)).astype(bf16)
    part = lambda m: (
        dot(above[...], m[:n, :]) + dot(below[...], m[n : 2 * n, :]) + dot(far, m[2 * n :, :])
    )
    a, b = part(mine), part(other)
    first = core[0] == 0
    out = dot(own[...], w_own[...]) + jnp.concatenate(
        [jnp.where(first, a, b), jnp.where(first, b, a)], axis=1
    )
    mid = x[...].astype(f32) + out
    r = lax.rsqrt(jnp.mean(mid * mid, axis=1, keepdims=True) + eps)
    middle[...] = mid
    scale[...] = r
    normed = mid * r * as_row(gain)
    acts[...] = normed.astype(bf16)
    turned[:width, :] = jnp.transpose(normed.astype(bf16))
    turned[width:, :] = jnp.transpose(own[...])


def project_out(core, x, pieces, w_own, mine, other, gain):
    rows, width = x.shape
    n = w_own.shape[0]
    half = rows // 2
    own, above, (fa, fb), below = pieces
    block = lambda c: pl.BlockSpec((half, c), lambda i, s: (i, 0))
    return pl.pallas_call(
        project_out_kernel,
        name="project_out",
        grid_spec=pltpu.PrefetchScalarGridSpec(
            num_scalar_prefetch=1,
            grid=(2,),
            in_specs=[
                block(width), block(n), block(n), whole((half, n)), whole((half, n)), block(n),
                whole(w_own.shape), whole(mine.shape), whole(other.shape), whole(gain.shape),
            ],
            out_specs=[
                block(width), block(width),
                pl.BlockSpec((width + n, half), lambda i, s: (0, i)),
                block(1),
            ],
        ),
        out_shape=[
            struct((rows, width), f32), struct((rows, width), bf16),
            struct((width + n, rows), bf16), struct((rows, 1), f32),
        ],
    )(core, x, own, above, fa, fb, below, w_own, mine, other, gain)


def ring_blocks(acc, mine, outs):
    block = acc.shape[0] // 4
    own, above, far_a, far_b, below = outs

    def take(k, first, size):
        at = ((mine[0] + k) % 4) * block + first
        return acc[pl.ds(pl.multiple_of(at, size), size), :].astype(bf16)

    own[...] = take(0, 0, block)
    above[...] = take(1, 0, block)
    far_a[...] = take(2, 0, block // 2)
    far_b[...] = take(2, block // 2, block // 2)
    below[...] = take(3, 0, block)


def block_sizes(rows):
    return [rows // 4, rows // 4, rows // 8, rows // 8, rows // 4]


def feed_kernel(n, mine, acts, cot, wg, wu, wd, hidden, grads, *refs):
    outs, acc = refs[:-1], refs[-1]
    j = pl.program_id(0)
    tile = wg.shape[0]
    part = min(256, tile)
    for lo in range(0, tile, part):
        cols = slice(lo, lo + part)
        gate = dot(acts[...], wg[cols, :], NT)
        up = dot(acts[...], wu[cols, :], NT)
        g = dot(cot[...], wd[cols, :], NT)
        sig = 1.0 / (1.0 + jnp.exp(-gate))
        silu = gate * sig
        column = j * tile + lo + lax.broadcasted_iota(jnp.int32, (1, part), 1)
        keep = lambda v: jnp.where(column < n, v, 0.0).astype(bf16)
        hidden[:, cols] = keep(silu * up)
        grads[0, :, cols] = keep(g * up * (sig * (1.0 + gate * (1.0 - sig))))
        grads[1, :, cols] = keep(g * silu)
    steps = pl.cdiv(n, tile)
    back = lambda k: dot(grads[0, :, :k], wg[:k, :]) + dot(grads[1, :, :k], wu[:k, :])

    @pl.when(j == 0)
    def _():
        acc[...] = jnp.zeros_like(acc)

    @pl.when(j < steps - 1)
    def _():
        acc[...] = acc[...] + back(tile)

    @pl.when(j == steps - 1)
    def _():
        acc[...] = acc[...] + back(n - (steps - 1) * tile)

    @pl.when(j == steps - 1)
    def _():
        ring_blocks(acc, mine, outs)


def feed(mine, acts, cot, wg, wu, wd, tile=768):
    rows, width = acts.shape
    n = wg.shape[0]
    steps = pl.cdiv(n, tile)
    w_spec = pl.BlockSpec((tile, width), lambda j, s: (j, 0))
    sizes = block_sizes(rows)
    outs = pl.pallas_call(
        functools.partial(feed_kernel, n),
        name="feed",
        grid_spec=pltpu.PrefetchScalarGridSpec(
            num_scalar_prefetch=1,
            grid=(steps,),
            in_specs=[whole((rows, width)), whole((rows, width)), w_spec, w_spec, w_spec],
            out_specs=[
                pl.BlockSpec((rows, tile), lambda j, s: (0, j)),
                pl.BlockSpec((2, rows, tile), lambda j, s: (0, 0, j)),
            ]
            + [whole((r, width)) for r in sizes],
            scratch_shapes=[pltpu.VMEM((rows, width), f32)],
        ),
        out_shape=[struct((rows, steps * tile), bf16), struct((2, rows, steps * tile), bf16)]
        + [struct((r, width), bf16) for r in sizes],
    )(mine, acts, cot, wg, wu, wd)
    return outs[0], outs[1], outs[2:]


def stack_kernel(cut, *refs):
    count = 1 if cut is None else 2
    ins, outs = refs[:-count], refs[-count:]
    cut = outs[0].shape[0]
    done = 0
    for ref in ins:
        rows = ref.shape[0]
        head = min(max(cut - done, 0), rows)
        if head:
            outs[0][done : done + head, :] = ref[:head, :]
        if head < rows:
            at = done + head - cut
            outs[1][at : at + rows - head, :] = ref[head:, :]
        done += rows


def stack(arrays, cut):
    rows = sum(a.shape[0] for a in arrays)
    width = arrays[0].shape[1]
    sizes = [cut, rows - cut] if cut < rows else [rows]
    return pl.pallas_call(
        functools.partial(stack_kernel, cut if cut < rows else None),
        name="stack",
        in_specs=[VMEM] * len(arrays),
        out_specs=[VMEM] * len(sizes),
        out_shape=[struct((size, width), bf16) for size in sizes],
    )(*arrays)


def assemble_kernel(plan, chip, *refs):
    out = refs[-1]
    n = out.shape[0] // 3
    block = n // plan[0]
    for ref, (names, first) in zip(refs, plan[1]):
        rows = ref.shape[1]
        for at, name in enumerate(names):
            source = lax.bitwise_xor(chip[0], name)
            done = 0
            while done < rows:
                piece, inside = divmod(first + done, block)
                size = min(rows - done, block - inside)
                to = pl.multiple_of(piece * n + source * block + inside, 16)
                out[pl.ds(to, size), :] = ref[at, done : done + size, :]
                done += size


def assemble(chip, chips, parts):
    one = sum({first: a.shape[1] for _, first, a in parts}.values())
    plan = (chips, [(names, first) for names, first, _ in parts])
    return pl.pallas_call(
        functools.partial(assemble_kernel, plan),
        name="assemble",
        in_specs=[SMEM] + [VMEM] * len(parts),
        out_specs=VMEM,
        out_shape=struct((chips * one, parts[0][2].shape[2]), bf16),
    )(chip, *[a for _, _, a in parts])


def partial_kernel(mine, a, w, *refs):
    refs[-1][...] = dot(a[:, : w.shape[0]], w[...])
    ring_blocks(refs[-1], mine, refs[:-1])


def partial_rows(mine, a, w, tile=512):
    rows, columns = a.shape
    inner, width = w.shape
    sizes = block_sizes(rows)
    return pl.pallas_call(
        partial_kernel,
        name="partial_down",
        grid_spec=pltpu.PrefetchScalarGridSpec(
            num_scalar_prefetch=1,
            grid=(width // tile,),
            in_specs=[whole(a.shape), pl.BlockSpec((inner, tile), lambda j, s: (0, j))],
            out_specs=[pl.BlockSpec((r, tile), lambda j, s: (0, j)) for r in sizes],
            scratch_shapes=[pltpu.VMEM((rows, tile), f32)],
        ),
        out_shape=[struct((r, width), bf16) for r in sizes],
    )(mine, a, w)


def pass_on_kernel(above, below, up, down, to_above, to_below):
    to_above[...] = (above[...].astype(f32) + up[...].astype(f32)).astype(bf16)
    to_below[...] = (below[...].astype(f32) + down[...].astype(f32)).astype(bf16)


def pass_on(above, below, up, down):
    block = up.shape
    first = pl.BlockSpec(block, lambda i: (0, 0))
    second = pl.BlockSpec(block, lambda i: (1, 0))
    return pl.pallas_call(
        pass_on_kernel,
        name="pass_on",
        grid=(1,),
        in_specs=[first, second, first, first],
        out_specs=[first, second],
        out_shape=[struct(above.shape, bf16)] * 2,
        input_output_aliases={0: 0, 1: 1},
    )(above, below, up, down)


def halves_kernel(below, above, first, second):
    first[...] = below[...]
    second[...] = above[...]


def halves(below, above):
    rows, width = below.shape
    block = (rows // 2, width)
    first = pl.BlockSpec(block, lambda i: (0, 0))
    return pl.pallas_call(
        halves_kernel,
        name="halves",
        grid=(1,),
        in_specs=[first, pl.BlockSpec(block, lambda i: (1, 0))],
        out_specs=[first, first],
        out_shape=[struct(block, bf16)] * 2,
    )(below, above)


def far_hop(below, above, pair=None):
    first, second = halves(below, above) if pair is None else pair
    return shift_narrow(first, 1), shift_narrow(second, -1)


def weigh_kernel(slots, half, mine, a_own, a_other, b_own, b_other, *refs):
    send_a, keep_a, send_b, keep_b, lhs = refs
    rows = a_own.shape[1]
    block = 2 * half

    @pl.when(pl.program_id(0) == 0)
    def _():
        for s in range(slots):
            at = pl.multiple_of(lax.bitwise_xor(mine[0], 2 * s) * block, 16)
            lhs[s * block : (s + 1) * block, :rows] = a_own[pl.ds(at, block), :]
            lhs[s * block : (s + 1) * block, rows:] = a_other[pl.ds(at, block), :]

    g = dot(lhs[:, :rows], b_own[0]) + dot(lhs[:, rows:], b_other[0])
    place_slots(g, slots, half, 0, send_a, keep_a, send_b, keep_b)


def place_slots(g, slots, half, group, send_a, keep_a, send_b, keep_b):
    cols = slice(0, g.shape[1])
    for s in range(slots):
        first = g[2 * s * half : (2 * s + 1) * half].astype(bf16)
        second = g[(2 * s + 1) * half : (2 * s + 2) * half].astype(bf16)
        (send_a if s % 2 else keep_a)[group, s // 2, :, cols] = first
        (send_b if s >= slots // 2 else keep_b)[group, s % (slots // 2), :, cols] = second


def weigh(mine, slots, width, a_own, a_other, b_own, b_other, group=0, tile=768):
    rows = a_own.shape[-1]
    n = b_own.shape[2]
    if a_own.ndim == 3:
        a_spec = pl.BlockSpec((None, width, rows), lambda j, s: (0, 0, 0))
    else:
        a_spec = pl.BlockSpec((width, rows), lambda j, s: (0, 0))
    half = width // slots // 4
    b_spec = pl.BlockSpec((1, rows, tile), lambda j, s: (group, 0, j))
    out = pl.BlockSpec((1, slots // 2, half, tile), lambda j, s: (0, 0, 0, j))
    outs = pl.pallas_call(
        functools.partial(weigh_kernel, slots, half),
        name="weigh",
        grid_spec=pltpu.PrefetchScalarGridSpec(
            num_scalar_prefetch=1,
            grid=(pl.cdiv(n, tile),),
            in_specs=[a_spec, a_spec, b_spec, b_spec],
            out_specs=[out] * 4,
            scratch_shapes=[pltpu.VMEM((width // 2, 2 * rows), bf16)],
        ),
        out_shape=[struct((1, slots // 2, half, n), bf16)] * 4,
    )(mine, a_own, a_other, b_own, b_other)
    return [outs[0], outs[2]], [outs[1], outs[3]]


def weigh_late_kernel(
    slots, half, mine, t_own, t_other, c_own, c_other, a_own, a_other, b_own, b_other, *refs
):
    send_a, keep_a, send_b, keep_b = refs
    block = 2 * half

    def gather(ref):
        pieces = []
        for s in range(slots):
            at = pl.multiple_of(lax.bitwise_xor(mine[0], 2 * s) * block, 16)
            pieces.append(ref[pl.ds(at, block), :])
        return jnp.concatenate(pieces, axis=0)

    n = c_own.shape[0]
    g = dot(gather(t_own), c_own[...], NT) + dot(gather(t_other), c_other[...], NT)
    late = dot(gather(a_own), b_own[...]) + dot(gather(a_other), b_other[...])
    g = jnp.concatenate([g, late], axis=1)
    place_slots(g, slots, half, 0, send_a, keep_a, send_b, keep_b)


def weigh_late(mine, slots, t_own, t_other, c_own, c_other, a_own, a_other, b_own, b_other):
    width, rows = t_own.shape
    n = c_own.shape[0] - width
    half = width // slots // 4
    total = n + b_own.shape[1]
    t_spec = whole((width, rows))
    c_spec = pl.BlockSpec((n, rows), lambda i, s: (width // n, 0))
    a_spec = pl.BlockSpec((None, width, rows), lambda i, s: (1, 0, 0))
    b_spec = whole(b_own.shape)
    shape = (1, slots // 2, half, total)
    outs = pl.pallas_call(
        functools.partial(weigh_late_kernel, slots, half),
        name="weigh_late",
        grid_spec=pltpu.PrefetchScalarGridSpec(
            num_scalar_prefetch=1,
            grid=(1,),
            in_specs=[t_spec, t_spec, c_spec, c_spec, a_spec, a_spec, b_spec, b_spec],
            out_specs=[whole(shape)] * 4,
        ),
        out_shape=[struct(shape, bf16)] * 4,
    )(mine, t_own, t_other, c_own, c_other, a_own, a_other, b_own, b_other)
    return [outs[0], outs[2]], [outs[1], outs[3]]


def total_of(refs, cols):
    total = None
    for t in refs:
        value = t[0, 0, :, cols].astype(f32)
        total = value if total is None else total + value
    return total


def finish_kernel(n, *refs):
    outs = refs[2 * n * (len(refs) // (2 * n + 1)) :]
    for g, out in enumerate(outs):
        half = out.shape[0] // 2
        for part in range(2):
            first = (2 * g + part) * n
            total = total_of(refs[first : first + n], slice(0, out.shape[1]))
            out[part * half : (part + 1) * half, :] = total


def finish(all_terms, columns):
    flat = [t for terms in all_terms for part in terms for t in part]
    _, _, half, width = flat[0][0].shape
    at = lambda g: pl.BlockSpec((1, 1, half, width), lambda i: (g, 0, 0, 0))
    groups = len(all_terms)
    return pl.pallas_call(
        functools.partial(finish_kernel, len(all_terms[0][0])),
        name="finish",
        grid=(1,),
        in_specs=[at(g) for _, g in flat],
        out_specs=[whole((2 * half, columns))] * groups,
        out_shape=[struct((2 * half, columns), f32)] * groups,
    )(*[a for a, _ in flat])


def finish_late_kernel(n, count, *refs):
    terms, outs = refs[:-count], refs[-count:]
    half = outs[0].shape[0] // 2
    for part in range(2):
        at = 0
        for out in outs:
            cols = slice(at, at + out.shape[1])
            total = total_of(terms[part * n : (part + 1) * n], cols)
            out[part * half : (part + 1) * half, :] = total
            at += out.shape[1]


def finish_late(terms, sizes):
    flat = terms[0] + terms[1]
    _, _, half, columns = flat[0].shape
    return pl.pallas_call(
        functools.partial(finish_late_kernel, len(terms[0]), len(sizes)),
        name="finish_late",
        grid=(1,),
        in_specs=[whole((1, 1, half, columns))] * len(flat),
        out_specs=[whole((2 * half, size)) for size in sizes],
        out_shape=[struct((2 * half, size), f32) for size in sizes],
    )(*flat)


def middle_back_kernel(
    mine, own, above, fa, fb, below, middle, scale, cot, gain, w_out,
    grad_middle, turned, grad_context, gain_grad, g_s,
):
    k = pl.program_id(0)
    half = fa.shape[0]
    for at, ref in ((0, own), (1, above), (3, below)):
        @pl.when(k == at)
        def _():
            g_s[...] = ref[...].astype(f32)

    @pl.when(k == 2)
    def _():
        g_s[:half, :] = fa[...].astype(f32)
        g_s[half:, :] = fb[...].astype(f32)

    g = g_s[...]
    r = scale[...]
    n2 = middle[...] * r
    u2 = g * as_row(gain)
    gm = cot[...].astype(f32) + r * (u2 - n2 * jnp.mean(u2 * n2, axis=1, keepdims=True))
    part = jnp.sum(g * n2, axis=0, keepdims=True)

    @pl.when(k == 0)
    def _():
        gain_grad[...] = part

    @pl.when(k > 0)
    def _():
        gain_grad[...] = gain_grad[...] + part

    grad_middle[...] = gm
    turned[...] = jnp.transpose(gm.astype(bf16))
    grad_context[...] = dot(gm.astype(bf16), w_out[...], NT).astype(bf16)


def middle_back(mine, pieces, middle, scale, cot, gain, w_out):
    rows, width = middle.shape
    block = rows // 4
    own, above, (fa, fb), below = pieces
    at = lambda c: pl.BlockSpec((block, c), lambda k, s: ((s[0] + k) % 4, 0))
    n = w_out.shape[0]
    return pl.pallas_call(
        middle_back_kernel,
        name="middle_back",
        grid_spec=pltpu.PrefetchScalarGridSpec(
            num_scalar_prefetch=1,
            grid=(4,),
            in_specs=[
                whole((block, width)), whole((block, width)),
                whole((block // 2, width)), whole((block // 2, width)), whole((block, width)),
                at(width), at(1), at(width), whole(gain.shape), whole(w_out.shape),
            ],
            out_specs=[
                at(width),
                pl.BlockSpec((width, block), lambda k, s: (0, (s[0] + k) % 4)),
                at(n),
                whole((1, width)),
            ],
            scratch_shapes=[pltpu.VMEM((block, width), f32)],
        ),
        out_shape=[
            struct((rows, width), f32), struct((width, rows), bf16),
            struct((rows, n), bf16), struct((1, width), f32),
        ],
    )(mine, own, above, fa, fb, below, middle, scale, cot, gain, w_out)


def in_rows_kernel(mine, own, above, fa, fb, below, out):
    block = own.shape[0]
    at = lambda k: pl.ds(pl.multiple_of((mine[0] + k) % 4 * block, block), block)
    out[at(0), :] = own[...]
    out[at(1), :] = above[...]
    out[at(2), :] = jnp.concatenate([fa[...], fb[...]], axis=0)
    out[at(3), :] = below[...]


def in_rows(mine, pieces):
    own, above, (fa, fb), below = pieces
    rows, width = own.shape
    return pl.pallas_call(
        in_rows_kernel,
        name="in_rows",
        in_specs=[SMEM] + [VMEM] * 5,
        out_specs=VMEM,
        out_shape=struct((4 * rows, width), bf16),
    )(mine, own, above, fa, fb, below)


def late_kernel(head, q, pair, cross, cosine, sine, late, bias):
    rows, n = q.shape
    kv = KEY_VALUE_HEADS * HEAD_SIZE

    def lin(ref):
        g = ref[:, :HEAD_SIZE].astype(f32)
        key = g * cosine[...] - pltpu.roll(g, HEAD_SIZE // 2, 1) * sine[...]
        return key, ref[:, HEAD_SIZE:].astype(f32)

    (own_k, own_v), (other_k, other_v) = lin(pair), lin(cross)
    first = head[0] == 0
    late[:, :n] = q[...]
    columns = [
        jnp.where(first, own_k, other_k), jnp.where(first, other_k, own_k),
        jnp.where(first, own_v, other_v), jnp.where(first, other_v, own_v),
    ]
    for c, value in enumerate(columns):
        late[:, n + c * HEAD_SIZE : n + (c + 1) * HEAD_SIZE] = value.astype(bf16)
    bias[...] = jnp.sum(late[...].astype(f32), axis=0, keepdims=True)


def late_grads(head, q, pair, cross, cosine, sine):
    rows, n = q.shape
    total = n + 2 * KEY_VALUE_HEADS * HEAD_SIZE
    return pl.pallas_call(
        late_kernel,
        name="late_grads",
        in_specs=[SMEM] + [VMEM] * 5,
        out_specs=[VMEM] * 2,
        out_shape=[struct((rows, total), bf16), struct((1, total), f32)],
    )(head, q, pair, cross, cosine, sine)


def project_back_kernel(
    core, x, late, above, fa, fb, below, w_own, mine, other, wk, wv, gain, grad_middle,
    gain_two_grad, bias, out, vectors,
):
    i = pl.program_id(0)
    n = w_own.shape[1]
    kv = wk.shape[1]
    far = jnp.where(i == 0, fa[...].astype(f32), fb[...].astype(f32)).astype(bf16)
    part = lambda m: (
        dot(above[...], m[:n, :]) + dot(below[...], m[n : 2 * n, :]) + dot(far, m[2 * n :, :])
    )
    a, b = part(mine), part(other)
    first = core[0] == 0
    g = jnp.concatenate([jnp.where(first, a, b), jnp.where(first, b, a)], axis=1)
    g = g + dot(late[:, :n], w_own[...], NT)
    g = g + dot(late[:, n : n + kv], wk[...], NT) + dot(late[:, n + kv :], wv[...], NT)
    xf = x[...].astype(f32)
    r = lax.rsqrt(jnp.mean(xf * xf, axis=1, keepdims=True) + eps)
    n1 = xf * r
    u1 = g * as_row(gain)
    out[...] = (
        grad_middle[...] + r * (u1 - n1 * jnp.mean(u1 * n1, axis=1, keepdims=True))
    ).astype(bf16)
    total = jnp.sum(g * n1, axis=0, keepdims=True)
    width = x.shape[1]

    @pl.when(i == 0)
    def _():
        vectors[:, :width] = total
        vectors[:, width : 2 * width] = gain_two_grad[...]
        vectors[:, 2 * width :] = bias[...]

    @pl.when(i > 0)
    def _():
        vectors[:, :width] = vectors[:, :width] + total


def project_back(
    core, x, late, pieces, w_own, mine, other, wk, wv, gain, grad_middle, gain_two_grad, bias
):
    rows, width = x.shape
    n = w_own.shape[1]
    half = rows // 2
    above, (fa, fb), below = pieces
    block = lambda c: pl.BlockSpec((half, c), lambda i, s: (i, 0))
    return pl.pallas_call(
        project_back_kernel,
        name="project_back",
        grid_spec=pltpu.PrefetchScalarGridSpec(
            num_scalar_prefetch=1,
            grid=(2,),
            in_specs=[
                block(width), block(late.shape[1]), block(n), whole((half, n)), whole((half, n)),
                block(n), whole(w_own.shape), whole(mine.shape), whole(other.shape),
                whole(wk.shape), whole(wv.shape), whole(gain.shape), block(width),
                whole(gain_two_grad.shape), whole(bias.shape),
            ],
            out_specs=[block(width), whole((1, 2 * width + bias.shape[1]))],
        ),
        out_shape=[struct((rows, width), bf16), struct((1, 2 * width + bias.shape[1]), f32)],
    )(
        core, x, late, above, fa, fb, below, w_own, mine, other, wk, wv, gain, grad_middle,
        gain_two_grad, bias,
    )


class Spread:
    def __init__(self, share, orders):
        self.share = share
        self.half = share.shape[0] // 2
        self.orders = [list(o) for o in orders]
        self.near = [shift_narrow(share, 1), shift_narrow(share, -1)]

    def fetch_far(self):
        self.far = list(far_hop(*self.near, getattr(self, "pair", None)))

    def collect(self):
        below, above = self.near
        pieces = [above, below] + self.far
        if not self.orders:
            (self.rows,) = stack(pieces, 6 * self.half)
            return
        rows = 6 * self.half
        self.cut = rows // len(self.orders)
        self.names = [[(0,)] for _ in self.orders]
        self.arrays = [[part[None]] for part in stack(pieces, self.cut)]

    def hop(self):
        if not self.orders or not self.orders[0]:
            return
        for part, order in enumerate(self.orders):
            bit = order.pop(0)
            held = self.arrays[part]
            payload = held[0] if len(held) == 1 else jnp.concatenate(held, axis=0)
            names = tuple(s ^ (bit >> 1) for group in self.names[part] for s in group)
            self.names[part].append(names)
            held.append(swap_wide(payload, bit))

    def whole(self, chip, chips):
        if not hasattr(self, "arrays"):
            return self.rows
        while self.orders[0]:
            self.hop()
        parts = []
        for part in range(len(self.orders)):
            for names, array in zip(self.names[part], self.arrays[part]):
                parts.append((names, part * self.cut, array))
        return assemble(chip, chips, parts)


def join_kernel(*refs):
    ins, outs = refs[:-2], refs[-2:]
    for part, out in enumerate(outs):
        for g in range(out.shape[0]):
            a, b = ins[4 * g + 2 * part], ins[4 * g + 2 * part + 1]
            out[g, 0] = (a[0, 0].astype(f32) + b[0, 0].astype(f32)).astype(bf16)


def join_sends(steps):
    slots = steps[0].views[0][0].shape[1]
    if slots != 1 or len(steps[0].terms[0]) != 2:
        return [jnp.concatenate([s.sends[part] for s in steps], axis=0) for part in range(2)]
    flat = [t for s in steps for terms in s.terms for t in terms]
    _, _, rows, columns = flat[0].shape
    shape = (len(steps), 1, rows, columns)
    return pl.pallas_call(
        join_kernel,
        name="join",
        grid=(1,),
        in_specs=[pl.BlockSpec((1, 1, rows, columns), lambda i: (0, 1, 0, 0))] * len(flat),
        out_specs=[whole(shape)] * 2,
        out_shape=[struct(shape, bf16)] * 2,
    )(*flat)


def finish_joint(steps, received):
    for s in steps:
        for order in s.orders:
            order.pop(0)
    if not steps[0].orders[0]:
        return [
            [[(t, 0) for t in s.terms[part]] + [(received[part], g)] for part in range(2)]
            for g, s in enumerate(steps)
        ]
    for g, s in enumerate(steps):
        s.settle([r[g : g + 1] for r in received])
        s.rest()
    return [[[(t, 0) for t in terms] for terms in s.terms] for s in steps]


def place_tokens(index, lengths):
    ends = jnp.cumsum(lengths)
    before = (ends[None, :] <= index[:, None]).astype(jnp.int32)
    return index - jnp.sum(before * lengths[None, :], axis=1)


def on_device(
    hidden_in,
    cotangent,
    lengths,
    valid,
    gain_one,
    w_query,
    b_query,
    key_projection,
    key_bias_vector,
    value_projection,
    value_bias_vector,
    w_out,
    gain_two,
    w_gate,
    w_up,
    w_down,
):
    rows, width = hidden_in.shape
    n_wide = lax.axis_size("wide")
    wide_index = lax.axis_index("wide")
    narrow_index = lax.axis_index("narrow")
    heads = w_query.shape[1] // HEAD_SIZE
    n_query = heads * HEAD_SIZE
    kv_width = KEY_VALUE_HEADS * HEAD_SIZE
    head = narrow_index * heads // (QUERY_HEADS // KEY_VALUE_HEADS)
    bits = [1 << b for b in reversed(range(n_wide.bit_length() - 1))]
    chip_bits = bits[:-1]
    low_chip = chip_bits[::-1]
    slots = n_wide // 2
    core = wide_index % 2
    base = wide_index * rows
    as_scalar = lambda v: v.astype(jnp.int32).reshape(1)
    mine_wide, mine_narrow, core_s, head_s = map(
        as_scalar, (wide_index, narrow_index, core, head)
    )
    swap_core = lambda v: swap_wide(v, 1)

    token_index = base + jnp.arange(rows, dtype=jnp.int32)
    positions = place_tokens(token_index, lengths)
    start = (token_index - positions)[None, :]
    info = jnp.concatenate([mine_wide, lengths])
    freqs = 10000.0 ** (-(jnp.arange(HEAD_SIZE // 2, dtype=f32) * 2.0) / HEAD_SIZE)
    angles = positions.astype(f32)[:, None] * freqs[None, :]
    cos_half, sin_half = jnp.cos(angles), jnp.sin(angles)
    cosine = jnp.concatenate([cos_half, cos_half], axis=1)
    sine = jnp.concatenate([-sin_half, sin_half], axis=1)

    flags = jnp.pad(
        valid.astype(bf16).reshape(rows // HEAD_SIZE, HEAD_SIZE),
        ((0, FLAG_ROWS - rows // HEAD_SIZE), (0, 0)),
    )
    acts_one, kv_own = front(
        head_s,
        hidden_in,
        gain_one,
        key_projection,
        value_projection,
        key_bias_vector,
        value_bias_vector,
        cosine,
        sine,
        flags,
    )

    col = width // 2
    n_half = n_query // 2
    split = n_query // slots % 32 == 0
    share = n_query // slots if split else n_query
    at = wide_index // 2 * share if split else 0
    half_query = lax.dynamic_slice_in_dim(w_query, core * col, col, 0).T
    half_out = lax.dynamic_slice(w_out, (at, core * col), (share, col))
    out_weights = Spread(half_out, [low_chip, chip_bits] if split else [])

    kv_slots, kv_arrays = [(0,)], [kv_own[None]]
    for step, bit in enumerate(bits):
        send = kv_arrays[0] if step == 0 else jnp.concatenate(kv_arrays, axis=0)
        if step == 1:
            send, out_weights.near = tie((send, out_weights.near))
            out_weights.fetch_far()
        if step + 1 == len(bits):
            send, queries, half_query, out_weights.far = tie(
                (send, queries, half_query, out_weights.far)
            )
            out_weights.collect()
            out_weights.hop()
        kv_arrays.append(swap_wide(send, bit))
        kv_slots.append(tuple(s ^ bit for group in kv_slots for s in group))
        if step == 0:
            acts_late = tie(acts_one, kv_arrays[1])
            queries, turned_one = project_queries(
                acts_late, cotangent, w_query, b_query, cosine, sine
            )
    kv_pieces = list(zip(kv_slots, kv_arrays))
    context, lse = attend(info, queries, start, kv_pieces)
    if split:
        context, out_weights.arrays = tie((context, out_weights.arrays))

    half = rows // 2
    ctx_below, ctx_above = shift_narrow(context, 1), shift_narrow(context, -1)
    out_mine = out_weights.whole(as_scalar(wide_index // 2), slots)
    out_mine, ctx_below, ctx_above = tie((out_mine, ctx_below, ctx_above))
    out_other = swap_core(out_mine)
    ctx_far = far_hop(ctx_below, ctx_above)
    turned_one_other = swap_core(turned_one)
    ctx_far, half_query = tie((ctx_far, half_query), turned_one_other, out_other)
    w_gate_t, w_up_t = w_gate.T, w_up.T
    middle, acts_two, turned_two, scale_two = project_out(
        core_s, hidden_in, (context, ctx_above, ctx_far, ctx_below),
        w_out, out_mine, out_other, gain_two,
    )

    query_weights = Spread(half_query, [])
    hidden, grads, blocks = feed(
        mine_narrow, acts_two, cotangent, w_gate_t, w_up_t, w_down
    )
    turned_two_other = swap_core(tie(turned_two, acts_two))
    (hidden, grads, blocks), query_weights.near = tie(
        ((hidden, grads, blocks), query_weights.near), turned_two_other
    )
    own, above, far_a, far_b, below = blocks
    up, down = shift_narrow(far_a, 1), shift_narrow(far_b, -1)
    hidden_other = swap_core(hidden)
    up, down, hidden_other = tie((up, down, hidden_other))
    grads_other = swap_core(tie(grads, up, down))
    to_above, to_below = pass_on(above, below, up, down)
    from_below, from_above = shift_narrow(to_above, 1), shift_narrow(to_below, -1)
    hidden_here = tie(hidden, to_above, to_below)
    down_pair = weigh(
        mine_wide, slots, width, turned_one, turned_one_other, hidden_here[None],
        hidden_other[None],
    )
    ffn = partial_rows(mine_narrow, hidden_here, w_down)
    from_below, from_above, grads, grads_other, down_pair, ffn = tie(
        (from_below, from_above, grads, grads_other, down_pair, ffn)
    )
    orders = (low_chip, chip_bits)
    down_steps = Halving(down_pair, orders)
    down_moved = down_steps.exchange()
    own = (own.astype(f32) + from_below.astype(f32) + from_above.astype(f32)).astype(bf16)
    q_rows = rows // 8
    g_below, g_above = shift_narrow(own, 1), shift_narrow(own, -1)
    grads_here = tie(grads, own)
    gate_pair, up_pair = [
        weigh(mine_wide, slots, width, turned_two, turned_two_other, grads_here, grads_other, k)
        for k in range(2)
    ]
    g_below, g_above, gate_pair, up_pair, down_moved = tie(
        (g_below, g_above, gate_pair, up_pair, down_moved)
    )
    gate_steps = Halving(gate_pair, orders)
    gate_moved = gate_steps.exchange()
    g_far = far_hop(g_below, g_above)
    down_steps.settle(down_moved)
    g_far = tie(g_far)
    grad_middle, turned_attn, grad_context, gain_two_grad = middle_back(
        mine_narrow, (own, g_above, g_far, g_below), middle, scale_two, cotangent,
        gain_two, w_out,
    )

    ffn_own, ffn_above, ffn_far_a, ffn_far_b, ffn_below = ffn
    ffn_far_a, ffn_far_b = tie((ffn_far_a, ffn_far_b), g_far)
    ffn_up, ffn_down = shift_narrow(ffn_far_a, 1), shift_narrow(ffn_far_b, -1)
    ffn_to = pass_on(ffn_above, ffn_below, ffn_up, ffn_down)
    grad_context, ffn_to, gate_moved = tie((grad_context, ffn_to, gate_moved))
    ffn_from_below, ffn_from_above = shift_narrow(ffn_to[0], 1), shift_narrow(ffn_to[1], -1)
    up_steps = Halving(tie(up_pair, gate_moved), orders)
    up_moved = up_steps.exchange()
    query_lin_grad, send, keep = attend_back(
        info, queries, grad_context, context, start, lse, cosine, sine, kv_pieces
    )
    query_lin_grad, send, keep, up_moved, ffn_from_below, ffn_from_above = tie(
        (query_lin_grad, send, keep, up_moved, ffn_from_below, ffn_from_above)
    )
    turned_attn = tie(turned_attn, send)
    turned_attn_other = swap_core(turned_attn)
    send_other, turned_attn_other = tie((swap_core(send), turned_attn_other))
    key_value = add_rounded(keep, send_other)
    ql_below, ql_above = shift_narrow(query_lin_grad, 1), shift_narrow(query_lin_grad, -1)
    spread = (2,) * len(chip_bits) + key_value.shape[2:]
    parts, axes = list(key_value.reshape((2,) + spread)), [list(chip_bits), list(chip_bits)]
    for step, bits_ in enumerate(zip(low_chip, chip_bits)):
        moved = []
        for part, bit in enumerate(bits_):
            axis = axes[part].index(bit)
            axes[part].remove(bit)
            moved.append(swap_wide(lax.index_in_dim(parts[part], 1, axis, keepdims=False), bit))
            parts[part] = lax.index_in_dim(parts[part], 0, axis, keepdims=False)
        if step == 0:
            moved, ql_below, ql_above = tie((moved, ql_below, ql_above))
            ql_far = far_hop(ql_below, ql_above)
        parts = [add_rounded(p, m) for p, m in zip(parts, moved)]
    key_part, value_part = parts
    n_narrow = lax.axis_size("narrow")
    pair = jnp.concatenate([key_part, value_part], axis=1)
    gate_steps.settle(gate_moved)
    up_steps.settle(up_moved)
    feed_steps = [down_steps, gate_steps, up_steps]
    pair, ql_far, joint = tie((pair, ql_far, join_sends(feed_steps)))
    joint_moved = [swap_wide(s, order[0]) for s, order in zip(joint, down_steps.orders)]
    partner = lax.ppermute(pair, "narrow", [(i, i ^ 1) for i in range(n_narrow)])
    pair = add_rounded(pair, partner)
    cross = lax.ppermute(pair, "narrow", [(i, n_narrow - 1 - i) for i in range(n_narrow)])
    query_weights.pair = halves(*query_weights.near)
    cross, query_weights.pair = tie((cross, query_weights.pair))
    query_weights.fetch_far()
    late, bias = late_grads(head_s, query_lin_grad, pair, cross, cosine, sine)
    late_other = swap_core(late)
    n_hidden = w_down.shape[0]
    late_pair = weigh_late(
        mine_wide, slots, turned_attn, turned_attn_other, turned_two, turned_two_other,
        turned_one, turned_one_other, late, late_other,
    )
    late_pair, joint_moved = tie((late_pair, joint_moved))
    late_steps = Halving(late_pair, orders)
    late_moved = late_steps.exchange()
    query_weights.far = tie(query_weights.far, late_pair)
    query_weights.collect()
    query_mine = query_weights.whole(None, 1)
    query_other = swap_core(query_mine)
    late, ffn_from_below, ffn_from_above = tie((late, ffn_from_below, ffn_from_above), late_pair)
    out_rows = lax.dynamic_slice_in_dim(middle, narrow_index * (rows // 4), rows // 4, 0)
    out_rows = (
        out_rows + ffn_own.astype(f32) + ffn_from_below.astype(f32) + ffn_from_above.astype(f32)
    ).astype(bf16)
    o_below, o_above = shift_narrow(out_rows, 1), shift_narrow(out_rows, -1)
    grad_hidden_in, vectors = project_back(
        core_s, hidden_in, late, (ql_above, ql_far, ql_below), w_query, query_mine, query_other,
        key_projection, value_projection, gain_one, grad_middle, gain_two_grad, bias,
    )
    late_moved, vectors = tie((late_moved, vectors))
    late_steps.settle(late_moved)
    late_steps.rest()
    for bit in bits[::-1]:
        vectors = vectors + swap_wide(vectors, bit)
        if bit == 1:
            vectors, o_below, o_above = tie((vectors, o_below, o_above))
        if bit == 2:
            joint_moved = tie(joint_moved, vectors)
    feed_terms = finish_joint(feed_steps, joint_moved)
    down_sum, gate_sum, up_sum = finish(feed_terms, n_hidden)

    vectors = vectors[0]

    def own_part(first, size):
        return lax.dynamic_slice_in_dim(vectors, first + wide_index * (size // n_wide), size // n_wide)

    bias_at = 2 * width
    query_bias = vectors[bias_at : bias_at + n_query].reshape(heads, n_wide, -1)
    query_bias = lax.dynamic_index_in_dim(query_bias, wide_index, 1, keepdims=False)

    o_far = far_hop(o_below, o_above)
    output = in_rows(mine_narrow, (out_rows, o_above, o_far, o_below))

    out_sum, query_sum, key_sum, value_sum = finish_late(
        late_steps.terms, [n_query, n_query, kv_width, kv_width]
    )
    return (
        output,
        grad_hidden_in,
        own_part(0, width),
        query_sum,
        query_bias,
        key_sum,
        own_part(bias_at + n_query, kv_width),
        value_sum,
        own_part(bias_at + n_query + kv_width, kv_width),
        out_sum.T,
        own_part(width, width),
        gate_sum,
        up_sum,
        down_sum.T,
    )


def solution(mesh):
    placed = (
        P("wide", None),
        P("wide", None),
        P(),
        P("wide"),
        P(),
        P(None, "narrow"),
        P("narrow"),
        P(),
        P(),
        P(),
        P(),
        P("narrow", None),
        P(),
        P(None, "narrow"),
        P(None, "narrow"),
        P("narrow", None),
    )
    return jax.shard_map(
        on_device,
        mesh=mesh,
        in_specs=placed,
        out_specs=(
            P("wide", None),
            P("wide", None),
            P("wide"),
            P("wide", "narrow"),
            P("narrow", "wide"),
            P("wide", None),
            P("wide"),
            P("wide", None),
            P("wide"),
            P("narrow", "wide"),
            P("wide"),
            P("wide", "narrow"),
            P("wide", "narrow"),
            P("narrow", "wide"),
        ),
        check_vma=False,
    )
```
